32 devices in a mesh: seq: 2 (over y), fsdp: 16 (over z, x, core).
Axes of the slice: x: 2, y: 2, z: 4, core: 2. Of those that a mesh axis runs over, the one named last changes fastest.
Arguments:
- inputs: bfloat16 [16, 512, 1536], P('fsdp', 'seq'), may hold values from -6 to 6
- segment_ids: int32 [16, 512], P('fsdp'), may hold values from 0 to 3, never falling along the last dimension, each value on 1 to 256 neighbouring positions
- attn_gain: bfloat16 [1536], P(('seq', 'fsdp')), may hold values from 0.5 to 1.5
- q_weight: bfloat16 [1536, 1536], P(('seq', 'fsdp')), may hold values from -0.15625 to 0.15625
- k_weight: bfloat16 [1536, 256], P(('seq', 'fsdp')), may hold values from -0.15625 to 0.15625
- v_weight: bfloat16 [1536, 256], P(('seq', 'fsdp')), may hold values from -0.15625 to 0.15625
- qkv_bias: bfloat16 [2048], P(('seq', 'fsdp')), may hold values from -3 to 3
- o_weight: bfloat16 [1536, 1536], P(('seq', 'fsdp')), may hold values from -1.5 to 1.5
- mlp_gain: bfloat16 [1536], P(('seq', 'fsdp')), may hold values from 0.5 to 1.5
- gate_weight: bfloat16 [1536, 8960], P(('seq', 'fsdp')), may hold values from -0.15625 to 0.15625
- up_weight: bfloat16 [1536, 8960], P(('seq', 'fsdp')), may hold values from -0.15625 to 0.15625
- down_weight: bfloat16 [8960, 1536], P(('seq', 'fsdp')), may hold values from -0.0625 to 0.0625
- cotangent: bfloat16 [16, 512, 1536], P('fsdp', 'seq'), may hold values from -6 to 6
Outputs:
- output: bfloat16 [16, 512, 1536], P('fsdp', 'seq')
- input_grad: bfloat16 [16, 512, 1536], P('fsdp', 'seq')
- attn_gain_grad: float32 [1536], P(('seq', 'fsdp'))
- q_weight_grad: float32 [1536, 1536], P(('seq', 'fsdp'))
- k_weight_grad: float32 [1536, 256], P(('seq', 'fsdp'))
- v_weight_grad: float32 [1536, 256], P(('seq', 'fsdp'))
- qkv_bias_grad: float32 [2048], P(('seq', 'fsdp'))
- o_weight_grad: float32 [1536, 1536], P(('seq', 'fsdp'))
- mlp_gain_grad: float32 [1536], P(('seq', 'fsdp'))
- gate_weight_grad: float32 [1536, 8960], P(('seq', 'fsdp'))
- up_weight_grad: float32 [1536, 8960], P(('seq', 'fsdp'))
- down_weight_grad: float32 [8960, 1536], P(('seq', 'fsdp'))
The draws below stay inside these ranges and needn't reach their ends.
Inputs may be any that keep to these rules, and one draw needn't show every extreme that they name: `segment_ids`: document numbers never fall along a sequence; each document has 1 to 256 positions and one has exactly 256.
All inputs are finite; a program needn't handle non-finite values.
Results may differ from the reference program's by a relative error of at most 0.013.
Values may be sent and summed in bfloat16 or wider, within the bound.
A program may use at most 512 MiB of HBM per device.

```python
import math
import jax
import jax.numpy as jnp
import numpy as np
from jax import lax

D = 1536
HEADS = 12
KV_HEADS = 2
HD = 128
FF = 8960
DOCS = 4
SEQ = 512
SEQS = 16


def with_spikes(entries, own_key, source, target, shards_of, factor):
    owner, partner = [(jnp.arange(entries.shape[axis_at]) // (entries.shape[axis_at] // shards_of)).reshape([-1 if axis == axis_at else 1 for axis in range(entries.ndim)]) for axis_at in (source, target)]
    chosen = jax.random.permutation(own_key, shards_of)[partner]
    strong = (owner == chosen) | (owner == (partner + shards_of // 2) % shards_of)
    return jnp.where(strong, factor * entries, entries)


def shard_levels(rng, extent, cuts, low, top_value):
    gain = 1.0
    for position, parts in cuts:
        draws = jax.random.uniform(jax.random.fold_in(jax.random.fold_in(rng, 6), position), (parts,), jnp.float32, low / len(cuts), top_value / len(cuts))
        gain = gain * jnp.repeat(jnp.exp(draws), extent[position] // parts).reshape((-1,) + (1,) * (len(extent) - 1 - position))
    return gain


def length_profile(count, total, limit, slope):
    loads = [(1 << 20) // math.isqrt(rank ** slope) + 1 for rank in range(2, count + 1)]
    surplus, counts = total - limit - (count - 1), [1] * (count - 1)
    while surplus > 0:
        candidates = [i for i in range(count - 1) if counts[i] < limit]
        whole, budget = sum([loads[i] for i in candidates]), surplus
        for i in candidates:
            addition = min(limit - counts[i], max(1, budget * loads[i] // whole), surplus)
            counts[i] = counts[i] + addition
            surplus = surplus - addition
    return np.array([limit] + counts)


def ragged_sizes(rng, amount, total, most, skew):
    if amount == 2:
        one = jax.random.randint(rng, (), max(1, total - most), min(most, total - 1) + 1)
        return jnp.stack([one, total - one])
    sizes = jnp.asarray(length_profile(amount, total, most, skew), jnp.int32)
    pairs = (amount - 1) // 2
    source_of, taker = sizes[1:1 + 2 * pairs:2], sizes[2:2 + 2 * pairs:2]
    slack = jnp.minimum(source_of - 1, most - taker)
    shifted = jax.random.randint(jax.random.fold_in(rng, 1), (pairs,), 0, 1 << 20) % (slack + 1)
    sizes = sizes.at[1:1 + 2 * pairs:2].set(source_of - shifted).at[2:2 + 2 * pairs:2].set(taker + shifted)
    return sizes[jax.random.permutation(jax.random.fold_in(rng, 2), amount)]


def scatter_about(rng, extent, width, most, cuts=(), held_as=jnp.bfloat16):
    entries = jax.random.normal(rng, extent, jnp.float32) * width
    if len(cuts) > 0:
        entries = shard_levels(rng, extent, cuts, -0.22, 0.18) * entries
    return jnp.clip(entries, min=-most, max=most).astype(held_as)


def bell_draw_with(own_key, dims, width, most, cuts, heavy, kind=jnp.bfloat16):
    array = width * jax.random.normal(own_key, dims, jnp.float32)
    if cuts:
        array = array * shard_levels(own_key, dims, cuts, -0.22, 0.18)
    return jnp.clip(with_spikes(array, jax.random.fold_in(own_key, 3), *heavy), -most, most).astype(kind)


def setup_inputs(seed: int = 0) -> dict:
    streams_of = jax.random.split(jax.random.key(seed), 14)
    return {
        "inputs": bell_draw_with(streams_of[0], (SEQS, SEQ, D), 1.0, 6.0, ((0, 16), (1, 2)), (0, 2, 16, 2.0)),
        "segment_ids": jax.vmap(lambda own: jnp.searchsorted(jnp.cumsum(ragged_sizes(own, DOCS, SEQ, SEQ // 2, 0)), jnp.arange(SEQ), side="right"))(jax.random.split(streams_of[1], SEQS)).reshape((SEQS, SEQ)).astype(jnp.int32),
        "attn_gain": jnp.clip(1.0 + 0.1 * jax.random.normal(streams_of[2], (D,), jnp.float32), 0.5, 1.5).astype(jnp.bfloat16),
        "q_weight": scatter_about(streams_of[3], (D, HEADS * HD), D ** -0.5, 0.15625, ((0, 32),)),
        "k_weight": scatter_about(streams_of[4], (D, KV_HEADS * HD), D ** -0.5, 0.15625, ((0, 32),)),
        "v_weight": scatter_about(streams_of[5], (D, KV_HEADS * HD), D ** -0.5, 0.15625, ((0, 32),)),
        "qkv_bias": scatter_about(streams_of[6], ((HEADS + 2 * KV_HEADS) * HD,), 0.5, 3.0, ((0, 32),)),
        "o_weight": scatter_about(streams_of[7], (HEADS * HD, D), (HD // 8) ** -0.5, 1.5, ((0, 32),)),
        "mlp_gain": jnp.clip(1.0 + 0.1 * jax.random.normal(streams_of[8], (D,), jnp.float32), 0.5, 1.5).astype(jnp.bfloat16),
        "gate_weight": scatter_about(streams_of[9], (D, FF), D ** -0.5, 0.15625, ((0, 32),)),
        "up_weight": scatter_about(streams_of[10], (D, FF), D ** -0.5, 0.15625, ((0, 32),)),
        "down_weight": scatter_about(streams_of[11], (FF, D), FF ** -0.5, 0.0625, ((0, 32),)),
        "cotangent": bell_draw_with(streams_of[12], (SEQS, SEQ, D), 1.0, 6.0, ((0, 16), (1, 2)), (0, 2, 16, 2.0)),
    }


EPS = 1e-06
ROPE_BASE = 1000000.0
MASKED = -1e+30

@jax.custom_vjp
def low(v):
    return lax.optimization_barrier(v.astype(jnp.bfloat16)).astype(jnp.float32)

@jax.custom_vjp
def low_back(v):
    return v

def low_keep(v):
    return (low(v), None)

def low_pass(kept, grad):
    return (grad,)

def back_keep(v):
    return (v, None)

def back_low(kept, grad):
    return (low(grad),)
low.defvjp(low_keep, low_pass)
low_back.defvjp(back_keep, back_low)

def highest(left, right):
    return jnp.dot(left, right, precision=lax.Precision.HIGHEST)

def tables(positions):
    freq = ROPE_BASE ** (-jnp.arange(0, HD, 2).astype(jnp.float32) / HD)
    angle = positions.astype(jnp.float32)[:, None] * freq[None, :]
    return (jnp.cos(angle), jnp.sin(angle))

def rotate(values, cosine, sine):
    count = values.shape[0]
    split = values.reshape(count, -1, HD)
    half = HD // 2
    first = split[..., :half]
    second = split[..., half:]
    cos_b = cosine[:, None, :]
    sin_b = sine[:, None, :]
    turned = jnp.concatenate([first * cos_b - second * sin_b, second * cos_b + first * sin_b], axis=-1)
    return turned.reshape(count, -1)

def layer(hidden_in, params, segments, cosine, sine):
    gain_one, full_query, full_key, full_value, all_bias, full_out, gain_two, full_gate, full_up, full_down = params
    query_cols = HEADS * HD
    key_cols = KV_HEADS * HD
    query_bias = all_bias[:query_cols]
    key_bias = all_bias[query_cols:query_cols + key_cols]
    value_bias = all_bias[query_cols + key_cols:]
    length = hidden_in.shape[0]
    rescale_one = lax.rsqrt(lax.optimization_barrier(jnp.mean(hidden_in * hidden_in, axis=-1, keepdims=True)) + EPS)
    input_one = low(hidden_in * rescale_one * gain_one)
    queries = low(rotate(low_back(highest(input_one, full_query) + query_bias), cosine, sine))
    keys = low(rotate(low_back(highest(input_one, full_key) + key_bias), cosine, sine))
    values = low(low_back(highest(input_one, full_value) + value_bias))
    group_size = HEADS // KV_HEADS
    query_heads = queries.reshape(length, KV_HEADS, group_size, HD)
    key_heads = keys.reshape(length, KV_HEADS, HD)
    value_heads = values.reshape(length, KV_HEADS, HD)
    scores = low_back(jnp.einsum('qkgd,pkd->kgqp', query_heads, key_heads, precision=lax.Precision.HIGHEST) * HD ** (-0.5))
    positions = jnp.arange(length)
    allowed = (positions[:, None] >= positions[None, :]) & (segments[:, None] == segments[None, :])
    scores = jnp.where(allowed[None, None], scores, MASKED)
    attn_probs = low(jax.nn.softmax(scores, axis=-1))
    mixture = jnp.einsum('kgqp,pkd->qkgd', attn_probs, value_heads, precision=lax.Precision.HIGHEST)
    mixture = low_back(low(mixture.reshape(length, HEADS * HD)))
    middle = hidden_in + low_back(highest(mixture, full_out))
    rescale_two = lax.rsqrt(lax.optimization_barrier(jnp.mean(middle * middle, axis=-1, keepdims=True)) + EPS)
    input_two = low(middle * rescale_two * gain_two)
    gate_pre = low_back(highest(input_two, full_gate))
    up_pre = low_back(highest(input_two, full_up))
    inner = low(jax.nn.silu(gate_pre) * up_pre)
    return middle + highest(inner, full_down)

def reference(inputs, segment_ids, attn_gain, q_weight, k_weight, v_weight, qkv_bias, o_weight, mlp_gain, gate_weight, up_weight, down_weight, cotangent):
    params = tuple((weight_arr.astype(jnp.float32) for weight_arr in (attn_gain, q_weight, k_weight, v_weight, qkv_bias, o_weight, mlp_gain, gate_weight, up_weight, down_weight)))
    length = inputs.shape[1]
    cosine, sine = tables(jnp.arange(length))

    def per_sequence(totals, item):
        hidden_in, segments, grad_out = item
        result, pullback = jax.vjp(lambda tokens_in, weights: layer(tokens_in, weights, segments, cosine, sine), hidden_in, params)
        grad_in, grad_params = pullback(grad_out)
        totals = tuple((summed + added for summed, added in zip(totals, grad_params)))
        return (totals, (result.astype(jnp.bfloat16), grad_in.astype(jnp.bfloat16)))
    starting = tuple((jnp.zeros_like(weight_arr) for weight_arr in params))
    totals, (outputs, input_grads) = lax.scan(per_sequence, starting, (inputs.astype(jnp.float32), segment_ids, cotangent.astype(jnp.float32)))
    return (outputs, input_grads, totals[0], totals[1], totals[2], totals[3], totals[4], totals[5], totals[6], totals[7], totals[8], totals[9])
```

```python
import jax
import jax.numpy as jnp
from jax import lax
from jax.sharding import Mesh, PartitionSpec as P

HD = 128
EPS = 1e-06
ROPE_BASE = 1000000.0
MASKED = -1e30
NZ = 4
NC = 2
ALL = ("y", "z", "x", "c")
TP = ("z", "c")
DP = ("y", "x")
F32 = jnp.float32
BF16 = jnp.bfloat16


def tables(positions):
    freq = ROPE_BASE ** (-jnp.arange(0, HD, 2).astype(F32) / HD)
    angle = positions.astype(F32)[:, None] * freq[None, :]
    return (jnp.cos(angle), jnp.sin(angle))


def rotate(values, cosine, sine):
    count = values.shape[0]
    split = values.reshape(count, -1, HD)
    half = HD // 2
    first = split[..., :half]
    second = split[..., half:]
    cos_b = cosine[:, None, :]
    sin_b = sine[:, None, :]
    turned = jnp.concatenate(
        [first * cos_b - second * sin_b, second * cos_b + first * sin_b], axis=-1
    )
    return turned.reshape(count, -1)


def dot(a, b):
    return jnp.dot(a, b, preferred_element_type=F32)


def dot_nt(a, b):
    return lax.dot_general(a, b, (((1,), (1,)), ((), ())), preferred_element_type=F32)


def dot_tn(a, b):
    return lax.dot_general(a, b, (((0,), (0,)), ((), ())), preferred_element_type=F32)


def norm_back(grad_normed, normed, rescale, gain_vec):
    grad_gain = jnp.sum(grad_normed * normed, axis=0)
    scaled = grad_normed * gain_vec
    grad_x = rescale * (scaled - normed * jnp.mean(scaled * normed, axis=-1, keepdims=True))
    return (grad_gain, grad_x)


def make_body(ny, nx):
    def spread_columns(shard):
        rows, cols = shard.shape
        fs = cols // (ny * NZ * nx * NC)
        view = shard.reshape(rows, ny, NZ, nx, NC, fs)
        return view.transpose(2, 4, 0, 1, 3, 5).reshape(NZ * NC, rows, ny * nx * fs)

    def unspread_columns(blocks):
        _, rows, width = blocks.shape
        fs = width // (ny * nx)
        view = blocks.reshape(NZ, NC, rows, ny, nx, fs)
        return view.transpose(2, 3, 0, 4, 1, 5).reshape(rows, -1)

    def gather_columns(shard):
        blocks = spread_columns(shard)
        rows, width = blocks.shape[1:]
        mine = lax.all_to_all(blocks, TP, split_axis=0, concat_axis=0, tiled=True)
        full = lax.all_gather(mine, DP, axis=0, tiled=False)
        view = full.reshape(ny, nx, NZ, NC, rows, width).transpose(0, 2, 1, 3, 4, 5)
        return view.reshape(-1, width)

    def scatter_columns(grad):
        width = grad.shape[1]
        rows = grad.shape[0] // (ny * NZ * nx * NC)
        view = grad.reshape(ny, NZ, nx, NC, rows, width).transpose(0, 2, 1, 3, 4, 5)
        view = view.reshape(ny * nx * NZ * NC, rows, width)
        part = lax.psum_scatter(view, DP, scatter_dimension=0, tiled=True)
        back = lax.all_to_all(part, TP, split_axis=0, concat_axis=0, tiled=True)
        return unspread_columns(back).astype(F32)

    def body(
        inputs,
        segment_ids,
        attn_gain,
        q_weight,
        k_weight,
        v_weight,
        qkv_bias,
        o_weight,
        mlp_gain,
        gate_weight,
        up_weight,
        down_weight,
        cotangent,
    ):
        tok_rows = inputs.shape[1]
        hidden_in = inputs[0].astype(F32)
        grad_out = cotangent[0]
        seg_all = segment_ids[0]
        length = seg_all.shape[0]
        seq_place = lax.axis_index("y")
        tok_pos = seq_place * tok_rows + jnp.arange(tok_rows)
        cos_tok, sin_tok = tables(tok_pos)
        query_width = q_weight.shape[1]
        key_width = k_weight.shape[1]
        kv_heads = key_width // HD
        q_heads = query_width // HD
        group = q_heads // kv_heads

        packed = jnp.concatenate([q_weight, k_weight, v_weight, o_weight], axis=1)
        full = lax.all_gather(packed, ALL, axis=0, tiled=True)
        qkv_width = query_width + 2 * key_width
        full_qkv = full[:, :qkv_width]
        full_out = full[:, qkv_width:]
        small = jnp.concatenate([attn_gain, qkv_bias, mlp_gain])[None]
        small_all = lax.all_gather(small, ALL, axis=0, tiled=True).astype(F32)
        g_rows = attn_gain.shape[0]
        b_rows = qkv_bias.shape[0]
        gain_one = small_all[:, :g_rows].reshape(-1)
        bias = small_all[:, g_rows : g_rows + b_rows].reshape(-1)
        gain_two = small_all[:, g_rows + b_rows :].reshape(-1)

        grad_out_all = lax.all_gather(grad_out, TP, axis=0, tiled=True)
        full_gate = gather_columns(gate_weight)
        full_up = gather_columns(up_weight)
        full_down = lax.all_gather(down_weight, DP, axis=0, tiled=True)

        rescale_one = lax.rsqrt(jnp.mean(hidden_in * hidden_in, axis=-1, keepdims=True) + EPS)
        normed_one = hidden_in * rescale_one
        input_one = (normed_one * gain_one).astype(BF16)
        qkv_pre = dot(input_one, full_qkv) + bias
        query = rotate(qkv_pre[:, :query_width], cos_tok, sin_tok).astype(BF16)
        key = rotate(qkv_pre[:, query_width : query_width + key_width], cos_tok, sin_tok)
        kv = jnp.concatenate([key, qkv_pre[:, query_width + key_width :]], axis=1).astype(BF16)
        kv_all = lax.all_gather(kv, "y", axis=0, tiled=True)
        key_heads = kv_all[:, :key_width].reshape(length, kv_heads, HD)
        value_heads = kv_all[:, key_width:].reshape(length, kv_heads, HD)
        query_heads = query.reshape(tok_rows, kv_heads, group, HD)
        score_scale = HD ** (-0.5)
        all_pos = jnp.arange(length)
        seg_tok = lax.dynamic_slice(seg_all, (seq_place * tok_rows,), (tok_rows,))
        allowed = (tok_pos[:, None] >= all_pos[None, :]) & (seg_tok[:, None] == seg_all[None, :])
        scores = (
            jnp.einsum("qkgd,pkd->kgqp", query_heads, key_heads, preferred_element_type=F32)
            * score_scale
        )
        masked = jnp.where(allowed[None, None], scores, MASKED)
        row_max = jnp.max(masked, axis=-1, keepdims=True)
        exponent = jnp.exp(masked - row_max)
        row_total = jnp.sum(exponent, axis=-1, keepdims=True)
        probs = exponent / row_total
        probs_low = probs.astype(BF16)
        mixture = jnp.einsum("kgqp,pkd->qkgd", probs_low, value_heads, preferred_element_type=F32)
        attn_tok = mixture.astype(BF16).reshape(tok_rows, query_width)
        middle = hidden_in + dot(attn_tok, full_out)

        rescale_two = lax.rsqrt(jnp.mean(middle * middle, axis=-1, keepdims=True) + EPS)
        normed_two = middle * rescale_two
        input_two = (normed_two * gain_two).astype(BF16)
        input_all = lax.all_gather(input_two, TP, axis=0, tiled=True)
        gate_pre = dot(input_all, full_gate)
        up_pre = dot(input_all, full_up)
        gate_sig = jax.nn.sigmoid(gate_pre)
        gate_act = gate_pre * gate_sig
        inner = (gate_act * up_pre).astype(BF16)
        grad_inner = dot_nt(grad_out_all, full_down)
        grad_gate = (
            grad_inner * up_pre * gate_sig * (1.0 + gate_pre * (1.0 - gate_sig))
        ).astype(BF16)
        grad_up = (grad_inner * gate_act).astype(BF16)
        grad_in_part = (dot_nt(grad_gate, full_gate) + dot_nt(grad_up, full_up)).astype(BF16)
        grad_input_two = lax.psum_scatter(
            grad_in_part, TP, scatter_dimension=0, tiled=True
        ).astype(F32)
        out_part = dot(inner, full_down).astype(BF16)
        out_sum = lax.psum_scatter(out_part, TP, scatter_dimension=0, tiled=True)
        output = (middle + out_sum.astype(F32)).astype(BF16)[None]

        grad_gate_w = scatter_columns(dot_tn(input_all, grad_gate).astype(BF16))
        grad_up_w = scatter_columns(dot_tn(input_all, grad_up).astype(BF16))
        grad_down_w = lax.psum_scatter(
            dot_tn(inner, grad_out_all).astype(BF16), DP, scatter_dimension=0, tiled=True
        ).astype(F32)

        grad_gain_two, grad_mid = norm_back(grad_input_two, normed_two, rescale_two, gain_two)
        grad_mid = grad_mid + grad_out.astype(F32)
        grad_branch = grad_mid.astype(BF16)
        grad_attn = dot_nt(grad_branch, full_out).astype(BF16)
        grad_heads = grad_attn.reshape(tok_rows, kv_heads, group, HD)
        grad_probs = jnp.einsum(
            "qkgd,pkd->kgqp", grad_heads, value_heads, preferred_element_type=F32
        )
        inner_sum = jnp.sum(probs * grad_probs, axis=-1, keepdims=True)
        grad_scores = (probs * (grad_probs - inner_sum)).astype(BF16)
        grad_query = (
            jnp.einsum("kgqp,pkd->qkgd", grad_scores, key_heads, preferred_element_type=F32)
            * score_scale
        ).reshape(tok_rows, query_width)
        grad_key = (
            jnp.einsum("kgqp,qkgd->pkd", grad_scores, query_heads, preferred_element_type=F32)
            * score_scale
        ).reshape(length, key_width)
        grad_value = jnp.einsum(
            "kgqp,qkgd->pkd", probs_low, grad_heads, preferred_element_type=F32
        ).reshape(length, key_width)
        grad_kv = jnp.concatenate([grad_key, grad_value], axis=1).astype(BF16)
        other = lax.dynamic_slice(
            grad_kv, ((1 - seq_place) * tok_rows, 0), (tok_rows, 2 * key_width)
        )
        own = lax.dynamic_slice(grad_kv, (seq_place * tok_rows, 0), (tok_rows, 2 * key_width))
        swapped = lax.ppermute(other, "y", [(0, 1), (1, 0)])
        grad_kv_tok = own.astype(F32) + swapped.astype(F32)
        grad_query_pre = rotate(grad_query, cos_tok, -sin_tok).astype(BF16)
        grad_key_pre = rotate(grad_kv_tok[:, :key_width], cos_tok, -sin_tok).astype(BF16)
        grad_value_pre = grad_kv_tok[:, key_width:].astype(BF16)
        grad_qkv = jnp.concatenate([grad_query_pre, grad_key_pre, grad_value_pre], axis=1)
        grad_attn_w = lax.psum_scatter(
            jnp.concatenate(
                [dot_tn(input_one, grad_qkv), dot_tn(attn_tok, grad_branch)], axis=1
            ).astype(BF16),
            ALL,
            scatter_dimension=0,
            tiled=True,
        ).astype(F32)
        grad_qkv_sum = jnp.sum(grad_qkv.astype(F32), axis=0)
        grad_input_one = dot_nt(grad_qkv, full_qkv)
        grad_gain_one, grad_first = norm_back(grad_input_one, normed_one, rescale_one, gain_one)
        grad_total = grad_mid + grad_first
        shards = small_all.shape[0]
        small_grads = jnp.concatenate(
            [
                grad_gain_one.reshape(shards, -1),
                grad_qkv_sum.reshape(shards, -1),
                grad_gain_two.reshape(shards, -1),
            ],
            axis=1,
        )
        small_sums = lax.psum_scatter(small_grads, ALL, scatter_dimension=0, tiled=True)[0]
        return (
            output,
            grad_total.astype(BF16)[None],
            small_sums[:g_rows],
            grad_attn_w[:, :query_width],
            grad_attn_w[:, query_width : query_width + key_width],
            grad_attn_w[:, query_width + key_width : qkv_width],
            small_sums[g_rows : g_rows + b_rows],
            grad_attn_w[:, qkv_width:],
            small_sums[g_rows + b_rows :],
            grad_gate_w,
            grad_up_w,
            grad_down_w,
        )

    return body


def solution(mesh):
    ny = mesh.shape["seq"]
    nx = mesh.shape["fsdp"] // (NZ * NC)
    grid = Mesh(mesh.devices.reshape(ny, NZ, nx, NC), ALL)
    tokens = P(("z", "x", "c"), "y", None)
    rows = P(ALL, None)
    vec = P(ALL)
    return jax.shard_map(
        make_body(ny, nx),
        mesh=grid,
        in_specs=(
            tokens,
            P(("z", "x", "c"), None),
            vec,
            rows,
            rows,
            rows,
            vec,
            rows,
            vec,
            rows,
            rows,
            rows,
            tokens,
        ),
        out_specs=(tokens, tokens, vec, rows, rows, rows, vec, rows, vec, rows, rows, rows),
        check_vma=False,
    )
```

```python
import jax
import jax.numpy as jnp
from jax import lax
from jax.experimental import pallas as pl
from jax.experimental.pallas import tpu as pltpu
from jax.sharding import Mesh, PartitionSpec as P

HD = 128
EPS = 1e-06
ROPE_BASE = 1000000.0
MASKED = -1e30
NZ = 4
NC = 2
ALL = ("y", "z", "x", "c")
TP = ("z", "c")
DP = ("y", "x")
F32 = jnp.float32
BF16 = jnp.bfloat16


def tables(positions):
    freq = ROPE_BASE ** (-jnp.arange(0, HD, 2).astype(F32) / HD)
    angle = positions.astype(F32)[:, None] * freq[None, :]
    return (jnp.cos(angle), jnp.sin(angle))


def rotate(values, cosine, sine):
    count = values.shape[0]
    split = values.reshape(count, -1, HD)
    half = HD // 2
    first = split[..., :half]
    second = split[..., half:]
    cos_b = cosine[:, None, :]
    sin_b = sine[:, None, :]
    turned = jnp.concatenate(
        [first * cos_b - second * sin_b, second * cos_b + first * sin_b], axis=-1
    )
    return turned.reshape(count, -1)


def dot(a, b):
    return jnp.dot(a, b, preferred_element_type=F32)


def dot_nt(a, b):
    return lax.dot_general(a, b, (((1,), (1,)), ((), ())), preferred_element_type=F32)


def dot_tn(a, b):
    return lax.dot_general(a, b, (((0,), (0,)), ((), ())), preferred_element_type=F32)


def norm_back(grad_normed, normed, rescale, gain_vec):
    grad_gain = jnp.sum(grad_normed * normed, axis=0)
    scaled = grad_normed * gain_vec
    grad_x = rescale * (scaled - normed * jnp.mean(scaled * normed, axis=-1, keepdims=True))
    return (grad_gain, grad_x)


class Wires:
    def __init__(self, sems):
        self.sems = sems
        self.used = 0
        self.started = []

    def send(self, src, dst, recv_sem, device, cond=None):
        copy = pltpu.make_async_remote_copy(
            src_ref=src,
            dst_ref=dst,
            send_sem=self.sems.at[self.used],
            recv_sem=recv_sem,
            device_id=device,
            device_id_type=pl.DeviceIdType.MESH,
        )
        self.used += 1
        if cond is None:
            copy.start()
        else:
            pl.when(cond)(copy.start)
        self.started.append((copy, cond))

    def arrived(self, dst, recv_sem, device):
        pltpu.make_async_remote_copy(
            src_ref=dst,
            dst_ref=dst,
            send_sem=self.sems.at[0],
            recv_sem=recv_sem,
            device_id=device,
            device_id_type=pl.DeviceIdType.MESH,
        ).wait_recv()

    def finish(self):
        for copy, cond in self.started:
            if cond is None:
                copy.wait_send()
            else:
                pl.when(cond)(copy.wait_send)


def line_order(z, k):
    if k == 0:
        return z + 1 - 2 * (z % 2)
    if k == 1:
        return 2 - z // 2
    return 3 - 3 * (z // 2)


def greet(peers):
    barrier = pltpu.get_barrier_semaphore()
    for peer in peers:
        pl.semaphore_signal(
            barrier, inc=1, device_id=peer, device_id_type=pl.DeviceIdType.MESH
        )
    pl.semaphore_wait(barrier, len(peers))


def place():
    return tuple(lax.axis_index(name) for name in ALL)


def line_peers(z, c):
    peers = [{"c": 1 - c}]
    for k in range(NZ - 1):
        peers.append({"z": (z + k + 1) % NZ})
    return peers


class LineGather:
    def __init__(self, wires, own, out, recv, z, c):
        self.wires, self.own, self.out, self.recv, self.z, self.c = wires, own, out, recv, z, c

    def begin(self):
        w, z, c = self.wires, self.z, self.c
        dst, sem = self.out.at[z, c], self.recv.at[z, c]
        w.send(self.own, dst, sem, {"z": jnp.minimum(z + 1, NZ - 1)}, z < NZ - 1)
        w.send(self.own, dst, sem, {"z": jnp.maximum(z - 1, 0)}, z > 0)
        w.send(self.own, dst, sem, {"c": 1 - c})

    def event(self, k):
        w, z, c = self.wires, self.z, self.c
        zq = line_order(z, k)
        slot, sem = self.out.at[zq, c], self.recv.at[zq, c]
        w.arrived(slot, sem, {"c": 1 - c})
        onward = jnp.where(zq < z, jnp.minimum(z + 1, NZ - 1), jnp.maximum(z - 1, 0))
        w.send(slot, slot, sem, {"z": onward}, (z > 0) & (z < NZ - 1))
        w.send(slot, slot, sem, {"c": 1 - c})

    def sibling(self, zq):
        w, c = self.wires, self.c
        w.arrived(self.out.at[zq, 1 - c], self.recv.at[zq, 1 - c], {"c": 1 - c})


def token_gather_kernel(own, out, send_sems, local_sem, recv):
    y, z, x, c = place()
    greet(line_peers(z, c))
    keep = pltpu.make_async_copy(own, out.at[z, c], local_sem)
    keep.start()
    wires = Wires(send_sems)
    line = LineGather(wires, own, out, recv, z, c)
    line.begin()
    for k in range(NZ - 1):
        line.event(k)
    for zq in range(NZ):
        line.sibling(zq)
    wires.finish()
    keep.wait()


def token_gather(own, collective_id):
    shape = (NZ, NC) + own.shape
    out = pl.pallas_call(
        token_gather_kernel,
        name="token_gather",
        out_shape=jax.ShapeDtypeStruct(shape, own.dtype),
        in_specs=[pl.BlockSpec(memory_space=pl.ANY)],
        out_specs=pl.BlockSpec(memory_space=pl.ANY),
        scratch_shapes=[
            pltpu.SemaphoreType.DMA((9,)),
            pltpu.SemaphoreType.DMA,
            pltpu.SemaphoreType.DMA((NZ, NC)),
        ],
        compiler_params=pltpu.CompilerParams(
            collective_id=collective_id, has_side_effects=True
        ),
    )(own)
    return out.reshape(-1, own.shape[1])


def weight_gather_kernel(
    nx, a, gu, d, tok, ao, guo, do, co, send_sems, local_sems, ra, rt, rw, rd, rc
):
    y, z, x, c = place()
    sib = {"c": 1 - c}
    ypeer = {"y": 1 - y}
    xpeers = [(x + i + 1) % nx for i in range(nx - 1)]
    planes = [{"x": xp} for xp in xpeers] + [ypeer]
    cross = [{"z": (z + k + 1) % NZ, "c": 1 - c} for k in range(NZ - 1)]
    greet(line_peers(z, c) + cross + planes)
    locals_ = [
        pltpu.make_async_copy(a, ao.at[y, z, x, c], local_sems.at[0]),
        pltpu.make_async_copy(gu.at[z, c], guo.at[:, y, z, x, c], local_sems.at[1]),
        pltpu.make_async_copy(d, do.at[y, x], local_sems.at[2]),
        pltpu.make_async_copy(tok, co.at[z, c], local_sems.at[3]),
    ]
    for copy in locals_:
        copy.start()
    wires = Wires(send_sems)

    def both_ways(src, dst, sem):
        for peer in planes:
            wires.send(src, dst, sem, peer)

    own_slot, own_sem = ao.at[y, z, x, c], ra.at[y, z, x, c]
    wires.send(a, own_slot, own_sem, {"z": jnp.minimum(z + 1, NZ - 1)}, z < NZ - 1)
    wires.send(a, own_slot, own_sem, {"z": jnp.maximum(z - 1, 0)}, z > 0)
    both_ways(a, own_slot, own_sem)
    wires.send(a, own_slot, own_sem, sib)
    for k in range(NZ - 1):
        zq = line_order(z, k)
        slot, sem = ao.at[y, zq, x, c], ra.at[y, zq, x, c]
        wires.arrived(slot, sem, sib)
        onward = jnp.where(zq < z, jnp.minimum(z + 1, NZ - 1), jnp.maximum(z - 1, 0))
        wires.send(slot, slot, sem, {"z": onward}, (z > 0) & (z < NZ - 1))
        both_ways(slot, slot, sem)
        wires.send(slot, slot, sem, sib)

    for k in range(NZ * NC - 1):
        step = k + 1
        zp, cp = (z + step // NC) % NZ, (c + step) % NC
        wires.send(
            gu.at[zp, cp], guo.at[:, y, z, x, c], rt.at[z, c], {"z": zp, "c": cp}
        )
    line = LineGather(wires, tok, co, rc, z, c)
    line.begin()
    half = d.shape[1] // 2
    parts = [pl.ds(0, half), pl.ds(half, half)]
    for h in range(2):
        both_ways(d.at[:, parts[h]], do.at[y, x, :, parts[h]], rd.at[h, y, x])

    def relay_attn(yq, xq, zq, peers):
        slot, sem = ao.at[yq, zq, xq, c], ra.at[yq, zq, xq, c]
        wires.arrived(slot, sem, sib)
        for peer in peers:
            wires.send(slot, slot, sem, peer)
        wires.send(slot, slot, sem, sib)

    for zq in range(NZ):
        for xp in xpeers:
            relay_attn(y, xp, zq, [ypeer] if zq < NZ // 2 else [])
        relay_attn(1 - y, x, zq, planes[:-1] if zq >= NZ // 2 else [])

    for k in range(NZ * NC - 1):
        step = k + 1
        zp, cp = (z + step // NC) % NZ, (c + step) % NC
        wires.arrived(guo.at[:, y, zp, x, cp], rt.at[zp, cp], sib)
    locals_[1].wait()
    for m in range(2):
        plane = guo.at[m, y, :, x]
        both_ways(plane, plane, rw.at[m, y, x])
    line.event(0)

    def relay(ref, sem, peers):
        wires.arrived(ref, sem, sib)
        for peer in peers:
            wires.send(ref, ref, sem, peer)

    for xp in xpeers:
        relay(do.at[y, xp, :, parts[0]], rd.at[0, y, xp], [ypeer])
        relay(do.at[y, xp, :, parts[1]], rd.at[1, y, xp], [])
    relay(do.at[1 - y, x, :, parts[1]], rd.at[1, 1 - y, x], planes[:-1])
    relay(do.at[1 - y, x, :, parts[0]], rd.at[0, 1 - y, x], [])
    for xp in xpeers:
        for zq in range(NZ):
            relay_attn(1 - y, xp, zq, [])
    line.event(1)
    for xp in xpeers:
        relay(guo.at[0, y, :, xp], rw.at[0, y, xp], [ypeer])
    relay(guo.at[1, 1 - y, :, x], rw.at[1, 1 - y, x], planes[:-1])
    line.event(2)
    for xp in xpeers:
        relay(guo.at[1, y, :, xp], rw.at[1, y, xp], [])
    relay(guo.at[0, 1 - y, :, x], rw.at[0, 1 - y, x], [])
    for xp in xpeers:
        for h in range(2):
            relay(do.at[1 - y, xp, :, parts[h]], rd.at[h, 1 - y, xp], [])
            relay(guo.at[h, 1 - y, :, xp], rw.at[h, 1 - y, xp], [])
    for zq in range(NZ):
        line.sibling(zq)
    for yq in range(2):
        for zq in range(NZ):
            for xq in range(nx):
                wires.arrived(ao.at[yq, zq, xq, 1 - c], ra.at[yq, zq, xq, 1 - c], sib)
    wires.finish()
    for i in (0, 2, 3):
        locals_[i].wait()


def weight_gather(ny, nx, a, gu, d, tok, collective_id):
    sends = 3 + (nx + 1) + 3 * (nx + 2)
    sends += 7 + 9 + 2 * nx
    sends += 4 * nx + 2 * (nx - 1) + 2 * (nx - 1)
    sends += 2 * nx + 2 * (nx - 1) + 4 * (nx - 1) + 2 * (nx - 1)
    hbm = pl.BlockSpec(memory_space=pl.ANY)
    grid = (ny, NZ, nx, NC)
    return pl.pallas_call(
        lambda *refs: weight_gather_kernel(nx, *refs),
        name="weight_gather",
        out_shape=(
            jax.ShapeDtypeStruct(grid + a.shape, BF16),
            jax.ShapeDtypeStruct((2,) + grid + gu.shape[3:], BF16),
            jax.ShapeDtypeStruct((ny, nx) + d.shape, BF16),
            jax.ShapeDtypeStruct((NZ, NC) + tok.shape, BF16),
        ),
        in_specs=[hbm] * 4,
        out_specs=(hbm,) * 4,
        scratch_shapes=[
            pltpu.SemaphoreType.DMA((sends + 16,)),
            pltpu.SemaphoreType.DMA((4,)),
            pltpu.SemaphoreType.DMA(grid),
            pltpu.SemaphoreType.DMA((NZ, NC)),
            pltpu.SemaphoreType.DMA((2, ny, nx)),
            pltpu.SemaphoreType.DMA((2, ny, nx)),
            pltpu.SemaphoreType.DMA((NZ, NC)),
        ],
        compiler_params=pltpu.CompilerParams(
            collective_id=collective_id, has_side_effects=True
        ),
    )(a, gu, d, tok)


def make_body(ny, nx):
    def spread_columns(shard):
        rows, cols = shard.shape
        fs = cols // (ny * NZ * nx * NC)
        view = shard.reshape(rows, ny, NZ, nx, NC, fs)
        return view.transpose(2, 4, 0, 1, 3, 5).reshape(NZ * NC, rows, ny * nx * fs)

    def unspread_columns(blocks):
        _, rows, width = blocks.shape
        fs = width // (ny * nx)
        view = blocks.reshape(NZ, NC, rows, ny, nx, fs)
        return view.transpose(2, 3, 0, 4, 1, 5).reshape(rows, -1)

    def scatter_columns(grad):
        width = grad.shape[1]
        rows = grad.shape[0] // (ny * NZ * nx * NC)
        view = grad.reshape(ny, NZ, nx, NC, rows, width).transpose(0, 2, 1, 3, 4, 5)
        view = view.reshape(ny * nx * NZ * NC, rows, width)
        part = lax.psum_scatter(view, DP, scatter_dimension=0, tiled=True)
        back = lax.all_to_all(part, TP, split_axis=0, concat_axis=0, tiled=True)
        return unspread_columns(back).astype(F32)

    def body(
        inputs,
        segment_ids,
        attn_gain,
        q_weight,
        k_weight,
        v_weight,
        qkv_bias,
        o_weight,
        mlp_gain,
        gate_weight,
        up_weight,
        down_weight,
        cotangent,
    ):
        tok_rows = inputs.shape[1]
        hidden_in = inputs[0].astype(F32)
        grad_out = cotangent[0]
        seg_all = segment_ids[0]
        length = seg_all.shape[0]
        seq_place = lax.axis_index("y")
        tok_pos = seq_place * tok_rows + jnp.arange(tok_rows)
        cos_tok, sin_tok = tables(tok_pos)
        query_width = q_weight.shape[1]
        key_width = k_weight.shape[1]
        kv_heads = key_width // HD
        q_heads = query_width // HD
        group = q_heads // kv_heads

        g_rows = attn_gain.shape[0]
        b_rows = qkv_bias.shape[0]
        qkv_width = query_width + 2 * key_width
        extra = jnp.concatenate(
            [
                attn_gain[:, None],
                mlp_gain[:, None],
                jnp.broadcast_to(qkv_bias[None], (g_rows, b_rows)),
                jnp.zeros((g_rows, HD - 2 - b_rows), BF16),
            ],
            axis=1,
        )
        packed = jnp.concatenate([q_weight, k_weight, v_weight, o_weight, extra], axis=1)
        columns = jnp.stack([spread_columns(gate_weight), spread_columns(up_weight)], axis=1)
        attn_all, columns_all, down_all, grad_out_all = weight_gather(
            ny,
            nx,
            packed,
            columns.reshape((NZ, NC) + columns.shape[1:]),
            down_weight,
            grad_out,
            0,
        )
        full = attn_all.reshape(-1, packed.shape[1])
        full_qkv = full[:, :qkv_width]
        full_out = full[:, qkv_width : qkv_width + query_width]
        tail = attn_all[..., qkv_width + query_width :].astype(F32)
        gain_one = tail[..., 0].reshape(-1)
        gain_two = tail[..., 1].reshape(-1)
        bias = tail[..., 0, 2 : 2 + b_rows].reshape(-1)
        width = columns.shape[-1]
        full_gate = columns_all[0].reshape(-1, width)
        full_up = columns_all[1].reshape(-1, width)
        full_down = down_all.reshape(width, -1)
        grad_out_all = grad_out_all.reshape(-1, grad_out.shape[1])

        rescale_one = lax.rsqrt(jnp.mean(hidden_in * hidden_in, axis=-1, keepdims=True) + EPS)
        normed_one = hidden_in * rescale_one
        input_one = (normed_one * gain_one).astype(BF16)
        qkv_pre = dot(input_one, full_qkv) + bias
        query = rotate(qkv_pre[:, :query_width], cos_tok, sin_tok).astype(BF16)
        key = rotate(qkv_pre[:, query_width : query_width + key_width], cos_tok, sin_tok)
        kv = jnp.concatenate([key, qkv_pre[:, query_width + key_width :]], axis=1).astype(BF16)
        kv_all = lax.all_gather(kv, "y", axis=0, tiled=True)
        key_heads = kv_all[:, :key_width].reshape(length, kv_heads, HD)
        value_heads = kv_all[:, key_width:].reshape(length, kv_heads, HD)
        query_heads = query.reshape(tok_rows, kv_heads, group, HD)
        score_scale = HD ** (-0.5)
        all_pos = jnp.arange(length)
        seg_tok = lax.dynamic_slice(seg_all, (seq_place * tok_rows,), (tok_rows,))
        allowed = (tok_pos[:, None] >= all_pos[None, :]) & (seg_tok[:, None] == seg_all[None, :])
        scores = (
            jnp.einsum("qkgd,pkd->kgqp", query_heads, key_heads, preferred_element_type=F32)
            * score_scale
        )
        masked = jnp.where(allowed[None, None], scores, MASKED)
        row_max = jnp.max(masked, axis=-1, keepdims=True)
        exponent = jnp.exp(masked - row_max)
        row_total = jnp.sum(exponent, axis=-1, keepdims=True)
        probs = exponent / row_total
        probs_low = probs.astype(BF16)
        mixture = jnp.einsum("kgqp,pkd->qkgd", probs_low, value_heads, preferred_element_type=F32)
        attn_tok = mixture.astype(BF16).reshape(tok_rows, query_width)
        middle = hidden_in + dot(attn_tok, full_out)

        rescale_two = lax.rsqrt(jnp.mean(middle * middle, axis=-1, keepdims=True) + EPS)
        normed_two = middle * rescale_two
        input_two = (normed_two * gain_two).astype(BF16)
        input_all = token_gather(input_two, 1)
        gate_pre = dot(input_all, full_gate)
        up_pre = dot(input_all, full_up)
        gate_sig = jax.nn.sigmoid(gate_pre)
        gate_act = gate_pre * gate_sig
        inner = (gate_act * up_pre).astype(BF16)
        grad_inner = dot_nt(grad_out_all, full_down)
        grad_gate = (
            grad_inner * up_pre * gate_sig * (1.0 + gate_pre * (1.0 - gate_sig))
        ).astype(BF16)
        grad_up = (grad_inner * gate_act).astype(BF16)
        grad_in_part = (dot_nt(grad_gate, full_gate) + dot_nt(grad_up, full_up)).astype(BF16)
        grad_input_two = lax.psum_scatter(
            grad_in_part, TP, scatter_dimension=0, tiled=True
        ).astype(F32)
        out_part = dot(inner, full_down).astype(BF16)
        out_sum = lax.psum_scatter(out_part, TP, scatter_dimension=0, tiled=True)
        output = (middle + out_sum.astype(F32)).astype(BF16)[None]

        grad_gate_w = scatter_columns(dot_tn(input_all, grad_gate).astype(BF16))
        grad_up_w = scatter_columns(dot_tn(input_all, grad_up).astype(BF16))
        grad_down_w = lax.psum_scatter(
            dot_tn(inner, grad_out_all).astype(BF16), DP, scatter_dimension=0, tiled=True
        ).astype(F32)

        grad_gain_two, grad_mid = norm_back(grad_input_two, normed_two, rescale_two, gain_two)
        grad_mid = grad_mid + grad_out.astype(F32)
        grad_branch = grad_mid.astype(BF16)
        grad_attn = dot_nt(grad_branch, full_out).astype(BF16)
        grad_heads = grad_attn.reshape(tok_rows, kv_heads, group, HD)
        grad_probs = jnp.einsum(
            "qkgd,pkd->kgqp", grad_heads, value_heads, preferred_element_type=F32
        )
        inner_sum = jnp.sum(probs * grad_probs, axis=-1, keepdims=True)
        grad_scores = (probs * (grad_probs - inner_sum)).astype(BF16)
        grad_query = (
            jnp.einsum("kgqp,pkd->qkgd", grad_scores, key_heads, preferred_element_type=F32)
            * score_scale
        ).reshape(tok_rows, query_width)
        grad_key = (
            jnp.einsum("kgqp,qkgd->pkd", grad_scores, query_heads, preferred_element_type=F32)
            * score_scale
        ).reshape(length, key_width)
        grad_value = jnp.einsum(
            "kgqp,qkgd->pkd", probs_low, grad_heads, preferred_element_type=F32
        ).reshape(length, key_width)
        grad_kv = jnp.concatenate([grad_key, grad_value], axis=1).astype(BF16)
        other = lax.dynamic_slice(
            grad_kv, ((1 - seq_place) * tok_rows, 0), (tok_rows, 2 * key_width)
        )
        own = lax.dynamic_slice(grad_kv, (seq_place * tok_rows, 0), (tok_rows, 2 * key_width))
        swapped = lax.ppermute(other, "y", [(0, 1), (1, 0)])
        grad_kv_tok = own.astype(F32) + swapped.astype(F32)
        grad_query_pre = rotate(grad_query, cos_tok, -sin_tok).astype(BF16)
        grad_key_pre = rotate(grad_kv_tok[:, :key_width], cos_tok, -sin_tok).astype(BF16)
        grad_value_pre = grad_kv_tok[:, key_width:].astype(BF16)
        grad_qkv = jnp.concatenate([grad_query_pre, grad_key_pre, grad_value_pre], axis=1)
        grad_attn_w = lax.psum_scatter(
            jnp.concatenate(
                [dot_tn(input_one, grad_qkv), dot_tn(attn_tok, grad_branch)], axis=1
            ).astype(BF16),
            ALL,
            scatter_dimension=0,
            tiled=True,
        ).astype(F32)
        grad_qkv_sum = jnp.sum(grad_qkv.astype(F32), axis=0)
        grad_input_one = dot_nt(grad_qkv, full_qkv)
        grad_gain_one, grad_first = norm_back(grad_input_one, normed_one, rescale_one, gain_one)
        grad_total = grad_mid + grad_first
        shards = ny * NZ * nx * NC
        small_grads = jnp.concatenate(
            [
                grad_gain_one.reshape(shards, -1),
                grad_qkv_sum.reshape(shards, -1),
                grad_gain_two.reshape(shards, -1),
            ],
            axis=1,
        )
        small_sums = lax.psum_scatter(small_grads, ALL, scatter_dimension=0, tiled=True)[0]
        return (
            output,
            grad_total.astype(BF16)[None],
            small_sums[:g_rows],
            grad_attn_w[:, :query_width],
            grad_attn_w[:, query_width : query_width + key_width],
            grad_attn_w[:, query_width + key_width : qkv_width],
            small_sums[g_rows : g_rows + b_rows],
            grad_attn_w[:, qkv_width:],
            small_sums[g_rows + b_rows :],
            grad_gate_w,
            grad_up_w,
            grad_down_w,
        )

    return body


def solution(mesh):
    ny = mesh.shape["seq"]
    nx = mesh.shape["fsdp"] // (NZ * NC)
    grid = Mesh(mesh.devices.reshape(ny, NZ, nx, NC), ALL)
    tokens = P(("z", "x", "c"), "y", None)
    rows = P(ALL, None)
    vec = P(ALL)
    return jax.shard_map(
        make_body(ny, nx),
        mesh=grid,
        in_specs=(
            tokens,
            P(("z", "x", "c"), None),
            vec,
            rows,
            rows,
            rows,
            vec,
            rows,
            vec,
            rows,
            rows,
            rows,
            tokens,
        ),
        out_specs=(tokens, tokens, vec, rows, rows, rows, vec, rows, vec, rows, rows, rows),
        check_vma=False,
    )
```

```python
import jax
import jax.numpy as jnp
from jax import lax
from jax.experimental import pallas as pl
from jax.experimental.pallas import tpu as pltpu
from jax.sharding import Mesh, PartitionSpec as P

HD = 128
EPS = 1e-06
ROPE_BASE = 1000000.0
MASKED = -1e30
NZ = 4
NC = 2
ALL = ("y", "z", "x", "c")
TP = ("z", "c")
DP = ("y", "x")
F32 = jnp.float32
BF16 = jnp.bfloat16


def tables(positions):
    freq = ROPE_BASE ** (-jnp.arange(0, HD, 2).astype(F32) / HD)
    angle = positions.astype(F32)[:, None] * freq[None, :]
    return (jnp.cos(angle), jnp.sin(angle))


def rotate(values, cosine, sine):
    count = values.shape[0]
    split = values.reshape(count, -1, HD)
    half = HD // 2
    first = split[..., :half]
    second = split[..., half:]
    cos_b = cosine[:, None, :]
    sin_b = sine[:, None, :]
    turned = jnp.concatenate(
        [first * cos_b - second * sin_b, second * cos_b + first * sin_b], axis=-1
    )
    return turned.reshape(count, -1)


def dot(a, b):
    return jnp.dot(a, b, preferred_element_type=F32)


def dot_nt(a, b):
    return lax.dot_general(a, b, (((1,), (1,)), ((), ())), preferred_element_type=F32)


def dot_tn(a, b):
    return lax.dot_general(a, b, (((0,), (0,)), ((), ())), preferred_element_type=F32)


def norm_back(grad_normed, normed, rescale, gain_vec):
    grad_gain = jnp.sum(grad_normed * normed, axis=0)
    scaled = grad_normed * gain_vec
    grad_x = rescale * (scaled - normed * jnp.mean(scaled * normed, axis=-1, keepdims=True))
    return (grad_gain, grad_x)


class Wires:
    def __init__(self, sems):
        self.sems = sems
        self.used = 0
        self.started = []

    def send(self, src, dst, recv_sem, device, cond=None):
        copy = pltpu.make_async_remote_copy(
            src_ref=src,
            dst_ref=dst,
            send_sem=self.sems.at[self.used],
            recv_sem=recv_sem,
            device_id=device,
            device_id_type=pl.DeviceIdType.MESH,
        )
        self.used += 1
        if cond is None:
            copy.start()
        else:
            pl.when(cond)(copy.start)
        self.started.append((copy, cond))

    def arrived(self, dst, recv_sem, device):
        pltpu.make_async_remote_copy(
            src_ref=dst,
            dst_ref=dst,
            send_sem=self.sems.at[0],
            recv_sem=recv_sem,
            device_id=device,
            device_id_type=pl.DeviceIdType.MESH,
        ).wait_recv()

    def finish(self):
        for copy, cond in self.started:
            if cond is None:
                copy.wait_send()
            else:
                pl.when(cond)(copy.wait_send)


def line_order(z, k):
    if k == 0:
        return z + 1 - 2 * (z % 2)
    if k == 1:
        return 2 - z // 2
    return 3 - 3 * (z // 2)


def greet(peers):
    barrier = pltpu.get_barrier_semaphore()
    for peer in peers:
        pl.semaphore_signal(
            barrier, inc=1, device_id=peer, device_id_type=pl.DeviceIdType.MESH
        )
    pl.semaphore_wait(barrier, len(peers))


def place():
    return tuple(lax.axis_index(name) for name in ALL)


def line_peers(z, c):
    peers = [{"c": 1 - c}]
    for k in range(NZ - 1):
        peers.append({"z": (z + k + 1) % NZ})
    return peers


class LineGather:
    def __init__(self, wires, own, out, recv, z, c):
        self.wires, self.own, self.out, self.recv, self.z, self.c = wires, own, out, recv, z, c

    def begin(self):
        w, z, c = self.wires, self.z, self.c
        dst, sem = self.out.at[z, c], self.recv.at[z, c]
        w.send(self.own, dst, sem, {"z": jnp.minimum(z + 1, NZ - 1)}, z < NZ - 1)
        w.send(self.own, dst, sem, {"z": jnp.maximum(z - 1, 0)}, z > 0)
        w.send(self.own, dst, sem, {"c": 1 - c})

    def event(self, k):
        w, z, c = self.wires, self.z, self.c
        zq = line_order(z, k)
        slot, sem = self.out.at[zq, c], self.recv.at[zq, c]
        w.arrived(slot, sem, {"c": 1 - c})
        onward = jnp.where(zq < z, jnp.minimum(z + 1, NZ - 1), jnp.maximum(z - 1, 0))
        w.send(slot, slot, sem, {"z": onward}, (z > 0) & (z < NZ - 1))
        w.send(slot, slot, sem, {"c": 1 - c})

    def sibling(self, zq):
        w, c = self.wires, self.c
        w.arrived(self.out.at[zq, 1 - c], self.recv.at[zq, 1 - c], {"c": 1 - c})


def segments(nx, fs):
    for yq in range(2):
        for zq in range(NZ):
            for xq in range(nx):
                for cq in range(NC):
                    first = (((yq * NZ + zq) * nx + xq) * NC + cq) * fs
                    yield zq, cq, (yq * nx + xq) * fs, first


def weight_gather_kernel(
    nx, a, g, u, d, tok, ao, guo, do, co, gu, send_sems, local_sems, ra, rt, rw, rd, rc
):
    y, z, x, c = place()
    sib = {"c": 1 - c}
    ypeer = {"y": 1 - y}
    xpeers = [(x + i + 1) % nx for i in range(nx - 1)]
    planes = [{"x": xp} for xp in xpeers] + [ypeer]
    cross = [{"z": (z + k + 1) % NZ, "c": 1 - c} for k in range(NZ - 1)]
    greet(line_peers(z, c) + cross + planes)
    locals_ = [
        pltpu.make_async_copy(a, ao.at[y, z, x, c], local_sems.at[0]),
        pltpu.make_async_copy(d, do.at[y, x], local_sems.at[1]),
        pltpu.make_async_copy(tok, co.at[z, c], local_sems.at[2]),
    ]
    keep = pltpu.make_async_copy(gu.at[z, c], guo.at[:, y, z, x, c], local_sems.at[3])
    for copy in locals_:
        copy.start()
    wires = Wires(send_sems)

    def both_ways(src, dst, sem):
        for peer in planes:
            wires.send(src, dst, sem, peer)

    own_slot, own_sem = ao.at[y, z, x, c], ra.at[y, z, x, c]
    wires.send(a, own_slot, own_sem, {"z": jnp.minimum(z + 1, NZ - 1)}, z < NZ - 1)
    wires.send(a, own_slot, own_sem, {"z": jnp.maximum(z - 1, 0)}, z > 0)
    both_ways(a, own_slot, own_sem)
    wires.send(a, own_slot, own_sem, sib)
    fs = gu.shape[-1] // (2 * nx)
    for m, shard in enumerate((g, u)):
        for zq, cq, run, first in segments(nx, fs):
            gu[zq, cq, m, :, run : run + fs] = shard[:, first : first + fs]
    keep.start()
    for k in range(NZ - 1):
        zq = line_order(z, k)
        slot, sem = ao.at[y, zq, x, c], ra.at[y, zq, x, c]
        wires.arrived(slot, sem, sib)
        onward = jnp.where(zq < z, jnp.minimum(z + 1, NZ - 1), jnp.maximum(z - 1, 0))
        wires.send(slot, slot, sem, {"z": onward}, (z > 0) & (z < NZ - 1))
        both_ways(slot, slot, sem)
        wires.send(slot, slot, sem, sib)

    for k in range(NZ * NC - 1):
        step = k + 1
        zp, cp = (z + step // NC) % NZ, (c + step) % NC
        wires.send(
            gu.at[zp, cp], guo.at[:, y, z, x, c], rt.at[z, c], {"z": zp, "c": cp}
        )
    line = LineGather(wires, tok, co, rc, z, c)
    line.begin()
    half = d.shape[1] // 2
    parts = [pl.ds(0, half), pl.ds(half, half)]
    for h in range(2):
        both_ways(d.at[:, parts[h]], do.at[y, x, :, parts[h]], rd.at[h, y, x])

    def relay_attn(yq, xq, zq, peers):
        slot, sem = ao.at[yq, zq, xq, c], ra.at[yq, zq, xq, c]
        wires.arrived(slot, sem, sib)
        for peer in peers:
            wires.send(slot, slot, sem, peer)
        wires.send(slot, slot, sem, sib)

    for zq in range(NZ):
        for xp in xpeers:
            relay_attn(y, xp, zq, [ypeer] if zq < NZ // 2 else [])
        relay_attn(1 - y, x, zq, planes[:-1] if zq >= NZ // 2 else [])

    for k in range(NZ * NC - 1):
        step = k + 1
        zp, cp = (z + step // NC) % NZ, (c + step) % NC
        wires.arrived(guo.at[:, y, zp, x, cp], rt.at[zp, cp], sib)
    keep.wait()
    for m in range(2):
        plane = guo.at[m, y, :, x]
        both_ways(plane, plane, rw.at[m, y, x])
    line.event(0)

    def relay(ref, sem, peers):
        wires.arrived(ref, sem, sib)
        for peer in peers:
            wires.send(ref, ref, sem, peer)

    for xp in xpeers:
        relay(do.at[y, xp, :, parts[0]], rd.at[0, y, xp], [ypeer])
        relay(do.at[y, xp, :, parts[1]], rd.at[1, y, xp], [])
    relay(do.at[1 - y, x, :, parts[1]], rd.at[1, 1 - y, x], planes[:-1])
    relay(do.at[1 - y, x, :, parts[0]], rd.at[0, 1 - y, x], [])
    for xp in xpeers:
        for zq in range(NZ):
            relay_attn(1 - y, xp, zq, [])
    line.event(1)
    for xp in xpeers:
        relay(guo.at[0, y, :, xp], rw.at[0, y, xp], [ypeer])
    relay(guo.at[1, 1 - y, :, x], rw.at[1, 1 - y, x], planes[:-1])
    line.event(2)
    for xp in xpeers:
        relay(guo.at[1, y, :, xp], rw.at[1, y, xp], [])
    relay(guo.at[0, 1 - y, :, x], rw.at[0, 1 - y, x], [])
    for xp in xpeers:
        for h in range(2):
            relay(do.at[1 - y, xp, :, parts[h]], rd.at[h, 1 - y, xp], [])
            relay(guo.at[h, 1 - y, :, xp], rw.at[h, 1 - y, xp], [])
    for zq in range(NZ):
        line.sibling(zq)
    for yq in range(2):
        for zq in range(NZ):
            for xq in range(nx):
                wires.arrived(ao.at[yq, zq, xq, 1 - c], ra.at[yq, zq, xq, 1 - c], sib)
    wires.finish()
    for copy in locals_:
        copy.wait()


def weight_gather(ny, nx, a, g, u, d, tok, collective_id):
    sends = 3 + (nx + 1) + 3 * (nx + 2)
    sends += 7 + 9 + 2 * nx
    sends += 4 * nx + 2 * (nx - 1) + 2 * (nx - 1)
    sends += 2 * nx + 2 * (nx - 1) + 4 * (nx - 1) + 2 * (nx - 1)
    hbm = pl.BlockSpec(memory_space=pl.ANY)
    vmem = pl.BlockSpec(memory_space=pltpu.VMEM)
    grid = (ny, NZ, nx, NC)
    block = g.shape[:1] + (g.shape[1] // (NZ * NC),)
    return pl.pallas_call(
        lambda *refs: weight_gather_kernel(nx, *refs),
        name="weight_gather",
        out_shape=(
            jax.ShapeDtypeStruct(grid + a.shape, BF16),
            jax.ShapeDtypeStruct((2,) + grid + block, BF16),
            jax.ShapeDtypeStruct((ny, nx) + d.shape, BF16),
            jax.ShapeDtypeStruct((NZ, NC) + tok.shape, BF16),
        ),
        in_specs=[hbm, vmem, vmem, hbm, hbm],
        out_specs=(hbm,) * 4,
        scratch_shapes=[
            pltpu.VMEM((NZ, NC, 2) + block, BF16),
            pltpu.SemaphoreType.DMA((sends + 16,)),
            pltpu.SemaphoreType.DMA((4,)),
            pltpu.SemaphoreType.DMA(grid),
            pltpu.SemaphoreType.DMA((NZ, NC)),
            pltpu.SemaphoreType.DMA((2, ny, nx)),
            pltpu.SemaphoreType.DMA((2, ny, nx)),
            pltpu.SemaphoreType.DMA((NZ, NC)),
        ],
        compiler_params=pltpu.CompilerParams(
            collective_id=collective_id, has_side_effects=True
        ),
    )(a, g, u, d, tok)


def total_into(dst, refs):
    flat = len(dst.shape) == 2

    def entry(i, carry):
        here = (slice(None), pl.ds(pl.multiple_of(i * 128, 128), 128)) if flat else i
        total = refs[0][here].astype(F32)
        for ref in refs[1:]:
            total = total + ref[here].astype(F32)
        dst[here] = total.astype(dst.dtype)
        return carry

    lax.fori_loop(0, dst.shape[1] // 128 if flat else dst.shape[0], entry, 0)


class PlaneScatter:
    def __init__(self, wires, src, first, second, bufs, loaded=False):
        self.wires, self.src = wires, src
        self.name_a, self.size_a, self.a = first
        self.name_b, self.size_b, self.b = second
        self.r1, self.own, self.r2, self.s1, self.sl, self.s2 = bufs
        self.loaded = loaded

    def mine(self, b):
        return self.src(self.a, b) if self.loaded else self.own.at[b]

    def order(self):
        return [(self.b + i + 1) % self.size_b for i in range(self.size_b)]

    def begin(self):
        for b in self.order():
            for i in range(self.size_a - 1):
                peer, j = (self.a + i + 1) % self.size_a, self.size_a - 2 - i
                self.wires.send(
                    self.src(peer, b), self.r1.at[j, b], self.s1.at[j, b], {self.name_a: peer}
                )
            if not self.loaded:
                self.load(b).start()

    def load(self, b):
        return pltpu.make_async_copy(self.src(self.a, b), self.own.at[b], self.sl.at[b])

    def gathered(self, b):
        if not self.loaded:
            self.load(b).wait()
        for j in range(self.size_a - 1):
            self.wires.arrived(self.r1.at[j, b], self.s1.at[j, b], {self.name_a: self.a})
        return [self.mine(b)] + [self.r1.at[j, b] for j in range(self.size_a - 1)]

    def relay(self):
        for i, b in enumerate(self.order()[:-1]):
            j = self.size_b - 2 - i
            total_into(self.mine(b), self.gathered(b))
            self.wires.send(self.mine(b), self.r2.at[j], self.s2.at[j], {self.name_b: b})

    def finish(self, dst):
        refs = self.gathered(self.b)
        for j in range(self.size_b - 1):
            self.wires.arrived(self.r2.at[j], self.s2.at[j], {self.name_b: self.b})
            refs.append(self.r2.at[j])
        total_into(dst, refs)


def plane_scratch(slot, size_a, size_b, loaded=False):
    own = (1,) * (1 + len(slot)) if loaded else (size_b,) + slot
    return [
        pltpu.VMEM((size_a - 1, size_b) + slot, BF16),
        pltpu.VMEM(own, BF16),
        pltpu.VMEM((size_b - 1,) + slot, BF16),
        pltpu.SemaphoreType.DMA((size_a - 1, size_b)),
        pltpu.SemaphoreType.DMA((size_b,)),
        pltpu.SemaphoreType.DMA((size_b - 1,)),
    ]


class LineScatter:
    def __init__(self, wires, part, bufs, z, c):
        self.wires, self.part, self.z, self.c = wires, part, z, c
        self.own, self.sib, self.left, self.right = bufs[:4]
        self.s_own, self.s_sib, self.s_left, self.s_right = bufs[4:]

    def order(self):
        return [line_order(self.z, k) for k in (2, 1, 0)] + [self.z]

    def load(self, zq):
        return pltpu.make_async_copy(
            self.part.at[zq, self.c], self.own.at[zq], self.s_own.at[zq]
        )

    def begin(self):
        for zq in self.order():
            self.wires.send(
                self.part.at[zq, 1 - self.c],
                self.sib.at[zq],
                self.s_sib.at[zq],
                {"c": 1 - self.c},
            )
            self.load(zq).start()

    def ready(self, zq):
        self.load(zq).wait()
        self.wires.arrived(self.sib.at[zq], self.s_sib.at[zq], {"c": 1 - self.c})

    def hop(self, k):
        z = self.z
        for sign, buf, sems in ((1, self.left, self.s_left), (-1, self.right, self.s_right)):
            target = z + sign * k
            inside = (target < NZ) if sign > 0 else (target >= 0)
            behind = (z > 0) if sign > 0 else (z < NZ - 1)
            target = jnp.clip(target, 0, NZ - 1)
            own, sib = self.own.at[target], self.sib.at[target]

            @pl.when(inside)
            def _():
                self.ready(target)

            if k < NZ - 1:

                @pl.when(inside & behind)
                def _():
                    self.wires.arrived(buf.at[k], sems.at[k], {"z": z})
                    total_into(own, [own, sib, buf.at[k]])

                @pl.when(inside & jnp.logical_not(behind))
                def _():
                    total_into(own, [own, sib])

            else:

                @pl.when(inside)
                def _():
                    total_into(own, [own, sib])

            onward = jnp.clip(z + sign, 0, NZ - 1)
            self.wires.send(own, buf.at[k - 1], sems.at[k - 1], {"z": onward}, inside)

    def finish(self, dst):
        z = self.z
        self.ready(z)
        own, sib = self.own.at[z], self.sib.at[z]

        @pl.when(z > 0)
        def _():
            self.wires.arrived(self.left.at[0], self.s_left.at[0], {"z": z})

        @pl.when(z < NZ - 1)
        def _():
            self.wires.arrived(self.right.at[0], self.s_right.at[0], {"z": z})

        @pl.when(z == 0)
        def _():
            total_into(dst, [own, sib, self.right.at[0]])

        @pl.when(z == NZ - 1)
        def _():
            total_into(dst, [own, sib, self.left.at[0]])

        @pl.when((z > 0) & (z < NZ - 1))
        def _():
            total_into(dst, [own, sib, self.left.at[0], self.right.at[0]])


def line_scratch(slot):
    return [
        pltpu.VMEM((NZ,) + slot, BF16),
        pltpu.VMEM((NZ,) + slot, BF16),
        pltpu.VMEM((NZ - 1,) + slot, BF16),
        pltpu.VMEM((NZ - 1,) + slot, BF16),
        pltpu.SemaphoreType.DMA((NZ,)),
        pltpu.SemaphoreType.DMA((NZ,)),
        pltpu.SemaphoreType.DMA((NZ - 1,)),
        pltpu.SemaphoreType.DMA((NZ - 1,)),
    ]


TILES = ((0, 640), (640, None))


def remote(src, dst, send_sem, recv_sem, device):
    return pltpu.make_async_remote_copy(
        src_ref=src,
        dst_ref=dst,
        send_sem=send_sem,
        recv_sem=recv_sem,
        device_id=device,
        device_id_type=pl.DeviceIdType.MESH,
    )


def mlp_kernel(
    h,
    wg,
    wu,
    wd,
    cot,
    dh,
    out_part,
    grad_g,
    grad_u,
    grad_d,
    hv,
    cv,
    wgv,
    wuv,
    wdv,
    av,
    dgv,
    duv,
    part,
    sib,
    ring,
    ob,
    s_load,
    s_cot,
    s_ob,
    s_out,
    h_send,
    h_on,
    h_sib,
    h_recv,
    p_send,
    p_recv,
    r_send,
    r_recv,
):
    y, z, x, c = place()
    rows, wide = h.shape
    units = wg.shape[1]
    other = 1 - c
    inner = (z > 0) & (z < NZ - 1)
    greet(line_peers(z, c))

    def block(zq, cq):
        return pl.ds(pl.multiple_of((zq * NC + cq) * rows, rows), rows)

    loads = [
        pltpu.make_async_copy(h, hv.at[block(z, c)], s_load.at[0]),
        pltpu.make_async_copy(wg, wgv, s_load.at[1]),
        pltpu.make_async_copy(wu, wuv, s_load.at[2]),
        pltpu.make_async_copy(wd, wdv, s_load.at[3]),
    ]

    def load_cot(zq, cq):
        return pltpu.make_async_copy(
            cot.at[block(zq, cq)], cv.at[block(zq, cq)], s_cot.at[zq, cq]
        )

    def send_own(i):
        there = hv.at[block(z, c)]
        device = (
            {"z": jnp.minimum(z + 1, NZ - 1)},
            {"z": jnp.maximum(z - 1, 0)},
            {"c": other},
        )[i]
        return remote(h, there, h_send.at[i], h_recv.at[z, c], device)

    pl.when(z < NZ - 1)(send_own(0).start)
    pl.when(z > 0)(send_own(1).start)
    send_own(2).start()
    for copy in loads[:3]:
        copy.start()
    load_cot(z, c).start()
    loads[3].start()
    load_cot(z, other).start()
    for k in range(NZ - 1):
        for i in range(NC):
            load_cot(line_order(z, k), (c + i) % NC).start()

    def arrival(zq, cq):
        here = hv.at[block(zq, cq)]
        return remote(here, here, h_send.at[0], h_recv.at[zq, cq], {"c": other})

    def onward(k):
        zq = line_order(z, k)
        here = hv.at[block(zq, c)]
        device = {"z": jnp.where(zq < z, jnp.minimum(z + 1, NZ - 1), jnp.maximum(z - 1, 0))}
        return remote(here, here, h_on.at[k], h_recv.at[zq, c], device)

    def to_sibling(k):
        zq = line_order(z, k)
        here = hv.at[block(zq, c)]
        return remote(here, here, h_sib.at[k], h_recv.at[zq, c], {"c": other})

    def take(k):
        arrival(line_order(z, k), c).wait_recv()
        pl.when(inner)(onward(k).start)
        to_sibling(k).start()

    def output(zq, cq):
        return pltpu.make_async_copy(ob.at[cq], out_part.at[block(zq, cq)], s_ob.at[cq])

    def partial_over(zq):
        return remote(
            part.at[block(zq, other)], sib.at[zq], p_send.at[zq], p_recv.at[zq], {"c": other}
        )

    def partial_home(zq):
        j = (z - zq + NZ) % NZ - 1
        return remote(
            part.at[block(zq, c)], ring.at[j], r_send.at[zq], r_recv.at[j], {"z": zq}
        )

    piece = rows // 8

    def combine(zq):
        remote(sib.at[zq], sib.at[zq], p_send.at[0], p_recv.at[zq], {"c": other}).wait_recv()

        def step(i, carry):
            here = pl.ds(pl.multiple_of((zq * NC + c) * rows + i * piece, piece), piece)
            there = pl.ds(pl.multiple_of(i * piece, piece), piece)
            total = part[here].astype(F32) + sib[zq, there].astype(F32)
            part[here] = total.astype(BF16)
            return carry

        lax.fori_loop(0, 8, step, 0)

    def place_of(k):
        near = line_order(z, 0)
        mid = line_order(z, 1)
        far = line_order(z, 2)
        return jnp.where(k == 0, z, jnp.where(k == 1, near, jnp.where(k == 2, mid, far)))

    def pair(k, carry):
        zq = place_of(k)

        @pl.when(k == 1)
        def _():
            take(0)
            pl.when(inner)(lambda: take(1))

        @pl.when(k == 2)
        def _():
            pl.when(jnp.logical_not(inner))(lambda: take(1))
            pl.when(inner)(lambda: take(2))

        @pl.when((k == 3) & jnp.logical_not(inner))
        def _():
            take(2)

        def one(j, carry):
            cq = (c + j) % NC
            here = block(zq, cq)

            @pl.when((k == 0) & (j == 0))
            def _():
                for copy in loads:
                    copy.wait()

            @pl.when(j == 1)
            def _():
                arrival(zq, cq).wait_recv()

            load_cot(zq, cq).wait()
            for low, high in TILES:
                high = units if high is None else high
                gate = dot(hv[here], wgv[:, low:high])
                up = dot(hv[here], wuv[:, low:high])
                grad = dot_nt(cv[here], wdv[low:high])
                sig = jax.nn.sigmoid(gate)
                act = gate * sig
                av[here, low:high] = (act * up).astype(BF16)
                duv[here, low:high] = (grad * act).astype(BF16)
                dgv[here, low:high] = (
                    grad * up * (sig * (1.0 + gate * (1.0 - sig)))
                ).astype(BF16)

            @pl.when(k > 0)
            def _():
                output(zq, cq).wait()

            ob[cq] = dot(av[here], wdv[...]).astype(BF16)
            output(zq, cq).start()
            part[here] = (dot_nt(dgv[here], wgv[...]) + dot_nt(duv[here], wuv[...])).astype(BF16)
            return carry

        lax.fori_loop(0, NC, one, 0)
        partial_over(zq).start()

        @pl.when(k > 1)
        def _():
            before = place_of(k - 1)
            combine(before)
            partial_home(before).start()

        return carry

    lax.fori_loop(0, NZ, pair, 0)
    last = line_order(z, NZ - 2)
    step_d = wide // 6

    def down_grad(t, carry):
        cols = pl.ds(pl.multiple_of(t * step_d, step_d), step_d)
        wdv[:, cols] = dot_tn(av[...], cv[:, cols]).astype(BF16)

        @pl.when(t == 0)
        def _():
            combine(last)
            partial_home(last).start()

        return carry

    lax.fori_loop(0, 6, down_grad, 0)
    outs = [
        pltpu.make_async_copy(wdv, grad_d, s_out.at[0]),
        pltpu.make_async_copy(wgv, grad_g, s_out.at[1]),
        pltpu.make_async_copy(wuv, grad_u, s_out.at[2]),
    ]
    outs[0].start()

    def gate_grad(t, carry):
        cols = pl.ds(pl.multiple_of(t * step_d, step_d), step_d)
        wgv[cols] = dot_tn(hv[:, cols], dgv[...]).astype(BF16)
        wuv[cols] = dot_tn(hv[:, cols], duv[...]).astype(BF16)
        return carry

    lax.fori_loop(0, 6, gate_grad, 0)
    outs[1].start()
    outs[2].start()
    combine(z)
    for j in range(NZ - 1):
        remote(ring.at[j], ring.at[j], r_send.at[0], r_recv.at[j], {"c": other}).wait_recv()

    def final(i, carry):
        here = pl.ds(pl.multiple_of((z * NC + c) * rows + i * piece, piece), piece)
        there = pl.ds(pl.multiple_of(i * piece, piece), piece)
        total = part[here].astype(F32)
        for j in range(NZ - 1):
            total = total + ring[j, there].astype(F32)
        dh[there] = total
        return carry

    lax.fori_loop(0, 8, final, 0)
    pl.when(z < NZ - 1)(send_own(0).wait_send)
    pl.when(z > 0)(send_own(1).wait_send)
    send_own(2).wait_send()
    for k in range(NZ - 1):
        pl.when(inner)(onward(k).wait_send)
        to_sibling(k).wait_send()
        partial_home(line_order(z, k)).wait_send()
    for zq in range(NZ):
        partial_over(zq).wait_send()
    for cq in range(NC):
        output(z, cq).wait()
    for copy in outs:
        copy.wait()


def mlp(h, wg, wu, wd, cot, collective_id):
    hbm = pl.BlockSpec(memory_space=pl.ANY)
    vmem = pl.BlockSpec(memory_space=pltpu.VMEM)
    rows, wide = h.shape
    units = wg.shape[1]
    every = NZ * NC * rows
    dma = pltpu.SemaphoreType.DMA
    return pl.pallas_call(
        mlp_kernel,
        name="mlp",
        out_shape=(
            jax.ShapeDtypeStruct((rows, wide), F32),
            jax.ShapeDtypeStruct((every, wide), BF16),
            jax.ShapeDtypeStruct((wide, units), BF16),
            jax.ShapeDtypeStruct((wide, units), BF16),
            jax.ShapeDtypeStruct((units, wide), BF16),
        ),
        in_specs=[hbm] * 5,
        out_specs=(vmem, hbm, hbm, hbm, hbm),
        scratch_shapes=[
            pltpu.VMEM((every, wide), BF16),
            pltpu.VMEM((every, wide), BF16),
            pltpu.VMEM((wide, units), BF16),
            pltpu.VMEM((wide, units), BF16),
            pltpu.VMEM((units, wide), BF16),
            pltpu.VMEM((every, units), BF16),
            pltpu.VMEM((every, units), BF16),
            pltpu.VMEM((every, units), BF16),
            pltpu.VMEM((every, wide), BF16),
            pltpu.VMEM((NZ, rows, wide), BF16),
            pltpu.VMEM((NZ - 1, rows, wide), BF16),
            pltpu.VMEM((NC, rows, wide), BF16),
            dma((4,)),
            dma((NZ, NC)),
            dma((NC,)),
            dma((3,)),
            dma((3,)),
            dma((NZ - 1,)),
            dma((NZ - 1,)),
            dma((NZ, NC)),
            dma((NZ,)),
            dma((NZ,)),
            dma((NZ,)),
            dma((NZ - 1,)),
        ],
        compiler_params=pltpu.CompilerParams(
            collective_id=collective_id, has_side_effects=True, vmem_limit_bytes=63 << 20
        ),
    )(h, wg, wu, wd, cot)


def plane_peers(nx, y, x):
    return [{"x": (x + i + 1) % nx} for i in range(nx - 1)] + [{"y": 1 - y}]


def last_scatter_kernel(nx, widths, grads, gate, up, down, result, *rest):
    y, z, x, c = place()
    outs, rest = rest[: len(widths)], rest[len(widths) :]
    gate_out, up_out, down_out, result_out, rest = rest[:4] + (rest[4:],)
    send_sems, blocks, own, sib, line_sum, line_in = rest[:6]
    s_block, s_keep, s_own, s_sib, s_line = rest[6:11]
    half_x, half_y = rest[11:17], rest[17:23]
    gate_bufs, up_bufs, gu = rest[23:29], rest[29:35], rest[35]
    left_bufs, right_bufs, line_bufs = rest[36:42], rest[42:48], rest[48:56]
    cross = [{"z": (z + k + 1) % NZ, "c": 1 - c} for k in range(NZ - 1)]
    greet(line_peers(z, c) + cross + plane_peers(nx, y, x))
    wires = Wires(send_sems)
    along_x, along_y = ("x", nx, x), ("y", 2, y)
    gate_plane = PlaneScatter(
        wires, lambda xq, yq: gate.at[yq, :, xq], along_x, along_y, gate_bufs
    )
    up_plane = PlaneScatter(wires, lambda yq, xq: up.at[yq, :, xq], along_y, along_x, up_bufs)
    cols = down.shape[-1] // 2
    left, right = pl.ds(0, cols), pl.ds(cols, cols)
    left_plane = PlaneScatter(
        wires, lambda xq, yq: down.at[yq, xq, :, left], along_x, along_y, left_bufs
    )
    right_plane = PlaneScatter(
        wires, lambda yq, xq: down.at[yq, xq, :, right], along_y, along_x, right_bufs
    )
    line = LineScatter(wires, result, line_bufs, z, c)
    gate_plane.begin()
    up_plane.begin()
    line.begin()
    n = NZ // 2
    halves = [pl.ds(0, n), pl.ds(n, n)]

    def load(h, yq):
        return pltpu.make_async_copy(
            grads.at[yq, halves[h], :, c], own.at[yq, halves[h]], s_own.at[h, yq]
        )

    for h in range(2):
        for yq in range(2):
            wires.send(
                grads.at[yq, halves[h], :, 1 - c],
                sib.at[yq, halves[h]],
                s_sib.at[h, yq],
                {"c": 1 - c},
            )
            load(h, yq).start()

    def combine(h):
        for yq in range(2):
            load(h, yq).wait()
            wires.arrived(sib.at[yq, halves[h]], s_sib.at[h, yq], {"c": 1 - c})
            for i in range(n):
                zq = h * n + i
                total_into(own.at[yq, zq], [own.at[yq, zq], sib.at[yq, zq]])

    by_x = PlaneScatter(
        wires, lambda xq, yq: own.at[yq, halves[0], xq], along_x, along_y, half_x, True
    )
    by_y = PlaneScatter(
        wires, lambda yq, xq: own.at[yq, halves[1], xq], along_y, along_x, half_y, True
    )
    combine(0)
    by_x.begin()
    combine(1)
    by_y.begin()
    line.hop(3)
    left_plane.begin()
    right_plane.begin()
    line.hop(2)
    gate_plane.relay()
    up_plane.relay()
    line.hop(1)
    by_x.relay()
    by_y.relay()
    left_plane.relay()
    right_plane.relay()
    gate_plane.finish(gu.at[0])
    up_plane.finish(gu.at[1])
    keep = pltpu.make_async_copy(gu.at[:, z, c], blocks.at[z, c], s_keep)
    keep.start()
    for k in range(NZ * NC - 1):
        step = k + 1
        zp, cp = (z + step // NC) % NZ, (c + step) % NC
        wires.send(gu.at[:, zp, cp], blocks.at[z, c], s_block.at[z, c], {"z": zp, "c": cp})
    by_x.finish(line_sum.at[halves[0]])
    by_y.finish(line_sum.at[halves[1]])
    for k in range(NZ - 1):
        zp = (z + k + 1) % NZ
        wires.send(line_sum.at[zp], line_in.at[NZ - 2 - k], s_line.at[NZ - 2 - k], {"z": zp})
    line.finish(result_out)
    left_plane.finish(down_out.at[:, left])
    right_plane.finish(down_out.at[:, right])
    keep.wait()
    for k in range(NZ * NC - 1):
        step = k + 1
        zp, cp = (z + step // NC) % NZ, (c + step) % NC
        wires.arrived(blocks.at[zp, cp], s_block.at[zp, cp], {"c": 1 - c})
    fs = blocks.shape[-1] // (2 * nx)
    for m, out in enumerate((gate_out, up_out)):
        for zq, cq, run, first in segments(nx, fs):
            out[:, first : first + fs] = blocks[zq, cq, m, :, run : run + fs].astype(F32)
    for k in range(NZ - 1):
        wires.arrived(line_in.at[k], s_line.at[k], {"c": 1 - c})
    first = 0
    for out, width in zip(outs, widths):
        columns = slice(first, first + width)
        total = line_sum[z, :, columns].astype(F32)
        for k in range(NZ - 1):
            total = total + line_in[k, :, columns].astype(F32)
        out[...] = total
        first += width
    wires.finish()


def last_scatter(ny, nx, grads, widths, gate, up, down, result, collective_id):
    hbm = pl.BlockSpec(memory_space=pl.ANY)
    vmem = pl.BlockSpec(memory_space=pltpu.VMEM)
    rows, width = grads.shape[4:]
    block = gate.shape[4:]
    slot = (NZ // 2, rows, width)
    gate_slot = (NZ, NC) + block
    down_slot = (down.shape[2], down.shape[3] // 2)
    sends = 4 + 7 + NZ - 1 + 3 * ((nx - 1) * 2 + 1 + nx + (nx - 1)) + NZ + 2 * (NZ - 1)
    spread = block[1] * NZ * NC
    shapes = [(rows, w) for w in widths] + [(rows, spread)] * 2
    shapes += [down.shape[2:], result.shape[2:]]
    return pl.pallas_call(
        lambda *refs: last_scatter_kernel(nx, widths, *refs),
        name="last_scatter",
        out_shape=tuple(jax.ShapeDtypeStruct(shape, F32) for shape in shapes),
        in_specs=[hbm] * 5,
        out_specs=(vmem,) * len(shapes),
        scratch_shapes=[
            pltpu.SemaphoreType.DMA((sends,)),
            pltpu.VMEM((NZ, NC, 2) + block, BF16),
            pltpu.VMEM((ny, NZ, nx, rows, width), BF16),
            pltpu.VMEM((ny, NZ, nx, rows, width), BF16),
            pltpu.VMEM((NZ, rows, width), BF16),
            pltpu.VMEM((NZ - 1, rows, width), BF16),
            pltpu.SemaphoreType.DMA((NZ, NC)),
            pltpu.SemaphoreType.DMA,
            pltpu.SemaphoreType.DMA((2, 2)),
            pltpu.SemaphoreType.DMA((2, 2)),
            pltpu.SemaphoreType.DMA((NZ - 1,)),
        ]
        + plane_scratch(slot, nx, ny, True)
        + plane_scratch(slot, ny, nx, True)
        + plane_scratch(gate_slot, nx, ny)
        + plane_scratch(gate_slot, ny, nx)
        + [pltpu.VMEM((2,) + gate_slot, BF16)]
        + plane_scratch(down_slot, nx, ny)
        + plane_scratch(down_slot, ny, nx)
        + line_scratch(result.shape[2:]),
        compiler_params=pltpu.CompilerParams(
            collective_id=collective_id, has_side_effects=True, vmem_limit_bytes=60 << 20
        ),
    )(grads, gate, up, down, result)


def make_body(ny, nx):
    def body(
        inputs,
        segment_ids,
        attn_gain,
        q_weight,
        k_weight,
        v_weight,
        qkv_bias,
        o_weight,
        mlp_gain,
        gate_weight,
        up_weight,
        down_weight,
        cotangent,
    ):
        tok_rows = inputs.shape[1]
        hidden_in = inputs[0].astype(F32)
        grad_out = cotangent[0]
        seg_all = segment_ids[0]
        length = seg_all.shape[0]
        seq_place = lax.axis_index("y")
        tok_pos = seq_place * tok_rows + jnp.arange(tok_rows)
        cos_tok, sin_tok = tables(tok_pos)
        query_width = q_weight.shape[1]
        key_width = k_weight.shape[1]
        kv_heads = key_width // HD
        q_heads = query_width // HD
        group = q_heads // kv_heads

        g_rows = attn_gain.shape[0]
        b_rows = qkv_bias.shape[0]
        qkv_width = query_width + 2 * key_width
        extra = jnp.concatenate(
            [
                attn_gain[:, None],
                mlp_gain[:, None],
                jnp.broadcast_to(qkv_bias[None], (g_rows, b_rows)),
                jnp.zeros((g_rows, HD - 2 - b_rows), BF16),
            ],
            axis=1,
        )
        packed = jnp.concatenate([q_weight, k_weight, v_weight, o_weight, extra], axis=1)
        attn_all, columns_all, down_all, grad_out_all = weight_gather(
            ny,
            nx,
            packed,
            gate_weight,
            up_weight,
            down_weight,
            grad_out,
            0,
        )
        full = attn_all.reshape(-1, packed.shape[1])
        full_qkv = full[:, :qkv_width]
        full_out = full[:, qkv_width : qkv_width + query_width]
        tail = attn_all[..., qkv_width + query_width :].astype(F32)
        gain_one = tail[..., 0].reshape(-1)
        gain_two = tail[..., 1].reshape(-1)
        bias = tail[..., 0, 2 : 2 + b_rows].reshape(-1)
        width = gate_weight.shape[1] // (NZ * NC)
        full_gate = columns_all[0].reshape(-1, width)
        full_up = columns_all[1].reshape(-1, width)
        full_down = down_all.reshape(width, -1)
        grad_out_all = grad_out_all.reshape(-1, grad_out.shape[1])

        rescale_one = lax.rsqrt(jnp.mean(hidden_in * hidden_in, axis=-1, keepdims=True) + EPS)
        normed_one = hidden_in * rescale_one
        input_one = (normed_one * gain_one).astype(BF16)
        qkv_pre = dot(input_one, full_qkv) + bias
        query = rotate(qkv_pre[:, :query_width], cos_tok, sin_tok).astype(BF16)
        key = rotate(qkv_pre[:, query_width : query_width + key_width], cos_tok, sin_tok)
        kv = jnp.concatenate([key, qkv_pre[:, query_width + key_width :]], axis=1).astype(BF16)
        kv_all = lax.all_gather(kv, "y", axis=0, tiled=True)
        key_heads = kv_all[:, :key_width].reshape(length, kv_heads, HD)
        value_heads = kv_all[:, key_width:].reshape(length, kv_heads, HD)
        query_heads = query.reshape(tok_rows, kv_heads, group, HD)
        score_scale = HD ** (-0.5)
        all_pos = jnp.arange(length)
        seg_tok = lax.dynamic_slice(seg_all, (seq_place * tok_rows,), (tok_rows,))
        allowed = (tok_pos[:, None] >= all_pos[None, :]) & (seg_tok[:, None] == seg_all[None, :])
        scores = (
            jnp.einsum("qkgd,pkd->kgqp", query_heads, key_heads, preferred_element_type=F32)
            * score_scale
        )
        masked = jnp.where(allowed[None, None], scores, MASKED)
        row_max = jnp.max(masked, axis=-1, keepdims=True)
        exponent = jnp.exp(masked - row_max)
        row_total = jnp.sum(exponent, axis=-1, keepdims=True)
        probs = exponent / row_total
        probs_low = probs.astype(BF16)
        mixture = jnp.einsum("kgqp,pkd->qkgd", probs_low, value_heads, preferred_element_type=F32)
        attn_tok = mixture.astype(BF16).reshape(tok_rows, query_width)
        middle = hidden_in + dot(attn_tok, full_out)

        rescale_two = lax.rsqrt(jnp.mean(middle * middle, axis=-1, keepdims=True) + EPS)
        normed_two = middle * rescale_two
        input_two = (normed_two * gain_two).astype(BF16)
        by_shard = (ny, NZ, nx, NC, g_rows, width)
        grad_input_two, out_part, part_gate, part_up, part_down = mlp(
            input_two, full_gate, full_up, full_down, grad_out_all, 1
        )
        grad_gain_two, grad_mid = norm_back(grad_input_two, normed_two, rescale_two, gain_two)
        grad_mid = grad_mid + grad_out.astype(F32)
        grad_branch = grad_mid.astype(BF16)
        grad_attn = dot_nt(grad_branch, full_out).astype(BF16)
        grad_heads = grad_attn.reshape(tok_rows, kv_heads, group, HD)
        grad_probs = jnp.einsum(
            "qkgd,pkd->kgqp", grad_heads, value_heads, preferred_element_type=F32
        )
        inner_sum = jnp.sum(probs * grad_probs, axis=-1, keepdims=True)
        grad_scores = (probs * (grad_probs - inner_sum)).astype(BF16)
        grad_query = (
            jnp.einsum("kgqp,pkd->qkgd", grad_scores, key_heads, preferred_element_type=F32)
            * score_scale
        ).reshape(tok_rows, query_width)
        grad_key = (
            jnp.einsum("kgqp,qkgd->pkd", grad_scores, query_heads, preferred_element_type=F32)
            * score_scale
        ).reshape(length, key_width)
        grad_value = jnp.einsum(
            "kgqp,qkgd->pkd", probs_low, grad_heads, preferred_element_type=F32
        ).reshape(length, key_width)
        grad_kv = jnp.concatenate([grad_key, grad_value], axis=1).astype(BF16)
        other = lax.dynamic_slice(
            grad_kv, ((1 - seq_place) * tok_rows, 0), (tok_rows, 2 * key_width)
        )
        own = lax.dynamic_slice(grad_kv, (seq_place * tok_rows, 0), (tok_rows, 2 * key_width))
        swapped = lax.ppermute(other, "y", [(0, 1), (1, 0)])
        grad_kv_tok = own.astype(F32) + swapped.astype(F32)
        grad_query_pre = rotate(grad_query, cos_tok, -sin_tok).astype(BF16)
        grad_key_pre = rotate(grad_kv_tok[:, :key_width], cos_tok, -sin_tok).astype(BF16)
        grad_value_pre = grad_kv_tok[:, key_width:].astype(BF16)
        grad_qkv = jnp.concatenate([grad_query_pre, grad_key_pre, grad_value_pre], axis=1)
        grad_qkv_sum = jnp.sum(grad_qkv.astype(F32), axis=0)
        grad_input_one = dot_nt(grad_qkv, full_qkv)
        grad_gain_one, grad_first = norm_back(grad_input_one, normed_one, rescale_one, gain_one)
        grad_total = grad_mid + grad_first
        shards = ny * NZ * nx * NC
        tail_grads = jnp.concatenate(
            [
                grad_gain_one[:, None],
                grad_gain_two[:, None],
                jnp.broadcast_to(
                    grad_qkv_sum.reshape(shards, 1, b_rows), (shards, g_rows, b_rows)
                ).reshape(-1, b_rows),
                jnp.zeros((shards * g_rows, HD - 2 - b_rows), F32),
            ],
            axis=1,
        )
        grad_attn_w = jnp.concatenate(
            [
                dot_tn(input_one, grad_qkv).astype(BF16),
                dot_tn(attn_tok, grad_branch).astype(BF16),
                tail_grads.astype(BF16),
            ],
            axis=1,
        )
        widths = (query_width, key_width, key_width, query_width, HD)
        pieces = (NZ, NC, tok_rows // 32, 32, hidden_in.shape[1])
        outs = last_scatter(
            ny,
            nx,
            grad_attn_w.reshape((ny, NZ, nx, NC, g_rows, -1)),
            widths,
            part_gate.reshape(by_shard),
            part_up.reshape(by_shard),
            part_down.reshape((ny, nx) + down_weight.shape),
            out_part.reshape(pieces),
            3,
        )
        grad_q, grad_k, grad_v, grad_o, tail_sum = outs[:5]
        grad_gate_w, grad_up_w, grad_down_w, out_sum = outs[5:]
        output = (middle + out_sum.reshape(middle.shape)).astype(BF16)[None]
        return (
            output,
            grad_total.astype(BF16)[None],
            tail_sum[:, 0],
            grad_q,
            grad_k,
            grad_v,
            tail_sum[0, 2 : 2 + b_rows],
            grad_o,
            tail_sum[:, 1],
            grad_gate_w,
            grad_up_w,
            grad_down_w,
        )

    return body


def solution(mesh):
    ny = mesh.shape["seq"]
    nx = mesh.shape["fsdp"] // (NZ * NC)
    grid = Mesh(mesh.devices.reshape(ny, NZ, nx, NC), ALL)
    tokens = P(("z", "x", "c"), "y", None)
    rows = P(ALL, None)
    vec = P(ALL)
    return jax.shard_map(
        make_body(ny, nx),
        mesh=grid,
        in_specs=(
            tokens,
            P(("z", "x", "c"), None),
            vec,
            rows,
            rows,
            rows,
            vec,
            rows,
            vec,
            rows,
            rows,
            rows,
            tokens,
        ),
        out_specs=(tokens, tokens, vec, rows, rows, rows, vec, rows, vec, rows, rows, rows),
        check_vma=False,
    )
```

```python
import jax
import jax.numpy as jnp
from jax import lax
from jax.experimental import pallas as pl
from jax.experimental.pallas import tpu as pltpu
from jax.sharding import Mesh, PartitionSpec as P

HD = 128
EPS = 1e-06
ROPE_BASE = 1000000.0
MASKED = -1e30
NZ = 4
NC = 2
ALL = ("y", "z", "x", "c")
TP = ("z", "c")
DP = ("y", "x")
F32 = jnp.float32
BF16 = jnp.bfloat16


def tables(positions):
    freq = ROPE_BASE ** (-jnp.arange(0, HD, 2).astype(F32) / HD)
    angle = positions.astype(F32)[:, None] * freq[None, :]
    return (jnp.cos(angle), jnp.sin(angle))


def rotate(values, cosine, sine):
    count = values.shape[0]
    split = values.reshape(count, -1, HD)
    half = HD // 2
    first = split[..., :half]
    second = split[..., half:]
    cos_b = cosine[:, None, :]
    sin_b = sine[:, None, :]
    turned = jnp.concatenate(
        [first * cos_b - second * sin_b, second * cos_b + first * sin_b], axis=-1
    )
    return turned.reshape(count, -1)


def dot(a, b):
    return jnp.dot(a, b, preferred_element_type=F32)


def dot_nt(a, b):
    return lax.dot_general(a, b, (((1,), (1,)), ((), ())), preferred_element_type=F32)


def dot_tn(a, b):
    return lax.dot_general(a, b, (((0,), (0,)), ((), ())), preferred_element_type=F32)


def norm_back(grad_normed, normed, rescale, gain_vec):
    grad_gain = jnp.sum(grad_normed * normed, axis=0)
    scaled = grad_normed * gain_vec
    grad_x = rescale * (scaled - normed * jnp.mean(scaled * normed, axis=-1, keepdims=True))
    return (grad_gain, grad_x)


class Wires:
    def __init__(self, sems):
        self.sems = sems
        self.used = 0
        self.started = []

    def send(self, src, dst, recv_sem, device, cond=None):
        copy = pltpu.make_async_remote_copy(
            src_ref=src,
            dst_ref=dst,
            send_sem=self.sems.at[self.used],
            recv_sem=recv_sem,
            device_id=device,
            device_id_type=pl.DeviceIdType.MESH,
        )
        self.used += 1
        if cond is None:
            copy.start()
        else:
            pl.when(cond)(copy.start)
        self.started.append((copy, cond))

    def arrived(self, dst, recv_sem, device):
        pltpu.make_async_remote_copy(
            src_ref=dst,
            dst_ref=dst,
            send_sem=self.sems.at[0],
            recv_sem=recv_sem,
            device_id=device,
            device_id_type=pl.DeviceIdType.MESH,
        ).wait_recv()

    def finish(self):
        for copy, cond in self.started:
            if cond is None:
                copy.wait_send()
            else:
                pl.when(cond)(copy.wait_send)


def line_order(z, k):
    if k == 0:
        return z + 1 - 2 * (z % 2)
    if k == 1:
        return 2 - z // 2
    return 3 - 3 * (z // 2)


def greet(peers):
    barrier = pltpu.get_barrier_semaphore()
    for peer in peers:
        pl.semaphore_signal(
            barrier, inc=1, device_id=peer, device_id_type=pl.DeviceIdType.MESH
        )
    pl.semaphore_wait(barrier, len(peers))


def place():
    return tuple(lax.axis_index(name) for name in ALL)


def line_peers(z, c):
    peers = [{"c": 1 - c}]
    for k in range(NZ - 1):
        peers.append({"z": (z + k + 1) % NZ})
    return peers


class LineGather:
    def __init__(self, wires, own, out, recv, z, c):
        self.wires, self.own, self.out, self.recv, self.z, self.c = wires, own, out, recv, z, c

    def begin(self):
        w, z, c = self.wires, self.z, self.c
        dst, sem = self.out.at[z, c], self.recv.at[z, c]
        w.send(self.own, dst, sem, {"z": jnp.minimum(z + 1, NZ - 1)}, z < NZ - 1)
        w.send(self.own, dst, sem, {"z": jnp.maximum(z - 1, 0)}, z > 0)
        w.send(self.own, dst, sem, {"c": 1 - c})

    def event(self, k):
        w, z, c = self.wires, self.z, self.c
        zq = line_order(z, k)
        slot, sem = self.out.at[zq, c], self.recv.at[zq, c]
        w.arrived(slot, sem, {"c": 1 - c})
        onward = jnp.where(zq < z, jnp.minimum(z + 1, NZ - 1), jnp.maximum(z - 1, 0))
        w.send(slot, slot, sem, {"z": onward}, (z > 0) & (z < NZ - 1))
        w.send(slot, slot, sem, {"c": 1 - c})

    def sibling(self, zq):
        w, c = self.wires, self.c
        w.arrived(self.out.at[zq, 1 - c], self.recv.at[zq, 1 - c], {"c": 1 - c})


def segments(nx, fs):
    for yq in range(2):
        for zq in range(NZ):
            for xq in range(nx):
                for cq in range(NC):
                    first = (((yq * NZ + zq) * nx + xq) * NC + cq) * fs
                    yield zq, cq, (yq * nx + xq) * fs, first


def weight_gather_kernel(
    nx, a, g, u, d, tok, ao, guo, do, co, gu, send_sems, local_sems, ra, rt, rw, rd, rc
):
    y, z, x, c = place()
    sib = {"c": 1 - c}
    ypeer = {"y": 1 - y}
    xpeers = [(x + i + 1) % nx for i in range(nx - 1)]
    planes = [{"x": xp} for xp in xpeers] + [ypeer]
    cross = [{"z": (z + k + 1) % NZ, "c": 1 - c} for k in range(NZ - 1)]
    greet(line_peers(z, c) + cross + planes)
    locals_ = [
        pltpu.make_async_copy(a, ao.at[y, z, x, c], local_sems.at[0]),
        pltpu.make_async_copy(d, do.at[y, x], local_sems.at[1]),
        pltpu.make_async_copy(tok, co.at[z, c], local_sems.at[2]),
    ]
    keep = pltpu.make_async_copy(gu.at[z, c], guo.at[:, y, z, x, c], local_sems.at[3])
    for copy in locals_:
        copy.start()
    wires = Wires(send_sems)

    def both_ways(src, dst, sem):
        for peer in planes:
            wires.send(src, dst, sem, peer)

    own_slot, own_sem = ao.at[y, z, x, c], ra.at[y, z, x, c]
    wires.send(a, own_slot, own_sem, {"z": jnp.minimum(z + 1, NZ - 1)}, z < NZ - 1)
    wires.send(a, own_slot, own_sem, {"z": jnp.maximum(z - 1, 0)}, z > 0)
    both_ways(a, own_slot, own_sem)
    wires.send(a, own_slot, own_sem, sib)
    fs = gu.shape[-1] // (2 * nx)
    for m, shard in enumerate((g, u)):
        for zq, cq, run, first in segments(nx, fs):
            gu[zq, cq, m, :, run : run + fs] = shard[:, first : first + fs]
    keep.start()
    for k in range(NZ - 1):
        zq = line_order(z, k)
        slot, sem = ao.at[y, zq, x, c], ra.at[y, zq, x, c]
        wires.arrived(slot, sem, sib)
        onward = jnp.where(zq < z, jnp.minimum(z + 1, NZ - 1), jnp.maximum(z - 1, 0))
        wires.send(slot, slot, sem, {"z": onward}, (z > 0) & (z < NZ - 1))
        both_ways(slot, slot, sem)
        wires.send(slot, slot, sem, sib)

    for k in range(NZ * NC - 1):
        step = k + 1
        zp, cp = (z + step // NC) % NZ, (c + step) % NC
        wires.send(
            gu.at[zp, cp], guo.at[:, y, z, x, c], rt.at[z, c], {"z": zp, "c": cp}
        )
    line = LineGather(wires, tok, co, rc, z, c)
    line.begin()
    half = d.shape[1] // 2
    parts = [pl.ds(0, half), pl.ds(half, half)]
    for h in range(2):
        both_ways(d.at[:, parts[h]], do.at[y, x, :, parts[h]], rd.at[h, y, x])

    def relay_attn(yq, xq, zq, peers):
        slot, sem = ao.at[yq, zq, xq, c], ra.at[yq, zq, xq, c]
        wires.arrived(slot, sem, sib)
        for peer in peers:
            wires.send(slot, slot, sem, peer)
        wires.send(slot, slot, sem, sib)

    for zq in range(NZ):
        for xp in xpeers:
            relay_attn(y, xp, zq, [ypeer] if zq < NZ // 2 else [])
        relay_attn(1 - y, x, zq, planes[:-1] if zq >= NZ // 2 else [])

    for k in range(NZ * NC - 1):
        step = k + 1
        zp, cp = (z + step // NC) % NZ, (c + step) % NC
        wires.arrived(guo.at[:, y, zp, x, cp], rt.at[zp, cp], sib)
    keep.wait()
    for m in range(2):
        plane = guo.at[m, y, :, x]
        both_ways(plane, plane, rw.at[m, y, x])
    line.event(0)

    def relay(ref, sem, peers):
        wires.arrived(ref, sem, sib)
        for peer in peers:
            wires.send(ref, ref, sem, peer)

    for xp in xpeers:
        relay(do.at[y, xp, :, parts[0]], rd.at[0, y, xp], [ypeer])
        relay(do.at[y, xp, :, parts[1]], rd.at[1, y, xp], [])
    relay(do.at[1 - y, x, :, parts[1]], rd.at[1, 1 - y, x], planes[:-1])
    relay(do.at[1 - y, x, :, parts[0]], rd.at[0, 1 - y, x], [])
    for xp in xpeers:
        for zq in range(NZ):
            relay_attn(1 - y, xp, zq, [])
    line.event(1)
    for xp in xpeers:
        relay(guo.at[0, y, :, xp], rw.at[0, y, xp], [ypeer])
    relay(guo.at[1, 1 - y, :, x], rw.at[1, 1 - y, x], planes[:-1])
    line.event(2)
    for xp in xpeers:
        relay(guo.at[1, y, :, xp], rw.at[1, y, xp], [])
    relay(guo.at[0, 1 - y, :, x], rw.at[0, 1 - y, x], [])
    for xp in xpeers:
        for h in range(2):
            relay(do.at[1 - y, xp, :, parts[h]], rd.at[h, 1 - y, xp], [])
            relay(guo.at[h, 1 - y, :, xp], rw.at[h, 1 - y, xp], [])
    for zq in range(NZ):
        line.sibling(zq)
    for yq in range(2):
        for zq in range(NZ):
            for xq in range(nx):
                wires.arrived(ao.at[yq, zq, xq, 1 - c], ra.at[yq, zq, xq, 1 - c], sib)
    wires.finish()
    for copy in locals_:
        copy.wait()


def weight_gather(ny, nx, a, g, u, d, tok, collective_id):
    sends = 3 + (nx + 1) + 3 * (nx + 2)
    sends += 7 + 9 + 2 * nx
    sends += 4 * nx + 2 * (nx - 1) + 2 * (nx - 1)
    sends += 2 * nx + 2 * (nx - 1) + 4 * (nx - 1) + 2 * (nx - 1)
    hbm = pl.BlockSpec(memory_space=pl.ANY)
    vmem = pl.BlockSpec(memory_space=pltpu.VMEM)
    grid = (ny, NZ, nx, NC)
    block = g.shape[:1] + (g.shape[1] // (NZ * NC),)
    return pl.pallas_call(
        lambda *refs: weight_gather_kernel(nx, *refs),
        name="weight_gather",
        out_shape=(
            jax.ShapeDtypeStruct(grid + a.shape, BF16),
            jax.ShapeDtypeStruct((2,) + grid + block, BF16),
            jax.ShapeDtypeStruct((ny, nx) + d.shape, BF16),
            jax.ShapeDtypeStruct((NZ, NC) + tok.shape, BF16),
        ),
        in_specs=[hbm, vmem, vmem, hbm, hbm],
        out_specs=(hbm,) * 4,
        scratch_shapes=[
            pltpu.VMEM((NZ, NC, 2) + block, BF16),
            pltpu.SemaphoreType.DMA((sends + 16,)),
            pltpu.SemaphoreType.DMA((4,)),
            pltpu.SemaphoreType.DMA(grid),
            pltpu.SemaphoreType.DMA((NZ, NC)),
            pltpu.SemaphoreType.DMA((2, ny, nx)),
            pltpu.SemaphoreType.DMA((2, ny, nx)),
            pltpu.SemaphoreType.DMA((NZ, NC)),
        ],
        compiler_params=pltpu.CompilerParams(
            collective_id=collective_id, has_side_effects=True
        ),
    )(a, g, u, d, tok)


def total_into(dst, refs, flat=None):
    flat = len(dst.shape) == 2

    def entry(i, carry):
        here = (slice(None), pl.ds(pl.multiple_of(i * 128, 128), 128)) if flat else i
        total = refs[0][here].astype(F32)
        for ref in refs[1:]:
            total = total + ref[here].astype(F32)
        dst[here] = total.astype(dst.dtype)
        return carry

    lax.fori_loop(0, dst.shape[1] // 128 if flat else dst.shape[0], entry, 0)


class PlaneScatter:
    def __init__(self, wires, src, first, second, bufs, loaded=False):
        self.wires, self.src = wires, src
        self.name_a, self.size_a, self.a = first
        self.name_b, self.size_b, self.b = second
        self.r1, self.own, self.r2, self.s1, self.sl, self.s2 = bufs
        self.loaded = loaded

    def mine(self, b):
        return self.src(self.a, b) if self.loaded else self.own.at[b]

    def order(self):
        return [(self.b + i + 1) % self.size_b for i in range(self.size_b)]

    def begin(self):
        for b in self.order():
            for i in range(self.size_a - 1):
                peer, j = (self.a + i + 1) % self.size_a, self.size_a - 2 - i
                self.wires.send(
                    self.src(peer, b), self.r1.at[j, b], self.s1.at[j, b], {self.name_a: peer}
                )
            if not self.loaded:
                self.load(b).start()

    def load(self, b):
        return pltpu.make_async_copy(self.src(self.a, b), self.own.at[b], self.sl.at[b])

    def gathered(self, b):
        if not self.loaded:
            self.load(b).wait()
        for j in range(self.size_a - 1):
            self.wires.arrived(self.r1.at[j, b], self.s1.at[j, b], {self.name_a: self.a})
        return [self.mine(b)] + [self.r1.at[j, b] for j in range(self.size_a - 1)]

    def relay(self):
        for i, b in enumerate(self.order()[:-1]):
            j = self.size_b - 2 - i
            total_into(self.mine(b), self.gathered(b))
            self.wires.send(self.mine(b), self.r2.at[j], self.s2.at[j], {self.name_b: b})

    def finish(self, dst):
        refs = self.gathered(self.b)
        for j in range(self.size_b - 1):
            self.wires.arrived(self.r2.at[j], self.s2.at[j], {self.name_b: self.b})
            refs.append(self.r2.at[j])
        total_into(dst, refs)


def plane_scratch(slot, size_a, size_b, loaded=False):
    own = (1,) * (1 + len(slot)) if loaded else (size_b,) + slot
    return [
        pltpu.VMEM((size_a - 1, size_b) + slot, BF16),
        pltpu.VMEM(own, BF16),
        pltpu.VMEM((size_b - 1,) + slot, BF16),
        pltpu.SemaphoreType.DMA((size_a - 1, size_b)),
        pltpu.SemaphoreType.DMA((size_b,)),
        pltpu.SemaphoreType.DMA((size_b - 1,)),
    ]


class LineScatter:
    def __init__(self, wires, part, bufs, z, c):
        self.wires, self.part, self.z, self.c = wires, part, z, c
        self.own, self.sib, self.left, self.right = bufs[:4]
        self.s_own, self.s_sib, self.s_left, self.s_right = bufs[4:]

    def order(self):
        return [line_order(self.z, k) for k in (2, 1, 0)] + [self.z]

    def load(self, zq):
        return pltpu.make_async_copy(
            self.part.at[zq, self.c], self.own.at[zq], self.s_own.at[zq]
        )

    def begin(self):
        for zq in self.order():
            self.wires.send(
                self.part.at[zq, 1 - self.c],
                self.sib.at[zq],
                self.s_sib.at[zq],
                {"c": 1 - self.c},
            )
            self.load(zq).start()

    def ready(self, zq):
        self.load(zq).wait()
        self.wires.arrived(self.sib.at[zq], self.s_sib.at[zq], {"c": 1 - self.c})

    def hop(self, k):
        z = self.z
        for sign, buf, sems in ((1, self.left, self.s_left), (-1, self.right, self.s_right)):
            target = z + sign * k
            inside = (target < NZ) if sign > 0 else (target >= 0)
            behind = (z > 0) if sign > 0 else (z < NZ - 1)
            target = jnp.clip(target, 0, NZ - 1)
            own, sib = self.own.at[target], self.sib.at[target]

            @pl.when(inside)
            def _():
                self.ready(target)

            if k < NZ - 1:

                @pl.when(inside & behind)
                def _():
                    self.wires.arrived(buf.at[k], sems.at[k], {"z": z})
                    total_into(own, [own, sib, buf.at[k]])

                @pl.when(inside & jnp.logical_not(behind))
                def _():
                    total_into(own, [own, sib])

            else:

                @pl.when(inside)
                def _():
                    total_into(own, [own, sib])

            onward = jnp.clip(z + sign, 0, NZ - 1)
            self.wires.send(own, buf.at[k - 1], sems.at[k - 1], {"z": onward}, inside)

    def finish(self, dst):
        z = self.z
        self.ready(z)
        own, sib = self.own.at[z], self.sib.at[z]

        @pl.when(z > 0)
        def _():
            self.wires.arrived(self.left.at[0], self.s_left.at[0], {"z": z})

        @pl.when(z < NZ - 1)
        def _():
            self.wires.arrived(self.right.at[0], self.s_right.at[0], {"z": z})

        @pl.when(z == 0)
        def _():
            total_into(dst, [own, sib, self.right.at[0]])

        @pl.when(z == NZ - 1)
        def _():
            total_into(dst, [own, sib, self.left.at[0]])

        @pl.when((z > 0) & (z < NZ - 1))
        def _():
            total_into(dst, [own, sib, self.left.at[0], self.right.at[0]])


def line_scratch(slot):
    return [
        pltpu.VMEM((NZ,) + slot, BF16),
        pltpu.VMEM((NZ,) + slot, BF16),
        pltpu.VMEM((NZ - 1,) + slot, BF16),
        pltpu.VMEM((NZ - 1,) + slot, BF16),
        pltpu.SemaphoreType.DMA((NZ,)),
        pltpu.SemaphoreType.DMA((NZ,)),
        pltpu.SemaphoreType.DMA((NZ - 1,)),
        pltpu.SemaphoreType.DMA((NZ - 1,)),
    ]


TILES = ((0, 640), (640, None))


def remote(src, dst, send_sem, recv_sem, device):
    return pltpu.make_async_remote_copy(
        src_ref=src,
        dst_ref=dst,
        send_sem=send_sem,
        recv_sem=recv_sem,
        device_id=device,
        device_id_type=pl.DeviceIdType.MESH,
    )


def mlp_kernel(
    nx,
    with_down,
    h,
    wg,
    wu,
    wd,
    cot,
    dh,
    out_part,
    grad_g,
    grad_u,
    grad_d,
    *scratch,
):
    if with_down:
        down_out, out_sib, scratch = scratch[0], scratch[1], scratch[2:]
    (
        hv,
        cv,
        wgv,
        wuv,
        wdv,
        av,
        dgv,
        duv,
        part,
        sib,
        ring,
        ob,
        s_load,
        s_cot,
        s_ob,
        s_out,
        h_send,
        h_on,
        h_sib,
        h_recv,
        p_send,
        p_recv,
        r_send,
        r_recv,
    ) = scratch[: 24]
    scratch = scratch[24:]
    if with_down:
        o_send, o_recv, scratch = scratch[0], scratch[1], scratch[2:]
    y, z, x, c = place()
    rows, wide = h.shape
    units = wg.shape[1]
    other = 1 - c
    inner = (z > 0) & (z < NZ - 1)
    greet(line_peers(z, c) + (plane_peers(nx, y, x) if with_down else []))

    def block(zq, cq):
        return pl.ds(pl.multiple_of((zq * NC + cq) * rows, rows), rows)

    loads = [
        pltpu.make_async_copy(h, hv.at[block(z, c)], s_load.at[0]),
        pltpu.make_async_copy(wg, wgv, s_load.at[1]),
        pltpu.make_async_copy(wu, wuv, s_load.at[2]),
        pltpu.make_async_copy(wd, wdv, s_load.at[3]),
    ]

    def load_cot(zq, cq):
        return pltpu.make_async_copy(
            cot.at[block(zq, cq)], cv.at[block(zq, cq)], s_cot.at[zq, cq]
        )

    def send_own(i):
        there = hv.at[block(z, c)]
        device = (
            {"z": jnp.minimum(z + 1, NZ - 1)},
            {"z": jnp.maximum(z - 1, 0)},
            {"c": other},
        )[i]
        return remote(h, there, h_send.at[i], h_recv.at[z, c], device)

    pl.when(z < NZ - 1)(send_own(0).start)
    pl.when(z > 0)(send_own(1).start)
    send_own(2).start()
    for copy in loads[:3]:
        copy.start()
    load_cot(z, c).start()
    loads[3].start()
    load_cot(z, other).start()
    for k in range(NZ - 1):
        for i in range(NC):
            load_cot(line_order(z, k), (c + i) % NC).start()

    def arrival(zq, cq):
        here = hv.at[block(zq, cq)]
        return remote(here, here, h_send.at[0], h_recv.at[zq, cq], {"c": other})

    def onward(k):
        zq = line_order(z, k)
        here = hv.at[block(zq, c)]
        device = {"z": jnp.where(zq < z, jnp.minimum(z + 1, NZ - 1), jnp.maximum(z - 1, 0))}
        return remote(here, here, h_on.at[k], h_recv.at[zq, c], device)

    def to_sibling(k):
        zq = line_order(z, k)
        here = hv.at[block(zq, c)]
        return remote(here, here, h_sib.at[k], h_recv.at[zq, c], {"c": other})

    def take(k):
        arrival(line_order(z, k), c).wait_recv()
        pl.when(inner)(onward(k).start)
        to_sibling(k).start()

    def output(zq, cq):
        if with_down:
            here = pl.ds(pl.multiple_of(zq * rows, rows), rows)
            return pltpu.make_async_copy(ob.at[cq], out_part.at[here], s_ob.at[0])
        return pltpu.make_async_copy(ob.at[cq], out_part.at[block(zq, cq)], s_ob.at[cq])

    def output_over(zq):
        here = pl.ds(pl.multiple_of(zq * rows, rows), rows)
        return remote(
            ob.at[other], out_sib.at[here], o_send.at[zq], o_recv.at[zq], {"c": other}
        )

    def partial_over(zq):
        return remote(
            part.at[block(zq, other)], sib.at[zq], p_send.at[zq], p_recv.at[zq], {"c": other}
        )

    def partial_home(zq):
        j = (z - zq + NZ) % NZ - 1
        return remote(
            part.at[block(zq, c)], ring.at[j], r_send.at[zq], r_recv.at[j], {"z": zq}
        )

    piece = rows // 8

    def combine(zq):
        remote(sib.at[zq], sib.at[zq], p_send.at[0], p_recv.at[zq], {"c": other}).wait_recv()

        def step(i, carry):
            here = pl.ds(pl.multiple_of((zq * NC + c) * rows + i * piece, piece), piece)
            there = pl.ds(pl.multiple_of(i * piece, piece), piece)
            total = part[here].astype(F32) + sib[zq, there].astype(F32)
            part[here] = total.astype(BF16)
            return carry

        lax.fori_loop(0, 8, step, 0)

    def place_of(k):
        near = line_order(z, 0)
        mid = line_order(z, 1)
        far = line_order(z, 2)
        return jnp.where(k == 0, z, jnp.where(k == 1, near, jnp.where(k == 2, mid, far)))

    def pair(k, carry):
        zq = place_of(k)

        @pl.when(k == 1)
        def _():
            take(0)
            pl.when(inner)(lambda: take(1))

        @pl.when(k == 2)
        def _():
            pl.when(jnp.logical_not(inner))(lambda: take(1))
            pl.when(inner)(lambda: take(2))

        @pl.when((k == 3) & jnp.logical_not(inner))
        def _():
            take(2)

        def one(j, carry):
            cq = (c + j) % NC
            here = block(zq, cq)

            @pl.when((k == 0) & (j == 0))
            def _():
                for copy in loads:
                    copy.wait()

            @pl.when(j == 1)
            def _():
                arrival(zq, cq).wait_recv()

            load_cot(zq, cq).wait()
            for low, high in TILES:
                high = units if high is None else high
                gate = dot(hv[here], wgv[:, low:high])
                up = dot(hv[here], wuv[:, low:high])
                grad = dot_nt(cv[here], wdv[low:high])
                sig = jax.nn.sigmoid(gate)
                act = gate * sig
                av[here, low:high] = (act * up).astype(BF16)
                duv[here, low:high] = (grad * act).astype(BF16)
                dgv[here, low:high] = (
                    grad * up * (sig * (1.0 + gate * (1.0 - sig)))
                ).astype(BF16)

            if with_down:

                @pl.when((k > 0) & (j == 0))
                def _():
                    output(zq, cq).wait()

                @pl.when((k > 0) & (j == 1))
                def _():
                    output_over(place_of(k - 1)).wait_send()

            else:

                @pl.when(k > 0)
                def _():
                    output(zq, cq).wait()

            ob[cq] = dot(av[here], wdv[...]).astype(BF16)
            if with_down:
                pl.when(j == 0)(output(zq, cq).start)
                pl.when(j == 1)(output_over(zq).start)
            else:
                output(zq, cq).start()
            part[here] = (dot_nt(dgv[here], wgv[...]) + dot_nt(duv[here], wuv[...])).astype(BF16)
            return carry

        lax.fori_loop(0, NC, one, 0)
        partial_over(zq).start()

        @pl.when(k > 1)
        def _():
            before = place_of(k - 1)
            combine(before)
            partial_home(before).start()

        return carry

    lax.fori_loop(0, NZ, pair, 0)
    last = line_order(z, NZ - 2)
    step_d = wide // 6

    def down_grad(t, carry):
        cols = pl.ds(pl.multiple_of(t * step_d, step_d), step_d)
        wdv[:, cols] = dot_tn(av[...], cv[:, cols]).astype(BF16)

        @pl.when(t == 0)
        def _():
            combine(last)
            partial_home(last).start()

        return carry

    lax.fori_loop(0, 6, down_grad, 0)
    outs = [
        pltpu.make_async_copy(wdv, grad_d, s_out.at[0]),
        pltpu.make_async_copy(wgv, grad_g, s_out.at[1]),
        pltpu.make_async_copy(wuv, grad_u, s_out.at[2]),
    ]
    outs[0].start()
    if with_down:
        wires = Wires(scratch[0])
        half, shard = wide // 2, units // (2 * nx)
        left, right = pl.ds(0, half), pl.ds(half, half)

        def term(yq, xq, cols):
            first = (yq * nx + xq) * shard
            return grad_d.at[pl.ds(pl.multiple_of(first, 8), shard), cols]

        along_x, along_y = ("x", nx, x), ("y", 2, y)
        by_x = PlaneScatter(
            wires, lambda xq, yq: term(yq, xq, left), along_x, along_y, scratch[1:7]
        )
        by_y = PlaneScatter(
            wires, lambda yq, xq: term(yq, xq, right), along_y, along_x, scratch[7:13]
        )

    def turned(src, dst, first, last):
        def step(t, carry):
            cols = pl.ds(pl.multiple_of(t * step_d, step_d), step_d)
            dst[cols] = dot_tn(hv[:, cols], src[...]).astype(BF16)
            return carry

        lax.fori_loop(first, last, step, 0)

    turned(dgv, wgv, 0, 1)
    if with_down:
        outs[0].wait()
        by_x.begin()
        by_y.begin()
    turned(dgv, wgv, 1, 6)
    outs[1].start()
    turned(duv, wuv, 0, 6)
    outs[2].start()
    if with_down:
        by_x.relay()
        by_y.relay()
    combine(z)
    for j in range(NZ - 1):
        remote(ring.at[j], ring.at[j], r_send.at[0], r_recv.at[j], {"c": other}).wait_recv()

    def final(i, carry):
        here = pl.ds(pl.multiple_of((z * NC + c) * rows + i * piece, piece), piece)
        there = pl.ds(pl.multiple_of(i * piece, piece), piece)
        total = part[here].astype(F32)
        for j in range(NZ - 1):
            total = total + ring[j, there].astype(F32)
        dh[there] = total
        return carry

    lax.fori_loop(0, 8, final, 0)
    if with_down:
        by_x.finish(down_out.at[:, left])
        by_y.finish(down_out.at[:, right])
        wires.finish()
    pl.when(z < NZ - 1)(send_own(0).wait_send)
    pl.when(z > 0)(send_own(1).wait_send)
    send_own(2).wait_send()
    for k in range(NZ - 1):
        pl.when(inner)(onward(k).wait_send)
        to_sibling(k).wait_send()
        partial_home(line_order(z, k)).wait_send()
    for zq in range(NZ):
        partial_over(zq).wait_send()
    if with_down:
        output(z, c).wait()
        output_over(last).wait_send()
        for zq in range(NZ):
            there = out_sib.at[pl.ds(zq * rows, rows)]
            remote(there, there, o_send.at[0], o_recv.at[zq], {"c": other}).wait_recv()
    else:
        for cq in range(NC):
            output(z, cq).wait()
    for copy in outs[1 if with_down else 0 :]:
        copy.wait()


def mlp(ny, nx, with_down, h, wg, wu, wd, cot, collective_id):
    hbm = pl.BlockSpec(memory_space=pl.ANY)
    vmem = pl.BlockSpec(memory_space=pltpu.VMEM)
    rows, wide = h.shape
    units = wg.shape[1]
    every = NZ * NC * rows
    dma = pltpu.SemaphoreType.DMA
    shard = units // (ny * nx)
    down_scratch = []
    if with_down:
        sends = 2 * ((nx - 1) * 2 + 1 + nx + (nx - 1))
        down_scratch = [dma((NZ,)), dma((NZ,)), dma((sends,))]
        down_scratch += plane_scratch((shard, wide // 2), nx, ny)
        down_scratch += plane_scratch((shard, wide // 2), ny, nx)
    extra_shape, extra_specs, kept = (), (), every
    if with_down:
        kept = NZ * rows
        extra_shape = (
            jax.ShapeDtypeStruct((shard, wide), BF16),
            jax.ShapeDtypeStruct((kept, wide), BF16),
        )
        extra_specs = (vmem, hbm)
    return pl.pallas_call(
        lambda *refs: mlp_kernel(nx, with_down, *refs),
        name="mlp",
        out_shape=(
            jax.ShapeDtypeStruct((rows, wide), F32),
            jax.ShapeDtypeStruct((kept, wide), BF16),
            jax.ShapeDtypeStruct((wide, units), BF16),
            jax.ShapeDtypeStruct((wide, units), BF16),
            jax.ShapeDtypeStruct((units, wide), BF16),
        )
        + extra_shape,
        in_specs=[hbm] * 5,
        out_specs=(vmem, hbm, hbm, hbm, hbm) + extra_specs,
        scratch_shapes=[
            pltpu.VMEM((every, wide), BF16),
            pltpu.VMEM((every, wide), BF16),
            pltpu.VMEM((wide, units), BF16),
            pltpu.VMEM((wide, units), BF16),
            pltpu.VMEM((units, wide), BF16),
            pltpu.VMEM((every, units), BF16),
            pltpu.VMEM((every, units), BF16),
            pltpu.VMEM((every, units), BF16),
            pltpu.VMEM((every, wide), BF16),
            pltpu.VMEM((NZ, rows, wide), BF16),
            pltpu.VMEM((NZ - 1, rows, wide), BF16),
            pltpu.VMEM((NC, rows, wide), BF16),
            dma((4,)),
            dma((NZ, NC)),
            dma((NC,)),
            dma((3,)),
            dma((3,)),
            dma((NZ - 1,)),
            dma((NZ - 1,)),
            dma((NZ, NC)),
            dma((NZ,)),
            dma((NZ,)),
            dma((NZ,)),
            dma((NZ - 1,)),
        ]
        + down_scratch,
        compiler_params=pltpu.CompilerParams(
            collective_id=collective_id, has_side_effects=True, vmem_limit_bytes=63 << 20
        ),
    )(h, wg, wu, wd, cot)


def plane_peers(nx, y, x):
    return [{"x": (x + i + 1) % nx} for i in range(nx - 1)] + [{"y": 1 - y}]


def last_scatter_kernel(nx, widths, grads, gate, up, down, result, *rest):
    y, z, x, c = place()
    outs, rest = rest[: len(widths)], rest[len(widths) :]
    gate_out, up_out, down_out, result_out, rest = rest[:4] + (rest[4:],)
    send_sems, blocks, own, sib, line_sum, line_in = rest[:6]
    s_block, s_keep, s_own, s_sib, s_line = rest[6:11]
    half_x, half_y = rest[11:17], rest[17:23]
    gate_bufs, up_bufs, gu = rest[23:29], rest[29:35], rest[35]
    left_bufs, right_bufs, line_bufs = rest[36:42], rest[42:48], rest[48:56]
    cross = [{"z": (z + k + 1) % NZ, "c": 1 - c} for k in range(NZ - 1)]
    greet(line_peers(z, c) + cross + plane_peers(nx, y, x))
    wires = Wires(send_sems)
    along_x, along_y = ("x", nx, x), ("y", 2, y)
    gate_plane = PlaneScatter(
        wires, lambda xq, yq: gate.at[yq, :, xq], along_x, along_y, gate_bufs
    )
    up_plane = PlaneScatter(wires, lambda yq, xq: up.at[yq, :, xq], along_y, along_x, up_bufs)
    cols = down.shape[-1] // 2
    left, right = pl.ds(0, cols), pl.ds(cols, cols)
    left_plane = PlaneScatter(
        wires, lambda xq, yq: down.at[yq, xq, :, left], along_x, along_y, left_bufs
    )
    right_plane = PlaneScatter(
        wires, lambda yq, xq: down.at[yq, xq, :, right], along_y, along_x, right_bufs
    )
    line = LineScatter(wires, result, line_bufs, z, c)
    gate_plane.begin()
    up_plane.begin()
    line.begin()
    n = NZ // 2
    halves = [pl.ds(0, n), pl.ds(n, n)]

    def load(h, yq):
        return pltpu.make_async_copy(
            grads.at[yq, halves[h], :, c], own.at[yq, halves[h]], s_own.at[h, yq]
        )

    for h in range(2):
        for yq in range(2):
            wires.send(
                grads.at[yq, halves[h], :, 1 - c],
                sib.at[yq, halves[h]],
                s_sib.at[h, yq],
                {"c": 1 - c},
            )
            load(h, yq).start()

    def combine(h):
        for yq in range(2):
            load(h, yq).wait()
            wires.arrived(sib.at[yq, halves[h]], s_sib.at[h, yq], {"c": 1 - c})
            for i in range(n):
                zq = h * n + i
                total_into(own.at[yq, zq], [own.at[yq, zq], sib.at[yq, zq]])

    by_x = PlaneScatter(
        wires, lambda xq, yq: own.at[yq, halves[0], xq], along_x, along_y, half_x, True
    )
    by_y = PlaneScatter(
        wires, lambda yq, xq: own.at[yq, halves[1], xq], along_y, along_x, half_y, True
    )
    combine(0)
    by_x.begin()
    combine(1)
    by_y.begin()
    line.hop(3)
    left_plane.begin()
    right_plane.begin()
    line.hop(2)
    gate_plane.relay()
    up_plane.relay()
    line.hop(1)
    by_x.relay()
    by_y.relay()
    left_plane.relay()
    right_plane.relay()
    gate_plane.finish(gu.at[0])
    up_plane.finish(gu.at[1])
    keep = pltpu.make_async_copy(gu.at[:, z, c], blocks.at[z, c], s_keep)
    keep.start()
    for k in range(NZ * NC - 1):
        step = k + 1
        zp, cp = (z + step // NC) % NZ, (c + step) % NC
        wires.send(gu.at[:, zp, cp], blocks.at[z, c], s_block.at[z, c], {"z": zp, "c": cp})
    by_x.finish(line_sum.at[halves[0]])
    by_y.finish(line_sum.at[halves[1]])
    for k in range(NZ - 1):
        zp = (z + k + 1) % NZ
        wires.send(line_sum.at[zp], line_in.at[NZ - 2 - k], s_line.at[NZ - 2 - k], {"z": zp})
    line.finish(result_out)
    left_plane.finish(down_out.at[:, left])
    right_plane.finish(down_out.at[:, right])
    keep.wait()
    for k in range(NZ * NC - 1):
        step = k + 1
        zp, cp = (z + step // NC) % NZ, (c + step) % NC
        wires.arrived(blocks.at[zp, cp], s_block.at[zp, cp], {"c": 1 - c})
    fs = blocks.shape[-1] // (2 * nx)
    for m, out in enumerate((gate_out, up_out)):
        for zq, cq, run, first in segments(nx, fs):
            out[:, first : first + fs] = blocks[zq, cq, m, :, run : run + fs].astype(F32)
    for k in range(NZ - 1):
        wires.arrived(line_in.at[k], s_line.at[k], {"c": 1 - c})
    first = 0
    for out, width in zip(outs, widths):
        columns = slice(first, first + width)
        total = line_sum[z, :, columns].astype(F32)
        for k in range(NZ - 1):
            total = total + line_in[k, :, columns].astype(F32)
        out[...] = total
        first += width
    wires.finish()


def last_scatter(ny, nx, grads, widths, gate, up, down, result, collective_id):
    hbm = pl.BlockSpec(memory_space=pl.ANY)
    vmem = pl.BlockSpec(memory_space=pltpu.VMEM)
    rows, width = grads.shape[4:]
    block = gate.shape[4:]
    slot = (NZ // 2, rows, width)
    gate_slot = (NZ, NC) + block
    down_slot = (down.shape[2], down.shape[3] // 2)
    sends = 4 + 7 + NZ - 1 + 3 * ((nx - 1) * 2 + 1 + nx + (nx - 1)) + NZ + 2 * (NZ - 1)
    spread = block[1] * NZ * NC
    shapes = [(rows, w) for w in widths] + [(rows, spread)] * 2
    shapes += [down.shape[2:], result.shape[2:]]
    return pl.pallas_call(
        lambda *refs: last_scatter_kernel(nx, widths, *refs),
        name="last_scatter",
        out_shape=tuple(jax.ShapeDtypeStruct(shape, F32) for shape in shapes),
        in_specs=[hbm] * 5,
        out_specs=(vmem,) * len(shapes),
        scratch_shapes=[
            pltpu.SemaphoreType.DMA((sends,)),
            pltpu.VMEM((NZ, NC, 2) + block, BF16),
            pltpu.VMEM((ny, NZ, nx, rows, width), BF16),
            pltpu.VMEM((ny, NZ, nx, rows, width), BF16),
            pltpu.VMEM((NZ, rows, width), BF16),
            pltpu.VMEM((NZ - 1, rows, width), BF16),
            pltpu.SemaphoreType.DMA((NZ, NC)),
            pltpu.SemaphoreType.DMA,
            pltpu.SemaphoreType.DMA((2, 2)),
            pltpu.SemaphoreType.DMA((2, 2)),
            pltpu.SemaphoreType.DMA((NZ - 1,)),
        ]
        + plane_scratch(slot, nx, ny, True)
        + plane_scratch(slot, ny, nx, True)
        + plane_scratch(gate_slot, nx, ny)
        + plane_scratch(gate_slot, ny, nx)
        + [pltpu.VMEM((2,) + gate_slot, BF16)]
        + plane_scratch(down_slot, nx, ny)
        + plane_scratch(down_slot, ny, nx)
        + line_scratch(result.shape[2:]),
        compiler_params=pltpu.CompilerParams(
            collective_id=collective_id, has_side_effects=True, vmem_limit_bytes=60 << 20
        ),
    )(grads, gate, up, down, result)


def back_kernel(
    nx,
    key_width,
    b_rows,
    gate,
    up,
    ao,
    kept,
    given,
    mid,
    branch,
    tokens,
    gain,
    attn,
    query,
    kv,
    mask,
    turn_c,
    turn_s,
    gain_term,
    out_q,
    out_k,
    out_v,
    out_o,
    out_tail,
    out_gate,
    out_up,
    out_in,
    out_ring,
    send_sems,
    weights,
    term_o,
    term_q,
    sib_o,
    sib_q,
    line_sum,
    line_in,
    blocks,
    gu,
    d_attn,
    d_qkv,
    d_kv,
    kv_send,
    kv_recv,
    first_in,
    s_weights,
    s_sib,
    s_line,
    s_block,
    s_kv,
    result,
    s_result,
    s_ring,
    *bufs,
):
    y, z, x, c = place()
    sib = {"c": 1 - c}
    cross = [{"z": (z + k + 1) % NZ, "c": 1 - c} for k in range(NZ - 1)]
    greet(line_peers(z, c) + cross + plane_peers(nx, y, x))
    wires = Wires(send_sems)
    along_x, along_y = ("x", nx, x), ("y", 2, y)
    gate_plane = PlaneScatter(
        wires, lambda xq, yq: gate.at[yq, :, xq], along_x, along_y, bufs[0:6]
    )
    up_plane = PlaneScatter(wires, lambda yq, xq: up.at[yq, :, xq], along_y, along_x, bufs[6:12])
    gate_plane.begin()
    up_plane.begin()
    rows, wide = branch.shape
    q_width = query.shape[1]
    qkv_width = q_width + 2 * key_width
    heads, kv_heads = q_width // HD, key_width // HD
    n = NZ // 2
    halves = [pl.ds(0, n), pl.ds(n, n)]
    tile = n * nx * NC * out_q.shape[0]
    shard = out_q.shape[0]

    def fetch(first, width):
        return pltpu.make_async_copy(
            ao.at[:, :, pl.ds(first, width)], weights.at[:, :, pl.ds(0, width)], s_weights
        )

    fetch(qkv_width, wide).start()

    def fill(term, yq, h, first, value):
        value = value.reshape((n, nx, NC, shard, value.shape[1]))
        term[yq, halves[h], :, :, :, first : first + value.shape[4]] = value.astype(BF16)

    def over(i, term, other, yq, h):
        wires.send(
            term.at[yq, halves[h], :, 1 - c],
            other.at[yq, halves[h]],
            s_sib.at[i, yq, h],
            sib,
        )

    def combine(i, term, other):
        for h in range(2):
            for yq in range(2):
                here = other.at[yq, halves[h]]
                wires.arrived(here, s_sib.at[i, yq, h], sib)
                for zq in range(h * n, h * n + n):
                    for xq in range(nx):
                        mine = term.at[yq, zq, xq, c]
                        total_into(mine, [mine, other.at[yq, zq, xq]], True)

    def planes(term, first):
        return (
            PlaneScatter(
                wires,
                lambda xq, yq: term.at[yq, halves[0], xq, c],
                along_x,
                along_y,
                bufs[first : first + 6],
                True,
            ),
            PlaneScatter(
                wires,
                lambda yq, xq: term.at[yq, halves[1], xq, c],
                along_y,
                along_x,
                bufs[first + 6 : first + 12],
                True,
            ),
        )

    for yq in range(2):
        for h in range(2):
            i = yq * 2 + h
            fill(term_o, yq, h, 0, dot_tn(attn[:, i * tile : (i + 1) * tile], branch[...]))
            over(0, term_o, sib_o, yq, h)

    for i, k in enumerate((2, 0, 1)):
        zq = line_order(z, k)
        here = pl.ds(pl.multiple_of(zq * rows, rows), rows)
        loads = [
            pltpu.make_async_copy(kept.at[here], result.at[i], s_result.at[0]),
            pltpu.make_async_copy(given.at[here], first_in, s_result.at[1]),
        ]
        for copy in loads:
            copy.start()
        for copy in loads:
            copy.wait()
        total_into(result.at[i], [result.at[i], first_in])
        j = (z - zq + NZ) % NZ - 1
        wires.send(result.at[i], out_ring.at[j], s_ring.at[j], {"z": zq})

    fetch(qkv_width, wide).wait()
    for_out = weights[:, :, :wide].reshape(q_width, wide)
    d_attn[...] = dot_nt(branch[...], for_out).astype(BF16)
    fetch(0, qkv_width).start()
    d_kv[...] = jnp.zeros_like(d_kv)
    scale = HD ** (-0.5)

    def turn_back(value):
        return value * turn_c[...] + pltpu.roll(value, HD // 2, 1) * turn_s[...]

    group = heads // kv_heads
    for kv_head in range(kv_heads):
        k_cols = pl.ds(kv_head * HD, HD)
        v_cols = pl.ds(key_width + kv_head * HD, HD)

        def head(i, carry):
            cols = pl.ds(pl.multiple_of((kv_head * group + i) * HD, HD), HD)
            q_h, do_h = query[:, cols], d_attn[:, cols]
            scores = jnp.where(mask[...] > 0, dot_nt(q_h, kv[:, k_cols]) * scale, MASKED)
            exponent = jnp.exp(scores - jnp.max(scores, axis=-1, keepdims=True))
            probs = exponent / jnp.sum(exponent, axis=-1, keepdims=True)
            d_probs = dot_nt(do_h, kv[:, v_cols])
            inner = jnp.sum(probs * d_probs, axis=-1, keepdims=True)
            d_scores = (probs * (d_probs - inner)).astype(BF16)
            d_qkv[:, cols] = turn_back(dot(d_scores, kv[:, k_cols]) * scale).astype(BF16)
            d_kv[:, k_cols] += dot_tn(d_scores, q_h) * scale
            d_kv[:, v_cols] += dot_tn(probs.astype(BF16), do_h)
            return carry

        lax.fori_loop(0, group, head, 0)

    other_rows = pl.ds(pl.multiple_of((1 - y) * rows, rows), rows)
    own_rows = pl.ds(pl.multiple_of(y * rows, rows), rows)
    kv_send[...] = d_kv[other_rows].astype(BF16)
    gate_plane.relay()
    wires.send(kv_send, kv_recv, s_kv, {"y": 1 - y})
    up_plane.relay()
    combine(0, term_o, sib_o)
    o_planes = planes(term_o, 12)
    for plane in o_planes:
        plane.begin()
    x32 = tokens[...].astype(F32)
    rescale = lax.rsqrt(jnp.mean(x32 * x32, axis=-1, keepdims=True) + EPS)
    first_in[...] = (x32 * rescale * gain[...]).astype(BF16)
    wires.arrived(kv_recv, s_kv, {"y": 1 - y})
    for kv_head in range(2 * kv_heads):
        cols = pl.ds(kv_head * HD, HD)
        total = d_kv[own_rows, cols] + kv_recv[:, cols].astype(F32)
        if kv_head < kv_heads:
            total = turn_back(total)
        d_qkv[:, pl.ds(q_width + kv_head * HD, HD)] = total.astype(BF16)
    fetch(0, qkv_width).wait()
    for_in = weights[...].reshape(wide, qkv_width)
    d_first = dot_nt(d_qkv[...], for_in)
    normed = x32 * rescale
    scaled = d_first * gain[...]
    d_x = rescale * (scaled - normed * jnp.mean(scaled * normed, axis=-1, keepdims=True))
    out_in[...] = (mid[...] + d_x).astype(BF16)
    first_term = (d_first * normed).astype(BF16)
    lane = lax.broadcasted_iota(jnp.int32, (rows, HD), 1)
    pick_one = (lane == 0).astype(F32).astype(BF16)
    pick_two = (lane == 1).astype(F32).astype(BF16)
    bias_sum = jnp.sum(d_qkv[...].astype(F32), axis=0, keepdims=True)
    top = lax.broadcasted_iota(jnp.int32, (shard, HD), 0) == 0
    wide_bias = jnp.concatenate([bias_sum, bias_sum[:, :HD]], axis=1)
    for yq in range(2):
        for h in range(2):
            i = yq * 2 + h
            cols = slice(i * tile, (i + 1) * tile)
            fill(term_q, yq, h, 0, dot_tn(first_in[:, cols], d_qkv[...]))
            tail = dot_tn(first_term[:, cols], pick_one) + dot_tn(gain_term[:, cols], pick_two)
            for zi in range(n):
                for xq in range(nx):
                    for cq in range(NC):
                        part = ((zi * nx + xq) * NC + cq) * shard
                        place_at = i * (tile // shard) + (zi * nx + xq) * NC + cq
                        first = place_at * b_rows
                        base = (first // HD) * HD
                        bias = wide_bias[:, base : base + HD]
                        bias = pltpu.roll(
                            jnp.broadcast_to(bias, (8, HD)), (HD // 2 - (first - base)) % HD, 1
                        )[:1]
                        keep = lax.broadcasted_iota(jnp.int32, (shard, HD), 1) >= HD // 2
                        mixed = tail[part : part + shard] + jnp.where(top & keep, bias, 0.0)
                        term_q[yq, h * n + zi, xq, cq, :, qkv_width:] = mixed.astype(BF16)
            over(1, term_q, sib_q, yq, h)
    combine(1, term_q, sib_q)
    q_planes = planes(term_q, 24)
    for plane in q_planes:
        plane.begin()
    gate_plane.finish(gu.at[0])
    up_plane.finish(gu.at[1])
    keep_block = pltpu.make_async_copy(gu.at[:, z, c], blocks.at[z, c], s_block.at[z, c])
    keep_block.start()
    for k in range(NZ * NC - 1):
        step = k + 1
        zp, cp = (z + step // NC) % NZ, (c + step) % NC
        wires.send(gu.at[:, zp, cp], blocks.at[z, c], s_block.at[z, c], {"z": zp, "c": cp})
    for plane in o_planes:
        plane.relay()
    for plane in q_planes:
        plane.relay()

    def along_line(i, first, width, pair):
        cols = pl.ds(first, width)
        pair[0].finish(line_sum.at[halves[0], :, cols])
        pair[1].finish(line_sum.at[halves[1], :, cols])
        for k in range(NZ - 1):
            zp, j = (z + k + 1) % NZ, NZ - 2 - k
            wires.send(
                line_sum.at[zp, :, cols], line_in.at[j, :, cols], s_line.at[i, j], {"z": zp}
            )

    q_all = qkv_width + HD
    along_line(0, q_all, wide, o_planes)
    along_line(1, 0, q_all, q_planes)
    keep_block.wait()
    for k in range(NZ * NC - 1):
        step = k + 1
        zp, cp = (z + step // NC) % NZ, (c + step) % NC
        wires.arrived(blocks.at[zp, cp], s_block.at[zp, cp], sib)
    fs = blocks.shape[-1] // (2 * nx)
    for m, out in enumerate((out_gate, out_up)):
        for zq, cq, run, first in segments(nx, fs):
            out[:, first : first + fs] = blocks[zq, cq, m, :, run : run + fs]

    def last(i, out, first, width):
        if i is not None:
            begin, size = (q_all, wide) if i == 0 else (0, q_all)
            for j in range(NZ - 1):
                wires.arrived(line_in.at[j, :, pl.ds(begin, size)], s_line.at[i, j], sib)
        columns = slice(first, first + width)
        total = line_sum[z, :, columns].astype(F32)
        for j in range(NZ - 1):
            total = total + line_in[j, :, columns].astype(F32)
        out[...] = total

    last(0, out_o, q_all, wide)
    last(1, out_q, 0, q_width)
    last(None, out_k, q_width, key_width)
    last(None, out_v, q_width + key_width, key_width)
    last(None, out_tail, qkv_width, HD)
    for j in range(NZ - 1):
        wires.arrived(out_ring.at[j], s_ring.at[j], sib)
    wires.finish()


def back(ny, nx, b_rows, gate, up, ao, kept, given, args, collective_id):
    hbm = pl.BlockSpec(memory_space=pl.ANY)
    vmem = pl.BlockSpec(memory_space=pltpu.VMEM)
    mid, branch, tokens, gain, attn, query, kv, mask, turn_c, turn_s, gain_term = args
    dma = pltpu.SemaphoreType.DMA
    shard = ao.shape[1]
    block = gate.shape[4:]
    rows, wide = branch.shape
    q_width = query.shape[1]
    key_width = kv.shape[1] // 2
    qkv_width = q_width + 2 * key_width
    q_all = qkv_width + HD
    spread = block[1] * NZ * NC
    one_plane = (nx - 1) * 2 + 1 + nx + (nx - 1)
    sends = 3 * one_plane + 8 + 1 + 7 + 3 * (NZ - 1)
    slot_o, slot_q = (NZ // 2, shard, wide), (NZ // 2, shard, q_all)
    gate_slot = (NZ, NC) + block
    place_all = (ny, NZ, nx, NC, shard)
    shapes = [(shard, q_width), (shard, key_width), (shard, key_width), (shard, wide), (shard, HD)]
    return pl.pallas_call(
        lambda *refs: back_kernel(nx, key_width, b_rows, *refs),
        name="back",
        cost_estimate=pl.CostEstimate(
            flops=100_000_000_000, bytes_accessed=100_000_000, transcendentals=0
        ),
        out_shape=tuple(jax.ShapeDtypeStruct(shape, F32) for shape in shapes)
        + (jax.ShapeDtypeStruct((shard, spread), BF16),) * 2
        + (jax.ShapeDtypeStruct((rows, wide), BF16),)
        + (jax.ShapeDtypeStruct((NZ - 1, rows, wide), BF16),),
        in_specs=[hbm] * 5 + [vmem] * len(args),
        out_specs=(vmem,) * 8 + (hbm,),
        scratch_shapes=[
            dma((sends,)),
            pltpu.VMEM((ny * NZ * nx * NC, shard, qkv_width), BF16),
            pltpu.VMEM(place_all + (wide,), BF16),
            pltpu.VMEM(place_all + (q_all,), BF16),
            pltpu.VMEM((ny, NZ, nx, shard, wide), BF16),
            pltpu.VMEM((ny, NZ, nx, shard, q_all), BF16),
            pltpu.VMEM((NZ, shard, q_all + wide), BF16),
            pltpu.VMEM((NZ - 1, shard, q_all + wide), BF16),
            pltpu.VMEM((NZ, NC, 2) + block, BF16),
            pltpu.VMEM((2,) + gate_slot, BF16),
            pltpu.VMEM((rows, q_width), BF16),
            pltpu.VMEM((rows, qkv_width), BF16),
            pltpu.VMEM((2 * rows, 2 * key_width), F32),
            pltpu.VMEM((rows, 2 * key_width), BF16),
            pltpu.VMEM((rows, 2 * key_width), BF16),
            pltpu.VMEM((rows, wide), BF16),
            dma,
            dma((2, 2, 2)),
            dma((2, NZ - 1)),
            dma((NZ, NC)),
            dma,
            pltpu.VMEM((NZ - 1, rows, wide), BF16),
            dma((2,)),
            dma((NZ - 1,)),
        ]
        + plane_scratch(gate_slot, nx, ny)
        + plane_scratch(gate_slot, ny, nx)
        + plane_scratch(slot_o, nx, ny, True)
        + plane_scratch(slot_o, ny, nx, True)
        + plane_scratch(slot_q, nx, ny, True)
        + plane_scratch(slot_q, ny, nx, True),
        compiler_params=pltpu.CompilerParams(
            collective_id=collective_id, has_side_effects=True, vmem_limit_bytes=67_043_328
        ),
    )(gate, up, ao, kept, given, *args)


def make_body(ny, nx):
    def body(
        inputs,
        segment_ids,
        attn_gain,
        q_weight,
        k_weight,
        v_weight,
        qkv_bias,
        o_weight,
        mlp_gain,
        gate_weight,
        up_weight,
        down_weight,
        cotangent,
    ):
        tok_rows = inputs.shape[1]
        hidden_in = inputs[0].astype(F32)
        grad_out = cotangent[0]
        seg_all = segment_ids[0]
        length = seg_all.shape[0]
        seq_place = lax.axis_index("y")
        tok_pos = seq_place * tok_rows + jnp.arange(tok_rows)
        cos_tok, sin_tok = tables(tok_pos)
        query_width = q_weight.shape[1]
        key_width = k_weight.shape[1]
        kv_heads = key_width // HD
        q_heads = query_width // HD
        group = q_heads // kv_heads

        g_rows = attn_gain.shape[0]
        b_rows = qkv_bias.shape[0]
        qkv_width = query_width + 2 * key_width
        extra = jnp.concatenate(
            [
                attn_gain[:, None],
                mlp_gain[:, None],
                jnp.broadcast_to(qkv_bias[None], (g_rows, b_rows)),
                jnp.zeros((g_rows, HD - 2 - b_rows), BF16),
            ],
            axis=1,
        )
        packed = jnp.concatenate([q_weight, k_weight, v_weight, o_weight, extra], axis=1)
        attn_all, columns_all, down_all, grad_out_all = weight_gather(
            ny,
            nx,
            packed,
            gate_weight,
            up_weight,
            down_weight,
            grad_out,
            0,
        )
        full = attn_all.reshape(-1, packed.shape[1])
        full_qkv = full[:, :qkv_width]
        full_out = full[:, qkv_width : qkv_width + query_width]
        tail = attn_all[..., qkv_width + query_width :].astype(F32)
        gain_one = tail[..., 0].reshape(-1)
        gain_two = tail[..., 1].reshape(-1)
        bias = tail[..., 0, 2 : 2 + b_rows].reshape(-1)
        width = gate_weight.shape[1] // (NZ * NC)
        full_gate = columns_all[0].reshape(-1, width)
        full_up = columns_all[1].reshape(-1, width)
        full_down = down_all.reshape(width, -1)
        grad_out_all = grad_out_all.reshape(-1, grad_out.shape[1])

        rescale_one = lax.rsqrt(jnp.mean(hidden_in * hidden_in, axis=-1, keepdims=True) + EPS)
        normed_one = hidden_in * rescale_one
        input_one = (normed_one * gain_one).astype(BF16)
        qkv_pre = dot(input_one, full_qkv) + bias
        query = rotate(qkv_pre[:, :query_width], cos_tok, sin_tok).astype(BF16)
        key = rotate(qkv_pre[:, query_width : query_width + key_width], cos_tok, sin_tok)
        kv = jnp.concatenate([key, qkv_pre[:, query_width + key_width :]], axis=1).astype(BF16)
        kv_all = lax.all_gather(kv, "y", axis=0, tiled=True)
        key_heads = kv_all[:, :key_width].reshape(length, kv_heads, HD)
        value_heads = kv_all[:, key_width:].reshape(length, kv_heads, HD)
        query_heads = query.reshape(tok_rows, kv_heads, group, HD)
        score_scale = HD ** (-0.5)
        all_pos = jnp.arange(length)
        seg_tok = lax.dynamic_slice(seg_all, (seq_place * tok_rows,), (tok_rows,))
        allowed = (tok_pos[:, None] >= all_pos[None, :]) & (seg_tok[:, None] == seg_all[None, :])
        scores = (
            jnp.einsum("qkgd,pkd->kgqp", query_heads, key_heads, preferred_element_type=F32)
            * score_scale
        )
        masked = jnp.where(allowed[None, None], scores, MASKED)
        row_max = jnp.max(masked, axis=-1, keepdims=True)
        exponent = jnp.exp(masked - row_max)
        row_total = jnp.sum(exponent, axis=-1, keepdims=True)
        probs = exponent / row_total
        probs_low = probs.astype(BF16)
        mixture = jnp.einsum("kgqp,pkd->qkgd", probs_low, value_heads, preferred_element_type=F32)
        attn_tok = mixture.astype(BF16).reshape(tok_rows, query_width)
        middle = hidden_in + dot(attn_tok, full_out)

        rescale_two = lax.rsqrt(jnp.mean(middle * middle, axis=-1, keepdims=True) + EPS)
        normed_two = middle * rescale_two
        input_two = (normed_two * gain_two).astype(BF16)
        by_shard = (ny, NZ, nx, NC, g_rows, width)
        fused = g_rows % 16 == 0
        grad_input_two, out_part, part_gate, part_up, *downs = mlp(
            ny, nx, fused, input_two, full_gate, full_up, full_down, grad_out_all, 1
        )
        grad_gain_two, grad_mid = norm_back(grad_input_two, normed_two, rescale_two, gain_two)
        grad_mid = grad_mid + grad_out.astype(F32)
        grad_branch = grad_mid.astype(BF16)
        if fused:
            args = (
                grad_mid,
                grad_branch,
                inputs[0],
                gain_one[None],
                attn_tok,
                query,
                kv_all,
                allowed.astype(F32),
                jnp.concatenate([cos_tok, cos_tok], axis=1),
                jnp.concatenate([sin_tok, -sin_tok], axis=1),
                (grad_input_two * normed_two).astype(BF16),
            )
            outs = back(
                ny,
                nx,
                b_rows,
                part_gate.reshape(by_shard),
                part_up.reshape(by_shard),
                attn_all.reshape((-1,) + packed.shape),
                out_part,
                downs[2],
                args,
                3,
            )
            grad_q, grad_k, grad_v, grad_o, tail_sum, grad_gate_w, grad_up_w = outs[:7]
            grad_in, ring = outs[7:]
            first_row = lax.axis_index("z") * tok_rows
            out_sum = jnp.sum(ring.astype(F32), axis=0)
            for half in (out_part, downs[2]):
                out_sum += lax.dynamic_slice_in_dim(half, first_row, tok_rows).astype(F32)
            output = (middle + out_sum).astype(BF16)[None]
            return (
                output,
                grad_in[None],
                tail_sum[:, 0],
                grad_q,
                grad_k,
                grad_v,
                tail_sum[0, HD // 2 : HD // 2 + b_rows],
                grad_o,
                tail_sum[:, 1],
                grad_gate_w.astype(F32),
                grad_up_w.astype(F32),
                downs[1].astype(F32),
            )
        grad_attn = dot_nt(grad_branch, full_out).astype(BF16)
        grad_heads = grad_attn.reshape(tok_rows, kv_heads, group, HD)
        grad_probs = jnp.einsum(
            "qkgd,pkd->kgqp", grad_heads, value_heads, preferred_element_type=F32
        )
        inner_sum = jnp.sum(probs * grad_probs, axis=-1, keepdims=True)
        grad_scores = (probs * (grad_probs - inner_sum)).astype(BF16)
        grad_query = (
            jnp.einsum("kgqp,pkd->qkgd", grad_scores, key_heads, preferred_element_type=F32)
            * score_scale
        ).reshape(tok_rows, query_width)
        grad_key = (
            jnp.einsum("kgqp,qkgd->pkd", grad_scores, query_heads, preferred_element_type=F32)
            * score_scale
        ).reshape(length, key_width)
        grad_value = jnp.einsum(
            "kgqp,qkgd->pkd", probs_low, grad_heads, preferred_element_type=F32
        ).reshape(length, key_width)
        grad_kv = jnp.concatenate([grad_key, grad_value], axis=1).astype(BF16)
        other = lax.dynamic_slice(
            grad_kv, ((1 - seq_place) * tok_rows, 0), (tok_rows, 2 * key_width)
        )
        own = lax.dynamic_slice(grad_kv, (seq_place * tok_rows, 0), (tok_rows, 2 * key_width))
        swapped = lax.ppermute(other, "y", [(0, 1), (1, 0)])
        grad_kv_tok = own.astype(F32) + swapped.astype(F32)
        grad_query_pre = rotate(grad_query, cos_tok, -sin_tok).astype(BF16)
        grad_key_pre = rotate(grad_kv_tok[:, :key_width], cos_tok, -sin_tok).astype(BF16)
        grad_value_pre = grad_kv_tok[:, key_width:].astype(BF16)
        grad_qkv = jnp.concatenate([grad_query_pre, grad_key_pre, grad_value_pre], axis=1)
        grad_qkv_sum = jnp.sum(grad_qkv.astype(F32), axis=0)
        grad_input_one = dot_nt(grad_qkv, full_qkv)
        grad_gain_one, grad_first = norm_back(grad_input_one, normed_one, rescale_one, gain_one)
        grad_total = grad_mid + grad_first
        shards = ny * NZ * nx * NC
        tail_grads = jnp.concatenate(
            [
                grad_gain_one[:, None],
                grad_gain_two[:, None],
                jnp.broadcast_to(
                    grad_qkv_sum.reshape(shards, 1, b_rows), (shards, g_rows, b_rows)
                ).reshape(-1, b_rows),
                jnp.zeros((shards * g_rows, HD - 2 - b_rows), F32),
            ],
            axis=1,
        )
        grad_attn_w = jnp.concatenate(
            [
                dot_tn(input_one, grad_qkv).astype(BF16),
                dot_tn(attn_tok, grad_branch).astype(BF16),
                tail_grads.astype(BF16),
            ],
            axis=1,
        )
        widths = (query_width, key_width, key_width, query_width, HD)
        pieces = (NZ, NC, tok_rows // 32, 32, hidden_in.shape[1])
        outs = last_scatter(
            ny,
            nx,
            grad_attn_w.reshape((ny, NZ, nx, NC, g_rows, -1)),
            widths,
            part_gate.reshape(by_shard),
            part_up.reshape(by_shard),
            downs[0].reshape((ny, nx) + down_weight.shape),
            out_part.reshape(pieces),
            3,
        )
        grad_q, grad_k, grad_v, grad_o, tail_sum = outs[:5]
        grad_gate_w, grad_up_w, grad_down_w, out_sum = outs[5:]
        output = (middle + out_sum.reshape(middle.shape)).astype(BF16)[None]
        return (
            output,
            grad_total.astype(BF16)[None],
            tail_sum[:, 0],
            grad_q,
            grad_k,
            grad_v,
            tail_sum[0, 2 : 2 + b_rows],
            grad_o,
            tail_sum[:, 1],
            grad_gate_w,
            grad_up_w,
            grad_down_w,
        )

    return body


def solution(mesh):
    ny = mesh.shape["seq"]
    nx = mesh.shape["fsdp"] // (NZ * NC)
    grid = Mesh(mesh.devices.reshape(ny, NZ, nx, NC), ALL)
    tokens = P(("z", "x", "c"), "y", None)
    rows = P(ALL, None)
    vec = P(ALL)
    return jax.shard_map(
        make_body(ny, nx),
        mesh=grid,
        in_specs=(
            tokens,
            P(("z", "x", "c"), None),
            vec,
            rows,
            rows,
            rows,
            vec,
            rows,
            vec,
            rows,
            rows,
            rows,
            tokens,
        ),
        out_specs=(tokens, tokens, vec, rows, rows, rows, vec, rows, vec, rows, rows, rows),
        check_vma=False,
    )
```

```python
import types

import jax
import jax.numpy as jnp
from jax import lax
from jax.experimental import pallas as pl
from jax.experimental.pallas import tpu as pltpu
from jax.sharding import Mesh, PartitionSpec as P

HD = 128
EPS = 1e-06
ROPE_BASE = 1000000.0
MASKED = -1e30
NZ = 4
NC = 2
ALL = ("y", "z", "x", "c")
TP = ("z", "c")
DP = ("y", "x")
F32 = jnp.float32
BF16 = jnp.bfloat16


def tables(positions):
    freq = ROPE_BASE ** (-jnp.arange(0, HD, 2).astype(F32) / HD)
    angle = positions.astype(F32)[:, None] * freq[None, :]
    return (jnp.cos(angle), jnp.sin(angle))


def rotate(values, cosine, sine):
    count = values.shape[0]
    split = values.reshape(count, -1, HD)
    half = HD // 2
    first = split[..., :half]
    second = split[..., half:]
    cos_b = cosine[:, None, :]
    sin_b = sine[:, None, :]
    turned = jnp.concatenate(
        [first * cos_b - second * sin_b, second * cos_b + first * sin_b], axis=-1
    )
    return turned.reshape(count, -1)


def dot(a, b):
    return jnp.dot(a, b, preferred_element_type=F32)


def dot_nt(a, b):
    return lax.dot_general(a, b, (((1,), (1,)), ((), ())), preferred_element_type=F32)


def dot_tn(a, b):
    return lax.dot_general(a, b, (((0,), (0,)), ((), ())), preferred_element_type=F32)


def norm_back(grad_normed, normed, rescale, gain_vec):
    grad_gain = jnp.sum(grad_normed * normed, axis=0)
    scaled = grad_normed * gain_vec
    grad_x = rescale * (scaled - normed * jnp.mean(scaled * normed, axis=-1, keepdims=True))
    return (grad_gain, grad_x)


class Wires:
    def __init__(self, sems):
        self.sems = sems
        self.used = 0
        self.started = []

    def send(self, src, dst, recv_sem, device, cond=None):
        copy = pltpu.make_async_remote_copy(
            src_ref=src,
            dst_ref=dst,
            send_sem=self.sems.at[self.used],
            recv_sem=recv_sem,
            device_id=device,
            device_id_type=pl.DeviceIdType.MESH,
        )
        if cond is None:
            copy.start()
        else:
            pl.when(cond())(copy.start)
        self.started.append((still(src), self.used, cond))
        self.used += 1

    def arrived(self, dst, recv_sem, device):
        pltpu.make_async_remote_copy(
            src_ref=dst,
            dst_ref=dst,
            send_sem=self.sems.at[0],
            recv_sem=recv_sem,
            device_id=device,
            device_id_type=pl.DeviceIdType.MESH,
        ).wait_recv()

    def finish(self, sent=None):
        for src, used, cond in self.started if sent is None else sent:
            sem = self.sems.at[used]
            src = taken(*src)
            copy = pltpu.make_async_remote_copy(
                src_ref=src,
                dst_ref=src,
                send_sem=sem,
                recv_sem=sem,
                device_id={"c": 1 - lax.axis_index("c")},
                device_id_type=pl.DeviceIdType.MESH,
            )
            if cond is None:
                copy.wait_send()
            else:
                pl.when(cond())(copy.wait_send)


def still(ref):
    steps = []
    for step in getattr(ref, "transforms", ()):
        steps.append([i.size if isinstance(i, pl.Slice) else None for i in step.indices])
    return getattr(ref, "ref", ref), steps


def taken(view, steps):
    for step in steps:
        view = view.at[tuple(0 if size is None else pl.ds(0, size) for size in step)]
    return view


def line_order(z, k):
    if k == 0:
        return z + 1 - 2 * (z % 2)
    if k == 1:
        return 2 - z // 2
    return 3 - 3 * (z // 2)


def greet(peers):
    barrier = pltpu.get_barrier_semaphore()
    for peer in peers:
        pl.semaphore_signal(
            barrier, inc=1, device_id=peer, device_id_type=pl.DeviceIdType.MESH
        )
    pl.semaphore_wait(barrier, len(peers))


def place():
    return tuple(lax.axis_index(name) for name in ALL)


def line_peers(z, c):
    peers = [{"c": 1 - c}]
    for k in range(NZ - 1):
        peers.append({"z": (z + k + 1) % NZ})
    return peers


class LineGather:
    def __init__(self, wires, own, out, recv, z, c):
        self.wires, self.own, self.out, self.recv, self.z, self.c = wires, own, out, recv, z, c

    def begin(self):
        w, z, c = self.wires, self.z, self.c
        dst, sem = self.out.at[z, c], self.recv.at[z, c]
        w.send(self.own, dst, sem, {"z": jnp.minimum(z + 1, NZ - 1)}, lambda: z < NZ - 1)
        w.send(self.own, dst, sem, {"z": jnp.maximum(z - 1, 0)}, lambda: z > 0)
        w.send(self.own, dst, sem, {"c": 1 - c})

    def event(self, k):
        w, z, c = self.wires, self.z, self.c
        zq = line_order(z, k)
        slot, sem = self.out.at[zq, c], self.recv.at[zq, c]
        w.arrived(slot, sem, {"c": 1 - c})
        onward = jnp.where(zq < z, jnp.minimum(z + 1, NZ - 1), jnp.maximum(z - 1, 0))
        w.send(slot, slot, sem, {"z": onward}, lambda: (z > 0) & (z < NZ - 1))
        w.send(slot, slot, sem, {"c": 1 - c})

    def sibling(self, zq):
        w, c = self.wires, self.c
        w.arrived(self.out.at[zq, 1 - c], self.recv.at[zq, 1 - c], {"c": 1 - c})


def segments(nx, fs):
    for yq in range(2):
        for zq in range(NZ):
            for xq in range(nx):
                for cq in range(NC):
                    first = (((yq * NZ + zq) * nx + xq) * NC + cq) * fs
                    yield zq, cq, (yq * nx + xq) * fs, first


def weight_gather_kernel(
    nx, a, g, u, d, tok, ao, guo, do, co, gu, send_sems, local_sems, ra, rt, rw, rd, rc
):
    y, z, x, c = place()
    sib = {"c": 1 - c}
    ypeer = {"y": 1 - y}
    xpeers = [(x + i + 1) % nx for i in range(nx - 1)]
    planes = [{"x": xp} for xp in xpeers] + [ypeer]
    cross = [{"z": (z + k + 1) % NZ, "c": 1 - c} for k in range(NZ - 1)]
    greet(line_peers(z, c) + cross + planes)
    locals_ = [
        pltpu.make_async_copy(a, ao.at[y, z, x, c], local_sems.at[0]),
        pltpu.make_async_copy(d, do.at[y, x], local_sems.at[1]),
        pltpu.make_async_copy(tok, co.at[z, c], local_sems.at[2]),
    ]
    keep = pltpu.make_async_copy(gu.at[z, c], guo.at[:, y, z, x, c], local_sems.at[3])
    for copy in locals_:
        copy.start()
    wires = Wires(send_sems)

    def both_ways(src, dst, sem):
        for peer in planes:
            wires.send(src, dst, sem, peer)

    own_slot, own_sem = ao.at[y, z, x, c], ra.at[y, z, x, c]
    wires.send(a, own_slot, own_sem, {"z": jnp.minimum(z + 1, NZ - 1)}, lambda: z < NZ - 1)
    wires.send(a, own_slot, own_sem, {"z": jnp.maximum(z - 1, 0)}, lambda: z > 0)
    both_ways(a, own_slot, own_sem)
    wires.send(a, own_slot, own_sem, sib)
    fs = gu.shape[-1] // (2 * nx)
    for m, shard in enumerate((g, u)):
        for zq, cq, run, first in segments(nx, fs):
            gu[zq, cq, m, :, run : run + fs] = shard[:, first : first + fs]
    keep.start()
    for k in range(NZ - 1):
        zq = line_order(z, k)
        slot, sem = ao.at[y, zq, x, c], ra.at[y, zq, x, c]
        wires.arrived(slot, sem, sib)
        onward = jnp.where(zq < z, jnp.minimum(z + 1, NZ - 1), jnp.maximum(z - 1, 0))
        wires.send(slot, slot, sem, {"z": onward}, lambda: (z > 0) & (z < NZ - 1))
        both_ways(slot, slot, sem)
        wires.send(slot, slot, sem, sib)

    for k in range(NZ * NC - 1):
        step = k + 1
        zp, cp = (z + step // NC) % NZ, (c + step) % NC
        wires.send(
            gu.at[zp, cp], guo.at[:, y, z, x, c], rt.at[z, c], {"z": zp, "c": cp}
        )
    line = LineGather(wires, tok, co, rc, z, c)
    line.begin()
    half = d.shape[1] // 2
    parts = [pl.ds(0, half), pl.ds(half, half)]
    for h in range(2):
        both_ways(d.at[:, parts[h]], do.at[y, x, :, parts[h]], rd.at[h, y, x])

    def relay_attn(yq, xq, zq, peers):
        slot, sem = ao.at[yq, zq, xq, c], ra.at[yq, zq, xq, c]
        wires.arrived(slot, sem, sib)
        for peer in peers:
            wires.send(slot, slot, sem, peer)
        wires.send(slot, slot, sem, sib)

    for zq in range(NZ):
        for xp in xpeers:
            relay_attn(y, xp, zq, [ypeer] if zq < NZ // 2 else [])
        relay_attn(1 - y, x, zq, planes[:-1] if zq >= NZ // 2 else [])

    for k in range(NZ * NC - 1):
        step = k + 1
        zp, cp = (z + step // NC) % NZ, (c + step) % NC
        wires.arrived(guo.at[:, y, zp, x, cp], rt.at[zp, cp], sib)
    keep.wait()
    for m in range(2):
        plane = guo.at[m, y, :, x]
        both_ways(plane, plane, rw.at[m, y, x])
    line.event(0)

    def relay(ref, sem, peers):
        wires.arrived(ref, sem, sib)
        for peer in peers:
            wires.send(ref, ref, sem, peer)

    for xp in xpeers:
        relay(do.at[y, xp, :, parts[0]], rd.at[0, y, xp], [ypeer])
        relay(do.at[y, xp, :, parts[1]], rd.at[1, y, xp], [])
    relay(do.at[1 - y, x, :, parts[1]], rd.at[1, 1 - y, x], planes[:-1])
    relay(do.at[1 - y, x, :, parts[0]], rd.at[0, 1 - y, x], [])
    for xp in xpeers:
        for zq in range(NZ):
            relay_attn(1 - y, xp, zq, [])
    line.event(1)
    for xp in xpeers:
        relay(guo.at[0, y, :, xp], rw.at[0, y, xp], [ypeer])
    relay(guo.at[1, 1 - y, :, x], rw.at[1, 1 - y, x], planes[:-1])
    line.event(2)
    for xp in xpeers:
        relay(guo.at[1, y, :, xp], rw.at[1, y, xp], [])
    relay(guo.at[0, 1 - y, :, x], rw.at[0, 1 - y, x], [])
    for xp in xpeers:
        for h in range(2):
            relay(do.at[1 - y, xp, :, parts[h]], rd.at[h, 1 - y, xp], [])
            relay(guo.at[h, 1 - y, :, xp], rw.at[h, 1 - y, xp], [])
    for zq in range(NZ):
        line.sibling(zq)
    for yq in range(2):
        for zq in range(NZ):
            for xq in range(nx):
                wires.arrived(ao.at[yq, zq, xq, 1 - c], ra.at[yq, zq, xq, 1 - c], sib)
    wires.finish()
    for copy in locals_:
        copy.wait()


def weight_gather(ny, nx, a, g, u, d, tok, collective_id):
    sends = 3 + (nx + 1) + 3 * (nx + 2)
    sends += 7 + 9 + 2 * nx
    sends += 4 * nx + 2 * (nx - 1) + 2 * (nx - 1)
    sends += 2 * nx + 2 * (nx - 1) + 4 * (nx - 1) + 2 * (nx - 1)
    hbm = pl.BlockSpec(memory_space=pl.ANY)
    vmem = pl.BlockSpec(memory_space=pltpu.VMEM)
    grid = (ny, NZ, nx, NC)
    block = g.shape[:1] + (g.shape[1] // (NZ * NC),)
    return pl.pallas_call(
        lambda *refs: weight_gather_kernel(nx, *refs),
        name="weight_gather",
        out_shape=(
            jax.ShapeDtypeStruct(grid + a.shape, BF16),
            jax.ShapeDtypeStruct((2,) + grid + block, BF16),
            jax.ShapeDtypeStruct((ny, nx) + d.shape, BF16),
            jax.ShapeDtypeStruct((NZ, NC) + tok.shape, BF16),
        ),
        in_specs=[hbm, vmem, vmem, hbm, hbm],
        out_specs=(hbm,) * 4,
        scratch_shapes=[
            pltpu.VMEM((NZ, NC, 2) + block, BF16),
            pltpu.SemaphoreType.DMA((sends + 16,)),
            pltpu.SemaphoreType.DMA((4,)),
            pltpu.SemaphoreType.DMA(grid),
            pltpu.SemaphoreType.DMA((NZ, NC)),
            pltpu.SemaphoreType.DMA((2, ny, nx)),
            pltpu.SemaphoreType.DMA((2, ny, nx)),
            pltpu.SemaphoreType.DMA((NZ, NC)),
        ],
        compiler_params=pltpu.CompilerParams(
            collective_id=collective_id, has_side_effects=True
        ),
    )(a, g, u, d, tok)


def total_into(dst, refs, flat=None):
    flat = len(dst.shape) == 2

    def entry(i, carry):
        here = (slice(None), pl.ds(pl.multiple_of(i * 128, 128), 128)) if flat else i
        total = refs[0][here].astype(F32)
        for ref in refs[1:]:
            total = total + ref[here].astype(F32)
        dst[here] = total.astype(dst.dtype)
        return carry

    lax.fori_loop(0, dst.shape[1] // 128 if flat else dst.shape[0], entry, 0)


class PlaneScatter:
    def __init__(self, wires, src, first, second, bufs, loaded=False):
        self.wires, self.src = wires, src
        self.name_a, self.size_a, self.a = first
        self.name_b, self.size_b, self.b = second
        self.r1, self.own, self.r2, self.s1, self.sl, self.s2 = bufs
        self.loaded = loaded

    def mine(self, b):
        return self.src(self.a, b) if self.loaded else self.own.at[b]

    def order(self):
        return [(self.b + i + 1) % self.size_b for i in range(self.size_b)]

    def begin(self):
        for b in self.order():
            for i in range(self.size_a - 1):
                peer, j = (self.a + i + 1) % self.size_a, self.size_a - 2 - i
                self.wires.send(
                    self.src(peer, b), self.r1.at[j, b], self.s1.at[j, b], {self.name_a: peer}
                )
            if not self.loaded:
                self.load(b).start()

    def load(self, b):
        return pltpu.make_async_copy(self.src(self.a, b), self.own.at[b], self.sl.at[b])

    def gathered(self, b):
        if not self.loaded:
            self.load(b).wait()
        for j in range(self.size_a - 1):
            self.wires.arrived(self.r1.at[j, b], self.s1.at[j, b], {self.name_a: self.a})
        return [self.mine(b)] + [self.r1.at[j, b] for j in range(self.size_a - 1)]

    def relay(self):
        for i, b in enumerate(self.order()[:-1]):
            j = self.size_b - 2 - i
            total_into(self.mine(b), self.gathered(b))
            self.wires.send(self.mine(b), self.r2.at[j], self.s2.at[j], {self.name_b: b})

    def finish(self, dst):
        refs = self.gathered(self.b)
        for j in range(self.size_b - 1):
            self.wires.arrived(self.r2.at[j], self.s2.at[j], {self.name_b: self.b})
            refs.append(self.r2.at[j])
        total_into(dst, refs)


def plane_scratch(slot, size_a, size_b, loaded=False):
    own = (1,) * (1 + len(slot)) if loaded else (size_b,) + slot
    return [
        pltpu.VMEM((size_a - 1, size_b) + slot, BF16),
        pltpu.VMEM(own, BF16),
        pltpu.VMEM((size_b - 1,) + slot, BF16),
        pltpu.SemaphoreType.DMA((size_a - 1, size_b)),
        pltpu.SemaphoreType.DMA((size_b,)),
        pltpu.SemaphoreType.DMA((size_b - 1,)),
    ]


class LineScatter:
    def __init__(self, wires, part, bufs, z, c):
        self.wires, self.part, self.z, self.c = wires, part, z, c
        self.own, self.sib, self.left, self.right = bufs[:4]
        self.s_own, self.s_sib, self.s_left, self.s_right = bufs[4:]

    def order(self):
        return [line_order(self.z, k) for k in (2, 1, 0)] + [self.z]

    def load(self, zq):
        return pltpu.make_async_copy(
            self.part.at[zq, self.c], self.own.at[zq], self.s_own.at[zq]
        )

    def begin(self):
        for zq in self.order():
            self.wires.send(
                self.part.at[zq, 1 - self.c],
                self.sib.at[zq],
                self.s_sib.at[zq],
                {"c": 1 - self.c},
            )
            self.load(zq).start()

    def ready(self, zq):
        self.load(zq).wait()
        self.wires.arrived(self.sib.at[zq], self.s_sib.at[zq], {"c": 1 - self.c})

    def hop(self, k):
        z = self.z
        for sign, buf, sems in ((1, self.left, self.s_left), (-1, self.right, self.s_right)):
            target = z + sign * k
            inside = (target < NZ) if sign > 0 else (target >= 0)
            behind = (z > 0) if sign > 0 else (z < NZ - 1)
            target = jnp.clip(target, 0, NZ - 1)
            own, sib = self.own.at[target], self.sib.at[target]

            @pl.when(inside)
            def _():
                self.ready(target)

            if k < NZ - 1:

                @pl.when(inside & behind)
                def _():
                    self.wires.arrived(buf.at[k], sems.at[k], {"z": z})
                    total_into(own, [own, sib, buf.at[k]])

                @pl.when(inside & jnp.logical_not(behind))
                def _():
                    total_into(own, [own, sib])

            else:

                @pl.when(inside)
                def _():
                    total_into(own, [own, sib])

            onward = jnp.clip(z + sign, 0, NZ - 1)
            self.wires.send(own, buf.at[k - 1], sems.at[k - 1], {"z": onward}, lambda: inside)

    def finish(self, dst):
        z = self.z
        self.ready(z)
        own, sib = self.own.at[z], self.sib.at[z]

        @pl.when(z > 0)
        def _():
            self.wires.arrived(self.left.at[0], self.s_left.at[0], {"z": z})

        @pl.when(z < NZ - 1)
        def _():
            self.wires.arrived(self.right.at[0], self.s_right.at[0], {"z": z})

        @pl.when(z == 0)
        def _():
            total_into(dst, [own, sib, self.right.at[0]])

        @pl.when(z == NZ - 1)
        def _():
            total_into(dst, [own, sib, self.left.at[0]])

        @pl.when((z > 0) & (z < NZ - 1))
        def _():
            total_into(dst, [own, sib, self.left.at[0], self.right.at[0]])


def line_scratch(slot):
    return [
        pltpu.VMEM((NZ,) + slot, BF16),
        pltpu.VMEM((NZ,) + slot, BF16),
        pltpu.VMEM((NZ - 1,) + slot, BF16),
        pltpu.VMEM((NZ - 1,) + slot, BF16),
        pltpu.SemaphoreType.DMA((NZ,)),
        pltpu.SemaphoreType.DMA((NZ,)),
        pltpu.SemaphoreType.DMA((NZ - 1,)),
        pltpu.SemaphoreType.DMA((NZ - 1,)),
    ]


TILES = ((0, 640), (640, None))


def remote(src, dst, send_sem, recv_sem, device):
    return pltpu.make_async_remote_copy(
        src_ref=src,
        dst_ref=dst,
        send_sem=send_sem,
        recv_sem=recv_sem,
        device_id=device,
        device_id_type=pl.DeviceIdType.MESH,
    )


def mlp_kernel(
    nx,
    with_down,
    h,
    wg,
    wu,
    wd,
    cot,
    dh,
    out_part,
    grad_g,
    grad_u,
    grad_d,
    *scratch,
):
    if with_down:
        down_out, out_sib, scratch = scratch[0], scratch[1], scratch[2:]
    (
        hv,
        cv,
        wgv,
        wuv,
        wdv,
        av,
        dgv,
        duv,
        part,
        sib,
        ring,
        ob,
        s_load,
        s_cot,
        s_ob,
        s_out,
        h_send,
        h_on,
        h_sib,
        h_recv,
        p_send,
        p_recv,
        r_send,
        r_recv,
    ) = scratch[: 24]
    scratch = scratch[24:]
    if with_down:
        o_send, o_recv, scratch = scratch[0], scratch[1], scratch[2:]
    y, z, x, c = place()
    rows, wide = h.shape
    units = wg.shape[1]
    other = 1 - c
    inner = (z > 0) & (z < NZ - 1)
    greet(line_peers(z, c) + (plane_peers(nx, y, x) if with_down else []))

    def block(zq, cq):
        return pl.ds(pl.multiple_of((zq * NC + cq) * rows, rows), rows)

    loads = [
        pltpu.make_async_copy(h, hv.at[block(z, c)], s_load.at[0]),
        pltpu.make_async_copy(wg, wgv, s_load.at[1]),
        pltpu.make_async_copy(wu, wuv, s_load.at[2]),
        pltpu.make_async_copy(wd, wdv, s_load.at[3]),
    ]

    def load_cot(zq, cq):
        return pltpu.make_async_copy(
            cot.at[block(zq, cq)], cv.at[block(zq, cq)], s_cot.at[zq, cq]
        )

    def send_own(i):
        there = hv.at[block(z, c)]
        device = (
            {"z": jnp.minimum(z + 1, NZ - 1)},
            {"z": jnp.maximum(z - 1, 0)},
            {"c": other},
        )[i]
        return remote(h, there, h_send.at[i], h_recv.at[z, c], device)

    pl.when(z < NZ - 1)(send_own(0).start)
    pl.when(z > 0)(send_own(1).start)
    send_own(2).start()
    for copy in loads[:3]:
        copy.start()
    load_cot(z, c).start()
    loads[3].start()
    load_cot(z, other).start()
    for k in range(NZ - 1):
        for i in range(NC):
            load_cot(line_order(z, k), (c + i) % NC).start()

    def arrival(zq, cq):
        here = hv.at[block(zq, cq)]
        return remote(here, here, h_send.at[0], h_recv.at[zq, cq], {"c": other})

    def onward(k):
        zq = line_order(z, k)
        here = hv.at[block(zq, c)]
        device = {"z": jnp.where(zq < z, jnp.minimum(z + 1, NZ - 1), jnp.maximum(z - 1, 0))}
        return remote(here, here, h_on.at[k], h_recv.at[zq, c], device)

    def to_sibling(k):
        zq = line_order(z, k)
        here = hv.at[block(zq, c)]
        return remote(here, here, h_sib.at[k], h_recv.at[zq, c], {"c": other})

    def take(k):
        arrival(line_order(z, k), c).wait_recv()
        pl.when(inner)(onward(k).start)
        to_sibling(k).start()

    def output(zq, cq):
        if with_down:
            here = pl.ds(pl.multiple_of(zq * rows, rows), rows)
            return pltpu.make_async_copy(ob.at[cq], out_part.at[here], s_ob.at[0])
        return pltpu.make_async_copy(ob.at[cq], out_part.at[block(zq, cq)], s_ob.at[cq])

    def output_over(zq):
        here = pl.ds(pl.multiple_of(zq * rows, rows), rows)
        return remote(
            ob.at[other], out_sib.at[here], o_send.at[zq], o_recv.at[zq], {"c": other}
        )

    def partial_over(zq):
        return remote(
            part.at[block(zq, other)], sib.at[zq], p_send.at[zq], p_recv.at[zq], {"c": other}
        )

    def partial_home(zq):
        j = (z - zq + NZ) % NZ - 1
        return remote(
            part.at[block(zq, c)], ring.at[j], r_send.at[zq], r_recv.at[j], {"z": zq}
        )

    piece = rows // 8

    def combine(zq):
        remote(sib.at[zq], sib.at[zq], p_send.at[0], p_recv.at[zq], {"c": other}).wait_recv()

        def step(i, carry):
            here = pl.ds(pl.multiple_of((zq * NC + c) * rows + i * piece, piece), piece)
            there = pl.ds(pl.multiple_of(i * piece, piece), piece)
            total = part[here].astype(F32) + sib[zq, there].astype(F32)
            part[here] = total.astype(BF16)
            return carry

        lax.fori_loop(0, 8, step, 0)

    def place_of(k):
        near = line_order(z, 0)
        mid = line_order(z, 1)
        far = line_order(z, 2)
        return jnp.where(k == 0, z, jnp.where(k == 1, near, jnp.where(k == 2, mid, far)))

    def pair(k, carry):
        zq = place_of(k)

        @pl.when(k == 1)
        def _():
            take(0)
            pl.when(inner)(lambda: take(1))

        @pl.when(k == 2)
        def _():
            pl.when(jnp.logical_not(inner))(lambda: take(1))
            pl.when(inner)(lambda: take(2))

        @pl.when((k == 3) & jnp.logical_not(inner))
        def _():
            take(2)

        def one(j, carry):
            cq = (c + j) % NC
            here = block(zq, cq)

            @pl.when((k == 0) & (j == 0))
            def _():
                for copy in loads:
                    copy.wait()

            @pl.when(j == 1)
            def _():
                arrival(zq, cq).wait_recv()

            load_cot(zq, cq).wait()
            for low, high in TILES:
                high = units if high is None else high
                gate = dot(hv[here], wgv[:, low:high])
                up = dot(hv[here], wuv[:, low:high])
                grad = dot_nt(cv[here], wdv[low:high])
                sig = jax.nn.sigmoid(gate)
                act = gate * sig
                av[here, low:high] = (act * up).astype(BF16)
                duv[here, low:high] = (grad * act).astype(BF16)
                dgv[here, low:high] = (
                    grad * up * (sig * (1.0 + gate * (1.0 - sig)))
                ).astype(BF16)

            if with_down:

                @pl.when((k > 0) & (j == 0))
                def _():
                    output(zq, cq).wait()

                @pl.when((k > 0) & (j == 1))
                def _():
                    output_over(place_of(k - 1)).wait_send()

            else:

                @pl.when(k > 0)
                def _():
                    output(zq, cq).wait()

            ob[cq] = dot(av[here], wdv[...]).astype(BF16)
            if with_down:
                pl.when(j == 0)(output(zq, cq).start)
                pl.when(j == 1)(output_over(zq).start)
            else:
                output(zq, cq).start()
            part[here] = (dot_nt(dgv[here], wgv[...]) + dot_nt(duv[here], wuv[...])).astype(BF16)
            return carry

        lax.fori_loop(0, NC, one, 0)
        partial_over(zq).start()

        @pl.when(k > 1)
        def _():
            before = place_of(k - 1)
            combine(before)
            partial_home(before).start()

        return carry

    lax.fori_loop(0, NZ, pair, 0)
    last = line_order(z, NZ - 2)
    step_d = wide // 6

    def down_grad(t, carry):
        cols = pl.ds(pl.multiple_of(t * step_d, step_d), step_d)
        wdv[:, cols] = dot_tn(av[...], cv[:, cols]).astype(BF16)

        @pl.when(t == 0)
        def _():
            combine(last)
            partial_home(last).start()

        return carry

    lax.fori_loop(0, 6, down_grad, 0)
    outs = [
        pltpu.make_async_copy(wdv, grad_d, s_out.at[0]),
        pltpu.make_async_copy(wgv, grad_g, s_out.at[1]),
        pltpu.make_async_copy(wuv, grad_u, s_out.at[2]),
    ]
    outs[0].start()
    if with_down:
        wires = Wires(scratch[0])
        half, shard = wide // 2, units // (2 * nx)
        left, right = pl.ds(0, half), pl.ds(half, half)

        def term(yq, xq, cols):
            first = (yq * nx + xq) * shard
            return grad_d.at[pl.ds(pl.multiple_of(first, 8), shard), cols]

        along_x, along_y = ("x", nx, x), ("y", 2, y)
        by_x = PlaneScatter(
            wires, lambda xq, yq: term(yq, xq, left), along_x, along_y, scratch[1:7]
        )
        by_y = PlaneScatter(
            wires, lambda yq, xq: term(yq, xq, right), along_y, along_x, scratch[7:13]
        )

    def turned(src, dst, first, last):
        def step(t, carry):
            cols = pl.ds(pl.multiple_of(t * step_d, step_d), step_d)
            dst[cols] = dot_tn(hv[:, cols], src[...]).astype(BF16)
            return carry

        lax.fori_loop(first, last, step, 0)

    turned(dgv, wgv, 0, 1)
    if with_down:
        outs[0].wait()
        by_x.begin()
        by_y.begin()
    turned(dgv, wgv, 1, 6)
    outs[1].start()
    turned(duv, wuv, 0, 6)
    outs[2].start()
    if with_down:
        by_x.relay()
        by_y.relay()
    combine(z)
    for j in range(NZ - 1):
        remote(ring.at[j], ring.at[j], r_send.at[0], r_recv.at[j], {"c": other}).wait_recv()

    def final(i, carry):
        here = pl.ds(pl.multiple_of((z * NC + c) * rows + i * piece, piece), piece)
        there = pl.ds(pl.multiple_of(i * piece, piece), piece)
        total = part[here].astype(F32)
        for j in range(NZ - 1):
            total = total + ring[j, there].astype(F32)
        dh[there] = total
        return carry

    lax.fori_loop(0, 8, final, 0)
    if with_down:
        by_x.finish(down_out.at[:, left])
        by_y.finish(down_out.at[:, right])
        wires.finish()
    pl.when(z < NZ - 1)(send_own(0).wait_send)
    pl.when(z > 0)(send_own(1).wait_send)
    send_own(2).wait_send()
    for k in range(NZ - 1):
        pl.when(inner)(onward(k).wait_send)
        to_sibling(k).wait_send()
        partial_home(line_order(z, k)).wait_send()
    for zq in range(NZ):
        partial_over(zq).wait_send()
    if with_down:
        output(z, c).wait()
        output_over(last).wait_send()
        for zq in range(NZ):
            there = out_sib.at[pl.ds(zq * rows, rows)]
            remote(there, there, o_send.at[0], o_recv.at[zq], {"c": other}).wait_recv()
    else:
        for cq in range(NC):
            output(z, cq).wait()
    for copy in outs[1 if with_down else 0 :]:
        copy.wait()


def mlp(ny, nx, with_down, h, wg, wu, wd, cot, collective_id):
    hbm = pl.BlockSpec(memory_space=pl.ANY)
    vmem = pl.BlockSpec(memory_space=pltpu.VMEM)
    rows, wide = h.shape
    units = wg.shape[1]
    every = NZ * NC * rows
    dma = pltpu.SemaphoreType.DMA
    shard = units // (ny * nx)
    down_scratch = []
    if with_down:
        sends = 2 * ((nx - 1) * 2 + 1 + nx + (nx - 1))
        down_scratch = [dma((NZ,)), dma((NZ,)), dma((sends,))]
        down_scratch += plane_scratch((shard, wide // 2), nx, ny)
        down_scratch += plane_scratch((shard, wide // 2), ny, nx)
    extra_shape, extra_specs, kept = (), (), every
    if with_down:
        kept = NZ * rows
        extra_shape = (
            jax.ShapeDtypeStruct((shard, wide), BF16),
            jax.ShapeDtypeStruct((kept, wide), BF16),
        )
        extra_specs = (vmem, hbm)
    return pl.pallas_call(
        lambda *refs: mlp_kernel(nx, with_down, *refs),
        name="mlp",
        out_shape=(
            jax.ShapeDtypeStruct((rows, wide), F32),
            jax.ShapeDtypeStruct((kept, wide), BF16),
            jax.ShapeDtypeStruct((wide, units), BF16),
            jax.ShapeDtypeStruct((wide, units), BF16),
            jax.ShapeDtypeStruct((units, wide), BF16),
        )
        + extra_shape,
        in_specs=[hbm] * 5,
        out_specs=(vmem, hbm, hbm, hbm, hbm) + extra_specs,
        scratch_shapes=[
            pltpu.VMEM((every, wide), BF16),
            pltpu.VMEM((every, wide), BF16),
            pltpu.VMEM((wide, units), BF16),
            pltpu.VMEM((wide, units), BF16),
            pltpu.VMEM((units, wide), BF16),
            pltpu.VMEM((every, units), BF16),
            pltpu.VMEM((every, units), BF16),
            pltpu.VMEM((every, units), BF16),
            pltpu.VMEM((every, wide), BF16),
            pltpu.VMEM((NZ, rows, wide), BF16),
            pltpu.VMEM((NZ - 1, rows, wide), BF16),
            pltpu.VMEM((NC, rows, wide), BF16),
            dma((4,)),
            dma((NZ, NC)),
            dma((NC,)),
            dma((3,)),
            dma((3,)),
            dma((NZ - 1,)),
            dma((NZ - 1,)),
            dma((NZ, NC)),
            dma((NZ,)),
            dma((NZ,)),
            dma((NZ,)),
            dma((NZ - 1,)),
        ]
        + down_scratch,
        compiler_params=pltpu.CompilerParams(
            collective_id=collective_id, has_side_effects=True, vmem_limit_bytes=63 << 20
        ),
    )(h, wg, wu, wd, cot)


def forward_kernel(nx, b_rows, names, *refs):
    r = types.SimpleNamespace(**dict(zip(names, refs)))
    y, z, x, c = place()
    other = 1 - c
    sib, ypeer = {"c": other}, {"y": 1 - y}
    xpeers = [(x + i + 1) % nx for i in range(nx - 1)]
    planes = [{"x": xp} for xp in xpeers] + [ypeer]
    cross = [{"z": (z + k + 1) % NZ, "c": other} for k in range(NZ - 1)]
    inner = (z > 0) & (z < NZ - 1)
    rows, wide = r.tok.shape
    shard = r.a.shape[0]
    key_width = r.kv_out.shape[1] // 2
    q_width = r.q_out.shape[1]
    qkv_width = q_width + 2 * key_width
    units = r.grad_d.shape[0]
    fs = units // (2 * nx)
    down_rows = r.d.shape[0]
    greet(line_peers(z, c) + cross + planes)
    ao, guo, co = r.ao, r.guo, r.co

    def down_at(yq, xq, cols):
        first = pl.multiple_of((yq * nx + xq) * down_rows, 8)
        return r.do.at[pl.ds(first, down_rows), cols]

    def remote_order(k):
        step = k + 1
        return (z + step // NC) % NZ, (c + step) % NC

    half = wide // 2
    parts = [pl.ds(0, half), pl.ds(half, half)]
    locals_ = [
        pltpu.make_async_copy(r.a, ao.at[y, z, x, c], r.s_local.at[0]),
        pltpu.make_async_copy(r.d, down_at(y, x, pl.ds(0, wide)), r.s_local.at[1]),
        pltpu.make_async_copy(r.tok, co.at[z, c], r.s_local.at[2]),
    ]
    for copy in locals_:
        copy.start()
    wires = Wires(r.send_sems)

    def both_ways(src, dst, sem):
        for peer in planes:
            wires.send(src, dst, sem, peer)

    def relay(ref, sem, peers):
        wires.arrived(ref, sem, sib)
        for peer in peers:
            wires.send(ref, ref, sem, peer)

    own_slot, own_sem = ao.at[y, z, x, c], r.ra.at[y, z, x, c]
    wires.send(r.a, own_slot, own_sem, {"z": jnp.minimum(z + 1, NZ - 1)}, lambda: z < NZ - 1)
    wires.send(r.a, own_slot, own_sem, {"z": jnp.maximum(z - 1, 0)}, lambda: z > 0)
    both_ways(r.a, own_slot, own_sem)
    wires.send(r.a, own_slot, own_sem, sib)
    line = LineGather(wires, r.tok, co, r.rc, z, c)

    def block(zq, cq):
        return pl.ds(pl.multiple_of((zq * NC + cq) * rows, rows), rows)

    hv = r.hv

    def send_own(i):
        here = hv.at[block(z, c)]
        device = (
            {"z": jnp.minimum(z + 1, NZ - 1)},
            {"z": jnp.maximum(z - 1, 0)},
            {"c": other},
        )[i]
        return remote(here, here, r.h_send.at[i], r.h_recv.at[z, c], device)

    def relay_attn(yq, xq, zq, peers):
        slot, sem = ao.at[yq, zq, xq, c], r.ra.at[yq, zq, xq, c]
        wires.arrived(slot, sem, sib)
        for peer in peers:
            wires.send(slot, slot, sem, peer)
        wires.send(slot, slot, sem, sib)

    def attention(gs, us, gu, weights, tail, first_in, qs, os, mid, s_in):
        loads = [
            pltpu.make_async_copy(r.g, gs, s_in.at[0]),
            pltpu.make_async_copy(r.u, us, s_in.at[1]),
        ]
        for copy in loads:
            copy.start()
        for m, (copy, ref) in enumerate(zip(loads, (gs, us))):
            copy.wait()
            for zq, cq, run, first in segments(nx, fs):
                gu[zq, cq, m, :, run : run + fs] = ref[:, first : first + fs]
        keep = pltpu.make_async_copy(gu.at[z, c], guo.at[:, y, z, x, c], r.s_local.at[3])
        keep.start()
        for k in range(NZ - 1):
            zq = line_order(z, k)
            slot, sem = ao.at[y, zq, x, c], r.ra.at[y, zq, x, c]
            wires.arrived(slot, sem, sib)
            onward = jnp.where(zq < z, jnp.minimum(z + 1, NZ - 1), jnp.maximum(z - 1, 0))
            wires.send(slot, slot, sem, {"z": onward}, lambda: inner)
            both_ways(slot, slot, sem)
            wires.send(slot, slot, sem, sib)
        mark = len(wires.started)
        for k in range(NZ * NC - 1):
            zp, cp = remote_order(k)
            wires.send(
                gu.at[zp, cp], guo.at[:, y, z, x, c], r.rt.at[z, c], {"z": zp, "c": cp}
            )
        block_sends = wires.started[mark:]
        del wires.started[mark:]
        line.begin()
        for zq in range(NZ):
            for xp in xpeers:
                relay_attn(y, xp, zq, [ypeer] if zq < NZ // 2 else [])
            relay_attn(1 - y, x, zq, planes[:-1] if zq >= NZ // 2 else [])
        both_ways(r.d.at[:, parts[0]], down_at(y, x, parts[0]), r.rd.at[0, y, x])
        for xp in xpeers:
            for zq in range(NZ):
                relay_attn(1 - y, xp, zq, [])
        locals_[0].wait()
        for yq in range(2):
            for zq in range(NZ):
                for xq in range(nx):
                    wires.arrived(ao.at[yq, zq, xq, other], r.ra.at[yq, zq, xq, other], sib)

        def fetch(first, width):
            return pltpu.make_async_copy(
                ao.at[:, :, :, :, :, pl.ds(first, width)],
                weights.at[:, :, :, :, :, pl.ds(0, width)],
                s_in.at[0],
            )

        tail_copy = pltpu.make_async_copy(
            ao.at[:, :, :, :, :, pl.ds(qkv_width + wide, HD)], tail, s_in.at[1]
        )
        tail_copy.start()
        fetch(0, qkv_width).start()
        x32 = r.x[...].astype(F32)
        tail_copy.wait()
        lane = lax.broadcasted_iota(jnp.int32, (16, HD), 1)
        row = lax.broadcasted_iota(jnp.int32, (16, HD), 0)
        pick = (lane == row).astype(F32).astype(BF16)
        flat_tail = tail[...].reshape(-1, HD)
        gains = dot_nt(pick, flat_tail)
        gain_one, gain_two = gains[0:1], gains[1:2]
        low = lax.broadcasted_iota(jnp.int32, (8, HD), 1) < HD // 2
        pieces = []
        tops = [
            tail[yq, zq, xq, cq, 0:8].astype(F32)
            for yq in range(2)
            for zq in range(NZ)
            for xq in range(nx)
            for cq in range(NC)
        ]
        for i in range(0, len(tops), 2):
            pieces.append(jnp.where(low, pltpu.roll(tops[i], HD // 2, 1), tops[i + 1])[0:1])
        bias = jnp.concatenate(pieces, axis=1)
        rescale = lax.rsqrt(jnp.mean(x32 * x32, axis=-1, keepdims=True) + EPS)
        first_in[...] = (x32 * rescale * gain_one).astype(BF16)
        fetch(0, qkv_width).wait()

        def turn(value):
            return value * r.turn_c[...] - pltpu.roll(value, HD // 2, 1) * r.turn_s[...]

        kv_own = pl.ds(pl.multiple_of(y * rows, rows), rows)
        pre = dot(first_in[...], weights[:, :, :, :, :, q_width:].reshape(wide, 2 * key_width))
        pre = pre + bias[:, q_width:]
        kv_heads = key_width // HD
        for i in range(2 * kv_heads):
            value = pre[:, i * HD : (i + 1) * HD]
            if i < kv_heads:
                value = turn(value)
            r.kvs[kv_own, i * HD : (i + 1) * HD] = value.astype(BF16)
        wires.send(r.kvs.at[kv_own], r.kvs.at[kv_own], r.s_kv, ypeer)
        pre = dot(first_in[...], weights[:, :, :, :, :, :q_width].reshape(wide, q_width))
        pre = pre + bias[:, :q_width]
        heads = q_width // HD
        for i in range(heads):
            cols = slice(i * HD, (i + 1) * HD)
            qs[:, cols] = turn(pre[:, cols]).astype(BF16)
        fetch(qkv_width, wide).start()
        for k in range(NZ * NC - 1):
            zp, cp = remote_order(k)
            wires.arrived(guo.at[:, y, zp, x, cp], r.rt.at[zp, cp], sib)
        keep.wait()
        for m in range(2):
            plane = guo.at[m, y, :, x]
            both_ways(plane, plane, r.rw.at[m, y, x])
        both_ways(r.d.at[:, parts[1]], down_at(y, x, parts[1]), r.rd.at[1, y, x])
        kv_other = r.kvs.at[pl.ds(pl.multiple_of((1 - y) * rows, rows), rows)]
        wires.arrived(kv_other, r.s_kv, ypeer)
        saves = [
            pltpu.make_async_copy(qs, r.q_out, s_in.at[1]),
            pltpu.make_async_copy(r.kvs, r.kv_out, s_in.at[2]),
            pltpu.make_async_copy(os, r.o_out, s_in.at[3]),
            pltpu.make_async_copy(mid, r.mid_out, s_in.at[4]),
        ]
        saves[0].start()
        saves[1].start()
        scale = HD ** (-0.5)
        group = heads // kv_heads
        for kv_head in range(kv_heads):
            k_cols = pl.ds(kv_head * HD, HD)
            v_cols = pl.ds(key_width + kv_head * HD, HD)

            def head(i, carry):
                cols = pl.ds(pl.multiple_of((kv_head * group + i) * HD, HD), HD)
                scores = dot_nt(qs[:, cols], r.kvs[:, k_cols]) * scale
                scores = jnp.where(r.mask[...] > 0, scores, MASKED)
                exponent = jnp.exp(scores - jnp.max(scores, axis=-1, keepdims=True))
                probs = exponent / jnp.sum(exponent, axis=-1, keepdims=True)
                os[:, cols] = dot(probs.astype(BF16), r.kvs[:, v_cols]).astype(BF16)
                return carry

            lax.fori_loop(0, group, head, 0)
            if kv_head == 0:
                line.event(0)
                for xp in xpeers:
                    relay(down_at(y, xp, parts[0]), r.rd.at[0, y, xp], [ypeer])
                relay(down_at(1 - y, x, parts[0]), r.rd.at[0, 1 - y, x], [])
        saves[2].start()
        fetch(qkv_width, wide).wait()
        for_out = weights[:, :, :, :, :, :wide].reshape(q_width, wide)
        middle = x32 + dot(os[...], for_out)
        mid[...] = middle
        saves[3].start()
        rescale_two = lax.rsqrt(jnp.mean(middle * middle, axis=-1, keepdims=True) + EPS)
        hv[block(z, c)] = (middle * rescale_two * gain_two).astype(BF16)
        pl.when(z < NZ - 1)(send_own(0).start)
        pl.when(z > 0)(send_own(1).start)
        send_own(2).start()
        wires.finish(block_sends)
        for copy in saves:
            copy.wait()

    block_shape = (shard, units)
    grid = (2, NZ, nx, NC)
    pl.run_scoped(
        attention,
        pltpu.VMEM(r.g.shape, BF16),
        pltpu.VMEM(r.u.shape, BF16),
        pltpu.VMEM((NZ, NC, 2) + block_shape, BF16),
        pltpu.VMEM(grid + (shard, qkv_width), BF16),
        pltpu.VMEM(grid + (shard, HD), BF16),
        pltpu.VMEM((rows, wide), BF16),
        pltpu.VMEM((rows, q_width), BF16),
        pltpu.VMEM((rows, q_width), BF16),
        pltpu.VMEM((rows, wide), F32),
        pltpu.SemaphoreType.DMA((5,)),
    )

    def feed_forward(cv, wgv, wuv, wdv, av, dgv, duv, part, ob, *half_own):
        line.event(1)
        for xp in xpeers:
            relay(guo.at[0, y, :, xp], r.rw.at[0, y, xp], [ypeer])
        relay(guo.at[1, 1 - y, :, x], r.rw.at[1, 1 - y, x], planes[:-1])
        for xp in xpeers:
            relay(down_at(y, xp, parts[1]), r.rd.at[1, y, xp], [])
        relay(down_at(1 - y, x, parts[1]), r.rd.at[1, 1 - y, x], planes[:-1])
        for copy in locals_[1:]:
            copy.wait()

        def load_cot(zq, cq):
            return pltpu.make_async_copy(co.at[zq, cq], cv.at[block(zq, cq)], r.s_cot.at[zq, cq])

        load_cot(z, c).start()
        line.sibling(z)
        load_cot(z, other).start()
        for xp in xpeers:
            relay(guo.at[1, y, :, xp], r.rw.at[1, y, xp], [])
        relay(guo.at[0, 1 - y, :, x], r.rw.at[0, 1 - y, x], [])
        for xp in xpeers:
            for h in range(2):
                relay(guo.at[h, 1 - y, :, xp], r.rw.at[h, 1 - y, xp], [])
                relay(down_at(1 - y, xp, parts[h]), r.rd.at[h, 1 - y, xp], [])
        loads = [
            pltpu.make_async_copy(guo.at[0], wgv, r.s_load.at[0]),
            pltpu.make_async_copy(guo.at[1], wuv, r.s_load.at[1]),
            pltpu.make_async_copy(r.do, wdv, r.s_load.at[2]),
        ]
        for copy in loads:
            copy.start()
        line.event(2)

        def arrival(zq, cq):
            here = hv.at[block(zq, cq)]
            return remote(here, here, r.h_send.at[0], r.h_recv.at[zq, cq], sib)

        def onward(k):
            zq = line_order(z, k)
            here = hv.at[block(zq, c)]
            device = {
                "z": jnp.where(zq < z, jnp.minimum(z + 1, NZ - 1), jnp.maximum(z - 1, 0))
            }
            return remote(here, here, r.h_on.at[k], r.h_recv.at[zq, c], device)

        def to_sibling(k):
            zq = line_order(z, k)
            here = hv.at[block(zq, c)]
            return remote(here, here, r.h_sib.at[k], r.h_recv.at[zq, c], sib)

        def take(k):
            arrival(line_order(z, k), c).wait_recv()
            pl.when(inner)(onward(k).start)
            to_sibling(k).start()

        def output(zq):
            here = pl.ds(pl.multiple_of(zq * rows, rows), rows)
            return pltpu.make_async_copy(ob.at[c], r.out_own.at[here], r.s_ob)

        def output_over(zq):
            here = pl.ds(pl.multiple_of(zq * rows, rows), rows)
            return remote(ob.at[other], r.out_sib.at[here], r.o_send.at[zq], r.o_recv.at[zq], sib)

        def partial_over(zq):
            return remote(
                part.at[block(zq, other)], r.sib.at[zq], r.p_send.at[zq], r.p_recv.at[zq], sib
            )

        def partial_home(zq):
            j = (z - zq + NZ) % NZ - 1
            return remote(
                part.at[block(zq, c)], r.ring.at[j], r.r_send.at[zq], r.r_recv.at[j], {"z": zq}
            )

        piece = rows // 8

        def combine(zq):
            remote(r.sib.at[zq], r.sib.at[zq], r.p_send.at[0], r.p_recv.at[zq], sib).wait_recv()

            def step(i, carry):
                here = pl.ds(pl.multiple_of((zq * NC + c) * rows + i * piece, piece), piece)
                there = pl.ds(pl.multiple_of(i * piece, piece), piece)
                total = part[here].astype(F32) + r.sib[zq, there].astype(F32)
                part[here] = total.astype(BF16)
                return carry

            lax.fori_loop(0, 8, step, 0)

        def place_of(k):
            far = jnp.where(k == 2, line_order(z, 1), line_order(z, 2))
            return jnp.where(k == 0, z, jnp.where(k == 1, line_order(z, 0), far))

        def flat(ref, low, high):
            return ref[:, :, :, :, :, low:high].reshape(wide, high - low)

        def pair(k, carry):
            zq = place_of(k)

            @pl.when(k == 0)
            def _():
                for i in range(NZ - 1):
                    near = line_order(z, i)
                    load_cot(near, c).start()
                    line.sibling(near)
                    load_cot(near, other).start()

            @pl.when(k == 1)
            def _():
                take(0)
                pl.when(inner)(lambda: take(1))

            @pl.when(k == 2)
            def _():
                pl.when(jnp.logical_not(inner))(lambda: take(1))
                pl.when(inner)(lambda: take(2))

            @pl.when((k == 3) & jnp.logical_not(inner))
            def _():
                take(2)

            def one(j, carry):
                cq = (c + j) % NC
                here = block(zq, cq)

                @pl.when((k == 0) & (j == 0))
                def _():
                    for copy in loads:
                        copy.wait()

                @pl.when(j == 1)
                def _():
                    arrival(zq, cq).wait_recv()

                load_cot(zq, cq).wait()
                for low, high in TILES:
                    high = units if high is None else high
                    gate = dot(hv[here], flat(wgv, low, high))
                    up = dot(hv[here], flat(wuv, low, high))
                    grad = dot_nt(cv[here], wdv[low:high])
                    sig = jax.nn.sigmoid(gate)
                    act = gate * sig
                    av[here, low:high] = (act * up).astype(BF16)
                    duv[here, low:high] = (grad * act).astype(BF16)
                    dgv[here, low:high] = (
                        grad * up * (sig * (1.0 + gate * (1.0 - sig)))
                    ).astype(BF16)

                @pl.when((k > 0) & (j == 0))
                def _():
                    output(zq).wait()

                @pl.when((k > 0) & (j == 1))
                def _():
                    output_over(place_of(k - 1)).wait_send()

                ob[cq] = dot(av[here], wdv[...]).astype(BF16)
                pl.when(j == 0)(output(zq).start)
                pl.when(j == 1)(output_over(zq).start)
                part[here] = (
                    dot_nt(dgv[here], flat(wgv, 0, units)) + dot_nt(duv[here], flat(wuv, 0, units))
                ).astype(BF16)
                return carry

            lax.fori_loop(0, NC, one, 0)
            partial_over(zq).start()

            @pl.when(k > 1)
            def _():
                before = place_of(k - 1)
                combine(before)
                partial_home(before).start()

            return carry

        lax.fori_loop(0, NZ, pair, 0)
        last = line_order(z, NZ - 2)
        step_d = wide // 6

        def down_grad(t, carry):
            cols = pl.ds(pl.multiple_of(t * step_d, step_d), step_d)
            wdv[:, cols] = dot_tn(av[...], cv[:, cols]).astype(BF16)

            @pl.when(t == 0)
            def _():
                combine(last)
                partial_home(last).start()

            return carry

        lax.fori_loop(0, 6, down_grad, 0)
        outs = [
            pltpu.make_async_copy(wdv, r.grad_d, r.s_out.at[0]),
            pltpu.make_async_copy(wgv, r.grad_g, r.s_out.at[1]),
            pltpu.make_async_copy(wuv, r.grad_u, r.s_out.at[2]),
        ]
        outs[0].start()

        def term(yq, xq, cols):
            first = pl.multiple_of((yq * nx + xq) * down_rows, 8)
            return r.grad_d.at[pl.ds(first, down_rows), cols]

        along_x, along_y = ("x", nx, x), ("y", 2, y)
        by_x = PlaneScatter(
            wires,
            lambda xq, yq: term(yq, xq, parts[0]),
            along_x,
            along_y,
            (r.xr1, half_own[0], r.xr2, r.xs1, r.xsl, r.xs2),
        )
        by_y = PlaneScatter(
            wires,
            lambda yq, xq: term(yq, xq, parts[1]),
            along_y,
            along_x,
            (r.yr1, half_own[1], r.yr2, r.ys1, r.ysl, r.ys2),
        )
        step_g = wide // NZ

        def turned(src, dst, first, last):
            def step(t, carry):
                cols = pl.ds(pl.multiple_of(t * step_g, step_g), step_g)
                value = dot_tn(hv[:, cols], src[...]).astype(BF16)
                here = pl.ds((t % 2) * (NZ // 2), NZ // 2)
                dst[t // 2, here] = value.reshape((NZ // 2, nx, NC, shard, units))
                return carry

            lax.fori_loop(first, last, step, 0)

        turned(dgv, wgv, 0, 1)
        outs[0].wait()
        by_x.begin()
        by_y.begin()
        turned(dgv, wgv, 1, NZ)
        outs[1].start()
        turned(duv, wuv, 0, NZ)
        outs[2].start()
        by_x.relay()
        by_y.relay()
        combine(z)
        for j in range(NZ - 1):
            here = r.ring.at[j]
            remote(here, here, r.r_send.at[0], r.r_recv.at[j], sib).wait_recv()

        def final(i, carry):
            here = pl.ds(pl.multiple_of((z * NC + c) * rows + i * piece, piece), piece)
            there = pl.ds(pl.multiple_of(i * piece, piece), piece)
            total = part[here].astype(F32)
            for j in range(NZ - 1):
                total = total + r.ring[j, there].astype(F32)
            r.dh[there] = total
            return carry

        lax.fori_loop(0, 8, final, 0)
        by_x.finish(r.down_out.at[:, parts[0]])
        by_y.finish(r.down_out.at[:, parts[1]])
        wires.finish()
        pl.when(z < NZ - 1)(send_own(0).wait_send)
        pl.when(z > 0)(send_own(1).wait_send)
        send_own(2).wait_send()
        for k in range(NZ - 1):
            pl.when(inner)(onward(k).wait_send)
            to_sibling(k).wait_send()
            partial_home(line_order(z, k)).wait_send()
        for zq in range(NZ):
            partial_over(zq).wait_send()
        output(last).wait()
        output_over(last).wait_send()
        for zq in range(NZ):
            there = r.out_sib.at[pl.ds(zq * rows, rows)]
            remote(there, there, r.o_send.at[0], r.o_recv.at[zq], sib).wait_recv()
        for copy in outs[1:]:
            copy.wait()

    every = NZ * NC * rows
    pl.run_scoped(
        feed_forward,
        pltpu.VMEM((every, wide), BF16),
        pltpu.VMEM(grid + block_shape, BF16),
        pltpu.VMEM(grid + block_shape, BF16),
        pltpu.VMEM((units, wide), BF16),
        pltpu.VMEM((every, units), BF16),
        pltpu.VMEM((every, units), BF16),
        pltpu.VMEM((every, units), BF16),
        pltpu.VMEM((every, wide), BF16),
        pltpu.VMEM((NC, rows, wide), BF16),
        pltpu.VMEM((2, down_rows, half), BF16),
        pltpu.VMEM((nx, down_rows, half), BF16),
    )


def forward(ny, nx, b_rows, a, g, u, d, tok, x, mask, turn_c, turn_s, widths, collective_id):
    hbm = pl.BlockSpec(memory_space=pl.ANY)
    vmem = pl.BlockSpec(memory_space=pltpu.VMEM)
    dma = pltpu.SemaphoreType.DMA
    rows, wide = tok.shape
    q_width, key_width = widths
    shard = a.shape[0]
    units = g.shape[1] // (NZ * NC)
    grid = (ny, NZ, nx, NC)
    half_slot = (d.shape[0], wide // 2)
    ins = dict(a=a, g=g, u=u, d=d, tok=tok, x=x, mask=mask, turn_c=turn_c, turn_s=turn_s)
    outs = dict(
        ao=(grid + a.shape, BF16),
        guo=((2,) + grid + (shard, units), BF16),
        do=((units, wide), BF16),
        co=((NZ, NC, rows, wide), BF16),
        q_out=((rows, q_width), BF16),
        kv_out=((2 * rows, 2 * key_width), BF16),
        o_out=((rows, q_width), BF16),
        mid_out=((rows, wide), F32),
        out_own=((NZ * rows, wide), BF16),
        out_sib=((NZ * rows, wide), BF16),
        grad_g=(grid + (shard, units), BF16),
        grad_u=(grid + (shard, units), BF16),
        grad_d=((units, wide), BF16),
        dh=((rows, wide), F32),
        down_out=(d.shape, BF16),
    )
    plane_x = plane_scratch(half_slot, nx, ny)
    plane_y = plane_scratch(half_slot, ny, nx)
    one_plane = (nx - 1) * 2 + 1 + nx + (nx - 1)
    sends = 3 + nx + 3 * (nx + 2) + 7 + 9 + 4 * (2 * nx - 1) + 4 * nx + 6 * nx
    scratch = dict(
        send_sems=dma((sends + 2 * one_plane + 24,)),
        s_local=dma((4,)),
        ra=dma(grid),
        rt=dma((NZ, NC)),
        rw=dma((2, ny, nx)),
        rd=dma((2, ny, nx)),
        rc=dma((NZ, NC)),
        s_kv=dma,
        kvs=pltpu.VMEM((2 * rows, 2 * key_width), BF16),
        hv=pltpu.VMEM((NZ * NC * rows, wide), BF16),
        sib=pltpu.VMEM((NZ, rows, wide), BF16),
        ring=pltpu.VMEM((NZ - 1, rows, wide), BF16),
        s_load=dma((3,)),
        s_cot=dma((NZ, NC)),
        s_ob=dma,
        s_out=dma((3,)),
        h_send=dma((3,)),
        h_on=dma((NZ - 1,)),
        h_sib=dma((NZ - 1,)),
        h_recv=dma((NZ, NC)),
        p_send=dma((NZ,)),
        p_recv=dma((NZ,)),
        r_send=dma((NZ,)),
        r_recv=dma((NZ - 1,)),
        o_send=dma((NZ,)),
        o_recv=dma((NZ,)),
        xr1=plane_x[0],
        xr2=plane_x[2],
        xs1=plane_x[3],
        xsl=plane_x[4],
        xs2=plane_x[5],
        yr1=plane_y[0],
        yr2=plane_y[2],
        ys1=plane_y[3],
        ysl=plane_y[4],
        ys2=plane_y[5],
    )
    names = tuple(ins) + tuple(outs) + tuple(scratch)
    results = pl.pallas_call(
        lambda *refs: forward_kernel(nx, b_rows, names, *refs),
        name="forward",
        out_shape=tuple(jax.ShapeDtypeStruct(*shape) for shape in outs.values()),
        in_specs=[hbm] * 5 + [vmem] * 4,
        out_specs=(hbm,) * 13 + (vmem,) * 2,
        scratch_shapes=list(scratch.values()),
        compiler_params=pltpu.CompilerParams(
            collective_id=collective_id, has_side_effects=True, vmem_limit_bytes=67_043_328
        ),
    )(*ins.values())
    return types.SimpleNamespace(**dict(zip(outs, results)))


def plane_peers(nx, y, x):
    return [{"x": (x + i + 1) % nx} for i in range(nx - 1)] + [{"y": 1 - y}]


def last_scatter_kernel(nx, widths, grads, gate, up, down, result, *rest):
    y, z, x, c = place()
    outs, rest = rest[: len(widths)], rest[len(widths) :]
    gate_out, up_out, down_out, result_out, rest = rest[:4] + (rest[4:],)
    send_sems, blocks, own, sib, line_sum, line_in = rest[:6]
    s_block, s_keep, s_own, s_sib, s_line = rest[6:11]
    half_x, half_y = rest[11:17], rest[17:23]
    gate_bufs, up_bufs, gu = rest[23:29], rest[29:35], rest[35]
    left_bufs, right_bufs, line_bufs = rest[36:42], rest[42:48], rest[48:56]
    cross = [{"z": (z + k + 1) % NZ, "c": 1 - c} for k in range(NZ - 1)]
    greet(line_peers(z, c) + cross + plane_peers(nx, y, x))
    wires = Wires(send_sems)
    along_x, along_y = ("x", nx, x), ("y", 2, y)
    gate_plane = PlaneScatter(
        wires, lambda xq, yq: gate.at[yq, :, xq], along_x, along_y, gate_bufs
    )
    up_plane = PlaneScatter(wires, lambda yq, xq: up.at[yq, :, xq], along_y, along_x, up_bufs)
    cols = down.shape[-1] // 2
    left, right = pl.ds(0, cols), pl.ds(cols, cols)
    left_plane = PlaneScatter(
        wires, lambda xq, yq: down.at[yq, xq, :, left], along_x, along_y, left_bufs
    )
    right_plane = PlaneScatter(
        wires, lambda yq, xq: down.at[yq, xq, :, right], along_y, along_x, right_bufs
    )
    line = LineScatter(wires, result, line_bufs, z, c)
    gate_plane.begin()
    up_plane.begin()
    line.begin()
    n = NZ // 2
    halves = [pl.ds(0, n), pl.ds(n, n)]

    def load(h, yq):
        return pltpu.make_async_copy(
            grads.at[yq, halves[h], :, c], own.at[yq, halves[h]], s_own.at[h, yq]
        )

    for h in range(2):
        for yq in range(2):
            wires.send(
                grads.at[yq, halves[h], :, 1 - c],
                sib.at[yq, halves[h]],
                s_sib.at[h, yq],
                {"c": 1 - c},
            )
            load(h, yq).start()

    def combine(h):
        for yq in range(2):
            load(h, yq).wait()
            wires.arrived(sib.at[yq, halves[h]], s_sib.at[h, yq], {"c": 1 - c})
            for i in range(n):
                zq = h * n + i
                total_into(own.at[yq, zq], [own.at[yq, zq], sib.at[yq, zq]])

    by_x = PlaneScatter(
        wires, lambda xq, yq: own.at[yq, halves[0], xq], along_x, along_y, half_x, True
    )
    by_y = PlaneScatter(
        wires, lambda yq, xq: own.at[yq, halves[1], xq], along_y, along_x, half_y, True
    )
    combine(0)
    by_x.begin()
    combine(1)
    by_y.begin()
    line.hop(3)
    left_plane.begin()
    right_plane.begin()
    line.hop(2)
    gate_plane.relay()
    up_plane.relay()
    line.hop(1)
    by_x.relay()
    by_y.relay()
    left_plane.relay()
    right_plane.relay()
    gate_plane.finish(gu.at[0])
    up_plane.finish(gu.at[1])
    keep = pltpu.make_async_copy(gu.at[:, z, c], blocks.at[z, c], s_keep)
    keep.start()
    for k in range(NZ * NC - 1):
        step = k + 1
        zp, cp = (z + step // NC) % NZ, (c + step) % NC
        wires.send(gu.at[:, zp, cp], blocks.at[z, c], s_block.at[z, c], {"z": zp, "c": cp})
    by_x.finish(line_sum.at[halves[0]])
    by_y.finish(line_sum.at[halves[1]])
    for k in range(NZ - 1):
        zp = (z + k + 1) % NZ
        wires.send(line_sum.at[zp], line_in.at[NZ - 2 - k], s_line.at[NZ - 2 - k], {"z": zp})
    line.finish(result_out)
    left_plane.finish(down_out.at[:, left])
    right_plane.finish(down_out.at[:, right])
    keep.wait()
    for k in range(NZ * NC - 1):
        step = k + 1
        zp, cp = (z + step // NC) % NZ, (c + step) % NC
        wires.arrived(blocks.at[zp, cp], s_block.at[zp, cp], {"c": 1 - c})
    fs = blocks.shape[-1] // (2 * nx)
    for m, out in enumerate((gate_out, up_out)):
        for zq, cq, run, first in segments(nx, fs):
            out[:, first : first + fs] = blocks[zq, cq, m, :, run : run + fs].astype(F32)
    for k in range(NZ - 1):
        wires.arrived(line_in.at[k], s_line.at[k], {"c": 1 - c})
    first = 0
    for out, width in zip(outs, widths):
        columns = slice(first, first + width)
        total = line_sum[z, :, columns].astype(F32)
        for k in range(NZ - 1):
            total = total + line_in[k, :, columns].astype(F32)
        out[...] = total
        first += width
    wires.finish()


def last_scatter(ny, nx, grads, widths, gate, up, down, result, collective_id):
    hbm = pl.BlockSpec(memory_space=pl.ANY)
    vmem = pl.BlockSpec(memory_space=pltpu.VMEM)
    rows, width = grads.shape[4:]
    block = gate.shape[4:]
    slot = (NZ // 2, rows, width)
    gate_slot = (NZ, NC) + block
    down_slot = (down.shape[2], down.shape[3] // 2)
    sends = 4 + 7 + NZ - 1 + 3 * ((nx - 1) * 2 + 1 + nx + (nx - 1)) + NZ + 2 * (NZ - 1)
    spread = block[1] * NZ * NC
    shapes = [(rows, w) for w in widths] + [(rows, spread)] * 2
    shapes += [down.shape[2:], result.shape[2:]]
    return pl.pallas_call(
        lambda *refs: last_scatter_kernel(nx, widths, *refs),
        name="last_scatter",
        out_shape=tuple(jax.ShapeDtypeStruct(shape, F32) for shape in shapes),
        in_specs=[hbm] * 5,
        out_specs=(vmem,) * len(shapes),
        scratch_shapes=[
            pltpu.SemaphoreType.DMA((sends,)),
            pltpu.VMEM((NZ, NC, 2) + block, BF16),
            pltpu.VMEM((ny, NZ, nx, rows, width), BF16),
            pltpu.VMEM((ny, NZ, nx, rows, width), BF16),
            pltpu.VMEM((NZ, rows, width), BF16),
            pltpu.VMEM((NZ - 1, rows, width), BF16),
            pltpu.SemaphoreType.DMA((NZ, NC)),
            pltpu.SemaphoreType.DMA,
            pltpu.SemaphoreType.DMA((2, 2)),
            pltpu.SemaphoreType.DMA((2, 2)),
            pltpu.SemaphoreType.DMA((NZ - 1,)),
        ]
        + plane_scratch(slot, nx, ny, True)
        + plane_scratch(slot, ny, nx, True)
        + plane_scratch(gate_slot, nx, ny)
        + plane_scratch(gate_slot, ny, nx)
        + [pltpu.VMEM((2,) + gate_slot, BF16)]
        + plane_scratch(down_slot, nx, ny)
        + plane_scratch(down_slot, ny, nx)
        + line_scratch(result.shape[2:]),
        compiler_params=pltpu.CompilerParams(
            collective_id=collective_id, has_side_effects=True, vmem_limit_bytes=60 << 20
        ),
    )(grads, gate, up, down, result)


def back_kernel(
    nx,
    key_width,
    b_rows,
    gate,
    up,
    ao,
    kept,
    given,
    mid,
    branch,
    tokens,
    gain,
    attn,
    query,
    kv,
    mask,
    turn_c,
    turn_s,
    gain_term,
    out_q,
    out_k,
    out_v,
    out_o,
    out_tail,
    out_gate,
    out_up,
    out_in,
    out_ring,
    send_sems,
    weights,
    term_o,
    term_q,
    sib_o,
    sib_q,
    line_sum,
    line_in,
    blocks,
    gu,
    d_attn,
    d_qkv,
    d_kv,
    kv_send,
    kv_recv,
    first_in,
    s_weights,
    s_sib,
    s_line,
    s_block,
    s_kv,
    result,
    s_result,
    s_ring,
    *bufs,
):
    y, z, x, c = place()
    sib = {"c": 1 - c}
    cross = [{"z": (z + k + 1) % NZ, "c": 1 - c} for k in range(NZ - 1)]
    greet(line_peers(z, c) + cross + plane_peers(nx, y, x))
    wires = Wires(send_sems)
    along_x, along_y = ("x", nx, x), ("y", 2, y)
    gate_plane = PlaneScatter(
        wires, lambda xq, yq: gate.at[yq, :, xq], along_x, along_y, bufs[0:6]
    )
    up_plane = PlaneScatter(wires, lambda yq, xq: up.at[yq, :, xq], along_y, along_x, bufs[6:12])
    gate_plane.begin()
    up_plane.begin()
    rows, wide = branch.shape
    q_width = query.shape[1]
    qkv_width = q_width + 2 * key_width
    heads, kv_heads = q_width // HD, key_width // HD
    n = NZ // 2
    halves = [pl.ds(0, n), pl.ds(n, n)]
    tile = n * nx * NC * out_q.shape[0]
    shard = out_q.shape[0]

    def fetch(first, width):
        return pltpu.make_async_copy(
            ao.at[:, :, pl.ds(first, width)], weights.at[:, :, pl.ds(0, width)], s_weights
        )

    fetch(qkv_width, wide).start()

    def fill(term, yq, h, first, value):
        value = value.reshape((n, nx, NC, shard, value.shape[1]))
        term[yq, halves[h], :, :, :, first : first + value.shape[4]] = value.astype(BF16)

    def over(i, term, other, yq, h):
        wires.send(
            term.at[yq, halves[h], :, 1 - c],
            other.at[yq, halves[h]],
            s_sib.at[i, yq, h],
            sib,
        )

    def combine(i, term, other):
        for h in range(2):
            for yq in range(2):
                here = other.at[yq, halves[h]]
                wires.arrived(here, s_sib.at[i, yq, h], sib)
                for zq in range(h * n, h * n + n):
                    for xq in range(nx):
                        mine = term.at[yq, zq, xq, c]
                        total_into(mine, [mine, other.at[yq, zq, xq]], True)

    def planes(term, first):
        return (
            PlaneScatter(
                wires,
                lambda xq, yq: term.at[yq, halves[0], xq, c],
                along_x,
                along_y,
                bufs[first : first + 6],
                True,
            ),
            PlaneScatter(
                wires,
                lambda yq, xq: term.at[yq, halves[1], xq, c],
                along_y,
                along_x,
                bufs[first + 6 : first + 12],
                True,
            ),
        )

    for yq in range(2):
        for h in range(2):
            i = yq * 2 + h
            fill(term_o, yq, h, 0, dot_tn(attn[:, i * tile : (i + 1) * tile], branch[...]))
            over(0, term_o, sib_o, yq, h)

    for i, k in enumerate((2, 0, 1)):
        zq = line_order(z, k)
        here = pl.ds(pl.multiple_of(zq * rows, rows), rows)
        loads = [
            pltpu.make_async_copy(kept.at[here], result.at[i], s_result.at[0]),
            pltpu.make_async_copy(given.at[here], first_in, s_result.at[1]),
        ]
        for copy in loads:
            copy.start()
        for copy in loads:
            copy.wait()
        total_into(result.at[i], [result.at[i], first_in])
        j = (z - zq + NZ) % NZ - 1
        wires.send(result.at[i], out_ring.at[j], s_ring.at[j], {"z": zq})

    fetch(qkv_width, wide).wait()
    for_out = weights[:, :, :wide].reshape(q_width, wide)
    d_attn[...] = dot_nt(branch[...], for_out).astype(BF16)
    fetch(0, qkv_width).start()
    d_kv[...] = jnp.zeros_like(d_kv)
    scale = HD ** (-0.5)

    def turn_back(value):
        return value * turn_c[...] + pltpu.roll(value, HD // 2, 1) * turn_s[...]

    group = heads // kv_heads
    for kv_head in range(kv_heads):
        k_cols = pl.ds(kv_head * HD, HD)
        v_cols = pl.ds(key_width + kv_head * HD, HD)

        def head(i, carry):
            cols = pl.ds(pl.multiple_of((kv_head * group + i) * HD, HD), HD)
            q_h, do_h = query[:, cols], d_attn[:, cols]
            scores = jnp.where(mask[...] > 0, dot_nt(q_h, kv[:, k_cols]) * scale, MASKED)
            exponent = jnp.exp(scores - jnp.max(scores, axis=-1, keepdims=True))
            probs = exponent / jnp.sum(exponent, axis=-1, keepdims=True)
            d_probs = dot_nt(do_h, kv[:, v_cols])
            inner = jnp.sum(probs * d_probs, axis=-1, keepdims=True)
            d_scores = (probs * (d_probs - inner)).astype(BF16)
            d_qkv[:, cols] = turn_back(dot(d_scores, kv[:, k_cols]) * scale).astype(BF16)
            d_kv[:, k_cols] += dot_tn(d_scores, q_h) * scale
            d_kv[:, v_cols] += dot_tn(probs.astype(BF16), do_h)
            return carry

        lax.fori_loop(0, group, head, 0)

    other_rows = pl.ds(pl.multiple_of((1 - y) * rows, rows), rows)
    own_rows = pl.ds(pl.multiple_of(y * rows, rows), rows)
    kv_send[...] = d_kv[other_rows].astype(BF16)
    gate_plane.relay()
    wires.send(kv_send, kv_recv, s_kv, {"y": 1 - y})
    up_plane.relay()
    combine(0, term_o, sib_o)
    o_planes = planes(term_o, 12)
    for plane in o_planes:
        plane.begin()
    x32 = tokens[...].astype(F32)
    rescale = lax.rsqrt(jnp.mean(x32 * x32, axis=-1, keepdims=True) + EPS)
    first_in[...] = (x32 * rescale * gain[...]).astype(BF16)
    wires.arrived(kv_recv, s_kv, {"y": 1 - y})
    for kv_head in range(2 * kv_heads):
        cols = pl.ds(kv_head * HD, HD)
        total = d_kv[own_rows, cols] + kv_recv[:, cols].astype(F32)
        if kv_head < kv_heads:
            total = turn_back(total)
        d_qkv[:, pl.ds(q_width + kv_head * HD, HD)] = total.astype(BF16)
    fetch(0, qkv_width).wait()
    for_in = weights[...].reshape(wide, qkv_width)
    d_first = dot_nt(d_qkv[...], for_in)
    normed = x32 * rescale
    scaled = d_first * gain[...]
    d_x = rescale * (scaled - normed * jnp.mean(scaled * normed, axis=-1, keepdims=True))
    out_in[...] = (mid[...] + d_x).astype(BF16)
    first_term = (d_first * normed).astype(BF16)
    lane = lax.broadcasted_iota(jnp.int32, (rows, HD), 1)
    pick_one = (lane == 0).astype(F32).astype(BF16)
    pick_two = (lane == 1).astype(F32).astype(BF16)
    bias_sum = jnp.sum(d_qkv[...].astype(F32), axis=0, keepdims=True)
    top = lax.broadcasted_iota(jnp.int32, (shard, HD), 0) == 0
    wide_bias = jnp.concatenate([bias_sum, bias_sum[:, :HD]], axis=1)
    for yq in range(2):
        for h in range(2):
            i = yq * 2 + h
            cols = slice(i * tile, (i + 1) * tile)
            fill(term_q, yq, h, 0, dot_tn(first_in[:, cols], d_qkv[...]))
            tail = dot_tn(first_term[:, cols], pick_one) + dot_tn(gain_term[:, cols], pick_two)
            for zi in range(n):
                for xq in range(nx):
                    for cq in range(NC):
                        part = ((zi * nx + xq) * NC + cq) * shard
                        place_at = i * (tile // shard) + (zi * nx + xq) * NC + cq
                        first = place_at * b_rows
                        base = (first // HD) * HD
                        bias = wide_bias[:, base : base + HD]
                        bias = pltpu.roll(
                            jnp.broadcast_to(bias, (8, HD)), (HD // 2 - (first - base)) % HD, 1
                        )[:1]
                        keep = lax.broadcasted_iota(jnp.int32, (shard, HD), 1) >= HD // 2
                        mixed = tail[part : part + shard] + jnp.where(top & keep, bias, 0.0)
                        term_q[yq, h * n + zi, xq, cq, :, qkv_width:] = mixed.astype(BF16)
            over(1, term_q, sib_q, yq, h)
    combine(1, term_q, sib_q)
    q_planes = planes(term_q, 24)
    for plane in q_planes:
        plane.begin()
    gate_plane.finish(gu.at[0])
    up_plane.finish(gu.at[1])
    keep_block = pltpu.make_async_copy(gu.at[:, z, c], blocks.at[z, c], s_block.at[z, c])
    keep_block.start()
    for k in range(NZ * NC - 1):
        step = k + 1
        zp, cp = (z + step // NC) % NZ, (c + step) % NC
        wires.send(gu.at[:, zp, cp], blocks.at[z, c], s_block.at[z, c], {"z": zp, "c": cp})
    for plane in o_planes:
        plane.relay()
    for plane in q_planes:
        plane.relay()

    def along_line(i, first, width, pair):
        cols = pl.ds(first, width)
        pair[0].finish(line_sum.at[halves[0], :, cols])
        pair[1].finish(line_sum.at[halves[1], :, cols])
        for k in range(NZ - 1):
            zp, j = (z + k + 1) % NZ, NZ - 2 - k
            wires.send(
                line_sum.at[zp, :, cols], line_in.at[j, :, cols], s_line.at[i, j], {"z": zp}
            )

    q_all = qkv_width + HD
    along_line(0, q_all, wide, o_planes)
    along_line(1, 0, q_all, q_planes)
    keep_block.wait()
    for k in range(NZ * NC - 1):
        step = k + 1
        zp, cp = (z + step // NC) % NZ, (c + step) % NC
        wires.arrived(blocks.at[zp, cp], s_block.at[zp, cp], sib)
    fs = blocks.shape[-1] // (2 * nx)
    for m, out in enumerate((out_gate, out_up)):
        for zq, cq, run, first in segments(nx, fs):
            out[:, first : first + fs] = blocks[zq, cq, m, :, run : run + fs]

    def last(i, out, first, width):
        if i is not None:
            begin, size = (q_all, wide) if i == 0 else (0, q_all)
            for j in range(NZ - 1):
                wires.arrived(line_in.at[j, :, pl.ds(begin, size)], s_line.at[i, j], sib)
        columns = slice(first, first + width)
        total = line_sum[z, :, columns].astype(F32)
        for j in range(NZ - 1):
            total = total + line_in[j, :, columns].astype(F32)
        out[...] = total

    last(0, out_o, q_all, wide)
    last(1, out_q, 0, q_width)
    last(None, out_k, q_width, key_width)
    last(None, out_v, q_width + key_width, key_width)
    last(None, out_tail, qkv_width, HD)
    for j in range(NZ - 1):
        wires.arrived(out_ring.at[j], s_ring.at[j], sib)
    wires.finish()


def back(ny, nx, b_rows, gate, up, ao, kept, given, args, collective_id):
    hbm = pl.BlockSpec(memory_space=pl.ANY)
    vmem = pl.BlockSpec(memory_space=pltpu.VMEM)
    mid, branch, tokens, gain, attn, query, kv, mask, turn_c, turn_s, gain_term = args
    dma = pltpu.SemaphoreType.DMA
    shard = ao.shape[1]
    block = gate.shape[4:]
    rows, wide = branch.shape
    q_width = query.shape[1]
    key_width = kv.shape[1] // 2
    qkv_width = q_width + 2 * key_width
    q_all = qkv_width + HD
    spread = block[1] * NZ * NC
    one_plane = (nx - 1) * 2 + 1 + nx + (nx - 1)
    sends = 3 * one_plane + 8 + 1 + 7 + 3 * (NZ - 1)
    slot_o, slot_q = (NZ // 2, shard, wide), (NZ // 2, shard, q_all)
    gate_slot = (NZ, NC) + block
    place_all = (ny, NZ, nx, NC, shard)
    shapes = [(shard, q_width), (shard, key_width), (shard, key_width), (shard, wide), (shard, HD)]
    return pl.pallas_call(
        lambda *refs: back_kernel(nx, key_width, b_rows, *refs),
        name="back",
        cost_estimate=pl.CostEstimate(
            flops=100_000_000_000, bytes_accessed=100_000_000, transcendentals=0
        ),
        out_shape=tuple(jax.ShapeDtypeStruct(shape, F32) for shape in shapes)
        + (jax.ShapeDtypeStruct((shard, spread), BF16),) * 2
        + (jax.ShapeDtypeStruct((rows, wide), BF16),)
        + (jax.ShapeDtypeStruct((NZ - 1, rows, wide), BF16),),
        in_specs=[hbm] * 5 + [vmem] * len(args),
        out_specs=(vmem,) * 8 + (hbm,),
        scratch_shapes=[
            dma((sends,)),
            pltpu.VMEM((ny * NZ * nx * NC, shard, qkv_width), BF16),
            pltpu.VMEM(place_all + (wide,), BF16),
            pltpu.VMEM(place_all + (q_all,), BF16),
            pltpu.VMEM((ny, NZ, nx, shard, wide), BF16),
            pltpu.VMEM((ny, NZ, nx, shard, q_all), BF16),
            pltpu.VMEM((NZ, shard, q_all + wide), BF16),
            pltpu.VMEM((NZ - 1, shard, q_all + wide), BF16),
            pltpu.VMEM((NZ, NC, 2) + block, BF16),
            pltpu.VMEM((2,) + gate_slot, BF16),
            pltpu.VMEM((rows, q_width), BF16),
            pltpu.VMEM((rows, qkv_width), BF16),
            pltpu.VMEM((2 * rows, 2 * key_width), F32),
            pltpu.VMEM((rows, 2 * key_width), BF16),
            pltpu.VMEM((rows, 2 * key_width), BF16),
            pltpu.VMEM((rows, wide), BF16),
            dma,
            dma((2, 2, 2)),
            dma((2, NZ - 1)),
            dma((NZ, NC)),
            dma,
            pltpu.VMEM((NZ - 1, rows, wide), BF16),
            dma((2,)),
            dma((NZ - 1,)),
        ]
        + plane_scratch(gate_slot, nx, ny)
        + plane_scratch(gate_slot, ny, nx)
        + plane_scratch(slot_o, nx, ny, True)
        + plane_scratch(slot_o, ny, nx, True)
        + plane_scratch(slot_q, nx, ny, True)
        + plane_scratch(slot_q, ny, nx, True),
        compiler_params=pltpu.CompilerParams(
            collective_id=collective_id, has_side_effects=True, vmem_limit_bytes=67_043_328
        ),
    )(gate, up, ao, kept, given, *args)


def make_body(ny, nx):
    def fused_layer(packed, x, seg_all, gate, up, down, grad_out, widths, b_rows):
        tok_rows = x.shape[0]
        length = seg_all.shape[0]
        seq_place = lax.axis_index("y")
        tok_pos = seq_place * tok_rows + jnp.arange(tok_rows)
        cos_tok, sin_tok = tables(tok_pos)
        all_pos = jnp.arange(length)
        seg_tok = lax.dynamic_slice(seg_all, (seq_place * tok_rows,), (tok_rows,))
        allowed = (tok_pos[:, None] >= all_pos[None, :]) & (seg_tok[:, None] == seg_all[None, :])
        mask = allowed.astype(F32)
        turn_c = jnp.concatenate([cos_tok, cos_tok], axis=1)
        turn_s = jnp.concatenate([sin_tok, -sin_tok], axis=1)
        made = forward(
            ny, nx, b_rows, packed, gate, up, down, grad_out, x, mask, turn_c, turn_s, widths, 0
        )
        lanes = sum(widths) + widths[1] + x.shape[1]
        tail = made.ao[..., lanes : lanes + 2].astype(F32).reshape(-1, 2)
        gain_one, gain_two = tail[:, 0], tail[:, 1]
        middle = made.mid_out
        rescale_two = lax.rsqrt(jnp.mean(middle * middle, axis=-1, keepdims=True) + EPS)
        normed_two = middle * rescale_two
        scaled = made.dh * gain_two
        grad_mid = grad_out.astype(F32) + rescale_two * (
            scaled - normed_two * jnp.mean(scaled * normed_two, axis=-1, keepdims=True)
        )
        args = (
            grad_mid,
            grad_mid.astype(BF16),
            x,
            gain_one[None],
            made.o_out,
            made.q_out,
            made.kv_out,
            mask,
            turn_c,
            turn_s,
            (made.dh * normed_two).astype(BF16),
        )
        outs = back(
            ny,
            nx,
            b_rows,
            made.grad_g,
            made.grad_u,
            made.ao.reshape((-1,) + packed.shape),
            made.out_own,
            made.out_sib,
            args,
            1,
        )
        grad_q, grad_k, grad_v, grad_o, tail_sum, grad_gate_w, grad_up_w, grad_in, ring = outs
        first_row = lax.axis_index("z") * tok_rows
        out_sum = jnp.sum(ring.astype(F32), axis=0)
        for half in (made.out_own, made.out_sib):
            out_sum += lax.dynamic_slice_in_dim(half, first_row, tok_rows).astype(F32)
        return (
            (middle + out_sum).astype(BF16)[None],
            grad_in[None],
            tail_sum[:, 0],
            grad_q,
            grad_k,
            grad_v,
            tail_sum[0, HD // 2 : HD // 2 + b_rows],
            grad_o,
            tail_sum[:, 1],
            grad_gate_w.astype(F32),
            grad_up_w.astype(F32),
            made.down_out.astype(F32),
        )

    def body(
        inputs,
        segment_ids,
        attn_gain,
        q_weight,
        k_weight,
        v_weight,
        qkv_bias,
        o_weight,
        mlp_gain,
        gate_weight,
        up_weight,
        down_weight,
        cotangent,
    ):
        tok_rows = inputs.shape[1]
        hidden_in = inputs[0].astype(F32)
        grad_out = cotangent[0]
        seg_all = segment_ids[0]
        length = seg_all.shape[0]
        seq_place = lax.axis_index("y")
        tok_pos = seq_place * tok_rows + jnp.arange(tok_rows)
        cos_tok, sin_tok = tables(tok_pos)
        query_width = q_weight.shape[1]
        key_width = k_weight.shape[1]
        kv_heads = key_width // HD
        q_heads = query_width // HD
        group = q_heads // kv_heads

        g_rows = attn_gain.shape[0]
        b_rows = qkv_bias.shape[0]
        qkv_width = query_width + 2 * key_width
        extra = jnp.concatenate(
            [
                attn_gain[:, None],
                mlp_gain[:, None],
                jnp.zeros((g_rows, HD // 2 - 2), BF16),
                jnp.broadcast_to(qkv_bias[None], (g_rows, b_rows)),
                jnp.zeros((g_rows, HD // 2 - b_rows), BF16),
            ],
            axis=1,
        )
        packed = jnp.concatenate([q_weight, k_weight, v_weight, o_weight, extra], axis=1)
        fused = g_rows % 16 == 0 and b_rows == HD // 2
        if fused:
            return fused_layer(
                packed,
                inputs[0],
                seg_all,
                gate_weight,
                up_weight,
                down_weight,
                grad_out,
                (query_width, key_width),
                b_rows,
            )
        attn_all, columns_all, down_all, grad_out_all = weight_gather(
            ny,
            nx,
            packed,
            gate_weight,
            up_weight,
            down_weight,
            grad_out,
            0,
        )
        full = attn_all.reshape(-1, packed.shape[1])
        full_qkv = full[:, :qkv_width]
        full_out = full[:, qkv_width : qkv_width + query_width]
        tail = attn_all[..., qkv_width + query_width :].astype(F32)
        gain_one = tail[..., 0].reshape(-1)
        gain_two = tail[..., 1].reshape(-1)
        bias = tail[..., 0, HD // 2 : HD // 2 + b_rows].reshape(-1)
        width = gate_weight.shape[1] // (NZ * NC)
        full_gate = columns_all[0].reshape(-1, width)
        full_up = columns_all[1].reshape(-1, width)
        full_down = down_all.reshape(width, -1)
        grad_out_all = grad_out_all.reshape(-1, grad_out.shape[1])

        rescale_one = lax.rsqrt(jnp.mean(hidden_in * hidden_in, axis=-1, keepdims=True) + EPS)
        normed_one = hidden_in * rescale_one
        input_one = (normed_one * gain_one).astype(BF16)
        qkv_pre = dot(input_one, full_qkv) + bias
        query = rotate(qkv_pre[:, :query_width], cos_tok, sin_tok).astype(BF16)
        key = rotate(qkv_pre[:, query_width : query_width + key_width], cos_tok, sin_tok)
        kv = jnp.concatenate([key, qkv_pre[:, query_width + key_width :]], axis=1).astype(BF16)
        kv_all = lax.all_gather(kv, "y", axis=0, tiled=True)
        key_heads = kv_all[:, :key_width].reshape(length, kv_heads, HD)
        value_heads = kv_all[:, key_width:].reshape(length, kv_heads, HD)
        query_heads = query.reshape(tok_rows, kv_heads, group, HD)
        score_scale = HD ** (-0.5)
        all_pos = jnp.arange(length)
        seg_tok = lax.dynamic_slice(seg_all, (seq_place * tok_rows,), (tok_rows,))
        allowed = (tok_pos[:, None] >= all_pos[None, :]) & (seg_tok[:, None] == seg_all[None, :])
        scores = (
            jnp.einsum("qkgd,pkd->kgqp", query_heads, key_heads, preferred_element_type=F32)
            * score_scale
        )
        masked = jnp.where(allowed[None, None], scores, MASKED)
        row_max = jnp.max(masked, axis=-1, keepdims=True)
        exponent = jnp.exp(masked - row_max)
        row_total = jnp.sum(exponent, axis=-1, keepdims=True)
        probs = exponent / row_total
        probs_low = probs.astype(BF16)
        mixture = jnp.einsum("kgqp,pkd->qkgd", probs_low, value_heads, preferred_element_type=F32)
        attn_tok = mixture.astype(BF16).reshape(tok_rows, query_width)
        middle = hidden_in + dot(attn_tok, full_out)

        rescale_two = lax.rsqrt(jnp.mean(middle * middle, axis=-1, keepdims=True) + EPS)
        normed_two = middle * rescale_two
        input_two = (normed_two * gain_two).astype(BF16)
        by_shard = (ny, NZ, nx, NC, g_rows, width)
        grad_input_two, out_part, part_gate, part_up, *downs = mlp(
            ny, nx, False, input_two, full_gate, full_up, full_down, grad_out_all, 1
        )
        grad_gain_two, grad_mid = norm_back(grad_input_two, normed_two, rescale_two, gain_two)
        grad_mid = grad_mid + grad_out.astype(F32)
        grad_branch = grad_mid.astype(BF16)
        grad_attn = dot_nt(grad_branch, full_out).astype(BF16)
        grad_heads = grad_attn.reshape(tok_rows, kv_heads, group, HD)
        grad_probs = jnp.einsum(
            "qkgd,pkd->kgqp", grad_heads, value_heads, preferred_element_type=F32
        )
        inner_sum = jnp.sum(probs * grad_probs, axis=-1, keepdims=True)
        grad_scores = (probs * (grad_probs - inner_sum)).astype(BF16)
        grad_query = (
            jnp.einsum("kgqp,pkd->qkgd", grad_scores, key_heads, preferred_element_type=F32)
            * score_scale
        ).reshape(tok_rows, query_width)
        grad_key = (
            jnp.einsum("kgqp,qkgd->pkd", grad_scores, query_heads, preferred_element_type=F32)
            * score_scale
        ).reshape(length, key_width)
        grad_value = jnp.einsum(
            "kgqp,qkgd->pkd", probs_low, grad_heads, preferred_element_type=F32
        ).reshape(length, key_width)
        grad_kv = jnp.concatenate([grad_key, grad_value], axis=1).astype(BF16)
        other = lax.dynamic_slice(
            grad_kv, ((1 - seq_place) * tok_rows, 0), (tok_rows, 2 * key_width)
        )
        own = lax.dynamic_slice(grad_kv, (seq_place * tok_rows, 0), (tok_rows, 2 * key_width))
        swapped = lax.ppermute(other, "y", [(0, 1), (1, 0)])
        grad_kv_tok = own.astype(F32) + swapped.astype(F32)
        grad_query_pre = rotate(grad_query, cos_tok, -sin_tok).astype(BF16)
        grad_key_pre = rotate(grad_kv_tok[:, :key_width], cos_tok, -sin_tok).astype(BF16)
        grad_value_pre = grad_kv_tok[:, key_width:].astype(BF16)
        grad_qkv = jnp.concatenate([grad_query_pre, grad_key_pre, grad_value_pre], axis=1)
        grad_qkv_sum = jnp.sum(grad_qkv.astype(F32), axis=0)
        grad_input_one = dot_nt(grad_qkv, full_qkv)
        grad_gain_one, grad_first = norm_back(grad_input_one, normed_one, rescale_one, gain_one)
        grad_total = grad_mid + grad_first
        shards = ny * NZ * nx * NC
        tail_grads = jnp.concatenate(
            [
                grad_gain_one[:, None],
                grad_gain_two[:, None],
                jnp.broadcast_to(
                    grad_qkv_sum.reshape(shards, 1, b_rows), (shards, g_rows, b_rows)
                ).reshape(-1, b_rows),
                jnp.zeros((shards * g_rows, HD - 2 - b_rows), F32),
            ],
            axis=1,
        )
        grad_attn_w = jnp.concatenate(
            [
                dot_tn(input_one, grad_qkv).astype(BF16),
                dot_tn(attn_tok, grad_branch).astype(BF16),
                tail_grads.astype(BF16),
            ],
            axis=1,
        )
        widths = (query_width, key_width, key_width, query_width, HD)
        pieces = (NZ, NC, tok_rows // 32, 32, hidden_in.shape[1])
        outs = last_scatter(
            ny,
            nx,
            grad_attn_w.reshape((ny, NZ, nx, NC, g_rows, -1)),
            widths,
            part_gate.reshape(by_shard),
            part_up.reshape(by_shard),
            downs[0].reshape((ny, nx) + down_weight.shape),
            out_part.reshape(pieces),
            3,
        )
        grad_q, grad_k, grad_v, grad_o, tail_sum = outs[:5]
        grad_gate_w, grad_up_w, grad_down_w, out_sum = outs[5:]
        output = (middle + out_sum.reshape(middle.shape)).astype(BF16)[None]
        return (
            output,
            grad_total.astype(BF16)[None],
            tail_sum[:, 0],
            grad_q,
            grad_k,
            grad_v,
            tail_sum[0, 2 : 2 + b_rows],
            grad_o,
            tail_sum[:, 1],
            grad_gate_w,
            grad_up_w,
            grad_down_w,
        )

    return body


def solution(mesh):
    ny = mesh.shape["seq"]
    nx = mesh.shape["fsdp"] // (NZ * NC)
    grid = Mesh(mesh.devices.reshape(ny, NZ, nx, NC), ALL)
    tokens = P(("z", "x", "c"), "y", None)
    rows = P(ALL, None)
    vec = P(ALL)
    return jax.shard_map(
        make_body(ny, nx),
        mesh=grid,
        in_specs=(
            tokens,
            P(("z", "x", "c"), None),
            vec,
            rows,
            rows,
            rows,
            vec,
            rows,
            vec,
            rows,
            rows,
            rows,
            tokens,
        ),
        out_specs=(tokens, tokens, vec, rows, rows, rows, vec, rows, vec, rows, rows, rows),
        check_vma=False,
    )
```

```python
import types

import jax
import jax.numpy as jnp
from jax import lax
from jax.experimental import pallas as pl
from jax.experimental.pallas import tpu as pltpu
from jax.sharding import Mesh, PartitionSpec as P

HD = 128
EPS = 1e-06
ROPE_BASE = 1000000.0
MASKED = -1e30
NZ = 4
NC = 2
ALL = ("y", "z", "x", "c")
TP = ("z", "c")
DP = ("y", "x")
F32 = jnp.float32
BF16 = jnp.bfloat16


def tables(positions):
    freq = ROPE_BASE ** (-jnp.arange(0, HD, 2).astype(F32) / HD)
    angle = positions.astype(F32)[:, None] * freq[None, :]
    return (jnp.cos(angle), jnp.sin(angle))


def rotate(values, cosine, sine):
    count = values.shape[0]
    split = values.reshape(count, -1, HD)
    half = HD // 2
    first = split[..., :half]
    second = split[..., half:]
    cos_b = cosine[:, None, :]
    sin_b = sine[:, None, :]
    turned = jnp.concatenate(
        [first * cos_b - second * sin_b, second * cos_b + first * sin_b], axis=-1
    )
    return turned.reshape(count, -1)


def dot(a, b):
    return jnp.dot(a, b, preferred_element_type=F32)


def dot_nt(a, b):
    return lax.dot_general(a, b, (((1,), (1,)), ((), ())), preferred_element_type=F32)


def dot_tn(a, b):
    return lax.dot_general(a, b, (((0,), (0,)), ((), ())), preferred_element_type=F32)


def norm_back(grad_normed, normed, rescale, gain_vec):
    grad_gain = jnp.sum(grad_normed * normed, axis=0)
    scaled = grad_normed * gain_vec
    grad_x = rescale * (scaled - normed * jnp.mean(scaled * normed, axis=-1, keepdims=True))
    return (grad_gain, grad_x)


class Wires:
    def __init__(self, sems):
        self.sems = sems
        self.used = 0
        self.started = []

    def send(self, src, dst, recv_sem, device, cond=None):
        copy = pltpu.make_async_remote_copy(
            src_ref=src,
            dst_ref=dst,
            send_sem=self.sems.at[self.used],
            recv_sem=recv_sem,
            device_id=device,
            device_id_type=pl.DeviceIdType.MESH,
        )
        if cond is None:
            copy.start()
        else:
            pl.when(cond())(copy.start)
        self.started.append((still(src), self.used, cond))
        self.used += 1

    def arrived(self, dst, recv_sem, device):
        pltpu.make_async_remote_copy(
            src_ref=dst,
            dst_ref=dst,
            send_sem=self.sems.at[0],
            recv_sem=recv_sem,
            device_id=device,
            device_id_type=pl.DeviceIdType.MESH,
        ).wait_recv()

    def finish(self, sent=None):
        for src, used, cond in self.started if sent is None else sent:
            sem = self.sems.at[used]
            src = taken(*src)
            copy = pltpu.make_async_remote_copy(
                src_ref=src,
                dst_ref=src,
                send_sem=sem,
                recv_sem=sem,
                device_id={"c": 1 - lax.axis_index("c")},
                device_id_type=pl.DeviceIdType.MESH,
            )
            if cond is None:
                copy.wait_send()
            else:
                pl.when(cond())(copy.wait_send)


def still(ref):
    steps = []
    for step in getattr(ref, "transforms", ()):
        steps.append([i.size if isinstance(i, pl.Slice) else None for i in step.indices])
    return getattr(ref, "ref", ref), steps


def taken(view, steps):
    for step in steps:
        view = view.at[tuple(0 if size is None else pl.ds(0, size) for size in step)]
    return view


def line_order(z, k):
    if k == 0:
        return z + 1 - 2 * (z % 2)
    if k == 1:
        return 2 - z // 2
    return 3 - 3 * (z // 2)


def greet(peers):
    barrier = pltpu.get_barrier_semaphore()
    for peer in peers:
        pl.semaphore_signal(
            barrier, inc=1, device_id=peer, device_id_type=pl.DeviceIdType.MESH
        )
    pl.semaphore_wait(barrier, len(peers))


def place():
    return tuple(lax.axis_index(name) for name in ALL)


def line_peers(z, c):
    peers = [{"c": 1 - c}]
    for k in range(NZ - 1):
        peers.append({"z": (z + k + 1) % NZ})
    return peers


class LineGather:
    def __init__(self, wires, own, out, recv, z, c):
        self.wires, self.own, self.out, self.recv, self.z, self.c = wires, own, out, recv, z, c

    def begin(self):
        w, z, c = self.wires, self.z, self.c
        dst, sem = self.out.at[z, c], self.recv.at[z, c]
        w.send(self.own, dst, sem, {"z": jnp.minimum(z + 1, NZ - 1)}, lambda: z < NZ - 1)
        w.send(self.own, dst, sem, {"z": jnp.maximum(z - 1, 0)}, lambda: z > 0)
        w.send(self.own, dst, sem, {"c": 1 - c})

    def event(self, k):
        w, z, c = self.wires, self.z, self.c
        zq = line_order(z, k)
        slot, sem = self.out.at[zq, c], self.recv.at[zq, c]
        w.arrived(slot, sem, {"c": 1 - c})
        onward = jnp.where(zq < z, jnp.minimum(z + 1, NZ - 1), jnp.maximum(z - 1, 0))
        w.send(slot, slot, sem, {"z": onward}, lambda: (z > 0) & (z < NZ - 1))
        w.send(slot, slot, sem, {"c": 1 - c})

    def sibling(self, zq):
        w, c = self.wires, self.c
        w.arrived(self.out.at[zq, 1 - c], self.recv.at[zq, 1 - c], {"c": 1 - c})


def segments(nx, fs):
    for yq in range(2):
        for zq in range(NZ):
            for xq in range(nx):
                for cq in range(NC):
                    first = (((yq * NZ + zq) * nx + xq) * NC + cq) * fs
                    yield zq, cq, (yq * nx + xq) * fs, first


def weight_gather_kernel(
    nx, a, g, u, d, tok, ao, guo, do, co, gu, send_sems, local_sems, ra, rt, rw, rd, rc
):
    y, z, x, c = place()
    sib = {"c": 1 - c}
    ypeer = {"y": 1 - y}
    xpeers = [(x + i + 1) % nx for i in range(nx - 1)]
    planes = [{"x": xp} for xp in xpeers] + [ypeer]
    cross = [{"z": (z + k + 1) % NZ, "c": 1 - c} for k in range(NZ - 1)]
    greet(line_peers(z, c) + cross + planes)
    locals_ = [
        pltpu.make_async_copy(a, ao.at[y, z, x, c], local_sems.at[0]),
        pltpu.make_async_copy(d, do.at[y, x], local_sems.at[1]),
        pltpu.make_async_copy(tok, co.at[z, c], local_sems.at[2]),
    ]
    keep = pltpu.make_async_copy(gu.at[z, c], guo.at[:, y, z, x, c], local_sems.at[3])
    for copy in locals_:
        copy.start()
    wires = Wires(send_sems)

    def both_ways(src, dst, sem):
        for peer in planes:
            wires.send(src, dst, sem, peer)

    own_slot, own_sem = ao.at[y, z, x, c], ra.at[y, z, x, c]
    wires.send(a, own_slot, own_sem, {"z": jnp.minimum(z + 1, NZ - 1)}, lambda: z < NZ - 1)
    wires.send(a, own_slot, own_sem, {"z": jnp.maximum(z - 1, 0)}, lambda: z > 0)
    both_ways(a, own_slot, own_sem)
    wires.send(a, own_slot, own_sem, sib)
    fs = gu.shape[-1] // (2 * nx)
    for m, shard in enumerate((g, u)):
        for zq, cq, run, first in segments(nx, fs):
            gu[zq, cq, m, :, run : run + fs] = shard[:, first : first + fs]
    keep.start()
    for k in range(NZ - 1):
        zq = line_order(z, k)
        slot, sem = ao.at[y, zq, x, c], ra.at[y, zq, x, c]
        wires.arrived(slot, sem, sib)
        onward = jnp.where(zq < z, jnp.minimum(z + 1, NZ - 1), jnp.maximum(z - 1, 0))
        wires.send(slot, slot, sem, {"z": onward}, lambda: (z > 0) & (z < NZ - 1))
        both_ways(slot, slot, sem)
        wires.send(slot, slot, sem, sib)

    for k in range(NZ * NC - 1):
        step = k + 1
        zp, cp = (z + step // NC) % NZ, (c + step) % NC
        wires.send(
            gu.at[zp, cp], guo.at[:, y, z, x, c], rt.at[z, c], {"z": zp, "c": cp}
        )
    line = LineGather(wires, tok, co, rc, z, c)
    line.begin()
    half = d.shape[1] // 2
    parts = [pl.ds(0, half), pl.ds(half, half)]
    for h in range(2):
        both_ways(d.at[:, parts[h]], do.at[y, x, :, parts[h]], rd.at[h, y, x])

    def relay_attn(yq, xq, zq, peers):
        slot, sem = ao.at[yq, zq, xq, c], ra.at[yq, zq, xq, c]
        wires.arrived(slot, sem, sib)
        for peer in peers:
            wires.send(slot, slot, sem, peer)
        wires.send(slot, slot, sem, sib)

    for zq in range(NZ):
        for xp in xpeers:
            relay_attn(y, xp, zq, [ypeer] if zq < NZ // 2 else [])
        relay_attn(1 - y, x, zq, planes[:-1] if zq >= NZ // 2 else [])

    for k in range(NZ * NC - 1):
        step = k + 1
        zp, cp = (z + step // NC) % NZ, (c + step) % NC
        wires.arrived(guo.at[:, y, zp, x, cp], rt.at[zp, cp], sib)
    keep.wait()
    for m in range(2):
        plane = guo.at[m, y, :, x]
        both_ways(plane, plane, rw.at[m, y, x])
    line.event(0)

    def relay(ref, sem, peers):
        wires.arrived(ref, sem, sib)
        for peer in peers:
            wires.send(ref, ref, sem, peer)

    for xp in xpeers:
        relay(do.at[y, xp, :, parts[0]], rd.at[0, y, xp], [ypeer])
        relay(do.at[y, xp, :, parts[1]], rd.at[1, y, xp], [])
    relay(do.at[1 - y, x, :, parts[1]], rd.at[1, 1 - y, x], planes[:-1])
    relay(do.at[1 - y, x, :, parts[0]], rd.at[0, 1 - y, x], [])
    for xp in xpeers:
        for zq in range(NZ):
            relay_attn(1 - y, xp, zq, [])
    line.event(1)
    for xp in xpeers:
        relay(guo.at[0, y, :, xp], rw.at[0, y, xp], [ypeer])
    relay(guo.at[1, 1 - y, :, x], rw.at[1, 1 - y, x], planes[:-1])
    line.event(2)
    for xp in xpeers:
        relay(guo.at[1, y, :, xp], rw.at[1, y, xp], [])
    relay(guo.at[0, 1 - y, :, x], rw.at[0, 1 - y, x], [])
    for xp in xpeers:
        for h in range(2):
            relay(do.at[1 - y, xp, :, parts[h]], rd.at[h, 1 - y, xp], [])
            relay(guo.at[h, 1 - y, :, xp], rw.at[h, 1 - y, xp], [])
    for zq in range(NZ):
        line.sibling(zq)
    for yq in range(2):
        for zq in range(NZ):
            for xq in range(nx):
                wires.arrived(ao.at[yq, zq, xq, 1 - c], ra.at[yq, zq, xq, 1 - c], sib)
    wires.finish()
    for copy in locals_:
        copy.wait()


def weight_gather(ny, nx, a, g, u, d, tok, collective_id):
    sends = 3 + (nx + 1) + 3 * (nx + 2)
    sends += 7 + 9 + 2 * nx
    sends += 4 * nx + 2 * (nx - 1) + 2 * (nx - 1)
    sends += 2 * nx + 2 * (nx - 1) + 4 * (nx - 1) + 2 * (nx - 1)
    hbm = pl.BlockSpec(memory_space=pl.ANY)
    vmem = pl.BlockSpec(memory_space=pltpu.VMEM)
    grid = (ny, NZ, nx, NC)
    block = g.shape[:1] + (g.shape[1] // (NZ * NC),)
    return pl.pallas_call(
        lambda *refs: weight_gather_kernel(nx, *refs),
        name="weight_gather",
        out_shape=(
            jax.ShapeDtypeStruct(grid + a.shape, BF16),
            jax.ShapeDtypeStruct((2,) + grid + block, BF16),
            jax.ShapeDtypeStruct((ny, nx) + d.shape, BF16),
            jax.ShapeDtypeStruct((NZ, NC) + tok.shape, BF16),
        ),
        in_specs=[hbm, vmem, vmem, hbm, hbm],
        out_specs=(hbm,) * 4,
        scratch_shapes=[
            pltpu.VMEM((NZ, NC, 2) + block, BF16),
            pltpu.SemaphoreType.DMA((sends + 16,)),
            pltpu.SemaphoreType.DMA((4,)),
            pltpu.SemaphoreType.DMA(grid),
            pltpu.SemaphoreType.DMA((NZ, NC)),
            pltpu.SemaphoreType.DMA((2, ny, nx)),
            pltpu.SemaphoreType.DMA((2, ny, nx)),
            pltpu.SemaphoreType.DMA((NZ, NC)),
        ],
        compiler_params=pltpu.CompilerParams(
            collective_id=collective_id, has_side_effects=True
        ),
    )(a, g, u, d, tok)


def total_into(dst, refs, flat=None):
    flat = len(dst.shape) == 2

    def entry(i, carry):
        here = (slice(None), pl.ds(pl.multiple_of(i * 128, 128), 128)) if flat else i
        total = refs[0][here].astype(F32)
        for ref in refs[1:]:
            total = total + ref[here].astype(F32)
        dst[here] = total.astype(dst.dtype)
        return carry

    lax.fori_loop(0, dst.shape[1] // 128 if flat else dst.shape[0], entry, 0)


class PlaneScatter:
    def __init__(self, wires, src, first, second, bufs, loaded=False):
        self.wires, self.src = wires, src
        self.name_a, self.size_a, self.a = first
        self.name_b, self.size_b, self.b = second
        self.r1, self.own, self.r2, self.s1, self.sl, self.s2 = bufs
        self.loaded = loaded

    def mine(self, b):
        return self.src(self.a, b) if self.loaded else self.own.at[b]

    def order(self):
        return [(self.b + i + 1) % self.size_b for i in range(self.size_b)]

    def begin(self):
        for b in self.order():
            for i in range(self.size_a - 1):
                peer, j = (self.a + i + 1) % self.size_a, self.size_a - 2 - i
                self.wires.send(
                    self.src(peer, b), self.r1.at[j, b], self.s1.at[j, b], {self.name_a: peer}
                )
            if not self.loaded:
                self.load(b).start()

    def load(self, b):
        return pltpu.make_async_copy(self.src(self.a, b), self.own.at[b], self.sl.at[b])

    def gathered(self, b):
        if not self.loaded:
            self.load(b).wait()
        for j in range(self.size_a - 1):
            self.wires.arrived(self.r1.at[j, b], self.s1.at[j, b], {self.name_a: self.a})
        return [self.mine(b)] + [self.r1.at[j, b] for j in range(self.size_a - 1)]

    def relay(self):
        for i, b in enumerate(self.order()[:-1]):
            j = self.size_b - 2 - i
            total_into(self.mine(b), self.gathered(b))
            self.wires.send(self.mine(b), self.r2.at[j], self.s2.at[j], {self.name_b: b})

    def finish(self, dst):
        refs = self.gathered(self.b)
        for j in range(self.size_b - 1):
            self.wires.arrived(self.r2.at[j], self.s2.at[j], {self.name_b: self.b})
            refs.append(self.r2.at[j])
        total_into(dst, refs)


def plane_scratch(slot, size_a, size_b, loaded=False):
    own = (1,) * (1 + len(slot)) if loaded else (size_b,) + slot
    return [
        pltpu.VMEM((size_a - 1, size_b) + slot, BF16),
        pltpu.VMEM(own, BF16),
        pltpu.VMEM((size_b - 1,) + slot, BF16),
        pltpu.SemaphoreType.DMA((size_a - 1, size_b)),
        pltpu.SemaphoreType.DMA((size_b,)),
        pltpu.SemaphoreType.DMA((size_b - 1,)),
    ]


class LineScatter:
    def __init__(self, wires, part, bufs, z, c):
        self.wires, self.part, self.z, self.c = wires, part, z, c
        self.own, self.sib, self.left, self.right = bufs[:4]
        self.s_own, self.s_sib, self.s_left, self.s_right = bufs[4:]

    def order(self):
        return [line_order(self.z, k) for k in (2, 1, 0)] + [self.z]

    def load(self, zq):
        return pltpu.make_async_copy(
            self.part.at[zq, self.c], self.own.at[zq], self.s_own.at[zq]
        )

    def begin(self):
        for zq in self.order():
            self.wires.send(
                self.part.at[zq, 1 - self.c],
                self.sib.at[zq],
                self.s_sib.at[zq],
                {"c": 1 - self.c},
            )
            self.load(zq).start()

    def ready(self, zq):
        self.load(zq).wait()
        self.wires.arrived(self.sib.at[zq], self.s_sib.at[zq], {"c": 1 - self.c})

    def hop(self, k):
        z = self.z
        for sign, buf, sems in ((1, self.left, self.s_left), (-1, self.right, self.s_right)):
            target = z + sign * k
            inside = (target < NZ) if sign > 0 else (target >= 0)
            behind = (z > 0) if sign > 0 else (z < NZ - 1)
            target = jnp.clip(target, 0, NZ - 1)
            own, sib = self.own.at[target], self.sib.at[target]

            @pl.when(inside)
            def _():
                self.ready(target)

            if k < NZ - 1:

                @pl.when(inside & behind)
                def _():
                    self.wires.arrived(buf.at[k], sems.at[k], {"z": z})
                    total_into(own, [own, sib, buf.at[k]])

                @pl.when(inside & jnp.logical_not(behind))
                def _():
                    total_into(own, [own, sib])

            else:

                @pl.when(inside)
                def _():
                    total_into(own, [own, sib])

            onward = jnp.clip(z + sign, 0, NZ - 1)
            self.wires.send(own, buf.at[k - 1], sems.at[k - 1], {"z": onward}, lambda: inside)

    def finish(self, dst):
        z = self.z
        self.ready(z)
        own, sib = self.own.at[z], self.sib.at[z]

        @pl.when(z > 0)
        def _():
            self.wires.arrived(self.left.at[0], self.s_left.at[0], {"z": z})

        @pl.when(z < NZ - 1)
        def _():
            self.wires.arrived(self.right.at[0], self.s_right.at[0], {"z": z})

        @pl.when(z == 0)
        def _():
            total_into(dst, [own, sib, self.right.at[0]])

        @pl.when(z == NZ - 1)
        def _():
            total_into(dst, [own, sib, self.left.at[0]])

        @pl.when((z > 0) & (z < NZ - 1))
        def _():
            total_into(dst, [own, sib, self.left.at[0], self.right.at[0]])


def line_scratch(slot):
    return [
        pltpu.VMEM((NZ,) + slot, BF16),
        pltpu.VMEM((NZ,) + slot, BF16),
        pltpu.VMEM((NZ - 1,) + slot, BF16),
        pltpu.VMEM((NZ - 1,) + slot, BF16),
        pltpu.SemaphoreType.DMA((NZ,)),
        pltpu.SemaphoreType.DMA((NZ,)),
        pltpu.SemaphoreType.DMA((NZ - 1,)),
        pltpu.SemaphoreType.DMA((NZ - 1,)),
    ]


TILES = ((0, 640), (640, None))


def remote(src, dst, send_sem, recv_sem, device):
    return pltpu.make_async_remote_copy(
        src_ref=src,
        dst_ref=dst,
        send_sem=send_sem,
        recv_sem=recv_sem,
        device_id=device,
        device_id_type=pl.DeviceIdType.MESH,
    )


def mlp_kernel(
    nx,
    with_down,
    h,
    wg,
    wu,
    wd,
    cot,
    dh,
    out_part,
    grad_g,
    grad_u,
    grad_d,
    *scratch,
):
    if with_down:
        down_out, out_sib, scratch = scratch[0], scratch[1], scratch[2:]
    (
        hv,
        cv,
        wgv,
        wuv,
        wdv,
        av,
        dgv,
        duv,
        part,
        sib,
        ring,
        ob,
        s_load,
        s_cot,
        s_ob,
        s_out,
        h_send,
        h_on,
        h_sib,
        h_recv,
        p_send,
        p_recv,
        r_send,
        r_recv,
    ) = scratch[: 24]
    scratch = scratch[24:]
    if with_down:
        o_send, o_recv, scratch = scratch[0], scratch[1], scratch[2:]
    y, z, x, c = place()
    rows, wide = h.shape
    units = wg.shape[1]
    other = 1 - c
    inner = (z > 0) & (z < NZ - 1)
    greet(line_peers(z, c) + (plane_peers(nx, y, x) if with_down else []))

    def block(zq, cq):
        return pl.ds(pl.multiple_of((zq * NC + cq) * rows, rows), rows)

    loads = [
        pltpu.make_async_copy(h, hv.at[block(z, c)], s_load.at[0]),
        pltpu.make_async_copy(wg, wgv, s_load.at[1]),
        pltpu.make_async_copy(wu, wuv, s_load.at[2]),
        pltpu.make_async_copy(wd, wdv, s_load.at[3]),
    ]

    def load_cot(zq, cq):
        return pltpu.make_async_copy(
            cot.at[block(zq, cq)], cv.at[block(zq, cq)], s_cot.at[zq, cq]
        )

    def send_own(i):
        there = hv.at[block(z, c)]
        device = (
            {"z": jnp.minimum(z + 1, NZ - 1)},
            {"z": jnp.maximum(z - 1, 0)},
            {"c": other},
        )[i]
        return remote(h, there, h_send.at[i], h_recv.at[z, c], device)

    pl.when(z < NZ - 1)(send_own(0).start)
    pl.when(z > 0)(send_own(1).start)
    send_own(2).start()
    for copy in loads[:3]:
        copy.start()
    load_cot(z, c).start()
    loads[3].start()
    load_cot(z, other).start()
    for k in range(NZ - 1):
        for i in range(NC):
            load_cot(line_order(z, k), (c + i) % NC).start()

    def arrival(zq, cq):
        here = hv.at[block(zq, cq)]
        return remote(here, here, h_send.at[0], h_recv.at[zq, cq], {"c": other})

    def onward(k):
        zq = line_order(z, k)
        here = hv.at[block(zq, c)]
        device = {"z": jnp.where(zq < z, jnp.minimum(z + 1, NZ - 1), jnp.maximum(z - 1, 0))}
        return remote(here, here, h_on.at[k], h_recv.at[zq, c], device)

    def to_sibling(k):
        zq = line_order(z, k)
        here = hv.at[block(zq, c)]
        return remote(here, here, h_sib.at[k], h_recv.at[zq, c], {"c": other})

    def take(k):
        arrival(line_order(z, k), c).wait_recv()
        pl.when(inner)(onward(k).start)
        to_sibling(k).start()

    def output(zq, cq):
        if with_down:
            here = pl.ds(pl.multiple_of(zq * rows, rows), rows)
            return pltpu.make_async_copy(ob.at[cq], out_part.at[here], s_ob.at[0])
        return pltpu.make_async_copy(ob.at[cq], out_part.at[block(zq, cq)], s_ob.at[cq])

    def output_over(zq):
        here = pl.ds(pl.multiple_of(zq * rows, rows), rows)
        return remote(
            ob.at[other], out_sib.at[here], o_send.at[zq], o_recv.at[zq], {"c": other}
        )

    def partial_over(zq):
        return remote(
            part.at[block(zq, other)], sib.at[zq], p_send.at[zq], p_recv.at[zq], {"c": other}
        )

    def partial_home(zq):
        j = (z - zq + NZ) % NZ - 1
        return remote(
            part.at[block(zq, c)], ring.at[j], r_send.at[zq], r_recv.at[j], {"z": zq}
        )

    piece = rows // 8

    def combine(zq):
        remote(sib.at[zq], sib.at[zq], p_send.at[0], p_recv.at[zq], {"c": other}).wait_recv()

        def step(i, carry):
            here = pl.ds(pl.multiple_of((zq * NC + c) * rows + i * piece, piece), piece)
            there = pl.ds(pl.multiple_of(i * piece, piece), piece)
            total = part[here].astype(F32) + sib[zq, there].astype(F32)
            part[here] = total.astype(BF16)
            return carry

        lax.fori_loop(0, 8, step, 0)

    def place_of(k):
        near = line_order(z, 0)
        mid = line_order(z, 1)
        far = line_order(z, 2)
        return jnp.where(k == 0, z, jnp.where(k == 1, near, jnp.where(k == 2, mid, far)))

    def pair(k, carry):
        zq = place_of(k)

        @pl.when(k == 1)
        def _():
            take(0)
            pl.when(inner)(lambda: take(1))

        @pl.when(k == 2)
        def _():
            pl.when(jnp.logical_not(inner))(lambda: take(1))
            pl.when(inner)(lambda: take(2))

        @pl.when((k == 3) & jnp.logical_not(inner))
        def _():
            take(2)

        def one(j, carry):
            cq = (c + j) % NC
            here = block(zq, cq)

            @pl.when((k == 0) & (j == 0))
            def _():
                for copy in loads:
                    copy.wait()

            @pl.when(j == 1)
            def _():
                arrival(zq, cq).wait_recv()

            load_cot(zq, cq).wait()
            for low, high in TILES:
                high = units if high is None else high
                gate = dot(hv[here], wgv[:, low:high])
                up = dot(hv[here], wuv[:, low:high])
                grad = dot_nt(cv[here], wdv[low:high])
                sig = jax.nn.sigmoid(gate)
                act = gate * sig
                av[here, low:high] = (act * up).astype(BF16)
                duv[here, low:high] = (grad * act).astype(BF16)
                dgv[here, low:high] = (
                    grad * up * (sig * (1.0 + gate * (1.0 - sig)))
                ).astype(BF16)

            if with_down:

                @pl.when((k > 0) & (j == 0))
                def _():
                    output(zq, cq).wait()

                @pl.when((k > 0) & (j == 1))
                def _():
                    output_over(place_of(k - 1)).wait_send()

            else:

                @pl.when(k > 0)
                def _():
                    output(zq, cq).wait()

            ob[cq] = dot(av[here], wdv[...]).astype(BF16)
            if with_down:
                pl.when(j == 0)(output(zq, cq).start)
                pl.when(j == 1)(output_over(zq).start)
            else:
                output(zq, cq).start()
            part[here] = (dot_nt(dgv[here], wgv[...]) + dot_nt(duv[here], wuv[...])).astype(BF16)
            return carry

        lax.fori_loop(0, NC, one, 0)
        partial_over(zq).start()

        @pl.when(k > 1)
        def _():
            before = place_of(k - 1)
            combine(before)
            partial_home(before).start()

        return carry

    lax.fori_loop(0, NZ, pair, 0)
    last = line_order(z, NZ - 2)
    step_d = wide // 6

    def down_grad(t, carry):
        cols = pl.ds(pl.multiple_of(t * step_d, step_d), step_d)
        wdv[:, cols] = dot_tn(av[...], cv[:, cols]).astype(BF16)

        @pl.when(t == 0)
        def _():
            combine(last)
            partial_home(last).start()

        return carry

    lax.fori_loop(0, 6, down_grad, 0)
    outs = [
        pltpu.make_async_copy(wdv, grad_d, s_out.at[0]),
        pltpu.make_async_copy(wgv, grad_g, s_out.at[1]),
        pltpu.make_async_copy(wuv, grad_u, s_out.at[2]),
    ]
    outs[0].start()
    if with_down:
        wires = Wires(scratch[0])
        half, shard = wide // 2, units // (2 * nx)
        left, right = pl.ds(0, half), pl.ds(half, half)

        def term(yq, xq, cols):
            first = (yq * nx + xq) * shard
            return grad_d.at[pl.ds(pl.multiple_of(first, 8), shard), cols]

        along_x, along_y = ("x", nx, x), ("y", 2, y)
        by_x = PlaneScatter(
            wires, lambda xq, yq: term(yq, xq, left), along_x, along_y, scratch[1:7]
        )
        by_y = PlaneScatter(
            wires, lambda yq, xq: term(yq, xq, right), along_y, along_x, scratch[7:13]
        )

    def turned(src, dst, first, last):
        def step(t, carry):
            cols = pl.ds(pl.multiple_of(t * step_d, step_d), step_d)
            dst[cols] = dot_tn(hv[:, cols], src[...]).astype(BF16)
            return carry

        lax.fori_loop(first, last, step, 0)

    turned(dgv, wgv, 0, 1)
    if with_down:
        outs[0].wait()
        by_x.begin()
        by_y.begin()
    turned(dgv, wgv, 1, 6)
    outs[1].start()
    turned(duv, wuv, 0, 6)
    outs[2].start()
    if with_down:
        by_x.relay()
        by_y.relay()
    combine(z)
    for j in range(NZ - 1):
        remote(ring.at[j], ring.at[j], r_send.at[0], r_recv.at[j], {"c": other}).wait_recv()

    def final(i, carry):
        here = pl.ds(pl.multiple_of((z * NC + c) * rows + i * piece, piece), piece)
        there = pl.ds(pl.multiple_of(i * piece, piece), piece)
        total = part[here].astype(F32)
        for j in range(NZ - 1):
            total = total + ring[j, there].astype(F32)
        dh[there] = total
        return carry

    lax.fori_loop(0, 8, final, 0)
    if with_down:
        by_x.finish(down_out.at[:, left])
        by_y.finish(down_out.at[:, right])
        wires.finish()
    pl.when(z < NZ - 1)(send_own(0).wait_send)
    pl.when(z > 0)(send_own(1).wait_send)
    send_own(2).wait_send()
    for k in range(NZ - 1):
        pl.when(inner)(onward(k).wait_send)
        to_sibling(k).wait_send()
        partial_home(line_order(z, k)).wait_send()
    for zq in range(NZ):
        partial_over(zq).wait_send()
    if with_down:
        output(z, c).wait()
        output_over(last).wait_send()
        for zq in range(NZ):
            there = out_sib.at[pl.ds(zq * rows, rows)]
            remote(there, there, o_send.at[0], o_recv.at[zq], {"c": other}).wait_recv()
    else:
        for cq in range(NC):
            output(z, cq).wait()
    for copy in outs[1 if with_down else 0 :]:
        copy.wait()


def mlp(ny, nx, with_down, h, wg, wu, wd, cot, collective_id):
    hbm = pl.BlockSpec(memory_space=pl.ANY)
    vmem = pl.BlockSpec(memory_space=pltpu.VMEM)
    rows, wide = h.shape
    units = wg.shape[1]
    every = NZ * NC * rows
    dma = pltpu.SemaphoreType.DMA
    shard = units // (ny * nx)
    down_scratch = []
    if with_down:
        sends = 2 * ((nx - 1) * 2 + 1 + nx + (nx - 1))
        down_scratch = [dma((NZ,)), dma((NZ,)), dma((sends,))]
        down_scratch += plane_scratch((shard, wide // 2), nx, ny)
        down_scratch += plane_scratch((shard, wide // 2), ny, nx)
    extra_shape, extra_specs, kept = (), (), every
    if with_down:
        kept = NZ * rows
        extra_shape = (
            jax.ShapeDtypeStruct((shard, wide), BF16),
            jax.ShapeDtypeStruct((kept, wide), BF16),
        )
        extra_specs = (vmem, hbm)
    return pl.pallas_call(
        lambda *refs: mlp_kernel(nx, with_down, *refs),
        name="mlp",
        out_shape=(
            jax.ShapeDtypeStruct((rows, wide), F32),
            jax.ShapeDtypeStruct((kept, wide), BF16),
            jax.ShapeDtypeStruct((wide, units), BF16),
            jax.ShapeDtypeStruct((wide, units), BF16),
            jax.ShapeDtypeStruct((units, wide), BF16),
        )
        + extra_shape,
        in_specs=[hbm] * 5,
        out_specs=(vmem, hbm, hbm, hbm, hbm) + extra_specs,
        scratch_shapes=[
            pltpu.VMEM((every, wide), BF16),
            pltpu.VMEM((every, wide), BF16),
            pltpu.VMEM((wide, units), BF16),
            pltpu.VMEM((wide, units), BF16),
            pltpu.VMEM((units, wide), BF16),
            pltpu.VMEM((every, units), BF16),
            pltpu.VMEM((every, units), BF16),
            pltpu.VMEM((every, units), BF16),
            pltpu.VMEM((every, wide), BF16),
            pltpu.VMEM((NZ, rows, wide), BF16),
            pltpu.VMEM((NZ - 1, rows, wide), BF16),
            pltpu.VMEM((NC, rows, wide), BF16),
            dma((4,)),
            dma((NZ, NC)),
            dma((NC,)),
            dma((3,)),
            dma((3,)),
            dma((NZ - 1,)),
            dma((NZ - 1,)),
            dma((NZ, NC)),
            dma((NZ,)),
            dma((NZ,)),
            dma((NZ,)),
            dma((NZ - 1,)),
        ]
        + down_scratch,
        compiler_params=pltpu.CompilerParams(
            collective_id=collective_id, has_side_effects=True, vmem_limit_bytes=63 << 20
        ),
    )(h, wg, wu, wd, cot)


def forward_kernel(nx, b_rows, names, *refs):
    r = types.SimpleNamespace(**dict(zip(names, refs)))
    y, z, x, c = place()
    other = 1 - c
    sib, ypeer = {"c": other}, {"y": 1 - y}
    xpeers = [(x + i + 1) % nx for i in range(nx - 1)]
    planes = [{"x": xp} for xp in xpeers] + [ypeer]
    cross = [{"z": (z + k + 1) % NZ, "c": other} for k in range(NZ - 1)]
    inner = (z > 0) & (z < NZ - 1)
    rows, wide = r.tok.shape
    shard = r.a.shape[0]
    key_width = r.kv_out.shape[1] // 2
    q_width = r.q_out.shape[1]
    qkv_width = q_width + 2 * key_width
    units = r.grad_d.shape[0]
    fs = units // (2 * nx)
    down_rows = r.d.shape[0]
    greet(line_peers(z, c) + cross + planes)
    ao, guo, co = r.ao, r.guo, r.co

    def down_at(yq, xq, cols):
        first = pl.multiple_of((yq * nx + xq) * down_rows, 8)
        return r.do.at[pl.ds(first, down_rows), cols]

    def remote_order(k):
        step = k + 1
        return (z + step // NC) % NZ, (c + step) % NC

    half = wide // 2
    parts = [pl.ds(0, half), pl.ds(half, half)]
    locals_ = [
        pltpu.make_async_copy(r.a, ao.at[y, z, x, c], r.s_local.at[0]),
        pltpu.make_async_copy(r.d, down_at(y, x, pl.ds(0, wide)), r.s_local.at[1]),
        pltpu.make_async_copy(r.tok, co.at[z, c], r.s_local.at[2]),
    ]
    for copy in locals_:
        copy.start()
    wires = Wires(r.send_sems)

    def both_ways(src, dst, sem):
        for peer in planes:
            wires.send(src, dst, sem, peer)

    def relay(ref, sem, peers):
        wires.arrived(ref, sem, sib)
        for peer in peers:
            wires.send(ref, ref, sem, peer)

    own_slot, own_sem = ao.at[y, z, x, c], r.ra.at[y, z, x, c]
    wires.send(r.a, own_slot, own_sem, {"z": jnp.minimum(z + 1, NZ - 1)}, lambda: z < NZ - 1)
    wires.send(r.a, own_slot, own_sem, {"z": jnp.maximum(z - 1, 0)}, lambda: z > 0)
    both_ways(r.a, own_slot, own_sem)
    wires.send(r.a, own_slot, own_sem, sib)
    line = LineGather(wires, r.tok, co, r.rc, z, c)

    def block(zq, cq):
        return pl.ds(pl.multiple_of((zq * NC + cq) * rows, rows), rows)

    hv = r.hv

    def send_own(i):
        here = hv.at[block(z, c)]
        device = (
            {"z": jnp.minimum(z + 1, NZ - 1)},
            {"z": jnp.maximum(z - 1, 0)},
            {"c": other},
        )[i]
        return remote(here, here, r.h_send.at[i], r.h_recv.at[z, c], device)

    def relay_attn(yq, xq, zq, peers):
        slot, sem = ao.at[yq, zq, xq, c], r.ra.at[yq, zq, xq, c]
        wires.arrived(slot, sem, sib)
        for peer in peers:
            wires.send(slot, slot, sem, peer)
        wires.send(slot, slot, sem, sib)

    def attention(gs, us, gu, weights, tail, first_in, qs, os, mid, s_in):
        loads = [
            pltpu.make_async_copy(r.g, gs, s_in.at[0]),
            pltpu.make_async_copy(r.u, us, s_in.at[1]),
        ]
        for copy in loads:
            copy.start()
        for m, (copy, ref) in enumerate(zip(loads, (gs, us))):
            copy.wait()
            for zq, cq, run, first in segments(nx, fs):
                gu[zq, cq, m, :, run : run + fs] = ref[:, first : first + fs]
        keep = pltpu.make_async_copy(gu.at[z, c], guo.at[:, y, z, x, c], r.s_local.at[3])
        keep.start()
        for k in range(NZ - 1):
            zq = line_order(z, k)
            slot, sem = ao.at[y, zq, x, c], r.ra.at[y, zq, x, c]
            wires.arrived(slot, sem, sib)
            onward = jnp.where(zq < z, jnp.minimum(z + 1, NZ - 1), jnp.maximum(z - 1, 0))
            wires.send(slot, slot, sem, {"z": onward}, lambda: inner)
            both_ways(slot, slot, sem)
            wires.send(slot, slot, sem, sib)
        mark = len(wires.started)
        for k in range(NZ * NC - 1):
            zp, cp = remote_order(k)
            wires.send(
                gu.at[zp, cp], guo.at[:, y, z, x, c], r.rt.at[z, c], {"z": zp, "c": cp}
            )
        block_sends = wires.started[mark:]
        del wires.started[mark:]
        line.begin()
        for zq in range(NZ):
            for xp in xpeers:
                relay_attn(y, xp, zq, [ypeer] if zq < NZ // 2 else [])
            relay_attn(1 - y, x, zq, planes[:-1] if zq >= NZ // 2 else [])
        for h in range(2):
            both_ways(r.d.at[:, parts[h]], down_at(y, x, parts[h]), r.rd.at[h, y, x])
        for xp in xpeers:
            for zq in range(NZ):
                relay_attn(1 - y, xp, zq, [])
        locals_[0].wait()
        for yq in range(2):
            for zq in range(NZ):
                for xq in range(nx):
                    wires.arrived(ao.at[yq, zq, xq, other], r.ra.at[yq, zq, xq, other], sib)

        def fetch(first, width):
            return pltpu.make_async_copy(
                ao.at[:, :, :, :, :, pl.ds(first, width)],
                weights.at[:, :, :, :, :, pl.ds(0, width)],
                s_in.at[0],
            )

        tail_copy = pltpu.make_async_copy(
            ao.at[:, :, :, :, :, pl.ds(qkv_width + wide, HD)], tail, s_in.at[1]
        )
        tail_copy.start()
        fetch(0, qkv_width).start()
        x32 = r.x[...].astype(F32)
        tail_copy.wait()
        lane = lax.broadcasted_iota(jnp.int32, (16, HD), 1)
        row = lax.broadcasted_iota(jnp.int32, (16, HD), 0)
        pick = (lane == row).astype(F32).astype(BF16)
        flat_tail = tail[...].reshape(-1, HD)
        gains = dot_nt(pick, flat_tail)
        gain_one, gain_two = gains[0:1], gains[1:2]
        low = lax.broadcasted_iota(jnp.int32, (8, HD), 1) < HD // 2
        pieces = []
        tops = [
            tail[yq, zq, xq, cq, 0:8].astype(F32)
            for yq in range(2)
            for zq in range(NZ)
            for xq in range(nx)
            for cq in range(NC)
        ]
        for i in range(0, len(tops), 2):
            pieces.append(jnp.where(low, pltpu.roll(tops[i], HD // 2, 1), tops[i + 1])[0:1])
        bias = jnp.concatenate(pieces, axis=1)
        rescale = lax.rsqrt(jnp.mean(x32 * x32, axis=-1, keepdims=True) + EPS)
        first_in[...] = (x32 * rescale * gain_one).astype(BF16)
        fetch(0, qkv_width).wait()

        def turn(value):
            return value * r.turn_c[...] - pltpu.roll(value, HD // 2, 1) * r.turn_s[...]

        kv_own = pl.ds(pl.multiple_of(y * rows, rows), rows)
        pre = dot(first_in[...], weights[:, :, :, :, :, q_width:].reshape(wide, 2 * key_width))
        pre = pre + bias[:, q_width:]
        kv_heads = key_width // HD
        for i in range(2 * kv_heads):
            value = pre[:, i * HD : (i + 1) * HD]
            if i < kv_heads:
                value = turn(value)
            r.kvs[kv_own, i * HD : (i + 1) * HD] = value.astype(BF16)
        wires.send(r.kvs.at[kv_own], r.kvs.at[kv_own], r.s_kv, ypeer)
        pre = dot(first_in[...], weights[:, :, :, :, :, :q_width].reshape(wide, q_width))
        pre = pre + bias[:, :q_width]
        heads = q_width // HD
        for i in range(heads):
            cols = slice(i * HD, (i + 1) * HD)
            qs[:, cols] = turn(pre[:, cols]).astype(BF16)
        fetch(qkv_width, wide).start()
        for k in range(NZ * NC - 1):
            zp, cp = remote_order(k)
            wires.arrived(guo.at[:, y, zp, x, cp], r.rt.at[zp, cp], sib)
        keep.wait()
        for m in range(2):
            plane = guo.at[m, y, :, x]
            both_ways(plane, plane, r.rw.at[m, y, x])
        kv_other = r.kvs.at[pl.ds(pl.multiple_of((1 - y) * rows, rows), rows)]
        wires.arrived(kv_other, r.s_kv, ypeer)
        saves = [
            pltpu.make_async_copy(qs, r.q_out, s_in.at[1]),
            pltpu.make_async_copy(r.kvs, r.kv_out, s_in.at[2]),
            pltpu.make_async_copy(os, r.o_out, s_in.at[3]),
            pltpu.make_async_copy(mid, r.mid_out, s_in.at[4]),
        ]
        saves[0].start()
        saves[1].start()
        scale = HD ** (-0.5)
        group = heads // kv_heads
        for kv_head in range(kv_heads):
            k_cols = pl.ds(kv_head * HD, HD)
            v_cols = pl.ds(key_width + kv_head * HD, HD)

            def head(i, carry):
                cols = pl.ds(pl.multiple_of((kv_head * group + i) * HD, HD), HD)
                scores = dot_nt(qs[:, cols], r.kvs[:, k_cols]) * scale
                scores = jnp.where(r.mask[...] > 0, scores, MASKED)
                exponent = jnp.exp(scores - jnp.max(scores, axis=-1, keepdims=True))
                probs = exponent / jnp.sum(exponent, axis=-1, keepdims=True)
                os[:, cols] = dot(probs.astype(BF16), r.kvs[:, v_cols]).astype(BF16)
                return carry

            lax.fori_loop(0, group, head, 0)
            if kv_head == 0:
                line.event(0)
                for xp in xpeers:
                    relay(down_at(y, xp, parts[0]), r.rd.at[0, y, xp], [ypeer])
                    relay(down_at(y, xp, parts[1]), r.rd.at[1, y, xp], [])
                relay(down_at(1 - y, x, parts[1]), r.rd.at[1, 1 - y, x], planes[:-1])
                relay(down_at(1 - y, x, parts[0]), r.rd.at[0, 1 - y, x], [])
        saves[2].start()
        fetch(qkv_width, wide).wait()
        for_out = weights[:, :, :, :, :, :wide].reshape(q_width, wide)
        middle = x32 + dot(os[...], for_out)
        mid[...] = middle
        saves[3].start()
        rescale_two = lax.rsqrt(jnp.mean(middle * middle, axis=-1, keepdims=True) + EPS)
        hv[block(z, c)] = (middle * rescale_two * gain_two).astype(BF16)
        pl.when(z < NZ - 1)(send_own(0).start)
        pl.when(z > 0)(send_own(1).start)
        send_own(2).start()
        wires.finish(block_sends)
        for copy in saves:
            copy.wait()

    block_shape = (shard, units)
    grid = (2, NZ, nx, NC)
    pl.run_scoped(
        attention,
        pltpu.VMEM(r.g.shape, BF16),
        pltpu.VMEM(r.u.shape, BF16),
        pltpu.VMEM((NZ, NC, 2) + block_shape, BF16),
        pltpu.VMEM(grid + (shard, qkv_width), BF16),
        pltpu.VMEM(grid + (shard, HD), BF16),
        pltpu.VMEM((rows, wide), BF16),
        pltpu.VMEM((rows, q_width), BF16),
        pltpu.VMEM((rows, q_width), BF16),
        pltpu.VMEM((rows, wide), F32),
        pltpu.SemaphoreType.DMA((5,)),
    )

    def feed_forward(cv, wgv, wuv, wdv, av, dgv, duv, part, ob, *half_own):
        def arrival(zq, cq):
            here = hv.at[block(zq, cq)]
            return remote(here, here, r.h_send.at[0], r.h_recv.at[zq, cq], sib)

        def onward(k):
            zq = line_order(z, k)
            here = hv.at[block(zq, c)]
            device = {
                "z": jnp.where(zq < z, jnp.minimum(z + 1, NZ - 1), jnp.maximum(z - 1, 0))
            }
            return remote(here, here, r.h_on.at[k], r.h_recv.at[zq, c], device)

        def to_sibling(k):
            zq = line_order(z, k)
            here = hv.at[block(zq, c)]
            return remote(here, here, r.h_sib.at[k], r.h_recv.at[zq, c], sib)

        def take(k):
            arrival(line_order(z, k), c).wait_recv()
            pl.when(inner)(onward(k).start)
            to_sibling(k).start()

        line.event(1)
        for xp in xpeers:
            relay(guo.at[0, y, :, xp], r.rw.at[0, y, xp], [ypeer])
        relay(guo.at[1, 1 - y, :, x], r.rw.at[1, 1 - y, x], planes[:-1])
        for copy in locals_[1:]:
            copy.wait()
        take(0)
        pl.when(inner)(lambda: take(1))

        def load_cot(zq, cq):
            return pltpu.make_async_copy(co.at[zq, cq], cv.at[block(zq, cq)], r.s_cot.at[zq, cq])

        load_cot(z, c).start()
        line.sibling(z)
        load_cot(z, other).start()
        for xp in xpeers:
            relay(guo.at[1, y, :, xp], r.rw.at[1, y, xp], [])
        relay(guo.at[0, 1 - y, :, x], r.rw.at[0, 1 - y, x], [])
        for xp in xpeers:
            for h in range(2):
                relay(guo.at[h, 1 - y, :, xp], r.rw.at[h, 1 - y, xp], [])
                relay(down_at(1 - y, xp, parts[h]), r.rd.at[h, 1 - y, xp], [])
        loads = [
            pltpu.make_async_copy(guo.at[0], wgv, r.s_load.at[0]),
            pltpu.make_async_copy(guo.at[1], wuv, r.s_load.at[1]),
            pltpu.make_async_copy(r.do, wdv, r.s_load.at[2]),
        ]
        for copy in loads:
            copy.start()
        line.event(2)

        def output(zq):
            here = pl.ds(pl.multiple_of(zq * rows, rows), rows)
            return pltpu.make_async_copy(ob.at[c], r.out_own.at[here], r.s_ob)

        def output_over(zq):
            here = pl.ds(pl.multiple_of(zq * rows, rows), rows)
            return remote(ob.at[other], r.out_sib.at[here], r.o_send.at[zq], r.o_recv.at[zq], sib)

        def partial_over(zq):
            return remote(
                part.at[block(zq, other)], r.sib.at[zq], r.p_send.at[zq], r.p_recv.at[zq], sib
            )

        def partial_home(zq):
            j = (z - zq + NZ) % NZ - 1
            return remote(
                part.at[block(zq, c)], r.ring.at[j], r.r_send.at[zq], r.r_recv.at[j], {"z": zq}
            )

        piece = rows // 8

        def combine(zq):
            remote(r.sib.at[zq], r.sib.at[zq], r.p_send.at[0], r.p_recv.at[zq], sib).wait_recv()

            def step(i, carry):
                here = pl.ds(pl.multiple_of((zq * NC + c) * rows + i * piece, piece), piece)
                there = pl.ds(pl.multiple_of(i * piece, piece), piece)
                total = part[here].astype(F32) + r.sib[zq, there].astype(F32)
                part[here] = total.astype(BF16)
                return carry

            lax.fori_loop(0, 8, step, 0)

        def place_of(k):
            late = jnp.where(k == 2, line_order(z, 2), line_order(z, 0))
            return jnp.where(k == 0, z, jnp.where(k == 1, line_order(z, 1), late))

        def flat(ref, low, high):
            return ref[:, :, :, :, :, low:high].reshape(wide, high - low)

        def pair(k, carry):
            zq = place_of(k)

            @pl.when(k == 0)
            def _():
                for i in range(NZ - 1):
                    near = line_order(z, i)
                    load_cot(near, c).start()
                    line.sibling(near)
                    load_cot(near, other).start()

            def one(j, carry):
                cq = (other + j) % NC
                here = block(zq, cq)

                @pl.when((k == 0) & (j == 0))
                def _():
                    for copy in loads:
                        copy.wait()

                @pl.when(j == 0)
                def _():
                    arrival(zq, cq).wait_recv()

                @pl.when((k == 0) & (j == 1))
                def _():
                    pl.when(jnp.logical_not(inner))(lambda: take(1))
                    pl.when(inner)(lambda: take(2))

                @pl.when((k == 1) & (j == 1) & jnp.logical_not(inner))
                def _():
                    take(2)

                load_cot(zq, cq).wait()
                for low, high in TILES:
                    high = units if high is None else high
                    gate = dot(hv[here], flat(wgv, low, high))
                    up = dot(hv[here], flat(wuv, low, high))
                    grad = dot_nt(cv[here], wdv[low:high])
                    sig = jax.nn.sigmoid(gate)
                    act = gate * sig
                    av[here, low:high] = (act * up).astype(BF16)
                    duv[here, low:high] = (grad * act).astype(BF16)
                    dgv[here, low:high] = (
                        grad * up * (sig * (1.0 + gate * (1.0 - sig)))
                    ).astype(BF16)

                @pl.when((k > 0) & (j == 1))
                def _():
                    output(zq).wait()

                @pl.when((k > 0) & (j == 0))
                def _():
                    output_over(place_of(k - 1)).wait_send()

                ob[cq] = dot(av[here], wdv[...]).astype(BF16)
                pl.when(j == 1)(output(zq).start)
                pl.when(j == 0)(output_over(zq).start)
                part[here] = (
                    dot_nt(dgv[here], flat(wgv, 0, units)) + dot_nt(duv[here], flat(wuv, 0, units))
                ).astype(BF16)
                pl.when(j == 0)(partial_over(zq).start)
                return carry

            lax.fori_loop(0, NC, one, 0)

            @pl.when(k > 0)
            def _():
                combine(zq)
                partial_home(zq).start()

            return carry

        lax.fori_loop(0, NZ, pair, 0)
        last = place_of(NZ - 1)
        step_d = wide // 6

        def down_grad(t, carry):
            cols = pl.ds(pl.multiple_of(t * step_d, step_d), step_d)
            wdv[:, cols] = dot_tn(av[...], cv[:, cols]).astype(BF16)
            return carry

        lax.fori_loop(0, 6, down_grad, 0)
        outs = [
            pltpu.make_async_copy(wdv, r.grad_d, r.s_out.at[0]),
            pltpu.make_async_copy(wgv, r.grad_g, r.s_out.at[1]),
            pltpu.make_async_copy(wuv, r.grad_u, r.s_out.at[2]),
        ]
        outs[0].start()

        def term(yq, xq, cols):
            first = pl.multiple_of((yq * nx + xq) * down_rows, 8)
            return r.grad_d.at[pl.ds(first, down_rows), cols]

        along_x, along_y = ("x", nx, x), ("y", 2, y)
        by_x = PlaneScatter(
            wires,
            lambda xq, yq: term(yq, xq, parts[0]),
            along_x,
            along_y,
            (r.xr1, half_own[0], r.xr2, r.xs1, r.xsl, r.xs2),
        )
        by_y = PlaneScatter(
            wires,
            lambda yq, xq: term(yq, xq, parts[1]),
            along_y,
            along_x,
            (r.yr1, half_own[1], r.yr2, r.ys1, r.ysl, r.ys2),
        )
        step_g = wide // NZ

        def turned(src, dst, first, last):
            def step(t, carry):
                cols = pl.ds(pl.multiple_of(t * step_g, step_g), step_g)
                value = dot_tn(hv[:, cols], src[...]).astype(BF16)
                here = pl.ds((t % 2) * (NZ // 2), NZ // 2)
                dst[t // 2, here] = value.reshape((NZ // 2, nx, NC, shard, units))
                return carry

            lax.fori_loop(first, last, step, 0)

        turned(dgv, wgv, 0, 1)
        outs[0].wait()
        by_x.begin()
        by_y.begin()
        turned(dgv, wgv, 1, NZ)
        outs[1].start()
        turned(duv, wuv, 0, NZ // 2)
        by_x.relay()
        by_y.relay()
        turned(duv, wuv, NZ // 2, NZ)
        outs[2].start()
        combine(z)
        for j in range(NZ - 1):
            here = r.ring.at[j]
            remote(here, here, r.r_send.at[0], r.r_recv.at[j], sib).wait_recv()

        def final(i, carry):
            here = pl.ds(pl.multiple_of((z * NC + c) * rows + i * piece, piece), piece)
            there = pl.ds(pl.multiple_of(i * piece, piece), piece)
            total = part[here].astype(F32)
            for j in range(NZ - 1):
                total = total + r.ring[j, there].astype(F32)
            r.dh[there] = total
            return carry

        lax.fori_loop(0, 8, final, 0)
        by_x.finish(r.down_out.at[:, parts[0]])
        by_y.finish(r.down_out.at[:, parts[1]])
        wires.finish()
        pl.when(z < NZ - 1)(send_own(0).wait_send)
        pl.when(z > 0)(send_own(1).wait_send)
        send_own(2).wait_send()
        for k in range(NZ - 1):
            pl.when(inner)(onward(k).wait_send)
            to_sibling(k).wait_send()
            partial_home(line_order(z, k)).wait_send()
        for zq in range(NZ):
            partial_over(zq).wait_send()
        output(last).wait()
        output_over(last).wait_send()
        for zq in range(NZ):
            there = r.out_sib.at[pl.ds(zq * rows, rows)]
            remote(there, there, r.o_send.at[0], r.o_recv.at[zq], sib).wait_recv()
        for copy in outs[1:]:
            copy.wait()

    every = NZ * NC * rows
    pl.run_scoped(
        feed_forward,
        pltpu.VMEM((every, wide), BF16),
        pltpu.VMEM(grid + block_shape, BF16),
        pltpu.VMEM(grid + block_shape, BF16),
        pltpu.VMEM((units, wide), BF16),
        pltpu.VMEM((every, units), BF16),
        pltpu.VMEM((every, units), BF16),
        pltpu.VMEM((every, units), BF16),
        pltpu.VMEM((every, wide), BF16),
        pltpu.VMEM((NC, rows, wide), BF16),
        pltpu.VMEM((2, down_rows, half), BF16),
        pltpu.VMEM((nx, down_rows, half), BF16),
    )


def forward(ny, nx, b_rows, a, g, u, d, tok, x, mask, turn_c, turn_s, widths, collective_id):
    hbm = pl.BlockSpec(memory_space=pl.ANY)
    vmem = pl.BlockSpec(memory_space=pltpu.VMEM)
    dma = pltpu.SemaphoreType.DMA
    rows, wide = tok.shape
    q_width, key_width = widths
    shard = a.shape[0]
    units = g.shape[1] // (NZ * NC)
    grid = (ny, NZ, nx, NC)
    half_slot = (d.shape[0], wide // 2)
    ins = dict(a=a, g=g, u=u, d=d, tok=tok, x=x, mask=mask, turn_c=turn_c, turn_s=turn_s)
    outs = dict(
        ao=(grid + a.shape, BF16),
        guo=((2,) + grid + (shard, units), BF16),
        do=((units, wide), BF16),
        co=((NZ, NC, rows, wide), BF16),
        q_out=((rows, q_width), BF16),
        kv_out=((2 * rows, 2 * key_width), BF16),
        o_out=((rows, q_width), BF16),
        mid_out=((rows, wide), F32),
        out_own=((NZ * rows, wide), BF16),
        out_sib=((NZ * rows, wide), BF16),
        grad_g=(grid + (shard, units), BF16),
        grad_u=(grid + (shard, units), BF16),
        grad_d=((units, wide), BF16),
        dh=((rows, wide), F32),
        down_out=(d.shape, BF16),
    )
    plane_x = plane_scratch(half_slot, nx, ny)
    plane_y = plane_scratch(half_slot, ny, nx)
    one_plane = (nx - 1) * 2 + 1 + nx + (nx - 1)
    sends = 3 + nx + 3 * (nx + 2) + 7 + 9 + 4 * (2 * nx - 1) + 4 * nx + 6 * nx
    scratch = dict(
        send_sems=dma((sends + 2 * one_plane + 24,)),
        s_local=dma((4,)),
        ra=dma(grid),
        rt=dma((NZ, NC)),
        rw=dma((2, ny, nx)),
        rd=dma((2, ny, nx)),
        rc=dma((NZ, NC)),
        s_kv=dma,
        kvs=pltpu.VMEM((2 * rows, 2 * key_width), BF16),
        hv=pltpu.VMEM((NZ * NC * rows, wide), BF16),
        sib=pltpu.VMEM((NZ, rows, wide), BF16),
        ring=pltpu.VMEM((NZ - 1, rows, wide), BF16),
        s_load=dma((3,)),
        s_cot=dma((NZ, NC)),
        s_ob=dma,
        s_out=dma((3,)),
        h_send=dma((3,)),
        h_on=dma((NZ - 1,)),
        h_sib=dma((NZ - 1,)),
        h_recv=dma((NZ, NC)),
        p_send=dma((NZ,)),
        p_recv=dma((NZ,)),
        r_send=dma((NZ,)),
        r_recv=dma((NZ - 1,)),
        o_send=dma((NZ,)),
        o_recv=dma((NZ,)),
        xr1=plane_x[0],
        xr2=plane_x[2],
        xs1=plane_x[3],
        xsl=plane_x[4],
        xs2=plane_x[5],
        yr1=plane_y[0],
        yr2=plane_y[2],
        ys1=plane_y[3],
        ysl=plane_y[4],
        ys2=plane_y[5],
    )
    names = tuple(ins) + tuple(outs) + tuple(scratch)
    results = pl.pallas_call(
        lambda *refs: forward_kernel(nx, b_rows, names, *refs),
        name="forward",
        out_shape=tuple(jax.ShapeDtypeStruct(*shape) for shape in outs.values()),
        in_specs=[hbm] * 5 + [vmem] * 4,
        out_specs=(hbm,) * 13 + (vmem,) * 2,
        scratch_shapes=list(scratch.values()),
        compiler_params=pltpu.CompilerParams(
            collective_id=collective_id, has_side_effects=True, vmem_limit_bytes=67_043_328
        ),
    )(*ins.values())
    return types.SimpleNamespace(**dict(zip(outs, results)))


def plane_peers(nx, y, x):
    return [{"x": (x + i + 1) % nx} for i in range(nx - 1)] + [{"y": 1 - y}]


def last_scatter_kernel(nx, widths, grads, gate, up, down, result, *rest):
    y, z, x, c = place()
    outs, rest = rest[: len(widths)], rest[len(widths) :]
    gate_out, up_out, down_out, result_out, rest = rest[:4] + (rest[4:],)
    send_sems, blocks, own, sib, line_sum, line_in = rest[:6]
    s_block, s_keep, s_own, s_sib, s_line = rest[6:11]
    half_x, half_y = rest[11:17], rest[17:23]
    gate_bufs, up_bufs, gu = rest[23:29], rest[29:35], rest[35]
    left_bufs, right_bufs, line_bufs = rest[36:42], rest[42:48], rest[48:56]
    cross = [{"z": (z + k + 1) % NZ, "c": 1 - c} for k in range(NZ - 1)]
    greet(line_peers(z, c) + cross + plane_peers(nx, y, x))
    wires = Wires(send_sems)
    along_x, along_y = ("x", nx, x), ("y", 2, y)
    gate_plane = PlaneScatter(
        wires, lambda xq, yq: gate.at[yq, :, xq], along_x, along_y, gate_bufs
    )
    up_plane = PlaneScatter(wires, lambda yq, xq: up.at[yq, :, xq], along_y, along_x, up_bufs)
    cols = down.shape[-1] // 2
    left, right = pl.ds(0, cols), pl.ds(cols, cols)
    left_plane = PlaneScatter(
        wires, lambda xq, yq: down.at[yq, xq, :, left], along_x, along_y, left_bufs
    )
    right_plane = PlaneScatter(
        wires, lambda yq, xq: down.at[yq, xq, :, right], along_y, along_x, right_bufs
    )
    line = LineScatter(wires, result, line_bufs, z, c)
    gate_plane.begin()
    up_plane.begin()
    line.begin()
    n = NZ // 2
    halves = [pl.ds(0, n), pl.ds(n, n)]

    def load(h, yq):
        return pltpu.make_async_copy(
            grads.at[yq, halves[h], :, c], own.at[yq, halves[h]], s_own.at[h, yq]
        )

    for h in range(2):
        for yq in range(2):
            wires.send(
                grads.at[yq, halves[h], :, 1 - c],
                sib.at[yq, halves[h]],
                s_sib.at[h, yq],
                {"c": 1 - c},
            )
            load(h, yq).start()

    def combine(h):
        for yq in range(2):
            load(h, yq).wait()
            wires.arrived(sib.at[yq, halves[h]], s_sib.at[h, yq], {"c": 1 - c})
            for i in range(n):
                zq = h * n + i
                total_into(own.at[yq, zq], [own.at[yq, zq], sib.at[yq, zq]])

    by_x = PlaneScatter(
        wires, lambda xq, yq: own.at[yq, halves[0], xq], along_x, along_y, half_x, True
    )
    by_y = PlaneScatter(
        wires, lambda yq, xq: own.at[yq, halves[1], xq], along_y, along_x, half_y, True
    )
    combine(0)
    by_x.begin()
    combine(1)
    by_y.begin()
    line.hop(3)
    left_plane.begin()
    right_plane.begin()
    line.hop(2)
    gate_plane.relay()
    up_plane.relay()
    line.hop(1)
    by_x.relay()
    by_y.relay()
    left_plane.relay()
    right_plane.relay()
    gate_plane.finish(gu.at[0])
    up_plane.finish(gu.at[1])
    keep = pltpu.make_async_copy(gu.at[:, z, c], blocks.at[z, c], s_keep)
    keep.start()
    for k in range(NZ * NC - 1):
        step = k + 1
        zp, cp = (z + step // NC) % NZ, (c + step) % NC
        wires.send(gu.at[:, zp, cp], blocks.at[z, c], s_block.at[z, c], {"z": zp, "c": cp})
    by_x.finish(line_sum.at[halves[0]])
    by_y.finish(line_sum.at[halves[1]])
    for k in range(NZ - 1):
        zp = (z + k + 1) % NZ
        wires.send(line_sum.at[zp], line_in.at[NZ - 2 - k], s_line.at[NZ - 2 - k], {"z": zp})
    line.finish(result_out)
    left_plane.finish(down_out.at[:, left])
    right_plane.finish(down_out.at[:, right])
    keep.wait()
    for k in range(NZ * NC - 1):
        step = k + 1
        zp, cp = (z + step // NC) % NZ, (c + step) % NC
        wires.arrived(blocks.at[zp, cp], s_block.at[zp, cp], {"c": 1 - c})
    fs = blocks.shape[-1] // (2 * nx)
    for m, out in enumerate((gate_out, up_out)):
        for zq, cq, run, first in segments(nx, fs):
            out[:, first : first + fs] = blocks[zq, cq, m, :, run : run + fs].astype(F32)
    for k in range(NZ - 1):
        wires.arrived(line_in.at[k], s_line.at[k], {"c": 1 - c})
    first = 0
    for out, width in zip(outs, widths):
        columns = slice(first, first + width)
        total = line_sum[z, :, columns].astype(F32)
        for k in range(NZ - 1):
            total = total + line_in[k, :, columns].astype(F32)
        out[...] = total
        first += width
    wires.finish()


def last_scatter(ny, nx, grads, widths, gate, up, down, result, collective_id):
    hbm = pl.BlockSpec(memory_space=pl.ANY)
    vmem = pl.BlockSpec(memory_space=pltpu.VMEM)
    rows, width = grads.shape[4:]
    block = gate.shape[4:]
    slot = (NZ // 2, rows, width)
    gate_slot = (NZ, NC) + block
    down_slot = (down.shape[2], down.shape[3] // 2)
    sends = 4 + 7 + NZ - 1 + 3 * ((nx - 1) * 2 + 1 + nx + (nx - 1)) + NZ + 2 * (NZ - 1)
    spread = block[1] * NZ * NC
    shapes = [(rows, w) for w in widths] + [(rows, spread)] * 2
    shapes += [down.shape[2:], result.shape[2:]]
    return pl.pallas_call(
        lambda *refs: last_scatter_kernel(nx, widths, *refs),
        name="last_scatter",
        out_shape=tuple(jax.ShapeDtypeStruct(shape, F32) for shape in shapes),
        in_specs=[hbm] * 5,
        out_specs=(vmem,) * len(shapes),
        scratch_shapes=[
            pltpu.SemaphoreType.DMA((sends,)),
            pltpu.VMEM((NZ, NC, 2) + block, BF16),
            pltpu.VMEM((ny, NZ, nx, rows, width), BF16),
            pltpu.VMEM((ny, NZ, nx, rows, width), BF16),
            pltpu.VMEM((NZ, rows, width), BF16),
            pltpu.VMEM((NZ - 1, rows, width), BF16),
            pltpu.SemaphoreType.DMA((NZ, NC)),
            pltpu.SemaphoreType.DMA,
            pltpu.SemaphoreType.DMA((2, 2)),
            pltpu.SemaphoreType.DMA((2, 2)),
            pltpu.SemaphoreType.DMA((NZ - 1,)),
        ]
        + plane_scratch(slot, nx, ny, True)
        + plane_scratch(slot, ny, nx, True)
        + plane_scratch(gate_slot, nx, ny)
        + plane_scratch(gate_slot, ny, nx)
        + [pltpu.VMEM((2,) + gate_slot, BF16)]
        + plane_scratch(down_slot, nx, ny)
        + plane_scratch(down_slot, ny, nx)
        + line_scratch(result.shape[2:]),
        compiler_params=pltpu.CompilerParams(
            collective_id=collective_id, has_side_effects=True, vmem_limit_bytes=60 << 20
        ),
    )(grads, gate, up, down, result)


def back_kernel(
    nx,
    key_width,
    b_rows,
    gate,
    up,
    ao,
    kept,
    given,
    mid,
    branch,
    tokens,
    gain,
    attn,
    query,
    kv,
    mask,
    turn_c,
    turn_s,
    gain_term,
    out_q,
    out_k,
    out_v,
    out_o,
    out_tail,
    out_gate,
    out_up,
    out_in,
    out_ring,
    send_sems,
    weights,
    term_o,
    term_q,
    sib_o,
    sib_q,
    line_sum,
    line_in,
    blocks,
    gu,
    d_attn,
    d_qkv,
    d_kv,
    kv_send,
    kv_recv,
    first_in,
    s_weights,
    s_sib,
    s_line,
    s_block,
    s_kv,
    result,
    s_result,
    s_ring,
    *bufs,
):
    y, z, x, c = place()
    sib = {"c": 1 - c}
    cross = [{"z": (z + k + 1) % NZ, "c": 1 - c} for k in range(NZ - 1)]
    greet(line_peers(z, c) + cross + plane_peers(nx, y, x))
    wires = Wires(send_sems)
    along_x, along_y = ("x", nx, x), ("y", 2, y)
    gate_plane = PlaneScatter(
        wires, lambda xq, yq: gate.at[yq, :, xq], along_x, along_y, bufs[0:6]
    )
    up_plane = PlaneScatter(wires, lambda yq, xq: up.at[yq, :, xq], along_y, along_x, bufs[6:12])
    gate_plane.begin()
    up_plane.begin()
    rows, wide = branch.shape
    q_width = query.shape[1]
    qkv_width = q_width + 2 * key_width
    heads, kv_heads = q_width // HD, key_width // HD
    n = NZ // 2
    halves = [pl.ds(0, n), pl.ds(n, n)]
    tile = n * nx * NC * out_q.shape[0]
    shard = out_q.shape[0]

    def fetch(first, width):
        return pltpu.make_async_copy(
            ao.at[:, :, pl.ds(first, width)], weights.at[:, :, pl.ds(0, width)], s_weights
        )

    fetch(qkv_width, wide).start()

    def fill(term, yq, h, first, value):
        value = value.reshape((n, nx, NC, shard, value.shape[1]))
        term[yq, halves[h], :, :, :, first : first + value.shape[4]] = value.astype(BF16)

    def over(i, term, other, yq, h):
        wires.send(
            term.at[yq, halves[h], :, 1 - c],
            other.at[yq, halves[h]],
            s_sib.at[i, yq, h],
            sib,
        )

    def combine(i, term, other):
        for h in range(2):
            for yq in range(2):
                here = other.at[yq, halves[h]]
                wires.arrived(here, s_sib.at[i, yq, h], sib)
                for zq in range(h * n, h * n + n):
                    for xq in range(nx):
                        mine = term.at[yq, zq, xq, c]
                        total_into(mine, [mine, other.at[yq, zq, xq]], True)

    def planes(term, first):
        return (
            PlaneScatter(
                wires,
                lambda xq, yq: term.at[yq, halves[0], xq, c],
                along_x,
                along_y,
                bufs[first : first + 6],
                True,
            ),
            PlaneScatter(
                wires,
                lambda yq, xq: term.at[yq, halves[1], xq, c],
                along_y,
                along_x,
                bufs[first + 6 : first + 12],
                True,
            ),
        )

    for yq in range(2):
        for h in range(2):
            i = yq * 2 + h
            fill(term_o, yq, h, 0, dot_tn(attn[:, i * tile : (i + 1) * tile], branch[...]))
            over(0, term_o, sib_o, yq, h)

    for i, k in enumerate((2, 0, 1)):
        zq = line_order(z, k)
        here = pl.ds(pl.multiple_of(zq * rows, rows), rows)
        loads = [
            pltpu.make_async_copy(kept.at[here], result.at[i], s_result.at[0]),
            pltpu.make_async_copy(given.at[here], first_in, s_result.at[1]),
        ]
        for copy in loads:
            copy.start()
        for copy in loads:
            copy.wait()
        total_into(result.at[i], [result.at[i], first_in])
        j = (z - zq + NZ) % NZ - 1
        wires.send(result.at[i], out_ring.at[j], s_ring.at[j], {"z": zq})

    fetch(qkv_width, wide).wait()
    for_out = weights[:, :, :wide].reshape(q_width, wide)
    d_attn[...] = dot_nt(branch[...], for_out).astype(BF16)
    fetch(0, qkv_width).start()
    d_kv[...] = jnp.zeros_like(d_kv)
    scale = HD ** (-0.5)

    def turn_back(value):
        return value * turn_c[...] + pltpu.roll(value, HD // 2, 1) * turn_s[...]

    group = heads // kv_heads
    for kv_head in range(kv_heads):
        k_cols = pl.ds(kv_head * HD, HD)
        v_cols = pl.ds(key_width + kv_head * HD, HD)

        def head(i, carry):
            cols = pl.ds(pl.multiple_of((kv_head * group + i) * HD, HD), HD)
            q_h, do_h = query[:, cols], d_attn[:, cols]
            scores = jnp.where(mask[...] > 0, dot_nt(q_h, kv[:, k_cols]) * scale, MASKED)
            exponent = jnp.exp(scores - jnp.max(scores, axis=-1, keepdims=True))
            probs = exponent / jnp.sum(exponent, axis=-1, keepdims=True)
            d_probs = dot_nt(do_h, kv[:, v_cols])
            inner = jnp.sum(probs * d_probs, axis=-1, keepdims=True)
            d_scores = (probs * (d_probs - inner)).astype(BF16)
            d_qkv[:, cols] = turn_back(dot(d_scores, kv[:, k_cols]) * scale).astype(BF16)
            d_kv[:, k_cols] += dot_tn(d_scores, q_h) * scale
            d_kv[:, v_cols] += dot_tn(probs.astype(BF16), do_h)
            return carry

        lax.fori_loop(0, group, head, 0)

    other_rows = pl.ds(pl.multiple_of((1 - y) * rows, rows), rows)
    own_rows = pl.ds(pl.multiple_of(y * rows, rows), rows)
    kv_send[...] = d_kv[other_rows].astype(BF16)
    gate_plane.relay()
    wires.send(kv_send, kv_recv, s_kv, {"y": 1 - y})
    up_plane.relay()
    combine(0, term_o, sib_o)
    o_planes = planes(term_o, 12)
    for plane in o_planes:
        plane.begin()
    x32 = tokens[...].astype(F32)
    rescale = lax.rsqrt(jnp.mean(x32 * x32, axis=-1, keepdims=True) + EPS)
    first_in[...] = (x32 * rescale * gain[...]).astype(BF16)
    wires.arrived(kv_recv, s_kv, {"y": 1 - y})
    for kv_head in range(2 * kv_heads):
        cols = pl.ds(kv_head * HD, HD)
        total = d_kv[own_rows, cols] + kv_recv[:, cols].astype(F32)
        if kv_head < kv_heads:
            total = turn_back(total)
        d_qkv[:, pl.ds(q_width + kv_head * HD, HD)] = total.astype(BF16)
    fetch(0, qkv_width).wait()
    for_in = weights[...].reshape(wide, qkv_width)
    d_first = dot_nt(d_qkv[...], for_in)
    normed = x32 * rescale
    scaled = d_first * gain[...]
    d_x = rescale * (scaled - normed * jnp.mean(scaled * normed, axis=-1, keepdims=True))
    out_in[...] = (mid[...] + d_x).astype(BF16)
    first_term = (d_first * normed).astype(BF16)
    lane = lax.broadcasted_iota(jnp.int32, (rows, HD), 1)
    pick_one = (lane == 0).astype(F32).astype(BF16)
    pick_two = (lane == 1).astype(F32).astype(BF16)
    bias_sum = jnp.sum(d_qkv[...].astype(F32), axis=0, keepdims=True)
    top = lax.broadcasted_iota(jnp.int32, (shard, HD), 0) == 0
    wide_bias = jnp.concatenate([bias_sum, bias_sum[:, :HD]], axis=1)
    for yq in range(2):
        for h in range(2):
            i = yq * 2 + h
            cols = slice(i * tile, (i + 1) * tile)
            fill(term_q, yq, h, 0, dot_tn(first_in[:, cols], d_qkv[...]))
            tail = dot_tn(first_term[:, cols], pick_one) + dot_tn(gain_term[:, cols], pick_two)
            for zi in range(n):
                for xq in range(nx):
                    for cq in range(NC):
                        part = ((zi * nx + xq) * NC + cq) * shard
                        place_at = i * (tile // shard) + (zi * nx + xq) * NC + cq
                        first = place_at * b_rows
                        base = (first // HD) * HD
                        bias = wide_bias[:, base : base + HD]
                        bias = pltpu.roll(
                            jnp.broadcast_to(bias, (8, HD)), (HD // 2 - (first - base)) % HD, 1
                        )[:1]
                        keep = lax.broadcasted_iota(jnp.int32, (shard, HD), 1) >= HD // 2
                        mixed = tail[part : part + shard] + jnp.where(top & keep, bias, 0.0)
                        term_q[yq, h * n + zi, xq, cq, :, qkv_width:] = mixed.astype(BF16)
            over(1, term_q, sib_q, yq, h)
    combine(1, term_q, sib_q)
    q_planes = planes(term_q, 24)
    for plane in q_planes:
        plane.begin()
    gate_plane.finish(gu.at[0])
    up_plane.finish(gu.at[1])
    keep_block = pltpu.make_async_copy(gu.at[:, z, c], blocks.at[z, c], s_block.at[z, c])
    keep_block.start()
    for k in range(NZ * NC - 1):
        step = k + 1
        zp, cp = (z + step // NC) % NZ, (c + step) % NC
        wires.send(gu.at[:, zp, cp], blocks.at[z, c], s_block.at[z, c], {"z": zp, "c": cp})
    for plane in o_planes:
        plane.relay()
    for plane in q_planes:
        plane.relay()

    def along_line(i, first, width, pair):
        cols = pl.ds(first, width)
        pair[0].finish(line_sum.at[halves[0], :, cols])
        pair[1].finish(line_sum.at[halves[1], :, cols])
        for k in range(NZ - 1):
            zp, j = (z + k + 1) % NZ, NZ - 2 - k
            wires.send(
                line_sum.at[zp, :, cols], line_in.at[j, :, cols], s_line.at[i, j], {"z": zp}
            )

    q_all = qkv_width + HD
    along_line(0, q_all, wide, o_planes)
    along_line(1, 0, q_all, q_planes)
    keep_block.wait()
    for k in range(NZ * NC - 1):
        step = k + 1
        zp, cp = (z + step // NC) % NZ, (c + step) % NC
        wires.arrived(blocks.at[zp, cp], s_block.at[zp, cp], sib)
    fs = blocks.shape[-1] // (2 * nx)
    for m, out in enumerate((out_gate, out_up)):
        for zq, cq, run, first in segments(nx, fs):
            out[:, first : first + fs] = blocks[zq, cq, m, :, run : run + fs]

    def last(i, out, first, width):
        if i is not None:
            begin, size = (q_all, wide) if i == 0 else (0, q_all)
            for j in range(NZ - 1):
                wires.arrived(line_in.at[j, :, pl.ds(begin, size)], s_line.at[i, j], sib)
        columns = slice(first, first + width)
        total = line_sum[z, :, columns].astype(F32)
        for j in range(NZ - 1):
            total = total + line_in[j, :, columns].astype(F32)
        out[...] = total

    last(0, out_o, q_all, wide)
    last(1, out_q, 0, q_width)
    last(None, out_k, q_width, key_width)
    last(None, out_v, q_width + key_width, key_width)
    last(None, out_tail, qkv_width, HD)
    for j in range(NZ - 1):
        wires.arrived(out_ring.at[j], s_ring.at[j], sib)
    wires.finish()


def back(ny, nx, b_rows, gate, up, ao, kept, given, args, collective_id):
    hbm = pl.BlockSpec(memory_space=pl.ANY)
    vmem = pl.BlockSpec(memory_space=pltpu.VMEM)
    mid, branch, tokens, gain, attn, query, kv, mask, turn_c, turn_s, gain_term = args
    dma = pltpu.SemaphoreType.DMA
    shard = ao.shape[1]
    block = gate.shape[4:]
    rows, wide = branch.shape
    q_width = query.shape[1]
    key_width = kv.shape[1] // 2
    qkv_width = q_width + 2 * key_width
    q_all = qkv_width + HD
    spread = block[1] * NZ * NC
    one_plane = (nx - 1) * 2 + 1 + nx + (nx - 1)
    sends = 3 * one_plane + 8 + 1 + 7 + 3 * (NZ - 1)
    slot_o, slot_q = (NZ // 2, shard, wide), (NZ // 2, shard, q_all)
    gate_slot = (NZ, NC) + block
    place_all = (ny, NZ, nx, NC, shard)
    shapes = [(shard, q_width), (shard, key_width), (shard, key_width), (shard, wide), (shard, HD)]
    return pl.pallas_call(
        lambda *refs: back_kernel(nx, key_width, b_rows, *refs),
        name="back",
        cost_estimate=pl.CostEstimate(
            flops=100_000_000_000, bytes_accessed=100_000_000, transcendentals=0
        ),
        out_shape=tuple(jax.ShapeDtypeStruct(shape, F32) for shape in shapes)
        + (jax.ShapeDtypeStruct((shard, spread), BF16),) * 2
        + (jax.ShapeDtypeStruct((rows, wide), BF16),)
        + (jax.ShapeDtypeStruct((NZ - 1, rows, wide), BF16),),
        in_specs=[hbm] * 5 + [vmem] * len(args),
        out_specs=(vmem,) * 8 + (hbm,),
        scratch_shapes=[
            dma((sends,)),
            pltpu.VMEM((ny * NZ * nx * NC, shard, qkv_width), BF16),
            pltpu.VMEM(place_all + (wide,), BF16),
            pltpu.VMEM(place_all + (q_all,), BF16),
            pltpu.VMEM((ny, NZ, nx, shard, wide), BF16),
            pltpu.VMEM((ny, NZ, nx, shard, q_all), BF16),
            pltpu.VMEM((NZ, shard, q_all + wide), BF16),
            pltpu.VMEM((NZ - 1, shard, q_all + wide), BF16),
            pltpu.VMEM((NZ, NC, 2) + block, BF16),
            pltpu.VMEM((2,) + gate_slot, BF16),
            pltpu.VMEM((rows, q_width), BF16),
            pltpu.VMEM((rows, qkv_width), BF16),
            pltpu.VMEM((2 * rows, 2 * key_width), F32),
            pltpu.VMEM((rows, 2 * key_width), BF16),
            pltpu.VMEM((rows, 2 * key_width), BF16),
            pltpu.VMEM((rows, wide), BF16),
            dma,
            dma((2, 2, 2)),
            dma((2, NZ - 1)),
            dma((NZ, NC)),
            dma,
            pltpu.VMEM((NZ - 1, rows, wide), BF16),
            dma((2,)),
            dma((NZ - 1,)),
        ]
        + plane_scratch(gate_slot, nx, ny)
        + plane_scratch(gate_slot, ny, nx)
        + plane_scratch(slot_o, nx, ny, True)
        + plane_scratch(slot_o, ny, nx, True)
        + plane_scratch(slot_q, nx, ny, True)
        + plane_scratch(slot_q, ny, nx, True),
        compiler_params=pltpu.CompilerParams(
            collective_id=collective_id, has_side_effects=True, vmem_limit_bytes=67_043_328
        ),
    )(gate, up, ao, kept, given, *args)


def make_body(ny, nx):
    def fused_layer(packed, x, seg_all, gate, up, down, grad_out, widths, b_rows):
        tok_rows = x.shape[0]
        length = seg_all.shape[0]
        seq_place = lax.axis_index("y")
        tok_pos = seq_place * tok_rows + jnp.arange(tok_rows)
        cos_tok, sin_tok = tables(tok_pos)
        all_pos = jnp.arange(length)
        seg_tok = lax.dynamic_slice(seg_all, (seq_place * tok_rows,), (tok_rows,))
        allowed = (tok_pos[:, None] >= all_pos[None, :]) & (seg_tok[:, None] == seg_all[None, :])
        mask = allowed.astype(F32)
        turn_c = jnp.concatenate([cos_tok, cos_tok], axis=1)
        turn_s = jnp.concatenate([sin_tok, -sin_tok], axis=1)
        made = forward(
            ny, nx, b_rows, packed, gate, up, down, grad_out, x, mask, turn_c, turn_s, widths, 0
        )
        lanes = sum(widths) + widths[1] + x.shape[1]
        tail = made.ao[..., lanes : lanes + 2].astype(F32).reshape(-1, 2)
        gain_one, gain_two = tail[:, 0], tail[:, 1]
        middle = made.mid_out
        rescale_two = lax.rsqrt(jnp.mean(middle * middle, axis=-1, keepdims=True) + EPS)
        normed_two = middle * rescale_two
        scaled = made.dh * gain_two
        grad_mid = grad_out.astype(F32) + rescale_two * (
            scaled - normed_two * jnp.mean(scaled * normed_two, axis=-1, keepdims=True)
        )
        args = (
            grad_mid,
            grad_mid.astype(BF16),
            x,
            gain_one[None],
            made.o_out,
            made.q_out,
            made.kv_out,
            mask,
            turn_c,
            turn_s,
            (made.dh * normed_two).astype(BF16),
        )
        outs = back(
            ny,
            nx,
            b_rows,
            made.grad_g,
            made.grad_u,
            made.ao.reshape((-1,) + packed.shape),
            made.out_own,
            made.out_sib,
            args,
            1,
        )
        grad_q, grad_k, grad_v, grad_o, tail_sum, grad_gate_w, grad_up_w, grad_in, ring = outs
        first_row = lax.axis_index("z") * tok_rows
        out_sum = jnp.sum(ring.astype(F32), axis=0)
        for half in (made.out_own, made.out_sib):
            out_sum += lax.dynamic_slice_in_dim(half, first_row, tok_rows).astype(F32)
        return (
            (middle + out_sum).astype(BF16)[None],
            grad_in[None],
            tail_sum[:, 0],
            grad_q,
            grad_k,
            grad_v,
            tail_sum[0, HD // 2 : HD // 2 + b_rows],
            grad_o,
            tail_sum[:, 1],
            grad_gate_w.astype(F32),
            grad_up_w.astype(F32),
            made.down_out.astype(F32),
        )

    def body(
        inputs,
        segment_ids,
        attn_gain,
        q_weight,
        k_weight,
        v_weight,
        qkv_bias,
        o_weight,
        mlp_gain,
        gate_weight,
        up_weight,
        down_weight,
        cotangent,
    ):
        tok_rows = inputs.shape[1]
        hidden_in = inputs[0].astype(F32)
        grad_out = cotangent[0]
        seg_all = segment_ids[0]
        length = seg_all.shape[0]
        seq_place = lax.axis_index("y")
        tok_pos = seq_place * tok_rows + jnp.arange(tok_rows)
        cos_tok, sin_tok = tables(tok_pos)
        query_width = q_weight.shape[1]
        key_width = k_weight.shape[1]
        kv_heads = key_width // HD
        q_heads = query_width // HD
        group = q_heads // kv_heads

        g_rows = attn_gain.shape[0]
        b_rows = qkv_bias.shape[0]
        qkv_width = query_width + 2 * key_width
        extra = jnp.concatenate(
            [
                attn_gain[:, None],
                mlp_gain[:, None],
                jnp.zeros((g_rows, HD // 2 - 2), BF16),
                jnp.broadcast_to(qkv_bias[None], (g_rows, b_rows)),
                jnp.zeros((g_rows, HD // 2 - b_rows), BF16),
            ],
            axis=1,
        )
        packed = jnp.concatenate([q_weight, k_weight, v_weight, o_weight, extra], axis=1)
        fused = g_rows % 16 == 0 and b_rows == HD // 2
        if fused:
            return fused_layer(
                packed,
                inputs[0],
                seg_all,
                gate_weight,
                up_weight,
                down_weight,
                grad_out,
                (query_width, key_width),
                b_rows,
            )
        attn_all, columns_all, down_all, grad_out_all = weight_gather(
            ny,
            nx,
            packed,
            gate_weight,
            up_weight,
            down_weight,
            grad_out,
            0,
        )
        full = attn_all.reshape(-1, packed.shape[1])
        full_qkv = full[:, :qkv_width]
        full_out = full[:, qkv_width : qkv_width + query_width]
        tail = attn_all[..., qkv_width + query_width :].astype(F32)
        gain_one = tail[..., 0].reshape(-1)
        gain_two = tail[..., 1].reshape(-1)
        bias = tail[..., 0, HD // 2 : HD // 2 + b_rows].reshape(-1)
        width = gate_weight.shape[1] // (NZ * NC)
        full_gate = columns_all[0].reshape(-1, width)
        full_up = columns_all[1].reshape(-1, width)
        full_down = down_all.reshape(width, -1)
        grad_out_all = grad_out_all.reshape(-1, grad_out.shape[1])

        rescale_one = lax.rsqrt(jnp.mean(hidden_in * hidden_in, axis=-1, keepdims=True) + EPS)
        normed_one = hidden_in * rescale_one
        input_one = (normed_one * gain_one).astype(BF16)
        qkv_pre = dot(input_one, full_qkv) + bias
        query = rotate(qkv_pre[:, :query_width], cos_tok, sin_tok).astype(BF16)
        key = rotate(qkv_pre[:, query_width : query_width + key_width], cos_tok, sin_tok)
        kv = jnp.concatenate([key, qkv_pre[:, query_width + key_width :]], axis=1).astype(BF16)
        kv_all = lax.all_gather(kv, "y", axis=0, tiled=True)
        key_heads = kv_all[:, :key_width].reshape(length, kv_heads, HD)
        value_heads = kv_all[:, key_width:].reshape(length, kv_heads, HD)
        query_heads = query.reshape(tok_rows, kv_heads, group, HD)
        score_scale = HD ** (-0.5)
        all_pos = jnp.arange(length)
        seg_tok = lax.dynamic_slice(seg_all, (seq_place * tok_rows,), (tok_rows,))
        allowed = (tok_pos[:, None] >= all_pos[None, :]) & (seg_tok[:, None] == seg_all[None, :])
        scores = (
            jnp.einsum("qkgd,pkd->kgqp", query_heads, key_heads, preferred_element_type=F32)
            * score_scale
        )
        masked = jnp.where(allowed[None, None], scores, MASKED)
        row_max = jnp.max(masked, axis=-1, keepdims=True)
        exponent = jnp.exp(masked - row_max)
        row_total = jnp.sum(exponent, axis=-1, keepdims=True)
        probs = exponent / row_total
        probs_low = probs.astype(BF16)
        mixture = jnp.einsum("kgqp,pkd->qkgd", probs_low, value_heads, preferred_element_type=F32)
        attn_tok = mixture.astype(BF16).reshape(tok_rows, query_width)
        middle = hidden_in + dot(attn_tok, full_out)

        rescale_two = lax.rsqrt(jnp.mean(middle * middle, axis=-1, keepdims=True) + EPS)
        normed_two = middle * rescale_two
        input_two = (normed_two * gain_two).astype(BF16)
        by_shard = (ny, NZ, nx, NC, g_rows, width)
        grad_input_two, out_part, part_gate, part_up, *downs = mlp(
            ny, nx, False, input_two, full_gate, full_up, full_down, grad_out_all, 1
        )
        grad_gain_two, grad_mid = norm_back(grad_input_two, normed_two, rescale_two, gain_two)
        grad_mid = grad_mid + grad_out.astype(F32)
        grad_branch = grad_mid.astype(BF16)
        grad_attn = dot_nt(grad_branch, full_out).astype(BF16)
        grad_heads = grad_attn.reshape(tok_rows, kv_heads, group, HD)
        grad_probs = jnp.einsum(
            "qkgd,pkd->kgqp", grad_heads, value_heads, preferred_element_type=F32
        )
        inner_sum = jnp.sum(probs * grad_probs, axis=-1, keepdims=True)
        grad_scores = (probs * (grad_probs - inner_sum)).astype(BF16)
        grad_query = (
            jnp.einsum("kgqp,pkd->qkgd", grad_scores, key_heads, preferred_element_type=F32)
            * score_scale
        ).reshape(tok_rows, query_width)
        grad_key = (
            jnp.einsum("kgqp,qkgd->pkd", grad_scores, query_heads, preferred_element_type=F32)
            * score_scale
        ).reshape(length, key_width)
        grad_value = jnp.einsum(
            "kgqp,qkgd->pkd", probs_low, grad_heads, preferred_element_type=F32
        ).reshape(length, key_width)
        grad_kv = jnp.concatenate([grad_key, grad_value], axis=1).astype(BF16)
        other = lax.dynamic_slice(
            grad_kv, ((1 - seq_place) * tok_rows, 0), (tok_rows, 2 * key_width)
        )
        own = lax.dynamic_slice(grad_kv, (seq_place * tok_rows, 0), (tok_rows, 2 * key_width))
        swapped = lax.ppermute(other, "y", [(0, 1), (1, 0)])
        grad_kv_tok = own.astype(F32) + swapped.astype(F32)
        grad_query_pre = rotate(grad_query, cos_tok, -sin_tok).astype(BF16)
        grad_key_pre = rotate(grad_kv_tok[:, :key_width], cos_tok, -sin_tok).astype(BF16)
        grad_value_pre = grad_kv_tok[:, key_width:].astype(BF16)
        grad_qkv = jnp.concatenate([grad_query_pre, grad_key_pre, grad_value_pre], axis=1)
        grad_qkv_sum = jnp.sum(grad_qkv.astype(F32), axis=0)
        grad_input_one = dot_nt(grad_qkv, full_qkv)
        grad_gain_one, grad_first = norm_back(grad_input_one, normed_one, rescale_one, gain_one)
        grad_total = grad_mid + grad_first
        shards = ny * NZ * nx * NC
        tail_grads = jnp.concatenate(
            [
                grad_gain_one[:, None],
                grad_gain_two[:, None],
                jnp.broadcast_to(
                    grad_qkv_sum.reshape(shards, 1, b_rows), (shards, g_rows, b_rows)
                ).reshape(-1, b_rows),
                jnp.zeros((shards * g_rows, HD - 2 - b_rows), F32),
            ],
            axis=1,
        )
        grad_attn_w = jnp.concatenate(
            [
                dot_tn(input_one, grad_qkv).astype(BF16),
                dot_tn(attn_tok, grad_branch).astype(BF16),
                tail_grads.astype(BF16),
            ],
            axis=1,
        )
        widths = (query_width, key_width, key_width, query_width, HD)
        pieces = (NZ, NC, tok_rows // 32, 32, hidden_in.shape[1])
        outs = last_scatter(
            ny,
            nx,
            grad_attn_w.reshape((ny, NZ, nx, NC, g_rows, -1)),
            widths,
            part_gate.reshape(by_shard),
            part_up.reshape(by_shard),
            downs[0].reshape((ny, nx) + down_weight.shape),
            out_part.reshape(pieces),
            3,
        )
        grad_q, grad_k, grad_v, grad_o, tail_sum = outs[:5]
        grad_gate_w, grad_up_w, grad_down_w, out_sum = outs[5:]
        output = (middle + out_sum.reshape(middle.shape)).astype(BF16)[None]
        return (
            output,
            grad_total.astype(BF16)[None],
            tail_sum[:, 0],
            grad_q,
            grad_k,
            grad_v,
            tail_sum[0, 2 : 2 + b_rows],
            grad_o,
            tail_sum[:, 1],
            grad_gate_w,
            grad_up_w,
            grad_down_w,
        )

    return body


def solution(mesh):
    ny = mesh.shape["seq"]
    nx = mesh.shape["fsdp"] // (NZ * NC)
    grid = Mesh(mesh.devices.reshape(ny, NZ, nx, NC), ALL)
    tokens = P(("z", "x", "c"), "y", None)
    rows = P(ALL, None)
    vec = P(ALL)
    return jax.shard_map(
        make_body(ny, nx),
        mesh=grid,
        in_specs=(
            tokens,
            P(("z", "x", "c"), None),
            vec,
            rows,
            rows,
            rows,
            vec,
            rows,
            vec,
            rows,
            rows,
            rows,
            tokens,
        ),
        out_specs=(tokens, tokens, vec, rows, rows, rows, vec, rows, vec, rows, rows, rows),
        check_vma=False,
    )
```

```python
import types

import jax
import jax.numpy as jnp
from jax import lax
from jax.experimental import pallas as pl
from jax.experimental.pallas import tpu as pltpu
from jax.sharding import Mesh, PartitionSpec as P

HD = 128
EPS = 1e-06
ROPE_BASE = 1000000.0
MASKED = -1e30
NZ = 4
NC = 2
ALL = ("y", "z", "x", "c")
TP = ("z", "c")
DP = ("y", "x")
F32 = jnp.float32
BF16 = jnp.bfloat16


def tables(positions):
    freq = ROPE_BASE ** (-jnp.arange(0, HD, 2).astype(F32) / HD)
    angle = positions.astype(F32)[:, None] * freq[None, :]
    return (jnp.cos(angle), jnp.sin(angle))


def rotate(values, cosine, sine):
    count = values.shape[0]
    split = values.reshape(count, -1, HD)
    half = HD // 2
    first = split[..., :half]
    second = split[..., half:]
    cos_b = cosine[:, None, :]
    sin_b = sine[:, None, :]
    turned = jnp.concatenate(
        [first * cos_b - second * sin_b, second * cos_b + first * sin_b], axis=-1
    )
    return turned.reshape(count, -1)


def dot(a, b):
    return jnp.dot(a, b, preferred_element_type=F32)


def dot_nt(a, b):
    return lax.dot_general(a, b, (((1,), (1,)), ((), ())), preferred_element_type=F32)


def dot_tn(a, b):
    return lax.dot_general(a, b, (((0,), (0,)), ((), ())), preferred_element_type=F32)


def norm_back(grad_normed, normed, rescale, gain_vec):
    grad_gain = jnp.sum(grad_normed * normed, axis=0)
    scaled = grad_normed * gain_vec
    grad_x = rescale * (scaled - normed * jnp.mean(scaled * normed, axis=-1, keepdims=True))
    return (grad_gain, grad_x)


class Wires:
    def __init__(self, sems):
        self.sems = sems
        self.used = 0
        self.started = []

    def send(self, src, dst, recv_sem, device, cond=None):
        copy = pltpu.make_async_remote_copy(
            src_ref=src,
            dst_ref=dst,
            send_sem=self.sems.at[self.used],
            recv_sem=recv_sem,
            device_id=device,
            device_id_type=pl.DeviceIdType.MESH,
        )
        if cond is None:
            copy.start()
        else:
            pl.when(cond())(copy.start)
        self.started.append((still(src), self.used, cond))
        self.used += 1

    def arrived(self, dst, recv_sem, device):
        pltpu.make_async_remote_copy(
            src_ref=dst,
            dst_ref=dst,
            send_sem=self.sems.at[0],
            recv_sem=recv_sem,
            device_id=device,
            device_id_type=pl.DeviceIdType.MESH,
        ).wait_recv()

    def finish(self, sent=None):
        for src, used, cond in self.started if sent is None else sent:
            sem = self.sems.at[used]
            src = taken(*src)
            copy = pltpu.make_async_remote_copy(
                src_ref=src,
                dst_ref=src,
                send_sem=sem,
                recv_sem=sem,
                device_id={"c": 1 - lax.axis_index("c")},
                device_id_type=pl.DeviceIdType.MESH,
            )
            if cond is None:
                copy.wait_send()
            else:
                pl.when(cond())(copy.wait_send)


def still(ref):
    steps = []
    for step in getattr(ref, "transforms", ()):
        steps.append([i.size if isinstance(i, pl.Slice) else None for i in step.indices])
    return getattr(ref, "ref", ref), steps


def taken(view, steps):
    for step in steps:
        view = view.at[tuple(0 if size is None else pl.ds(0, size) for size in step)]
    return view


def line_order(z, k):
    if k == 0:
        return z + 1 - 2 * (z % 2)
    if k == 1:
        return 2 - z // 2
    return 3 - 3 * (z // 2)


def greet(peers):
    barrier = pltpu.get_barrier_semaphore()
    for peer in peers:
        pl.semaphore_signal(
            barrier, inc=1, device_id=peer, device_id_type=pl.DeviceIdType.MESH
        )
    pl.semaphore_wait(barrier, len(peers))


def place():
    return tuple(lax.axis_index(name) for name in ALL)


def line_peers(z, c):
    peers = [{"c": 1 - c}]
    for k in range(NZ - 1):
        peers.append({"z": (z + k + 1) % NZ})
    return peers


class LineGather:
    def __init__(self, wires, own, out, recv, z, c):
        self.wires, self.own, self.out, self.recv, self.z, self.c = wires, own, out, recv, z, c

    def begin(self):
        w, z, c = self.wires, self.z, self.c
        dst, sem = self.out.at[z, c], self.recv.at[z, c]
        w.send(self.own, dst, sem, {"z": jnp.minimum(z + 1, NZ - 1)}, lambda: z < NZ - 1)
        w.send(self.own, dst, sem, {"z": jnp.maximum(z - 1, 0)}, lambda: z > 0)
        w.send(self.own, dst, sem, {"c": 1 - c})

    def event(self, k):
        w, z, c = self.wires, self.z, self.c
        zq = line_order(z, k)
        slot, sem = self.out.at[zq, c], self.recv.at[zq, c]
        w.arrived(slot, sem, {"c": 1 - c})
        onward = jnp.where(zq < z, jnp.minimum(z + 1, NZ - 1), jnp.maximum(z - 1, 0))
        w.send(slot, slot, sem, {"z": onward}, lambda: (z > 0) & (z < NZ - 1))
        w.send(slot, slot, sem, {"c": 1 - c})

    def sibling(self, zq):
        w, c = self.wires, self.c
        w.arrived(self.out.at[zq, 1 - c], self.recv.at[zq, 1 - c], {"c": 1 - c})


def segments(nx, fs):
    for yq in range(2):
        for zq in range(NZ):
            for xq in range(nx):
                for cq in range(NC):
                    first = (((yq * NZ + zq) * nx + xq) * NC + cq) * fs
                    yield zq, cq, (yq * nx + xq) * fs, first


def weight_gather_kernel(
    nx, a, g, u, d, tok, ao, guo, do, co, gu, send_sems, local_sems, ra, rt, rw, rd, rc
):
    y, z, x, c = place()
    sib = {"c": 1 - c}
    ypeer = {"y": 1 - y}
    xpeers = [(x + i + 1) % nx for i in range(nx - 1)]
    planes = [{"x": xp} for xp in xpeers] + [ypeer]
    cross = [{"z": (z + k + 1) % NZ, "c": 1 - c} for k in range(NZ - 1)]
    greet(line_peers(z, c) + cross + planes)
    locals_ = [
        pltpu.make_async_copy(a, ao.at[y, z, x, c], local_sems.at[0]),
        pltpu.make_async_copy(d, do.at[y, x], local_sems.at[1]),
        pltpu.make_async_copy(tok, co.at[z, c], local_sems.at[2]),
    ]
    keep = pltpu.make_async_copy(gu.at[z, c], guo.at[:, y, z, x, c], local_sems.at[3])
    for copy in locals_:
        copy.start()
    wires = Wires(send_sems)

    def both_ways(src, dst, sem):
        for peer in planes:
            wires.send(src, dst, sem, peer)

    own_slot, own_sem = ao.at[y, z, x, c], ra.at[y, z, x, c]
    wires.send(a, own_slot, own_sem, {"z": jnp.minimum(z + 1, NZ - 1)}, lambda: z < NZ - 1)
    wires.send(a, own_slot, own_sem, {"z": jnp.maximum(z - 1, 0)}, lambda: z > 0)
    both_ways(a, own_slot, own_sem)
    wires.send(a, own_slot, own_sem, sib)
    fs = gu.shape[-1] // (2 * nx)
    for m, shard in enumerate((g, u)):
        for zq, cq, run, first in segments(nx, fs):
            gu[zq, cq, m, :, run : run + fs] = shard[:, first : first + fs]
    keep.start()
    for k in range(NZ - 1):
        zq = line_order(z, k)
        slot, sem = ao.at[y, zq, x, c], ra.at[y, zq, x, c]
        wires.arrived(slot, sem, sib)
        onward = jnp.where(zq < z, jnp.minimum(z + 1, NZ - 1), jnp.maximum(z - 1, 0))
        wires.send(slot, slot, sem, {"z": onward}, lambda: (z > 0) & (z < NZ - 1))
        both_ways(slot, slot, sem)
        wires.send(slot, slot, sem, sib)

    for k in range(NZ * NC - 1):
        step = k + 1
        zp, cp = (z + step // NC) % NZ, (c + step) % NC
        wires.send(
            gu.at[zp, cp], guo.at[:, y, z, x, c], rt.at[z, c], {"z": zp, "c": cp}
        )
    line = LineGather(wires, tok, co, rc, z, c)
    line.begin()
    half = d.shape[1] // 2
    parts = [pl.ds(0, half), pl.ds(half, half)]
    for h in range(2):
        both_ways(d.at[:, parts[h]], do.at[y, x, :, parts[h]], rd.at[h, y, x])

    def relay_attn(yq, xq, zq, peers):
        slot, sem = ao.at[yq, zq, xq, c], ra.at[yq, zq, xq, c]
        wires.arrived(slot, sem, sib)
        for peer in peers:
            wires.send(slot, slot, sem, peer)
        wires.send(slot, slot, sem, sib)

    for zq in range(NZ):
        for xp in xpeers:
            relay_attn(y, xp, zq, [ypeer] if zq < NZ // 2 else [])
        relay_attn(1 - y, x, zq, planes[:-1] if zq >= NZ // 2 else [])

    for k in range(NZ * NC - 1):
        step = k + 1
        zp, cp = (z + step // NC) % NZ, (c + step) % NC
        wires.arrived(guo.at[:, y, zp, x, cp], rt.at[zp, cp], sib)
    keep.wait()
    for m in range(2):
        plane = guo.at[m, y, :, x]
        both_ways(plane, plane, rw.at[m, y, x])
    line.event(0)

    def relay(ref, sem, peers):
        wires.arrived(ref, sem, sib)
        for peer in peers:
            wires.send(ref, ref, sem, peer)

    for xp in xpeers:
        relay(do.at[y, xp, :, parts[0]], rd.at[0, y, xp], [ypeer])
        relay(do.at[y, xp, :, parts[1]], rd.at[1, y, xp], [])
    relay(do.at[1 - y, x, :, parts[1]], rd.at[1, 1 - y, x], planes[:-1])
    relay(do.at[1 - y, x, :, parts[0]], rd.at[0, 1 - y, x], [])
    for xp in xpeers:
        for zq in range(NZ):
            relay_attn(1 - y, xp, zq, [])
    line.event(1)
    for xp in xpeers:
        relay(guo.at[0, y, :, xp], rw.at[0, y, xp], [ypeer])
    relay(guo.at[1, 1 - y, :, x], rw.at[1, 1 - y, x], planes[:-1])
    line.event(2)
    for xp in xpeers:
        relay(guo.at[1, y, :, xp], rw.at[1, y, xp], [])
    relay(guo.at[0, 1 - y, :, x], rw.at[0, 1 - y, x], [])
    for xp in xpeers:
        for h in range(2):
            relay(do.at[1 - y, xp, :, parts[h]], rd.at[h, 1 - y, xp], [])
            relay(guo.at[h, 1 - y, :, xp], rw.at[h, 1 - y, xp], [])
    for zq in range(NZ):
        line.sibling(zq)
    for yq in range(2):
        for zq in range(NZ):
            for xq in range(nx):
                wires.arrived(ao.at[yq, zq, xq, 1 - c], ra.at[yq, zq, xq, 1 - c], sib)
    wires.finish()
    for copy in locals_:
        copy.wait()


def weight_gather(ny, nx, a, g, u, d, tok, collective_id):
    sends = 3 + (nx + 1) + 3 * (nx + 2)
    sends += 7 + 9 + 2 * nx
    sends += 4 * nx + 2 * (nx - 1) + 2 * (nx - 1)
    sends += 2 * nx + 2 * (nx - 1) + 4 * (nx - 1) + 2 * (nx - 1)
    hbm = pl.BlockSpec(memory_space=pl.ANY)
    vmem = pl.BlockSpec(memory_space=pltpu.VMEM)
    grid = (ny, NZ, nx, NC)
    block = g.shape[:1] + (g.shape[1] // (NZ * NC),)
    return pl.pallas_call(
        lambda *refs: weight_gather_kernel(nx, *refs),
        name="weight_gather",
        out_shape=(
            jax.ShapeDtypeStruct(grid + a.shape, BF16),
            jax.ShapeDtypeStruct((2,) + grid + block, BF16),
            jax.ShapeDtypeStruct((ny, nx) + d.shape, BF16),
            jax.ShapeDtypeStruct((NZ, NC) + tok.shape, BF16),
        ),
        in_specs=[hbm, vmem, vmem, hbm, hbm],
        out_specs=(hbm,) * 4,
        scratch_shapes=[
            pltpu.VMEM((NZ, NC, 2) + block, BF16),
            pltpu.SemaphoreType.DMA((sends + 16,)),
            pltpu.SemaphoreType.DMA((4,)),
            pltpu.SemaphoreType.DMA(grid),
            pltpu.SemaphoreType.DMA((NZ, NC)),
            pltpu.SemaphoreType.DMA((2, ny, nx)),
            pltpu.SemaphoreType.DMA((2, ny, nx)),
            pltpu.SemaphoreType.DMA((NZ, NC)),
        ],
        compiler_params=pltpu.CompilerParams(
            collective_id=collective_id, has_side_effects=True
        ),
    )(a, g, u, d, tok)


def total_into(dst, refs, flat=None):
    flat = len(dst.shape) == 2

    def entry(i, carry):
        here = (slice(None), pl.ds(pl.multiple_of(i * 128, 128), 128)) if flat else i
        total = refs[0][here].astype(F32)
        for ref in refs[1:]:
            total = total + ref[here].astype(F32)
        dst[here] = total.astype(dst.dtype)
        return carry

    lax.fori_loop(0, dst.shape[1] // 128 if flat else dst.shape[0], entry, 0)


class PlaneScatter:
    def __init__(self, wires, src, first, second, bufs, loaded=False):
        self.wires, self.src = wires, src
        self.name_a, self.size_a, self.a = first
        self.name_b, self.size_b, self.b = second
        self.r1, self.own, self.r2, self.s1, self.sl, self.s2 = bufs
        self.loaded = loaded

    def mine(self, b):
        return self.src(self.a, b) if self.loaded else self.own.at[b]

    def order(self):
        return [(self.b + i + 1) % self.size_b for i in range(self.size_b)]

    def begin(self):
        for b in self.order():
            for i in range(self.size_a - 1):
                peer, j = (self.a + i + 1) % self.size_a, self.size_a - 2 - i
                self.wires.send(
                    self.src(peer, b), self.r1.at[j, b], self.s1.at[j, b], {self.name_a: peer}
                )
            if not self.loaded:
                self.load(b).start()

    def load(self, b):
        return pltpu.make_async_copy(self.src(self.a, b), self.own.at[b], self.sl.at[b])

    def gathered(self, b):
        if not self.loaded:
            self.load(b).wait()
        for j in range(self.size_a - 1):
            self.wires.arrived(self.r1.at[j, b], self.s1.at[j, b], {self.name_a: self.a})
        return [self.mine(b)] + [self.r1.at[j, b] for j in range(self.size_a - 1)]

    def relay(self):
        for i, b in enumerate(self.order()[:-1]):
            j = self.size_b - 2 - i
            total_into(self.mine(b), self.gathered(b))
            self.wires.send(self.mine(b), self.r2.at[j], self.s2.at[j], {self.name_b: b})

    def finish(self, dst):
        refs = self.gathered(self.b)
        for j in range(self.size_b - 1):
            self.wires.arrived(self.r2.at[j], self.s2.at[j], {self.name_b: self.b})
            refs.append(self.r2.at[j])
        total_into(dst, refs)


def plane_scratch(slot, size_a, size_b, loaded=False):
    own = (1,) * (1 + len(slot)) if loaded else (size_b,) + slot
    return [
        pltpu.VMEM((size_a - 1, size_b) + slot, BF16),
        pltpu.VMEM(own, BF16),
        pltpu.VMEM((size_b - 1,) + slot, BF16),
        pltpu.SemaphoreType.DMA((size_a - 1, size_b)),
        pltpu.SemaphoreType.DMA((size_b,)),
        pltpu.SemaphoreType.DMA((size_b - 1,)),
    ]


class LineScatter:
    def __init__(self, wires, part, bufs, z, c):
        self.wires, self.part, self.z, self.c = wires, part, z, c
        self.own, self.sib, self.left, self.right = bufs[:4]
        self.s_own, self.s_sib, self.s_left, self.s_right = bufs[4:]

    def order(self):
        return [line_order(self.z, k) for k in (2, 1, 0)] + [self.z]

    def load(self, zq):
        return pltpu.make_async_copy(
            self.part.at[zq, self.c], self.own.at[zq], self.s_own.at[zq]
        )

    def begin(self):
        for zq in self.order():
            self.wires.send(
                self.part.at[zq, 1 - self.c],
                self.sib.at[zq],
                self.s_sib.at[zq],
                {"c": 1 - self.c},
            )
            self.load(zq).start()

    def ready(self, zq):
        self.load(zq).wait()
        self.wires.arrived(self.sib.at[zq], self.s_sib.at[zq], {"c": 1 - self.c})

    def hop(self, k):
        z = self.z
        for sign, buf, sems in ((1, self.left, self.s_left), (-1, self.right, self.s_right)):
            target = z + sign * k
            inside = (target < NZ) if sign > 0 else (target >= 0)
            behind = (z > 0) if sign > 0 else (z < NZ - 1)
            target = jnp.clip(target, 0, NZ - 1)
            own, sib = self.own.at[target], self.sib.at[target]

            @pl.when(inside)
            def _():
                self.ready(target)

            if k < NZ - 1:

                @pl.when(inside & behind)
                def _():
                    self.wires.arrived(buf.at[k], sems.at[k], {"z": z})
                    total_into(own, [own, sib, buf.at[k]])

                @pl.when(inside & jnp.logical_not(behind))
                def _():
                    total_into(own, [own, sib])

            else:

                @pl.when(inside)
                def _():
                    total_into(own, [own, sib])

            onward = jnp.clip(z + sign, 0, NZ - 1)
            self.wires.send(own, buf.at[k - 1], sems.at[k - 1], {"z": onward}, lambda: inside)

    def finish(self, dst):
        z = self.z
        self.ready(z)
        own, sib = self.own.at[z], self.sib.at[z]

        @pl.when(z > 0)
        def _():
            self.wires.arrived(self.left.at[0], self.s_left.at[0], {"z": z})

        @pl.when(z < NZ - 1)
        def _():
            self.wires.arrived(self.right.at[0], self.s_right.at[0], {"z": z})

        @pl.when(z == 0)
        def _():
            total_into(dst, [own, sib, self.right.at[0]])

        @pl.when(z == NZ - 1)
        def _():
            total_into(dst, [own, sib, self.left.at[0]])

        @pl.when((z > 0) & (z < NZ - 1))
        def _():
            total_into(dst, [own, sib, self.left.at[0], self.right.at[0]])


def line_scratch(slot):
    return [
        pltpu.VMEM((NZ,) + slot, BF16),
        pltpu.VMEM((NZ,) + slot, BF16),
        pltpu.VMEM((NZ - 1,) + slot, BF16),
        pltpu.VMEM((NZ - 1,) + slot, BF16),
        pltpu.SemaphoreType.DMA((NZ,)),
        pltpu.SemaphoreType.DMA((NZ,)),
        pltpu.SemaphoreType.DMA((NZ - 1,)),
        pltpu.SemaphoreType.DMA((NZ - 1,)),
    ]


TILES = ((0, 640), (640, None))


def remote(src, dst, send_sem, recv_sem, device):
    return pltpu.make_async_remote_copy(
        src_ref=src,
        dst_ref=dst,
        send_sem=send_sem,
        recv_sem=recv_sem,
        device_id=device,
        device_id_type=pl.DeviceIdType.MESH,
    )


def mlp_kernel(
    nx,
    with_down,
    h,
    wg,
    wu,
    wd,
    cot,
    dh,
    out_part,
    grad_g,
    grad_u,
    grad_d,
    *scratch,
):
    if with_down:
        down_out, out_sib, scratch = scratch[0], scratch[1], scratch[2:]
    (
        hv,
        cv,
        wgv,
        wuv,
        wdv,
        av,
        dgv,
        duv,
        part,
        sib,
        ring,
        ob,
        s_load,
        s_cot,
        s_ob,
        s_out,
        h_send,
        h_on,
        h_sib,
        h_recv,
        p_send,
        p_recv,
        r_send,
        r_recv,
    ) = scratch[: 24]
    scratch = scratch[24:]
    if with_down:
        o_send, o_recv, scratch = scratch[0], scratch[1], scratch[2:]
    y, z, x, c = place()
    rows, wide = h.shape
    units = wg.shape[1]
    other = 1 - c
    inner = (z > 0) & (z < NZ - 1)
    greet(line_peers(z, c) + (plane_peers(nx, y, x) if with_down else []))

    def block(zq, cq):
        return pl.ds(pl.multiple_of((zq * NC + cq) * rows, rows), rows)

    loads = [
        pltpu.make_async_copy(h, hv.at[block(z, c)], s_load.at[0]),
        pltpu.make_async_copy(wg, wgv, s_load.at[1]),
        pltpu.make_async_copy(wu, wuv, s_load.at[2]),
        pltpu.make_async_copy(wd, wdv, s_load.at[3]),
    ]

    def load_cot(zq, cq):
        return pltpu.make_async_copy(
            cot.at[block(zq, cq)], cv.at[block(zq, cq)], s_cot.at[zq, cq]
        )

    def send_own(i):
        there = hv.at[block(z, c)]
        device = (
            {"z": jnp.minimum(z + 1, NZ - 1)},
            {"z": jnp.maximum(z - 1, 0)},
            {"c": other},
        )[i]
        return remote(h, there, h_send.at[i], h_recv.at[z, c], device)

    pl.when(z < NZ - 1)(send_own(0).start)
    pl.when(z > 0)(send_own(1).start)
    send_own(2).start()
    for copy in loads[:3]:
        copy.start()
    load_cot(z, c).start()
    loads[3].start()
    load_cot(z, other).start()
    for k in range(NZ - 1):
        for i in range(NC):
            load_cot(line_order(z, k), (c + i) % NC).start()

    def arrival(zq, cq):
        here = hv.at[block(zq, cq)]
        return remote(here, here, h_send.at[0], h_recv.at[zq, cq], {"c": other})

    def onward(k):
        zq = line_order(z, k)
        here = hv.at[block(zq, c)]
        device = {"z": jnp.where(zq < z, jnp.minimum(z + 1, NZ - 1), jnp.maximum(z - 1, 0))}
        return remote(here, here, h_on.at[k], h_recv.at[zq, c], device)

    def to_sibling(k):
        zq = line_order(z, k)
        here = hv.at[block(zq, c)]
        return remote(here, here, h_sib.at[k], h_recv.at[zq, c], {"c": other})

    def take(k):
        arrival(line_order(z, k), c).wait_recv()
        pl.when(inner)(onward(k).start)
        to_sibling(k).start()

    def output(zq, cq):
        if with_down:
            here = pl.ds(pl.multiple_of(zq * rows, rows), rows)
            return pltpu.make_async_copy(ob.at[cq], out_part.at[here], s_ob.at[0])
        return pltpu.make_async_copy(ob.at[cq], out_part.at[block(zq, cq)], s_ob.at[cq])

    def output_over(zq):
        here = pl.ds(pl.multiple_of(zq * rows, rows), rows)
        return remote(
            ob.at[other], out_sib.at[here], o_send.at[zq], o_recv.at[zq], {"c": other}
        )

    def partial_over(zq):
        return remote(
            part.at[block(zq, other)], sib.at[zq], p_send.at[zq], p_recv.at[zq], {"c": other}
        )

    def partial_home(zq):
        j = (z - zq + NZ) % NZ - 1
        return remote(
            part.at[block(zq, c)], ring.at[j], r_send.at[zq], r_recv.at[j], {"z": zq}
        )

    piece = rows // 8

    def combine(zq):
        remote(sib.at[zq], sib.at[zq], p_send.at[0], p_recv.at[zq], {"c": other}).wait_recv()

        def step(i, carry):
            here = pl.ds(pl.multiple_of((zq * NC + c) * rows + i * piece, piece), piece)
            there = pl.ds(pl.multiple_of(i * piece, piece), piece)
            total = part[here].astype(F32) + sib[zq, there].astype(F32)
            part[here] = total.astype(BF16)
            return carry

        lax.fori_loop(0, 8, step, 0)

    def place_of(k):
        near = line_order(z, 0)
        mid = line_order(z, 1)
        far = line_order(z, 2)
        return jnp.where(k == 0, z, jnp.where(k == 1, near, jnp.where(k == 2, mid, far)))

    def pair(k, carry):
        zq = place_of(k)

        @pl.when(k == 1)
        def _():
            take(0)
            pl.when(inner)(lambda: take(1))

        @pl.when(k == 2)
        def _():
            pl.when(jnp.logical_not(inner))(lambda: take(1))
            pl.when(inner)(lambda: take(2))

        @pl.when((k == 3) & jnp.logical_not(inner))
        def _():
            take(2)

        def one(j, carry):
            cq = (c + j) % NC
            here = block(zq, cq)

            @pl.when((k == 0) & (j == 0))
            def _():
                for copy in loads:
                    copy.wait()

            @pl.when(j == 1)
            def _():
                arrival(zq, cq).wait_recv()

            load_cot(zq, cq).wait()
            for low, high in TILES:
                high = units if high is None else high
                gate = dot(hv[here], wgv[:, low:high])
                up = dot(hv[here], wuv[:, low:high])
                grad = dot_nt(cv[here], wdv[low:high])
                sig = jax.nn.sigmoid(gate)
                act = gate * sig
                av[here, low:high] = (act * up).astype(BF16)
                duv[here, low:high] = (grad * act).astype(BF16)
                dgv[here, low:high] = (
                    grad * up * (sig * (1.0 + gate * (1.0 - sig)))
                ).astype(BF16)

            if with_down:

                @pl.when((k > 0) & (j == 0))
                def _():
                    output(zq, cq).wait()

                @pl.when((k > 0) & (j == 1))
                def _():
                    output_over(place_of(k - 1)).wait_send()

            else:

                @pl.when(k > 0)
                def _():
                    output(zq, cq).wait()

            ob[cq] = dot(av[here], wdv[...]).astype(BF16)
            if with_down:
                pl.when(j == 0)(output(zq, cq).start)
                pl.when(j == 1)(output_over(zq).start)
            else:
                output(zq, cq).start()
            part[here] = (dot_nt(dgv[here], wgv[...]) + dot_nt(duv[here], wuv[...])).astype(BF16)
            return carry

        lax.fori_loop(0, NC, one, 0)
        partial_over(zq).start()

        @pl.when(k > 1)
        def _():
            before = place_of(k - 1)
            combine(before)
            partial_home(before).start()

        return carry

    lax.fori_loop(0, NZ, pair, 0)
    last = line_order(z, NZ - 2)
    step_d = wide // 6

    def down_grad(t, carry):
        cols = pl.ds(pl.multiple_of(t * step_d, step_d), step_d)
        wdv[:, cols] = dot_tn(av[...], cv[:, cols]).astype(BF16)

        @pl.when(t == 0)
        def _():
            combine(last)
            partial_home(last).start()

        return carry

    lax.fori_loop(0, 6, down_grad, 0)
    outs = [
        pltpu.make_async_copy(wdv, grad_d, s_out.at[0]),
        pltpu.make_async_copy(wgv, grad_g, s_out.at[1]),
        pltpu.make_async_copy(wuv, grad_u, s_out.at[2]),
    ]
    outs[0].start()
    if with_down:
        wires = Wires(scratch[0])
        half, shard = wide // 2, units // (2 * nx)
        left, right = pl.ds(0, half), pl.ds(half, half)

        def term(yq, xq, cols):
            first = (yq * nx + xq) * shard
            return grad_d.at[pl.ds(pl.multiple_of(first, 8), shard), cols]

        along_x, along_y = ("x", nx, x), ("y", 2, y)
        by_x = PlaneScatter(
            wires, lambda xq, yq: term(yq, xq, left), along_x, along_y, scratch[1:7]
        )
        by_y = PlaneScatter(
            wires, lambda yq, xq: term(yq, xq, right), along_y, along_x, scratch[7:13]
        )

    def turned(src, dst, first, last):
        def step(t, carry):
            cols = pl.ds(pl.multiple_of(t * step_d, step_d), step_d)
            dst[cols] = dot_tn(hv[:, cols], src[...]).astype(BF16)
            return carry

        lax.fori_loop(first, last, step, 0)

    turned(dgv, wgv, 0, 1)
    if with_down:
        outs[0].wait()
        by_x.begin()
        by_y.begin()
    turned(dgv, wgv, 1, 6)
    outs[1].start()
    turned(duv, wuv, 0, 6)
    outs[2].start()
    if with_down:
        by_x.relay()
        by_y.relay()
    combine(z)
    for j in range(NZ - 1):
        remote(ring.at[j], ring.at[j], r_send.at[0], r_recv.at[j], {"c": other}).wait_recv()

    def final(i, carry):
        here = pl.ds(pl.multiple_of((z * NC + c) * rows + i * piece, piece), piece)
        there = pl.ds(pl.multiple_of(i * piece, piece), piece)
        total = part[here].astype(F32)
        for j in range(NZ - 1):
            total = total + ring[j, there].astype(F32)
        dh[there] = total
        return carry

    lax.fori_loop(0, 8, final, 0)
    if with_down:
        by_x.finish(down_out.at[:, left])
        by_y.finish(down_out.at[:, right])
        wires.finish()
    pl.when(z < NZ - 1)(send_own(0).wait_send)
    pl.when(z > 0)(send_own(1).wait_send)
    send_own(2).wait_send()
    for k in range(NZ - 1):
        pl.when(inner)(onward(k).wait_send)
        to_sibling(k).wait_send()
        partial_home(line_order(z, k)).wait_send()
    for zq in range(NZ):
        partial_over(zq).wait_send()
    if with_down:
        output(z, c).wait()
        output_over(last).wait_send()
        for zq in range(NZ):
            there = out_sib.at[pl.ds(zq * rows, rows)]
            remote(there, there, o_send.at[0], o_recv.at[zq], {"c": other}).wait_recv()
    else:
        for cq in range(NC):
            output(z, cq).wait()
    for copy in outs[1 if with_down else 0 :]:
        copy.wait()


def mlp(ny, nx, with_down, h, wg, wu, wd, cot, collective_id):
    hbm = pl.BlockSpec(memory_space=pl.ANY)
    vmem = pl.BlockSpec(memory_space=pltpu.VMEM)
    rows, wide = h.shape
    units = wg.shape[1]
    every = NZ * NC * rows
    dma = pltpu.SemaphoreType.DMA
    shard = units // (ny * nx)
    down_scratch = []
    if with_down:
        sends = 2 * ((nx - 1) * 2 + 1 + nx + (nx - 1))
        down_scratch = [dma((NZ,)), dma((NZ,)), dma((sends,))]
        down_scratch += plane_scratch((shard, wide // 2), nx, ny)
        down_scratch += plane_scratch((shard, wide // 2), ny, nx)
    extra_shape, extra_specs, kept = (), (), every
    if with_down:
        kept = NZ * rows
        extra_shape = (
            jax.ShapeDtypeStruct((shard, wide), BF16),
            jax.ShapeDtypeStruct((kept, wide), BF16),
        )
        extra_specs = (vmem, hbm)
    return pl.pallas_call(
        lambda *refs: mlp_kernel(nx, with_down, *refs),
        name="mlp",
        out_shape=(
            jax.ShapeDtypeStruct((rows, wide), F32),
            jax.ShapeDtypeStruct((kept, wide), BF16),
            jax.ShapeDtypeStruct((wide, units), BF16),
            jax.ShapeDtypeStruct((wide, units), BF16),
            jax.ShapeDtypeStruct((units, wide), BF16),
        )
        + extra_shape,
        in_specs=[hbm] * 5,
        out_specs=(vmem, hbm, hbm, hbm, hbm) + extra_specs,
        scratch_shapes=[
            pltpu.VMEM((every, wide), BF16),
            pltpu.VMEM((every, wide), BF16),
            pltpu.VMEM((wide, units), BF16),
            pltpu.VMEM((wide, units), BF16),
            pltpu.VMEM((units, wide), BF16),
            pltpu.VMEM((every, units), BF16),
            pltpu.VMEM((every, units), BF16),
            pltpu.VMEM((every, units), BF16),
            pltpu.VMEM((every, wide), BF16),
            pltpu.VMEM((NZ, rows, wide), BF16),
            pltpu.VMEM((NZ - 1, rows, wide), BF16),
            pltpu.VMEM((NC, rows, wide), BF16),
            dma((4,)),
            dma((NZ, NC)),
            dma((NC,)),
            dma((3,)),
            dma((3,)),
            dma((NZ - 1,)),
            dma((NZ - 1,)),
            dma((NZ, NC)),
            dma((NZ,)),
            dma((NZ,)),
            dma((NZ,)),
            dma((NZ - 1,)),
        ]
        + down_scratch,
        compiler_params=pltpu.CompilerParams(
            collective_id=collective_id, has_side_effects=True, vmem_limit_bytes=63 << 20
        ),
    )(h, wg, wu, wd, cot)


def forward_kernel(nx, b_rows, names, *refs):
    r = types.SimpleNamespace(**dict(zip(names, refs)))
    y, z, x, c = place()
    other = 1 - c
    sib, ypeer = {"c": other}, {"y": 1 - y}
    xpeers = [(x + i + 1) % nx for i in range(nx - 1)]
    planes = [{"x": xp} for xp in xpeers] + [ypeer]
    cross = [{"z": (z + k + 1) % NZ, "c": other} for k in range(NZ - 1)]
    inner = (z > 0) & (z < NZ - 1)
    rows, wide = r.tok.shape
    shard = r.a.shape[0]
    key_width = r.kv_out.shape[1] // 2
    q_width = r.q_out.shape[1]
    qkv_width = q_width + 2 * key_width
    units = r.grad_d.shape[0]
    fs = units // (2 * nx)
    down_rows = r.d.shape[0]
    greet(line_peers(z, c) + cross + planes)
    ao, guo, co = r.ao, r.guo, r.co

    def down_at(yq, xq, cols):
        first = pl.multiple_of((yq * nx + xq) * down_rows, 8)
        return r.do.at[pl.ds(first, down_rows), cols]

    def remote_order(k):
        step = k + 1
        return (z + step // NC) % NZ, (c + step) % NC

    half = wide // 2
    parts = [pl.ds(0, half), pl.ds(half, half)]
    locals_ = [
        pltpu.make_async_copy(r.a, ao.at[y, z, x, c], r.s_local.at[0]),
        pltpu.make_async_copy(r.d, down_at(y, x, pl.ds(0, wide)), r.s_local.at[1]),
        pltpu.make_async_copy(r.tok, co.at[z, c], r.s_local.at[2]),
    ]
    for copy in locals_:
        copy.start()
    wires = Wires(r.send_sems)

    def both_ways(src, dst, sem):
        for peer in planes:
            wires.send(src, dst, sem, peer)

    def relay(ref, sem, peers):
        wires.arrived(ref, sem, sib)
        for peer in peers:
            wires.send(ref, ref, sem, peer)

    own_slot, own_sem = ao.at[y, z, x, c], r.ra.at[y, z, x, c]
    wires.send(r.a, own_slot, own_sem, {"z": jnp.minimum(z + 1, NZ - 1)}, lambda: z < NZ - 1)
    wires.send(r.a, own_slot, own_sem, {"z": jnp.maximum(z - 1, 0)}, lambda: z > 0)
    both_ways(r.a, own_slot, own_sem)
    wires.send(r.a, own_slot, own_sem, sib)
    line = LineGather(wires, r.tok, co, r.rc, z, c)

    def block(zq, cq):
        return pl.ds(pl.multiple_of((zq * NC + cq) * rows, rows), rows)

    hv = r.hv

    def send_own(i):
        here = hv.at[block(z, c)]
        device = (
            {"z": jnp.minimum(z + 1, NZ - 1)},
            {"z": jnp.maximum(z - 1, 0)},
            {"c": other},
        )[i]
        return remote(here, here, r.h_send.at[i], r.h_recv.at[z, c], device)

    def relay_attn(yq, xq, zq, peers):
        slot, sem = ao.at[yq, zq, xq, c], r.ra.at[yq, zq, xq, c]
        wires.arrived(slot, sem, sib)
        for peer in peers:
            wires.send(slot, slot, sem, peer)
        wires.send(slot, slot, sem, sib)

    def attention(gs, us, gu, weights, tail, first_in, qs, os, mid, s_in):
        loads = [
            pltpu.make_async_copy(r.g, gs, s_in.at[0]),
            pltpu.make_async_copy(r.u, us, s_in.at[1]),
        ]
        for copy in loads:
            copy.start()
        for m, (copy, ref) in enumerate(zip(loads, (gs, us))):
            copy.wait()
            for zq, cq, run, first in segments(nx, fs):
                gu[zq, cq, m, :, run : run + fs] = ref[:, first : first + fs]
        keep = pltpu.make_async_copy(gu.at[z, c], guo.at[:, y, z, x, c], r.s_local.at[3])
        keep.start()
        for k in range(NZ - 1):
            zq = line_order(z, k)
            slot, sem = ao.at[y, zq, x, c], r.ra.at[y, zq, x, c]
            wires.arrived(slot, sem, sib)
            onward = jnp.where(zq < z, jnp.minimum(z + 1, NZ - 1), jnp.maximum(z - 1, 0))
            wires.send(slot, slot, sem, {"z": onward}, lambda: inner)
            both_ways(slot, slot, sem)
            wires.send(slot, slot, sem, sib)
        mark = len(wires.started)
        for k in range(NZ * NC - 1):
            zp, cp = remote_order(k)
            wires.send(
                gu.at[zp, cp], guo.at[:, y, z, x, c], r.rt.at[z, c], {"z": zp, "c": cp}
            )
        block_sends = wires.started[mark:]
        del wires.started[mark:]
        line.begin()
        for zq in range(NZ):
            for xp in xpeers:
                relay_attn(y, xp, zq, [ypeer] if zq < NZ // 2 else [])
            relay_attn(1 - y, x, zq, planes[:-1] if zq >= NZ // 2 else [])
        for h in range(2):
            both_ways(r.d.at[:, parts[h]], down_at(y, x, parts[h]), r.rd.at[h, y, x])
        for xp in xpeers:
            for zq in range(NZ):
                relay_attn(1 - y, xp, zq, [])
        locals_[0].wait()
        for yq in range(2):
            for zq in range(NZ):
                for xq in range(nx):
                    wires.arrived(ao.at[yq, zq, xq, other], r.ra.at[yq, zq, xq, other], sib)

        def fetch(first, width):
            return pltpu.make_async_copy(
                ao.at[:, :, :, :, :, pl.ds(first, width)],
                weights.at[:, :, :, :, :, pl.ds(0, width)],
                s_in.at[0],
            )

        tail_copy = pltpu.make_async_copy(
            ao.at[:, :, :, :, :, pl.ds(qkv_width + wide, HD)], tail, s_in.at[1]
        )
        tail_copy.start()
        fetch(0, qkv_width).start()
        x32 = r.x[...].astype(F32)
        tail_copy.wait()
        lane = lax.broadcasted_iota(jnp.int32, (16, HD), 1)
        row = lax.broadcasted_iota(jnp.int32, (16, HD), 0)
        pick = (lane == row).astype(F32).astype(BF16)
        flat_tail = tail[...].reshape(-1, HD)
        gains = dot_nt(pick, flat_tail)
        gain_one, gain_two = gains[0:1], gains[1:2]
        low = lax.broadcasted_iota(jnp.int32, (8, HD), 1) < HD // 2
        pieces = []
        tops = [
            tail[yq, zq, xq, cq, 0:8].astype(F32)
            for yq in range(2)
            for zq in range(NZ)
            for xq in range(nx)
            for cq in range(NC)
        ]
        for i in range(0, len(tops), 2):
            pieces.append(jnp.where(low, pltpu.roll(tops[i], HD // 2, 1), tops[i + 1])[0:1])
        bias = jnp.concatenate(pieces, axis=1)
        rescale = lax.rsqrt(jnp.mean(x32 * x32, axis=-1, keepdims=True) + EPS)
        first_in[...] = (x32 * rescale * gain_one).astype(BF16)
        fetch(0, qkv_width).wait()

        def turn(value):
            return value * r.turn_c[...] - pltpu.roll(value, HD // 2, 1) * r.turn_s[...]

        kv_own = pl.ds(pl.multiple_of(y * rows, rows), rows)
        pre = dot(first_in[...], weights[:, :, :, :, :, q_width:].reshape(wide, 2 * key_width))
        pre = pre + bias[:, q_width:]
        kv_heads = key_width // HD
        for i in range(2 * kv_heads):
            value = pre[:, i * HD : (i + 1) * HD]
            if i < kv_heads:
                value = turn(value)
            r.kvs[kv_own, i * HD : (i + 1) * HD] = value.astype(BF16)
        wires.send(r.kvs.at[kv_own], r.kvs.at[kv_own], r.s_kv, ypeer)
        pre = dot(first_in[...], weights[:, :, :, :, :, :q_width].reshape(wide, q_width))
        pre = pre + bias[:, :q_width]
        heads = q_width // HD
        for i in range(heads):
            cols = slice(i * HD, (i + 1) * HD)
            qs[:, cols] = turn(pre[:, cols]).astype(BF16)
        fetch(qkv_width, wide).start()
        for k in range(NZ * NC - 1):
            zp, cp = remote_order(k)
            wires.arrived(guo.at[:, y, zp, x, cp], r.rt.at[zp, cp], sib)
        keep.wait()
        for m in range(2):
            plane = guo.at[m, y, :, x]
            both_ways(plane, plane, r.rw.at[m, y, x])
        kv_other = r.kvs.at[pl.ds(pl.multiple_of((1 - y) * rows, rows), rows)]
        wires.arrived(kv_other, r.s_kv, ypeer)
        saves = [
            pltpu.make_async_copy(qs, r.q_out, s_in.at[1]),
            pltpu.make_async_copy(r.kvs, r.kv_out, s_in.at[2]),
            pltpu.make_async_copy(os, r.o_out, s_in.at[3]),
            pltpu.make_async_copy(mid, r.mid_out, s_in.at[4]),
        ]
        saves[0].start()
        saves[1].start()
        scale = HD ** (-0.5)
        group = heads // kv_heads
        for kv_head in range(kv_heads):
            k_cols = pl.ds(kv_head * HD, HD)
            v_cols = pl.ds(key_width + kv_head * HD, HD)

            def head(i, carry):
                cols = pl.ds(pl.multiple_of((kv_head * group + i) * HD, HD), HD)
                scores = dot_nt(qs[:, cols], r.kvs[:, k_cols]) * scale
                scores = jnp.where(r.mask[...] > 0, scores, MASKED)
                exponent = jnp.exp(scores - jnp.max(scores, axis=-1, keepdims=True))
                probs = exponent / jnp.sum(exponent, axis=-1, keepdims=True)
                os[:, cols] = dot(probs.astype(BF16), r.kvs[:, v_cols]).astype(BF16)
                return carry

            lax.fori_loop(0, group, head, 0)
            if kv_head == 0:
                line.event(0)
                for xp in xpeers:
                    relay(down_at(y, xp, parts[0]), r.rd.at[0, y, xp], [ypeer])
                    relay(down_at(y, xp, parts[1]), r.rd.at[1, y, xp], [])
                relay(down_at(1 - y, x, parts[1]), r.rd.at[1, 1 - y, x], planes[:-1])
                relay(down_at(1 - y, x, parts[0]), r.rd.at[0, 1 - y, x], [])
        saves[2].start()
        fetch(qkv_width, wide).wait()
        for_out = weights[:, :, :, :, :, :wide].reshape(q_width, wide)
        middle = x32 + dot(os[...], for_out)
        mid[...] = middle
        saves[3].start()
        rescale_two = lax.rsqrt(jnp.mean(middle * middle, axis=-1, keepdims=True) + EPS)
        hv[block(z, c)] = (middle * rescale_two * gain_two).astype(BF16)
        pl.when(z < NZ - 1)(send_own(0).start)
        pl.when(z > 0)(send_own(1).start)
        send_own(2).start()
        wires.finish(block_sends)
        for copy in saves:
            copy.wait()

    block_shape = (shard, units)
    grid = (2, NZ, nx, NC)
    pl.run_scoped(
        attention,
        pltpu.VMEM(r.g.shape, BF16),
        pltpu.VMEM(r.u.shape, BF16),
        pltpu.VMEM((NZ, NC, 2) + block_shape, BF16),
        pltpu.VMEM(grid + (shard, qkv_width), BF16),
        pltpu.VMEM(grid + (shard, HD), BF16),
        pltpu.VMEM((rows, wide), BF16),
        pltpu.VMEM((rows, q_width), BF16),
        pltpu.VMEM((rows, q_width), BF16),
        pltpu.VMEM((rows, wide), F32),
        pltpu.SemaphoreType.DMA((5,)),
    )

    def feed_forward(cv, wgv, wuv, wdv, av, dgv, duv, part, ob, *half_own):
        def arrival(zq, cq):
            here = hv.at[block(zq, cq)]
            return remote(here, here, r.h_send.at[0], r.h_recv.at[zq, cq], sib)

        def onward(k):
            zq = line_order(z, k)
            here = hv.at[block(zq, c)]
            device = {
                "z": jnp.where(zq < z, jnp.minimum(z + 1, NZ - 1), jnp.maximum(z - 1, 0))
            }
            return remote(here, here, r.h_on.at[k], r.h_recv.at[zq, c], device)

        def to_sibling(k):
            zq = line_order(z, k)
            here = hv.at[block(zq, c)]
            return remote(here, here, r.h_sib.at[k], r.h_recv.at[zq, c], sib)

        def take(k):
            arrival(line_order(z, k), c).wait_recv()
            pl.when(inner)(onward(k).start)
            to_sibling(k).start()

        line.event(1)
        for xp in xpeers:
            relay(guo.at[0, y, :, xp], r.rw.at[0, y, xp], [ypeer])
        relay(guo.at[1, 1 - y, :, x], r.rw.at[1, 1 - y, x], planes[:-1])
        for copy in locals_[1:]:
            copy.wait()
        take(0)
        pl.when(inner)(lambda: take(1))

        def load_cot(zq, cq):
            return pltpu.make_async_copy(co.at[zq, cq], cv.at[block(zq, cq)], r.s_cot.at[zq, cq])

        load_cot(z, c).start()
        line.sibling(z)
        load_cot(z, other).start()
        for xp in xpeers:
            relay(guo.at[1, y, :, xp], r.rw.at[1, y, xp], [])
        relay(guo.at[0, 1 - y, :, x], r.rw.at[0, 1 - y, x], [])
        for xp in xpeers:
            for h in range(2):
                relay(guo.at[h, 1 - y, :, xp], r.rw.at[h, 1 - y, xp], [])
                relay(down_at(1 - y, xp, parts[h]), r.rd.at[h, 1 - y, xp], [])
        loads = [
            pltpu.make_async_copy(guo.at[0], wgv, r.s_load.at[0]),
            pltpu.make_async_copy(guo.at[1], wuv, r.s_load.at[1]),
            pltpu.make_async_copy(r.do, wdv, r.s_load.at[2]),
        ]
        for copy in loads:
            copy.start()
        line.event(2)

        def output(zq):
            here = pl.ds(pl.multiple_of(zq * rows, rows), rows)
            return pltpu.make_async_copy(ob.at[c], r.out_own.at[here], r.s_ob)

        def output_over(zq):
            here = pl.ds(pl.multiple_of(zq * rows, rows), rows)
            return remote(ob.at[other], r.out_sib.at[here], r.o_send.at[zq], r.o_recv.at[zq], sib)

        def partial_over(zq):
            return remote(
                part.at[block(zq, other)], r.sib.at[zq], r.p_send.at[zq], r.p_recv.at[zq], sib
            )

        def partial_home(zq):
            j = (z - zq + NZ) % NZ - 1
            return remote(
                part.at[block(zq, c)], r.ring.at[j], r.r_send.at[zq], r.r_recv.at[j], {"z": zq}
            )

        piece = rows // 8

        def combine(zq):
            remote(r.sib.at[zq], r.sib.at[zq], r.p_send.at[0], r.p_recv.at[zq], sib).wait_recv()

            def step(i, carry):
                here = pl.ds(pl.multiple_of((zq * NC + c) * rows + i * piece, piece), piece)
                there = pl.ds(pl.multiple_of(i * piece, piece), piece)
                total = part[here].astype(F32) + r.sib[zq, there].astype(F32)
                part[here] = total.astype(BF16)
                return carry

            lax.fori_loop(0, 8, step, 0)

        def place_of(k):
            late = jnp.where(k == 2, line_order(z, 2), line_order(z, 0))
            return jnp.where(k == 0, z, jnp.where(k == 1, line_order(z, 1), late))

        def flat(ref, low, high):
            return ref[:, :, :, :, :, low:high].reshape(wide, high - low)

        def pair(k, carry):
            zq = place_of(k)

            @pl.when(k == 0)
            def _():
                for i in range(NZ - 1):
                    near = line_order(z, i)
                    load_cot(near, c).start()
                    line.sibling(near)
                    load_cot(near, other).start()

            def one(j, carry):
                cq = (other + j) % NC
                here = block(zq, cq)

                @pl.when((k == 0) & (j == 0))
                def _():
                    for copy in loads:
                        copy.wait()

                @pl.when(j == 0)
                def _():
                    arrival(zq, cq).wait_recv()

                @pl.when((k == 0) & (j == 1))
                def _():
                    pl.when(jnp.logical_not(inner))(lambda: take(1))
                    pl.when(inner)(lambda: take(2))

                @pl.when((k == 1) & (j == 1) & jnp.logical_not(inner))
                def _():
                    take(2)

                load_cot(zq, cq).wait()
                for low, high in TILES:
                    high = units if high is None else high
                    gate = dot(hv[here], flat(wgv, low, high))
                    up = dot(hv[here], flat(wuv, low, high))
                    grad = dot_nt(cv[here], wdv[low:high])
                    sig = jax.nn.sigmoid(gate)
                    act = gate * sig
                    av[here, low:high] = (act * up).astype(BF16)
                    duv[here, low:high] = (grad * act).astype(BF16)
                    dgv[here, low:high] = (
                        grad * up * (sig * (1.0 + gate * (1.0 - sig)))
                    ).astype(BF16)

                @pl.when((k > 0) & (j == 1))
                def _():
                    output(zq).wait()

                @pl.when((k > 0) & (j == 0))
                def _():
                    output_over(place_of(k - 1)).wait_send()

                ob[cq] = dot(av[here], wdv[...]).astype(BF16)
                pl.when(j == 1)(output(zq).start)
                pl.when(j == 0)(output_over(zq).start)
                part[here] = (
                    dot_nt(dgv[here], flat(wgv, 0, units)) + dot_nt(duv[here], flat(wuv, 0, units))
                ).astype(BF16)
                pl.when(j == 0)(partial_over(zq).start)
                return carry

            lax.fori_loop(0, NC, one, 0)

            @pl.when(k > 0)
            def _():
                combine(zq)
                partial_home(zq).start()

            return carry

        lax.fori_loop(0, NZ, pair, 0)
        last = place_of(NZ - 1)
        step_d = wide // 6

        def down_grad(t, carry):
            cols = pl.ds(pl.multiple_of(t * step_d, step_d), step_d)
            wdv[:, cols] = dot_tn(av[...], cv[:, cols]).astype(BF16)
            return carry

        lax.fori_loop(0, 6, down_grad, 0)
        outs = [
            pltpu.make_async_copy(wdv, r.grad_d, r.s_out.at[0]),
            pltpu.make_async_copy(wgv, r.grad_g, r.s_out.at[1]),
            pltpu.make_async_copy(wuv, r.grad_u, r.s_out.at[2]),
        ]
        outs[0].start()

        def term(yq, xq, cols):
            first = pl.multiple_of((yq * nx + xq) * down_rows, 8)
            return r.grad_d.at[pl.ds(first, down_rows), cols]

        along_x, along_y = ("x", nx, x), ("y", 2, y)
        by_x = PlaneScatter(
            wires,
            lambda xq, yq: term(yq, xq, parts[0]),
            along_x,
            along_y,
            (r.xr1, half_own[0], r.xr2, r.xs1, r.xsl, r.xs2),
        )
        by_y = PlaneScatter(
            wires,
            lambda yq, xq: term(yq, xq, parts[1]),
            along_y,
            along_x,
            (r.yr1, half_own[1], r.yr2, r.ys1, r.ysl, r.ys2),
        )
        step_g = wide // NZ

        def turned(src, dst, first, last):
            def step(t, carry):
                cols = pl.ds(pl.multiple_of(t * step_g, step_g), step_g)
                value = dot_tn(hv[:, cols], src[...]).astype(BF16)
                here = pl.ds((t % 2) * (NZ // 2), NZ // 2)
                dst[t // 2, here] = value.reshape((NZ // 2, nx, NC, shard, units))
                return carry

            lax.fori_loop(first, last, step, 0)

        turned(dgv, wgv, 0, 1)
        outs[0].wait()
        by_x.begin()
        by_y.begin()
        turned(dgv, wgv, 1, NZ)
        outs[1].start()
        turned(duv, wuv, 0, NZ // 2)
        by_x.relay()
        by_y.relay()
        turned(duv, wuv, NZ // 2, NZ)
        outs[2].start()
        combine(z)
        for j in range(NZ - 1):
            here = r.ring.at[j]
            remote(here, here, r.r_send.at[0], r.r_recv.at[j], sib).wait_recv()

        def final(i, carry):
            here = pl.ds(pl.multiple_of((z * NC + c) * rows + i * piece, piece), piece)
            there = pl.ds(pl.multiple_of(i * piece, piece), piece)
            total = part[here].astype(F32)
            for j in range(NZ - 1):
                total = total + r.ring[j, there].astype(F32)
            r.dh[there] = total
            return carry

        lax.fori_loop(0, 8, final, 0)
        by_x.finish(r.down_out.at[:, parts[0]])
        by_y.finish(r.down_out.at[:, parts[1]])
        wires.finish()
        pl.when(z < NZ - 1)(send_own(0).wait_send)
        pl.when(z > 0)(send_own(1).wait_send)
        send_own(2).wait_send()
        for k in range(NZ - 1):
            pl.when(inner)(onward(k).wait_send)
            to_sibling(k).wait_send()
            partial_home(line_order(z, k)).wait_send()
        for zq in range(NZ):
            partial_over(zq).wait_send()
        output(last).wait()
        output_over(last).wait_send()
        for zq in range(NZ):
            there = r.out_sib.at[pl.ds(zq * rows, rows)]
            remote(there, there, r.o_send.at[0], r.o_recv.at[zq], sib).wait_recv()
        for copy in outs[1:]:
            copy.wait()

    every = NZ * NC * rows
    pl.run_scoped(
        feed_forward,
        pltpu.VMEM((every, wide), BF16),
        pltpu.VMEM(grid + block_shape, BF16),
        pltpu.VMEM(grid + block_shape, BF16),
        pltpu.VMEM((units, wide), BF16),
        pltpu.VMEM((every, units), BF16),
        pltpu.VMEM((every, units), BF16),
        pltpu.VMEM((every, units), BF16),
        pltpu.VMEM((every, wide), BF16),
        pltpu.VMEM((NC, rows, wide), BF16),
        pltpu.VMEM((2, down_rows, half), BF16),
        pltpu.VMEM((nx, down_rows, half), BF16),
    )


def forward(ny, nx, b_rows, a, g, u, d, tok, x, mask, turn_c, turn_s, widths, collective_id):
    hbm = pl.BlockSpec(memory_space=pl.ANY)
    vmem = pl.BlockSpec(memory_space=pltpu.VMEM)
    dma = pltpu.SemaphoreType.DMA
    rows, wide = tok.shape
    q_width, key_width = widths
    shard = a.shape[0]
    units = g.shape[1] // (NZ * NC)
    grid = (ny, NZ, nx, NC)
    half_slot = (d.shape[0], wide // 2)
    ins = dict(a=a, g=g, u=u, d=d, tok=tok, x=x, mask=mask, turn_c=turn_c, turn_s=turn_s)
    outs = dict(
        ao=(grid + a.shape, BF16),
        guo=((2,) + grid + (shard, units), BF16),
        do=((units, wide), BF16),
        co=((NZ, NC, rows, wide), BF16),
        q_out=((rows, q_width), BF16),
        kv_out=((2 * rows, 2 * key_width), BF16),
        o_out=((rows, q_width), BF16),
        mid_out=((rows, wide), F32),
        out_own=((NZ * rows, wide), BF16),
        out_sib=((NZ * rows, wide), BF16),
        grad_g=(grid + (shard, units), BF16),
        grad_u=(grid + (shard, units), BF16),
        grad_d=((units, wide), BF16),
        dh=((rows, wide), F32),
        down_out=(d.shape, BF16),
    )
    plane_x = plane_scratch(half_slot, nx, ny)
    plane_y = plane_scratch(half_slot, ny, nx)
    one_plane = (nx - 1) * 2 + 1 + nx + (nx - 1)
    sends = 3 + nx + 3 * (nx + 2) + 7 + 9 + 4 * (2 * nx - 1) + 4 * nx + 6 * nx
    scratch = dict(
        send_sems=dma((sends + 2 * one_plane + 24,)),
        s_local=dma((4,)),
        ra=dma(grid),
        rt=dma((NZ, NC)),
        rw=dma((2, ny, nx)),
        rd=dma((2, ny, nx)),
        rc=dma((NZ, NC)),
        s_kv=dma,
        kvs=pltpu.VMEM((2 * rows, 2 * key_width), BF16),
        hv=pltpu.VMEM((NZ * NC * rows, wide), BF16),
        sib=pltpu.VMEM((NZ, rows, wide), BF16),
        ring=pltpu.VMEM((NZ - 1, rows, wide), BF16),
        s_load=dma((3,)),
        s_cot=dma((NZ, NC)),
        s_ob=dma,
        s_out=dma((3,)),
        h_send=dma((3,)),
        h_on=dma((NZ - 1,)),
        h_sib=dma((NZ - 1,)),
        h_recv=dma((NZ, NC)),
        p_send=dma((NZ,)),
        p_recv=dma((NZ,)),
        r_send=dma((NZ,)),
        r_recv=dma((NZ - 1,)),
        o_send=dma((NZ,)),
        o_recv=dma((NZ,)),
        xr1=plane_x[0],
        xr2=plane_x[2],
        xs1=plane_x[3],
        xsl=plane_x[4],
        xs2=plane_x[5],
        yr1=plane_y[0],
        yr2=plane_y[2],
        ys1=plane_y[3],
        ysl=plane_y[4],
        ys2=plane_y[5],
    )
    names = tuple(ins) + tuple(outs) + tuple(scratch)
    results = pl.pallas_call(
        lambda *refs: forward_kernel(nx, b_rows, names, *refs),
        name="forward",
        out_shape=tuple(jax.ShapeDtypeStruct(*shape) for shape in outs.values()),
        in_specs=[hbm] * 5 + [vmem] * 4,
        out_specs=(hbm,) * 13 + (vmem,) * 2,
        scratch_shapes=list(scratch.values()),
        compiler_params=pltpu.CompilerParams(
            collective_id=collective_id, has_side_effects=True, vmem_limit_bytes=67_043_328
        ),
    )(*ins.values())
    return types.SimpleNamespace(**dict(zip(outs, results)))


def plane_peers(nx, y, x):
    return [{"x": (x + i + 1) % nx} for i in range(nx - 1)] + [{"y": 1 - y}]


def last_scatter_kernel(nx, widths, grads, gate, up, down, result, *rest):
    y, z, x, c = place()
    outs, rest = rest[: len(widths)], rest[len(widths) :]
    gate_out, up_out, down_out, result_out, rest = rest[:4] + (rest[4:],)
    send_sems, blocks, own, sib, line_sum, line_in = rest[:6]
    s_block, s_keep, s_own, s_sib, s_line = rest[6:11]
    half_x, half_y = rest[11:17], rest[17:23]
    gate_bufs, up_bufs, gu = rest[23:29], rest[29:35], rest[35]
    left_bufs, right_bufs, line_bufs = rest[36:42], rest[42:48], rest[48:56]
    cross = [{"z": (z + k + 1) % NZ, "c": 1 - c} for k in range(NZ - 1)]
    greet(line_peers(z, c) + cross + plane_peers(nx, y, x))
    wires = Wires(send_sems)
    along_x, along_y = ("x", nx, x), ("y", 2, y)
    gate_plane = PlaneScatter(
        wires, lambda xq, yq: gate.at[yq, :, xq], along_x, along_y, gate_bufs
    )
    up_plane = PlaneScatter(wires, lambda yq, xq: up.at[yq, :, xq], along_y, along_x, up_bufs)
    cols = down.shape[-1] // 2
    left, right = pl.ds(0, cols), pl.ds(cols, cols)
    left_plane = PlaneScatter(
        wires, lambda xq, yq: down.at[yq, xq, :, left], along_x, along_y, left_bufs
    )
    right_plane = PlaneScatter(
        wires, lambda yq, xq: down.at[yq, xq, :, right], along_y, along_x, right_bufs
    )
    line = LineScatter(wires, result, line_bufs, z, c)
    gate_plane.begin()
    up_plane.begin()
    line.begin()
    n = NZ // 2
    halves = [pl.ds(0, n), pl.ds(n, n)]

    def load(h, yq):
        return pltpu.make_async_copy(
            grads.at[yq, halves[h], :, c], own.at[yq, halves[h]], s_own.at[h, yq]
        )

    for h in range(2):
        for yq in range(2):
            wires.send(
                grads.at[yq, halves[h], :, 1 - c],
                sib.at[yq, halves[h]],
                s_sib.at[h, yq],
                {"c": 1 - c},
            )
            load(h, yq).start()

    def combine(h):
        for yq in range(2):
            load(h, yq).wait()
            wires.arrived(sib.at[yq, halves[h]], s_sib.at[h, yq], {"c": 1 - c})
            for i in range(n):
                zq = h * n + i
                total_into(own.at[yq, zq], [own.at[yq, zq], sib.at[yq, zq]])

    by_x = PlaneScatter(
        wires, lambda xq, yq: own.at[yq, halves[0], xq], along_x, along_y, half_x, True
    )
    by_y = PlaneScatter(
        wires, lambda yq, xq: own.at[yq, halves[1], xq], along_y, along_x, half_y, True
    )
    combine(0)
    by_x.begin()
    combine(1)
    by_y.begin()
    line.hop(3)
    left_plane.begin()
    right_plane.begin()
    line.hop(2)
    gate_plane.relay()
    up_plane.relay()
    line.hop(1)
    by_x.relay()
    by_y.relay()
    left_plane.relay()
    right_plane.relay()
    gate_plane.finish(gu.at[0])
    up_plane.finish(gu.at[1])
    keep = pltpu.make_async_copy(gu.at[:, z, c], blocks.at[z, c], s_keep)
    keep.start()
    for k in range(NZ * NC - 1):
        step = k + 1
        zp, cp = (z + step // NC) % NZ, (c + step) % NC
        wires.send(gu.at[:, zp, cp], blocks.at[z, c], s_block.at[z, c], {"z": zp, "c": cp})
    by_x.finish(line_sum.at[halves[0]])
    by_y.finish(line_sum.at[halves[1]])
    for k in range(NZ - 1):
        zp = (z + k + 1) % NZ
        wires.send(line_sum.at[zp], line_in.at[NZ - 2 - k], s_line.at[NZ - 2 - k], {"z": zp})
    line.finish(result_out)
    left_plane.finish(down_out.at[:, left])
    right_plane.finish(down_out.at[:, right])
    keep.wait()
    for k in range(NZ * NC - 1):
        step = k + 1
        zp, cp = (z + step // NC) % NZ, (c + step) % NC
        wires.arrived(blocks.at[zp, cp], s_block.at[zp, cp], {"c": 1 - c})
    fs = blocks.shape[-1] // (2 * nx)
    for m, out in enumerate((gate_out, up_out)):
        for zq, cq, run, first in segments(nx, fs):
            out[:, first : first + fs] = blocks[zq, cq, m, :, run : run + fs].astype(F32)
    for k in range(NZ - 1):
        wires.arrived(line_in.at[k], s_line.at[k], {"c": 1 - c})
    first = 0
    for out, width in zip(outs, widths):
        columns = slice(first, first + width)
        total = line_sum[z, :, columns].astype(F32)
        for k in range(NZ - 1):
            total = total + line_in[k, :, columns].astype(F32)
        out[...] = total
        first += width
    wires.finish()


def last_scatter(ny, nx, grads, widths, gate, up, down, result, collective_id):
    hbm = pl.BlockSpec(memory_space=pl.ANY)
    vmem = pl.BlockSpec(memory_space=pltpu.VMEM)
    rows, width = grads.shape[4:]
    block = gate.shape[4:]
    slot = (NZ // 2, rows, width)
    gate_slot = (NZ, NC) + block
    down_slot = (down.shape[2], down.shape[3] // 2)
    sends = 4 + 7 + NZ - 1 + 3 * ((nx - 1) * 2 + 1 + nx + (nx - 1)) + NZ + 2 * (NZ - 1)
    spread = block[1] * NZ * NC
    shapes = [(rows, w) for w in widths] + [(rows, spread)] * 2
    shapes += [down.shape[2:], result.shape[2:]]
    return pl.pallas_call(
        lambda *refs: last_scatter_kernel(nx, widths, *refs),
        name="last_scatter",
        out_shape=tuple(jax.ShapeDtypeStruct(shape, F32) for shape in shapes),
        in_specs=[hbm] * 5,
        out_specs=(vmem,) * len(shapes),
        scratch_shapes=[
            pltpu.SemaphoreType.DMA((sends,)),
            pltpu.VMEM((NZ, NC, 2) + block, BF16),
            pltpu.VMEM((ny, NZ, nx, rows, width), BF16),
            pltpu.VMEM((ny, NZ, nx, rows, width), BF16),
            pltpu.VMEM((NZ, rows, width), BF16),
            pltpu.VMEM((NZ - 1, rows, width), BF16),
            pltpu.SemaphoreType.DMA((NZ, NC)),
            pltpu.SemaphoreType.DMA,
            pltpu.SemaphoreType.DMA((2, 2)),
            pltpu.SemaphoreType.DMA((2, 2)),
            pltpu.SemaphoreType.DMA((NZ - 1,)),
        ]
        + plane_scratch(slot, nx, ny, True)
        + plane_scratch(slot, ny, nx, True)
        + plane_scratch(gate_slot, nx, ny)
        + plane_scratch(gate_slot, ny, nx)
        + [pltpu.VMEM((2,) + gate_slot, BF16)]
        + plane_scratch(down_slot, nx, ny)
        + plane_scratch(down_slot, ny, nx)
        + line_scratch(result.shape[2:]),
        compiler_params=pltpu.CompilerParams(
            collective_id=collective_id, has_side_effects=True, vmem_limit_bytes=60 << 20
        ),
    )(grads, gate, up, down, result)


def back_kernel(
    nx,
    key_width,
    b_rows,
    gate,
    up,
    ao,
    kept,
    given,
    mid,
    branch,
    tokens,
    gain,
    attn,
    query,
    kv,
    mask,
    turn_c,
    turn_s,
    gain_term,
    out_q,
    out_k,
    out_v,
    out_o,
    out_tail,
    out_gate,
    out_up,
    out_in,
    out_ring,
    send_sems,
    weights,
    term_o,
    term_q,
    sib_o,
    sib_q,
    line_sum,
    line_in,
    blocks,
    gu,
    d_attn,
    d_qkv,
    d_kv,
    kv_send,
    kv_recv,
    first_in,
    s_weights,
    s_sib,
    s_line,
    s_block,
    s_kv,
    result,
    s_result,
    s_ring,
    s_toward,
    *bufs,
):
    y, z, x, c = place()
    sib = {"c": 1 - c}
    cross = [{"z": (z + k + 1) % NZ, "c": 1 - c} for k in range(NZ - 1)]
    greet(line_peers(z, c) + cross + plane_peers(nx, y, x))
    wires = Wires(send_sems)
    along_x, along_y = ("x", nx, x), ("y", 2, y)
    gate_plane = PlaneScatter(
        wires, lambda xq, yq: gate.at[yq, :, xq], along_x, along_y, bufs[0:6]
    )
    up_plane = PlaneScatter(wires, lambda yq, xq: up.at[yq, :, xq], along_y, along_x, bufs[6:12])
    gate_plane.begin()
    up_plane.begin()
    rows, wide = branch.shape
    q_width = query.shape[1]
    qkv_width = q_width + 2 * key_width
    heads, kv_heads = q_width // HD, key_width // HD
    n = NZ // 2
    halves = [pl.ds(0, n), pl.ds(n, n)]
    tile = n * nx * NC * out_q.shape[0]
    shard = out_q.shape[0]

    def fetch(first, width):
        return pltpu.make_async_copy(
            ao.at[:, :, pl.ds(first, width)], weights.at[:, :, pl.ds(0, width)], s_weights
        )

    fetch(qkv_width, wide).start()

    def fill(term, yq, h, first, value):
        value = value.reshape((n, nx, NC, shard, value.shape[1]))
        term[yq, halves[h], :, :, :, first : first + value.shape[4]] = value.astype(BF16)

    def over(i, term, other, yq, h):
        wires.send(
            term.at[yq, halves[h], :, 1 - c],
            other.at[yq, halves[h]],
            s_sib.at[i, yq, h],
            sib,
        )

    def combine(i, term, other):
        for h in range(2):
            for yq in range(2):
                here = other.at[yq, halves[h]]
                wires.arrived(here, s_sib.at[i, yq, h], sib)
                for zq in range(h * n, h * n + n):
                    for xq in range(nx):
                        mine = term.at[yq, zq, xq, c]
                        total_into(mine, [mine, other.at[yq, zq, xq]], True)

    def planes(term, first):
        return (
            PlaneScatter(
                wires,
                lambda xq, yq: term.at[yq, halves[0], xq, c],
                along_x,
                along_y,
                bufs[first : first + 6],
                True,
            ),
            PlaneScatter(
                wires,
                lambda yq, xq: term.at[yq, halves[1], xq, c],
                along_y,
                along_x,
                bufs[first + 6 : first + 12],
                True,
            ),
        )

    for yq in range(2):
        for h in range(2):
            i = yq * 2 + h
            fill(term_o, yq, h, 0, dot_tn(attn[:, i * tile : (i + 1) * tile], branch[...]))
            over(0, term_o, sib_o, yq, h)

    def landing(sign, k):
        return NZ if k == NZ - 2 else (k if sign > 0 else 2 + k)

    def inside(sign, k):
        return z + k < NZ if sign > 0 else z >= k

    def toward(sign, k):
        at = landing(sign, k - 1)
        return remote(
            result.at[int(sign < 0)],
            out_ring.at[at],
            s_toward.at[2 * (k - 1) + (sign < 0)],
            s_ring.at[at],
            {"z": jnp.clip(z + sign, 0, NZ - 1)},
        )

    def landed(at):
        here = out_ring.at[at]
        remote(here, here, s_toward.at[0], s_ring.at[at], sib).wait_recv()

    def hop(k):
        for sign in (1, -1):
            behind = z > 0 if sign > 0 else z < NZ - 1
            held = result.at[int(sign < 0)]
            if k < NZ - 1:
                pl.when(inside(sign, k + 1))(toward(sign, k + 1).wait_send)

            @pl.when(inside(sign, k))
            def _():
                first = jnp.clip(z + sign * k, 0, NZ - 1) * rows
                here = pl.ds(pl.multiple_of(first, rows), rows)
                loads = [
                    pltpu.make_async_copy(kept.at[here], held, s_result.at[0]),
                    pltpu.make_async_copy(given.at[here], first_in, s_result.at[1]),
                ]
                for copy in loads:
                    copy.start()
                for copy in loads:
                    copy.wait()
                total_into(held, [held, first_in])

            if k < NZ - 1:

                @pl.when(inside(sign, k) & behind)
                def _():
                    at = landing(sign, k)
                    landed(at)
                    copy = pltpu.make_async_copy(out_ring.at[at], result.at[2], s_result.at[0])
                    copy.start()
                    copy.wait()
                    total_into(held, [held, result.at[2]])

            pl.when(inside(sign, k))(toward(sign, k).start)

    hop(3)
    fetch(qkv_width, wide).wait()
    for_out = weights[:, :, :wide].reshape(q_width, wide)
    d_attn[...] = dot_nt(branch[...], for_out).astype(BF16)
    fetch(0, qkv_width).start()
    d_kv[...] = jnp.zeros_like(d_kv)
    scale = HD ** (-0.5)

    def turn_back(value):
        return value * turn_c[...] + pltpu.roll(value, HD // 2, 1) * turn_s[...]

    group = heads // kv_heads
    for kv_head in range(kv_heads):
        k_cols = pl.ds(kv_head * HD, HD)
        v_cols = pl.ds(key_width + kv_head * HD, HD)

        def head(i, carry):
            cols = pl.ds(pl.multiple_of((kv_head * group + i) * HD, HD), HD)
            q_h, do_h = query[:, cols], d_attn[:, cols]
            scores = jnp.where(mask[...] > 0, dot_nt(q_h, kv[:, k_cols]) * scale, MASKED)
            exponent = jnp.exp(scores - jnp.max(scores, axis=-1, keepdims=True))
            probs = exponent / jnp.sum(exponent, axis=-1, keepdims=True)
            d_probs = dot_nt(do_h, kv[:, v_cols])
            inner = jnp.sum(probs * d_probs, axis=-1, keepdims=True)
            d_scores = (probs * (d_probs - inner)).astype(BF16)
            d_qkv[:, cols] = turn_back(dot(d_scores, kv[:, k_cols]) * scale).astype(BF16)
            d_kv[:, k_cols] += dot_tn(d_scores, q_h) * scale
            d_kv[:, v_cols] += dot_tn(probs.astype(BF16), do_h)
            return carry

        lax.fori_loop(0, group, head, 0)
        if kv_head == 0:
            hop(2)

    other_rows = pl.ds(pl.multiple_of((1 - y) * rows, rows), rows)
    own_rows = pl.ds(pl.multiple_of(y * rows, rows), rows)
    kv_send[...] = d_kv[other_rows].astype(BF16)
    hop(1)
    gate_plane.relay()
    wires.send(kv_send, kv_recv, s_kv, {"y": 1 - y})
    up_plane.relay()
    combine(0, term_o, sib_o)
    o_planes = planes(term_o, 12)
    for plane in o_planes:
        plane.begin()
    x32 = tokens[...].astype(F32)
    rescale = lax.rsqrt(jnp.mean(x32 * x32, axis=-1, keepdims=True) + EPS)
    first_in[...] = (x32 * rescale * gain[...]).astype(BF16)
    wires.arrived(kv_recv, s_kv, {"y": 1 - y})
    for kv_head in range(2 * kv_heads):
        cols = pl.ds(kv_head * HD, HD)
        total = d_kv[own_rows, cols] + kv_recv[:, cols].astype(F32)
        if kv_head < kv_heads:
            total = turn_back(total)
        d_qkv[:, pl.ds(q_width + kv_head * HD, HD)] = total.astype(BF16)
    gate_plane.finish(gu.at[0])
    up_plane.finish(gu.at[1])
    keep_block = pltpu.make_async_copy(gu.at[:, z, c], blocks.at[z, c], s_block.at[z, c])
    keep_block.start()
    for k in range(NZ * NC - 1):
        step = k + 1
        zp, cp = (z + step // NC) % NZ, (c + step) % NC
        wires.send(gu.at[:, zp, cp], blocks.at[z, c], s_block.at[z, c], {"z": zp, "c": cp})
    fetch(0, qkv_width).wait()
    for_in = weights[...].reshape(wide, qkv_width)
    d_first = dot_nt(d_qkv[...], for_in)
    normed = x32 * rescale
    scaled = d_first * gain[...]
    d_x = rescale * (scaled - normed * jnp.mean(scaled * normed, axis=-1, keepdims=True))
    out_in[...] = (mid[...] + d_x).astype(BF16)
    first_term = (d_first * normed).astype(BF16)
    lane = lax.broadcasted_iota(jnp.int32, (rows, HD), 1)
    pick_one = (lane == 0).astype(F32).astype(BF16)
    pick_two = (lane == 1).astype(F32).astype(BF16)
    bias_sum = jnp.sum(d_qkv[...].astype(F32), axis=0, keepdims=True)
    top = lax.broadcasted_iota(jnp.int32, (shard, HD), 0) == 0
    wide_bias = jnp.concatenate([bias_sum, bias_sum[:, :HD]], axis=1)
    for yq in range(2):
        for h in range(2):
            i = yq * 2 + h
            cols = slice(i * tile, (i + 1) * tile)
            fill(term_q, yq, h, 0, dot_tn(first_in[:, cols], d_qkv[...]))
            tail = dot_tn(first_term[:, cols], pick_one) + dot_tn(gain_term[:, cols], pick_two)
            for zi in range(n):
                for xq in range(nx):
                    for cq in range(NC):
                        part = ((zi * nx + xq) * NC + cq) * shard
                        place_at = i * (tile // shard) + (zi * nx + xq) * NC + cq
                        first = place_at * b_rows
                        base = (first // HD) * HD
                        bias = wide_bias[:, base : base + HD]
                        bias = pltpu.roll(
                            jnp.broadcast_to(bias, (8, HD)), (HD // 2 - (first - base)) % HD, 1
                        )[:1]
                        keep = lax.broadcasted_iota(jnp.int32, (shard, HD), 1) >= HD // 2
                        mixed = tail[part : part + shard] + jnp.where(top & keep, bias, 0.0)
                        term_q[yq, h * n + zi, xq, cq, :, qkv_width:] = mixed.astype(BF16)
            over(1, term_q, sib_q, yq, h)
    combine(1, term_q, sib_q)
    q_planes = planes(term_q, 24)
    for plane in q_planes:
        plane.begin()
    for plane in o_planes:
        plane.relay()
    for plane in q_planes:
        plane.relay()

    def along_line(i, first, width, pair):
        cols = pl.ds(first, width)
        pair[0].finish(line_sum.at[halves[0], :, cols])
        pair[1].finish(line_sum.at[halves[1], :, cols])
        for k in range(NZ - 1):
            zp, j = (z + k + 1) % NZ, NZ - 2 - k
            wires.send(
                line_sum.at[zp, :, cols], line_in.at[j, :, cols], s_line.at[i, j], {"z": zp}
            )

    q_all = qkv_width + HD
    along_line(0, q_all, wide, o_planes)
    along_line(1, 0, q_all, q_planes)
    keep_block.wait()
    for k in range(NZ * NC - 1):
        step = k + 1
        zp, cp = (z + step // NC) % NZ, (c + step) % NC
        wires.arrived(blocks.at[zp, cp], s_block.at[zp, cp], sib)
    fs = blocks.shape[-1] // (2 * nx)
    for m, out in enumerate((out_gate, out_up)):
        for zq, cq, run, first in segments(nx, fs):
            out[:, first : first + fs] = blocks[zq, cq, m, :, run : run + fs]

    def last(i, out, first, width):
        if i is not None:
            begin, size = (q_all, wide) if i == 0 else (0, q_all)
            for j in range(NZ - 1):
                wires.arrived(line_in.at[j, :, pl.ds(begin, size)], s_line.at[i, j], sib)
        columns = slice(first, first + width)
        total = line_sum[z, :, columns].astype(F32)
        for j in range(NZ - 1):
            total = total + line_in[j, :, columns].astype(F32)
        out[...] = total

    last(0, out_o, q_all, wide)
    last(1, out_q, 0, q_width)
    last(None, out_k, q_width, key_width)
    last(None, out_v, q_width + key_width, key_width)
    last(None, out_tail, qkv_width, HD)
    for sign in (1, -1):
        pl.when(z > 0 if sign > 0 else z < NZ - 1)(lambda: landed(landing(sign, 0)))
        pl.when(inside(sign, 1))(toward(sign, 1).wait_send)
    wires.finish()


def back(ny, nx, b_rows, gate, up, ao, kept, given, args, collective_id):
    hbm = pl.BlockSpec(memory_space=pl.ANY)
    vmem = pl.BlockSpec(memory_space=pltpu.VMEM)
    mid, branch, tokens, gain, attn, query, kv, mask, turn_c, turn_s, gain_term = args
    dma = pltpu.SemaphoreType.DMA
    shard = ao.shape[1]
    block = gate.shape[4:]
    rows, wide = branch.shape
    q_width = query.shape[1]
    key_width = kv.shape[1] // 2
    qkv_width = q_width + 2 * key_width
    q_all = qkv_width + HD
    spread = block[1] * NZ * NC
    one_plane = (nx - 1) * 2 + 1 + nx + (nx - 1)
    sends = 3 * one_plane + 8 + 1 + 7 + 3 * (NZ - 1)
    slot_o, slot_q = (NZ // 2, shard, wide), (NZ // 2, shard, q_all)
    gate_slot = (NZ, NC) + block
    place_all = (ny, NZ, nx, NC, shard)
    shapes = [(shard, q_width), (shard, key_width), (shard, key_width), (shard, wide), (shard, HD)]
    return pl.pallas_call(
        lambda *refs: back_kernel(nx, key_width, b_rows, *refs),
        name="back",
        cost_estimate=pl.CostEstimate(
            flops=100_000_000_000, bytes_accessed=100_000_000, transcendentals=0
        ),
        out_shape=tuple(jax.ShapeDtypeStruct(shape, F32) for shape in shapes)
        + (jax.ShapeDtypeStruct((shard, spread), BF16),) * 2
        + (jax.ShapeDtypeStruct((rows, wide), BF16),)
        + (jax.ShapeDtypeStruct((NZ + 1, rows, wide), BF16),),
        in_specs=[hbm] * 5 + [vmem] * len(args),
        out_specs=(vmem,) * 8 + (hbm,),
        scratch_shapes=[
            dma((sends,)),
            pltpu.VMEM((ny * NZ * nx * NC, shard, qkv_width), BF16),
            pltpu.VMEM(place_all + (wide,), BF16),
            pltpu.VMEM(place_all + (q_all,), BF16),
            pltpu.VMEM((ny, NZ, nx, shard, wide), BF16),
            pltpu.VMEM((ny, NZ, nx, shard, q_all), BF16),
            pltpu.VMEM((NZ, shard, q_all + wide), BF16),
            pltpu.VMEM((NZ - 1, shard, q_all + wide), BF16),
            pltpu.VMEM((NZ, NC, 2) + block, BF16),
            pltpu.VMEM((2,) + gate_slot, BF16),
            pltpu.VMEM((rows, q_width), BF16),
            pltpu.VMEM((rows, qkv_width), BF16),
            pltpu.VMEM((2 * rows, 2 * key_width), F32),
            pltpu.VMEM((rows, 2 * key_width), BF16),
            pltpu.VMEM((rows, 2 * key_width), BF16),
            pltpu.VMEM((rows, wide), BF16),
            dma,
            dma((2, 2, 2)),
            dma((2, NZ - 1)),
            dma((NZ, NC)),
            dma,
            pltpu.VMEM((NZ - 1, rows, wide), BF16),
            dma((2,)),
            dma((NZ + 1,)),
            dma((2 * (NZ - 1),)),
        ]
        + plane_scratch(gate_slot, nx, ny)
        + plane_scratch(gate_slot, ny, nx)
        + plane_scratch(slot_o, nx, ny, True)
        + plane_scratch(slot_o, ny, nx, True)
        + plane_scratch(slot_q, nx, ny, True)
        + plane_scratch(slot_q, ny, nx, True),
        compiler_params=pltpu.CompilerParams(
            collective_id=collective_id, has_side_effects=True, vmem_limit_bytes=67_043_328
        ),
    )(gate, up, ao, kept, given, *args)


def make_body(ny, nx):
    def fused_layer(packed, x, seg_all, gate, up, down, grad_out, widths, b_rows):
        tok_rows = x.shape[0]
        length = seg_all.shape[0]
        seq_place = lax.axis_index("y")
        tok_pos = seq_place * tok_rows + jnp.arange(tok_rows)
        cos_tok, sin_tok = tables(tok_pos)
        all_pos = jnp.arange(length)
        seg_tok = lax.dynamic_slice(seg_all, (seq_place * tok_rows,), (tok_rows,))
        allowed = (tok_pos[:, None] >= all_pos[None, :]) & (seg_tok[:, None] == seg_all[None, :])
        mask = allowed.astype(F32)
        turn_c = jnp.concatenate([cos_tok, cos_tok], axis=1)
        turn_s = jnp.concatenate([sin_tok, -sin_tok], axis=1)
        made = forward(
            ny, nx, b_rows, packed, gate, up, down, grad_out, x, mask, turn_c, turn_s, widths, 0
        )
        lanes = sum(widths) + widths[1] + x.shape[1]
        tail = made.ao[..., lanes : lanes + 2].astype(F32).reshape(-1, 2)
        gain_one, gain_two = tail[:, 0], tail[:, 1]
        middle = made.mid_out
        rescale_two = lax.rsqrt(jnp.mean(middle * middle, axis=-1, keepdims=True) + EPS)
        normed_two = middle * rescale_two
        scaled = made.dh * gain_two
        grad_mid = grad_out.astype(F32) + rescale_two * (
            scaled - normed_two * jnp.mean(scaled * normed_two, axis=-1, keepdims=True)
        )
        args = (
            grad_mid,
            grad_mid.astype(BF16),
            x,
            gain_one[None],
            made.o_out,
            made.q_out,
            made.kv_out,
            mask,
            turn_c,
            turn_s,
            (made.dh * normed_two).astype(BF16),
        )
        outs = back(
            ny,
            nx,
            b_rows,
            made.grad_g,
            made.grad_u,
            made.ao.reshape((-1,) + packed.shape),
            made.out_own,
            made.out_sib,
            args,
            1,
        )
        grad_q, grad_k, grad_v, grad_o, tail_sum, grad_gate_w, grad_up_w, grad_in, ring = outs
        z_place = lax.axis_index("z")
        first_row = z_place * tok_rows
        out_sum = jnp.where(z_place > 0, ring[0].astype(F32), 0.0)
        out_sum += jnp.where(z_place < NZ - 1, ring[2].astype(F32), 0.0)
        for half in (made.out_own, made.out_sib):
            out_sum += lax.dynamic_slice_in_dim(half, first_row, tok_rows).astype(F32)
        return (
            (middle + out_sum).astype(BF16)[None],
            grad_in[None],
            tail_sum[:, 0],
            grad_q,
            grad_k,
            grad_v,
            tail_sum[0, HD // 2 : HD // 2 + b_rows],
            grad_o,
            tail_sum[:, 1],
            grad_gate_w.astype(F32),
            grad_up_w.astype(F32),
            made.down_out.astype(F32),
        )

    def body(
        inputs,
        segment_ids,
        attn_gain,
        q_weight,
        k_weight,
        v_weight,
        qkv_bias,
        o_weight,
        mlp_gain,
        gate_weight,
        up_weight,
        down_weight,
        cotangent,
    ):
        tok_rows = inputs.shape[1]
        hidden_in = inputs[0].astype(F32)
        grad_out = cotangent[0]
        seg_all = segment_ids[0]
        length = seg_all.shape[0]
        seq_place = lax.axis_index("y")
        tok_pos = seq_place * tok_rows + jnp.arange(tok_rows)
        cos_tok, sin_tok = tables(tok_pos)
        query_width = q_weight.shape[1]
        key_width = k_weight.shape[1]
        kv_heads = key_width // HD
        q_heads = query_width // HD
        group = q_heads // kv_heads

        g_rows = attn_gain.shape[0]
        b_rows = qkv_bias.shape[0]
        qkv_width = query_width + 2 * key_width
        extra = jnp.concatenate(
            [
                attn_gain[:, None],
                mlp_gain[:, None],
                jnp.zeros((g_rows, HD // 2 - 2), BF16),
                jnp.broadcast_to(qkv_bias[None], (g_rows, b_rows)),
                jnp.zeros((g_rows, HD // 2 - b_rows), BF16),
            ],
            axis=1,
        )
        packed = jnp.concatenate([q_weight, k_weight, v_weight, o_weight, extra], axis=1)
        fused = g_rows % 16 == 0 and b_rows == HD // 2
        if fused:
            return fused_layer(
                packed,
                inputs[0],
                seg_all,
                gate_weight,
                up_weight,
                down_weight,
                grad_out,
                (query_width, key_width),
                b_rows,
            )
        attn_all, columns_all, down_all, grad_out_all = weight_gather(
            ny,
            nx,
            packed,
            gate_weight,
            up_weight,
            down_weight,
            grad_out,
            0,
        )
        full = attn_all.reshape(-1, packed.shape[1])
        full_qkv = full[:, :qkv_width]
        full_out = full[:, qkv_width : qkv_width + query_width]
        tail = attn_all[..., qkv_width + query_width :].astype(F32)
        gain_one = tail[..., 0].reshape(-1)
        gain_two = tail[..., 1].reshape(-1)
        bias = tail[..., 0, HD // 2 : HD // 2 + b_rows].reshape(-1)
        width = gate_weight.shape[1] // (NZ * NC)
        full_gate = columns_all[0].reshape(-1, width)
        full_up = columns_all[1].reshape(-1, width)
        full_down = down_all.reshape(width, -1)
        grad_out_all = grad_out_all.reshape(-1, grad_out.shape[1])

        rescale_one = lax.rsqrt(jnp.mean(hidden_in * hidden_in, axis=-1, keepdims=True) + EPS)
        normed_one = hidden_in * rescale_one
        input_one = (normed_one * gain_one).astype(BF16)
        qkv_pre = dot(input_one, full_qkv) + bias
        query = rotate(qkv_pre[:, :query_width], cos_tok, sin_tok).astype(BF16)
        key = rotate(qkv_pre[:, query_width : query_width + key_width], cos_tok, sin_tok)
        kv = jnp.concatenate([key, qkv_pre[:, query_width + key_width :]], axis=1).astype(BF16)
        kv_all = lax.all_gather(kv, "y", axis=0, tiled=True)
        key_heads = kv_all[:, :key_width].reshape(length, kv_heads, HD)
        value_heads = kv_all[:, key_width:].reshape(length, kv_heads, HD)
        query_heads = query.reshape(tok_rows, kv_heads, group, HD)
        score_scale = HD ** (-0.5)
        all_pos = jnp.arange(length)
        seg_tok = lax.dynamic_slice(seg_all, (seq_place * tok_rows,), (tok_rows,))
        allowed = (tok_pos[:, None] >= all_pos[None, :]) & (seg_tok[:, None] == seg_all[None, :])
        scores = (
            jnp.einsum("qkgd,pkd->kgqp", query_heads, key_heads, preferred_element_type=F32)
            * score_scale
        )
        masked = jnp.where(allowed[None, None], scores, MASKED)
        row_max = jnp.max(masked, axis=-1, keepdims=True)
        exponent = jnp.exp(masked - row_max)
        row_total = jnp.sum(exponent, axis=-1, keepdims=True)
        probs = exponent / row_total
        probs_low = probs.astype(BF16)
        mixture = jnp.einsum("kgqp,pkd->qkgd", probs_low, value_heads, preferred_element_type=F32)
        attn_tok = mixture.astype(BF16).reshape(tok_rows, query_width)
        middle = hidden_in + dot(attn_tok, full_out)

        rescale_two = lax.rsqrt(jnp.mean(middle * middle, axis=-1, keepdims=True) + EPS)
        normed_two = middle * rescale_two
        input_two = (normed_two * gain_two).astype(BF16)
        by_shard = (ny, NZ, nx, NC, g_rows, width)
        grad_input_two, out_part, part_gate, part_up, *downs = mlp(
            ny, nx, False, input_two, full_gate, full_up, full_down, grad_out_all, 1
        )
        grad_gain_two, grad_mid = norm_back(grad_input_two, normed_two, rescale_two, gain_two)
        grad_mid = grad_mid + grad_out.astype(F32)
        grad_branch = grad_mid.astype(BF16)
        grad_attn = dot_nt(grad_branch, full_out).astype(BF16)
        grad_heads = grad_attn.reshape(tok_rows, kv_heads, group, HD)
        grad_probs = jnp.einsum(
            "qkgd,pkd->kgqp", grad_heads, value_heads, preferred_element_type=F32
        )
        inner_sum = jnp.sum(probs * grad_probs, axis=-1, keepdims=True)
        grad_scores = (probs * (grad_probs - inner_sum)).astype(BF16)
        grad_query = (
            jnp.einsum("kgqp,pkd->qkgd", grad_scores, key_heads, preferred_element_type=F32)
            * score_scale
        ).reshape(tok_rows, query_width)
        grad_key = (
            jnp.einsum("kgqp,qkgd->pkd", grad_scores, query_heads, preferred_element_type=F32)
            * score_scale
        ).reshape(length, key_width)
        grad_value = jnp.einsum(
            "kgqp,qkgd->pkd", probs_low, grad_heads, preferred_element_type=F32
        ).reshape(length, key_width)
        grad_kv = jnp.concatenate([grad_key, grad_value], axis=1).astype(BF16)
        other = lax.dynamic_slice(
            grad_kv, ((1 - seq_place) * tok_rows, 0), (tok_rows, 2 * key_width)
        )
        own = lax.dynamic_slice(grad_kv, (seq_place * tok_rows, 0), (tok_rows, 2 * key_width))
        swapped = lax.ppermute(other, "y", [(0, 1), (1, 0)])
        grad_kv_tok = own.astype(F32) + swapped.astype(F32)
        grad_query_pre = rotate(grad_query, cos_tok, -sin_tok).astype(BF16)
        grad_key_pre = rotate(grad_kv_tok[:, :key_width], cos_tok, -sin_tok).astype(BF16)
        grad_value_pre = grad_kv_tok[:, key_width:].astype(BF16)
        grad_qkv = jnp.concatenate([grad_query_pre, grad_key_pre, grad_value_pre], axis=1)
        grad_qkv_sum = jnp.sum(grad_qkv.astype(F32), axis=0)
        grad_input_one = dot_nt(grad_qkv, full_qkv)
        grad_gain_one, grad_first = norm_back(grad_input_one, normed_one, rescale_one, gain_one)
        grad_total = grad_mid + grad_first
        shards = ny * NZ * nx * NC
        tail_grads = jnp.concatenate(
            [
                grad_gain_one[:, None],
                grad_gain_two[:, None],
                jnp.broadcast_to(
                    grad_qkv_sum.reshape(shards, 1, b_rows), (shards, g_rows, b_rows)
                ).reshape(-1, b_rows),
                jnp.zeros((shards * g_rows, HD - 2 - b_rows), F32),
            ],
            axis=1,
        )
        grad_attn_w = jnp.concatenate(
            [
                dot_tn(input_one, grad_qkv).astype(BF16),
                dot_tn(attn_tok, grad_branch).astype(BF16),
                tail_grads.astype(BF16),
            ],
            axis=1,
        )
        widths = (query_width, key_width, key_width, query_width, HD)
        pieces = (NZ, NC, tok_rows // 32, 32, hidden_in.shape[1])
        outs = last_scatter(
            ny,
            nx,
            grad_attn_w.reshape((ny, NZ, nx, NC, g_rows, -1)),
            widths,
            part_gate.reshape(by_shard),
            part_up.reshape(by_shard),
            downs[0].reshape((ny, nx) + down_weight.shape),
            out_part.reshape(pieces),
            3,
        )
        grad_q, grad_k, grad_v, grad_o, tail_sum = outs[:5]
        grad_gate_w, grad_up_w, grad_down_w, out_sum = outs[5:]
        output = (middle + out_sum.reshape(middle.shape)).astype(BF16)[None]
        return (
            output,
            grad_total.astype(BF16)[None],
            tail_sum[:, 0],
            grad_q,
            grad_k,
            grad_v,
            tail_sum[0, 2 : 2 + b_rows],
            grad_o,
            tail_sum[:, 1],
            grad_gate_w,
            grad_up_w,
            grad_down_w,
        )

    return body


def solution(mesh):
    ny = mesh.shape["seq"]
    nx = mesh.shape["fsdp"] // (NZ * NC)
    grid = Mesh(mesh.devices.reshape(ny, NZ, nx, NC), ALL)
    tokens = P(("z", "x", "c"), "y", None)
    rows = P(ALL, None)
    vec = P(ALL)
    return jax.shard_map(
        make_body(ny, nx),
        mesh=grid,
        in_specs=(
            tokens,
            P(("z", "x", "c"), None),
            vec,
            rows,
            rows,
            rows,
            vec,
            rows,
            vec,
            rows,
            rows,
            rows,
            tokens,
        ),
        out_specs=(tokens, tokens, vec, rows, rows, rows, vec, rows, vec, rows, rows, rows),
        check_vma=False,
    )
```

```python
import types

import jax
import jax.numpy as jnp
from jax import lax
from jax.experimental import pallas as pl
from jax.experimental.pallas import tpu as pltpu
from jax.sharding import Mesh, PartitionSpec as P

HD = 128
EPS = 1e-06
ROPE_BASE = 1000000.0
MASKED = -1e30
NZ = 4
NC = 2
ALL = ("y", "z", "x", "c")
TP = ("z", "c")
DP = ("y", "x")
F32 = jnp.float32
BF16 = jnp.bfloat16


def tables(positions):
    freq = ROPE_BASE ** (-jnp.arange(0, HD, 2).astype(F32) / HD)
    angle = positions.astype(F32)[:, None] * freq[None, :]
    return (jnp.cos(angle), jnp.sin(angle))


def rotate(values, cosine, sine):
    count = values.shape[0]
    split = values.reshape(count, -1, HD)
    half = HD // 2
    first = split[..., :half]
    second = split[..., half:]
    cos_b = cosine[:, None, :]
    sin_b = sine[:, None, :]
    turned = jnp.concatenate(
        [first * cos_b - second * sin_b, second * cos_b + first * sin_b], axis=-1
    )
    return turned.reshape(count, -1)


def dot(a, b):
    return jnp.dot(a, b, preferred_element_type=F32)


def dot_nt(a, b):
    return lax.dot_general(a, b, (((1,), (1,)), ((), ())), preferred_element_type=F32)


def dot_tn(a, b):
    return lax.dot_general(a, b, (((0,), (0,)), ((), ())), preferred_element_type=F32)


def norm_back(grad_normed, normed, rescale, gain_vec):
    grad_gain = jnp.sum(grad_normed * normed, axis=0)
    scaled = grad_normed * gain_vec
    grad_x = rescale * (scaled - normed * jnp.mean(scaled * normed, axis=-1, keepdims=True))
    return (grad_gain, grad_x)


class Wires:
    def __init__(self, sems):
        self.sems = sems
        self.used = 0
        self.started = []

    def send(self, src, dst, recv_sem, device, cond=None):
        copy = pltpu.make_async_remote_copy(
            src_ref=src,
            dst_ref=dst,
            send_sem=self.sems.at[self.used],
            recv_sem=recv_sem,
            device_id=device,
            device_id_type=pl.DeviceIdType.MESH,
        )
        if cond is None:
            copy.start()
        else:
            pl.when(cond())(copy.start)
        self.started.append((still(src), self.used, cond))
        self.used += 1

    def arrived(self, dst, recv_sem, device):
        pltpu.make_async_remote_copy(
            src_ref=dst,
            dst_ref=dst,
            send_sem=self.sems.at[0],
            recv_sem=recv_sem,
            device_id=device,
            device_id_type=pl.DeviceIdType.MESH,
        ).wait_recv()

    def finish(self, sent=None):
        for src, used, cond in self.started if sent is None else sent:
            sem = self.sems.at[used]
            src = taken(*src)
            copy = pltpu.make_async_remote_copy(
                src_ref=src,
                dst_ref=src,
                send_sem=sem,
                recv_sem=sem,
                device_id={"c": 1 - lax.axis_index("c")},
                device_id_type=pl.DeviceIdType.MESH,
            )
            if cond is None:
                copy.wait_send()
            else:
                pl.when(cond())(copy.wait_send)


def still(ref):
    steps = []
    for step in getattr(ref, "transforms", ()):
        steps.append([i.size if isinstance(i, pl.Slice) else None for i in step.indices])
    return getattr(ref, "ref", ref), steps


def taken(view, steps):
    for step in steps:
        view = view.at[tuple(0 if size is None else pl.ds(0, size) for size in step)]
    return view


def line_order(z, k):
    if k == 0:
        return z + 1 - 2 * (z % 2)
    if k == 1:
        return 2 - z // 2
    return 3 - 3 * (z // 2)


def greet(peers):
    barrier = pltpu.get_barrier_semaphore()
    for peer in peers:
        pl.semaphore_signal(
            barrier, inc=1, device_id=peer, device_id_type=pl.DeviceIdType.MESH
        )
    pl.semaphore_wait(barrier, len(peers))


def place():
    return tuple(lax.axis_index(name) for name in ALL)


def line_peers(z, c):
    peers = [{"c": 1 - c}]
    for k in range(NZ - 1):
        peers.append({"z": (z + k + 1) % NZ})
    return peers


class LineGather:
    def __init__(self, wires, own, out, recv, z, c):
        self.wires, self.own, self.out, self.recv, self.z, self.c = wires, own, out, recv, z, c

    def begin(self):
        w, z, c = self.wires, self.z, self.c
        dst, sem = self.out.at[z, c], self.recv.at[z, c]
        w.send(self.own, dst, sem, {"z": jnp.minimum(z + 1, NZ - 1)}, lambda: z < NZ - 1)
        w.send(self.own, dst, sem, {"z": jnp.maximum(z - 1, 0)}, lambda: z > 0)
        w.send(self.own, dst, sem, {"c": 1 - c})

    def event(self, k, cond=None):
        w, z, c = self.wires, self.z, self.c
        zq = line_order(z, k)
        slot, sem = self.out.at[zq, c], self.recv.at[zq, c]
        if cond is None:
            w.arrived(slot, sem, {"c": 1 - c})
        else:
            pl.when(cond())(lambda: w.arrived(slot, sem, {"c": 1 - c}))
        onward = jnp.where(zq < z, jnp.minimum(z + 1, NZ - 1), jnp.maximum(z - 1, 0))
        inner = lambda: (z > 0) & (z < NZ - 1)
        both = inner if cond is None else lambda: inner() & cond()
        w.send(slot, slot, sem, {"z": onward}, both)
        w.send(slot, slot, sem, {"c": 1 - c}, cond)

    def sibling(self, zq):
        w, c = self.wires, self.c
        w.arrived(self.out.at[zq, 1 - c], self.recv.at[zq, 1 - c], {"c": 1 - c})


def segments(nx, fs):
    for yq in range(2):
        for zq in range(NZ):
            for xq in range(nx):
                for cq in range(NC):
                    first = (((yq * NZ + zq) * nx + xq) * NC + cq) * fs
                    yield zq, cq, (yq * nx + xq) * fs, first


def weight_gather_kernel(
    nx, a, g, u, d, tok, ao, guo, do, co, gu, send_sems, local_sems, ra, rt, rw, rd, rc
):
    y, z, x, c = place()
    sib = {"c": 1 - c}
    ypeer = {"y": 1 - y}
    xpeers = [(x + i + 1) % nx for i in range(nx - 1)]
    planes = [{"x": xp} for xp in xpeers] + [ypeer]
    cross = [{"z": (z + k + 1) % NZ, "c": 1 - c} for k in range(NZ - 1)]
    greet(line_peers(z, c) + cross + planes)
    locals_ = [
        pltpu.make_async_copy(a, ao.at[y, z, x, c], local_sems.at[0]),
        pltpu.make_async_copy(d, do.at[y, x], local_sems.at[1]),
        pltpu.make_async_copy(tok, co.at[z, c], local_sems.at[2]),
    ]
    keep = pltpu.make_async_copy(gu.at[z, c], guo.at[:, y, z, x, c], local_sems.at[3])
    for copy in locals_:
        copy.start()
    wires = Wires(send_sems)

    def both_ways(src, dst, sem):
        for peer in planes:
            wires.send(src, dst, sem, peer)

    own_slot, own_sem = ao.at[y, z, x, c], ra.at[y, z, x, c]
    wires.send(a, own_slot, own_sem, {"z": jnp.minimum(z + 1, NZ - 1)}, lambda: z < NZ - 1)
    wires.send(a, own_slot, own_sem, {"z": jnp.maximum(z - 1, 0)}, lambda: z > 0)
    both_ways(a, own_slot, own_sem)
    wires.send(a, own_slot, own_sem, sib)
    fs = gu.shape[-1] // (2 * nx)
    for m, shard in enumerate((g, u)):
        for zq, cq, run, first in segments(nx, fs):
            gu[zq, cq, m, :, run : run + fs] = shard[:, first : first + fs]
    keep.start()
    for k in range(NZ - 1):
        zq = line_order(z, k)
        slot, sem = ao.at[y, zq, x, c], ra.at[y, zq, x, c]
        wires.arrived(slot, sem, sib)
        onward = jnp.where(zq < z, jnp.minimum(z + 1, NZ - 1), jnp.maximum(z - 1, 0))
        wires.send(slot, slot, sem, {"z": onward}, lambda: (z > 0) & (z < NZ - 1))
        both_ways(slot, slot, sem)
        wires.send(slot, slot, sem, sib)

    for k in range(NZ * NC - 1):
        step = k + 1
        zp, cp = (z + step // NC) % NZ, (c + step) % NC
        wires.send(
            gu.at[zp, cp], guo.at[:, y, z, x, c], rt.at[z, c], {"z": zp, "c": cp}
        )
    line = LineGather(wires, tok, co, rc, z, c)
    line.begin()
    half = d.shape[1] // 2
    parts = [pl.ds(0, half), pl.ds(half, half)]
    for h in range(2):
        both_ways(d.at[:, parts[h]], do.at[y, x, :, parts[h]], rd.at[h, y, x])

    def relay_attn(yq, xq, zq, peers):
        slot, sem = ao.at[yq, zq, xq, c], ra.at[yq, zq, xq, c]
        wires.arrived(slot, sem, sib)
        for peer in peers:
            wires.send(slot, slot, sem, peer)
        wires.send(slot, slot, sem, sib)

    for zq in range(NZ):
        for xp in xpeers:
            relay_attn(y, xp, zq, [ypeer] if zq < NZ // 2 else [])
        relay_attn(1 - y, x, zq, planes[:-1] if zq >= NZ // 2 else [])

    for k in range(NZ * NC - 1):
        step = k + 1
        zp, cp = (z + step // NC) % NZ, (c + step) % NC
        wires.arrived(guo.at[:, y, zp, x, cp], rt.at[zp, cp], sib)
    keep.wait()
    for m in range(2):
        plane = guo.at[m, y, :, x]
        both_ways(plane, plane, rw.at[m, y, x])
    line.event(0)

    def relay(ref, sem, peers):
        wires.arrived(ref, sem, sib)
        for peer in peers:
            wires.send(ref, ref, sem, peer)

    for xp in xpeers:
        relay(do.at[y, xp, :, parts[0]], rd.at[0, y, xp], [ypeer])
        relay(do.at[y, xp, :, parts[1]], rd.at[1, y, xp], [])
    relay(do.at[1 - y, x, :, parts[1]], rd.at[1, 1 - y, x], planes[:-1])
    relay(do.at[1 - y, x, :, parts[0]], rd.at[0, 1 - y, x], [])
    for xp in xpeers:
        for zq in range(NZ):
            relay_attn(1 - y, xp, zq, [])
    line.event(1)
    for xp in xpeers:
        relay(guo.at[0, y, :, xp], rw.at[0, y, xp], [ypeer])
    relay(guo.at[1, 1 - y, :, x], rw.at[1, 1 - y, x], planes[:-1])
    line.event(2)
    for xp in xpeers:
        relay(guo.at[1, y, :, xp], rw.at[1, y, xp], [])
    relay(guo.at[0, 1 - y, :, x], rw.at[0, 1 - y, x], [])
    for xp in xpeers:
        for h in range(2):
            relay(do.at[1 - y, xp, :, parts[h]], rd.at[h, 1 - y, xp], [])
            relay(guo.at[h, 1 - y, :, xp], rw.at[h, 1 - y, xp], [])
    for zq in range(NZ):
        line.sibling(zq)
    for yq in range(2):
        for zq in range(NZ):
            for xq in range(nx):
                wires.arrived(ao.at[yq, zq, xq, 1 - c], ra.at[yq, zq, xq, 1 - c], sib)
    wires.finish()
    for copy in locals_:
        copy.wait()


def weight_gather(ny, nx, a, g, u, d, tok, collective_id):
    sends = 3 + (nx + 1) + 3 * (nx + 2)
    sends += 7 + 9 + 2 * nx
    sends += 4 * nx + 2 * (nx - 1) + 2 * (nx - 1)
    sends += 2 * nx + 2 * (nx - 1) + 4 * (nx - 1) + 2 * (nx - 1)
    hbm = pl.BlockSpec(memory_space=pl.ANY)
    vmem = pl.BlockSpec(memory_space=pltpu.VMEM)
    grid = (ny, NZ, nx, NC)
    block = g.shape[:1] + (g.shape[1] // (NZ * NC),)
    return pl.pallas_call(
        lambda *refs: weight_gather_kernel(nx, *refs),
        name="weight_gather",
        out_shape=(
            jax.ShapeDtypeStruct(grid + a.shape, BF16),
            jax.ShapeDtypeStruct((2,) + grid + block, BF16),
            jax.ShapeDtypeStruct((ny, nx) + d.shape, BF16),
            jax.ShapeDtypeStruct((NZ, NC) + tok.shape, BF16),
        ),
        in_specs=[hbm, vmem, vmem, hbm, hbm],
        out_specs=(hbm,) * 4,
        scratch_shapes=[
            pltpu.VMEM((NZ, NC, 2) + block, BF16),
            pltpu.SemaphoreType.DMA((sends + 16,)),
            pltpu.SemaphoreType.DMA((4,)),
            pltpu.SemaphoreType.DMA(grid),
            pltpu.SemaphoreType.DMA((NZ, NC)),
            pltpu.SemaphoreType.DMA((2, ny, nx)),
            pltpu.SemaphoreType.DMA((2, ny, nx)),
            pltpu.SemaphoreType.DMA((NZ, NC)),
        ],
        compiler_params=pltpu.CompilerParams(
            collective_id=collective_id, has_side_effects=True
        ),
    )(a, g, u, d, tok)


def total_into(dst, refs, flat=None):
    flat = len(dst.shape) == 2

    def entry(i, carry):
        here = (slice(None), pl.ds(pl.multiple_of(i * 128, 128), 128)) if flat else i
        total = refs[0][here].astype(F32)
        for ref in refs[1:]:
            total = total + ref[here].astype(F32)
        dst[here] = total.astype(dst.dtype)
        return carry

    lax.fori_loop(0, dst.shape[1] // 128 if flat else dst.shape[0], entry, 0)


class PlaneScatter:
    def __init__(self, wires, src, first, second, bufs, loaded=False):
        self.wires, self.src = wires, src
        self.name_a, self.size_a, self.a = first
        self.name_b, self.size_b, self.b = second
        self.r1, self.own, self.r2, self.s1, self.sl, self.s2 = bufs
        self.loaded = loaded

    def mine(self, b):
        return self.src(self.a, b) if self.loaded else self.own.at[b]

    def order(self):
        return [(self.b + i + 1) % self.size_b for i in range(self.size_b)]

    def begin(self):
        for b in self.order():
            for i in range(self.size_a - 1):
                peer, j = (self.a + i + 1) % self.size_a, self.size_a - 2 - i
                self.wires.send(
                    self.src(peer, b), self.r1.at[j, b], self.s1.at[j, b], {self.name_a: peer}
                )
            if not self.loaded:
                self.load(b).start()

    def load(self, b):
        return pltpu.make_async_copy(self.src(self.a, b), self.own.at[b], self.sl.at[b])

    def gathered(self, b):
        if not self.loaded:
            self.load(b).wait()
        for j in range(self.size_a - 1):
            self.wires.arrived(self.r1.at[j, b], self.s1.at[j, b], {self.name_a: self.a})
        return [self.mine(b)] + [self.r1.at[j, b] for j in range(self.size_a - 1)]

    def relay(self):
        for i, b in enumerate(self.order()[:-1]):
            j = self.size_b - 2 - i
            total_into(self.mine(b), self.gathered(b))
            self.wires.send(self.mine(b), self.r2.at[j], self.s2.at[j], {self.name_b: b})

    def finish(self, dst):
        refs = self.gathered(self.b)
        for j in range(self.size_b - 1):
            self.wires.arrived(self.r2.at[j], self.s2.at[j], {self.name_b: self.b})
            refs.append(self.r2.at[j])
        total_into(dst, refs)


def plane_scratch(slot, size_a, size_b, loaded=False):
    own = (1,) * (1 + len(slot)) if loaded else (size_b,) + slot
    return [
        pltpu.VMEM((size_a - 1, size_b) + slot, BF16),
        pltpu.VMEM(own, BF16),
        pltpu.VMEM((size_b - 1,) + slot, BF16),
        pltpu.SemaphoreType.DMA((size_a - 1, size_b)),
        pltpu.SemaphoreType.DMA((size_b,)),
        pltpu.SemaphoreType.DMA((size_b - 1,)),
    ]


class LineScatter:
    def __init__(self, wires, part, bufs, z, c):
        self.wires, self.part, self.z, self.c = wires, part, z, c
        self.own, self.sib, self.left, self.right = bufs[:4]
        self.s_own, self.s_sib, self.s_left, self.s_right = bufs[4:]

    def order(self):
        return [line_order(self.z, k) for k in (2, 1, 0)] + [self.z]

    def load(self, zq):
        return pltpu.make_async_copy(
            self.part.at[zq, self.c], self.own.at[zq], self.s_own.at[zq]
        )

    def begin(self):
        for zq in self.order():
            self.wires.send(
                self.part.at[zq, 1 - self.c],
                self.sib.at[zq],
                self.s_sib.at[zq],
                {"c": 1 - self.c},
            )
            self.load(zq).start()

    def ready(self, zq):
        self.load(zq).wait()
        self.wires.arrived(self.sib.at[zq], self.s_sib.at[zq], {"c": 1 - self.c})

    def hop(self, k):
        z = self.z
        for sign, buf, sems in ((1, self.left, self.s_left), (-1, self.right, self.s_right)):
            target = z + sign * k
            inside = (target < NZ) if sign > 0 else (target >= 0)
            behind = (z > 0) if sign > 0 else (z < NZ - 1)
            target = jnp.clip(target, 0, NZ - 1)
            own, sib = self.own.at[target], self.sib.at[target]

            @pl.when(inside)
            def _():
                self.ready(target)

            if k < NZ - 1:

                @pl.when(inside & behind)
                def _():
                    self.wires.arrived(buf.at[k], sems.at[k], {"z": z})
                    total_into(own, [own, sib, buf.at[k]])

                @pl.when(inside & jnp.logical_not(behind))
                def _():
                    total_into(own, [own, sib])

            else:

                @pl.when(inside)
                def _():
                    total_into(own, [own, sib])

            onward = jnp.clip(z + sign, 0, NZ - 1)
            self.wires.send(own, buf.at[k - 1], sems.at[k - 1], {"z": onward}, lambda: inside)

    def finish(self, dst):
        z = self.z
        self.ready(z)
        own, sib = self.own.at[z], self.sib.at[z]

        @pl.when(z > 0)
        def _():
            self.wires.arrived(self.left.at[0], self.s_left.at[0], {"z": z})

        @pl.when(z < NZ - 1)
        def _():
            self.wires.arrived(self.right.at[0], self.s_right.at[0], {"z": z})

        @pl.when(z == 0)
        def _():
            total_into(dst, [own, sib, self.right.at[0]])

        @pl.when(z == NZ - 1)
        def _():
            total_into(dst, [own, sib, self.left.at[0]])

        @pl.when((z > 0) & (z < NZ - 1))
        def _():
            total_into(dst, [own, sib, self.left.at[0], self.right.at[0]])


def line_scratch(slot):
    return [
        pltpu.VMEM((NZ,) + slot, BF16),
        pltpu.VMEM((NZ,) + slot, BF16),
        pltpu.VMEM((NZ - 1,) + slot, BF16),
        pltpu.VMEM((NZ - 1,) + slot, BF16),
        pltpu.SemaphoreType.DMA((NZ,)),
        pltpu.SemaphoreType.DMA((NZ,)),
        pltpu.SemaphoreType.DMA((NZ - 1,)),
        pltpu.SemaphoreType.DMA((NZ - 1,)),
    ]


TILES = ((0, 640), (640, None))


def remote(src, dst, send_sem, recv_sem, device):
    return pltpu.make_async_remote_copy(
        src_ref=src,
        dst_ref=dst,
        send_sem=send_sem,
        recv_sem=recv_sem,
        device_id=device,
        device_id_type=pl.DeviceIdType.MESH,
    )


def mlp_kernel(
    nx,
    with_down,
    h,
    wg,
    wu,
    wd,
    cot,
    dh,
    out_part,
    grad_g,
    grad_u,
    grad_d,
    *scratch,
):
    if with_down:
        down_out, out_sib, scratch = scratch[0], scratch[1], scratch[2:]
    (
        hv,
        cv,
        wgv,
        wuv,
        wdv,
        av,
        dgv,
        duv,
        part,
        sib,
        ring,
        ob,
        s_load,
        s_cot,
        s_ob,
        s_out,
        h_send,
        h_on,
        h_sib,
        h_recv,
        p_send,
        p_recv,
        r_send,
        r_recv,
    ) = scratch[: 24]
    scratch = scratch[24:]
    if with_down:
        o_send, o_recv, scratch = scratch[0], scratch[1], scratch[2:]
    y, z, x, c = place()
    rows, wide = h.shape
    units = wg.shape[1]
    other = 1 - c
    inner = (z > 0) & (z < NZ - 1)
    greet(line_peers(z, c) + (plane_peers(nx, y, x) if with_down else []))

    def block(zq, cq):
        return pl.ds(pl.multiple_of((zq * NC + cq) * rows, rows), rows)

    loads = [
        pltpu.make_async_copy(h, hv.at[block(z, c)], s_load.at[0]),
        pltpu.make_async_copy(wg, wgv, s_load.at[1]),
        pltpu.make_async_copy(wu, wuv, s_load.at[2]),
        pltpu.make_async_copy(wd, wdv, s_load.at[3]),
    ]

    def load_cot(zq, cq):
        return pltpu.make_async_copy(
            cot.at[block(zq, cq)], cv.at[block(zq, cq)], s_cot.at[zq, cq]
        )

    def send_own(i):
        there = hv.at[block(z, c)]
        device = (
            {"z": jnp.minimum(z + 1, NZ - 1)},
            {"z": jnp.maximum(z - 1, 0)},
            {"c": other},
        )[i]
        return remote(h, there, h_send.at[i], h_recv.at[z, c], device)

    pl.when(z < NZ - 1)(send_own(0).start)
    pl.when(z > 0)(send_own(1).start)
    send_own(2).start()
    for copy in loads[:3]:
        copy.start()
    load_cot(z, c).start()
    loads[3].start()
    load_cot(z, other).start()
    for k in range(NZ - 1):
        for i in range(NC):
            load_cot(line_order(z, k), (c + i) % NC).start()

    def arrival(zq, cq):
        here = hv.at[block(zq, cq)]
        return remote(here, here, h_send.at[0], h_recv.at[zq, cq], {"c": other})

    def onward(k):
        zq = line_order(z, k)
        here = hv.at[block(zq, c)]
        device = {"z": jnp.where(zq < z, jnp.minimum(z + 1, NZ - 1), jnp.maximum(z - 1, 0))}
        return remote(here, here, h_on.at[k], h_recv.at[zq, c], device)

    def to_sibling(k):
        zq = line_order(z, k)
        here = hv.at[block(zq, c)]
        return remote(here, here, h_sib.at[k], h_recv.at[zq, c], {"c": other})

    def take(k):
        arrival(line_order(z, k), c).wait_recv()
        pl.when(inner)(onward(k).start)
        to_sibling(k).start()

    def output(zq, cq):
        if with_down:
            here = pl.ds(pl.multiple_of(zq * rows, rows), rows)
            return pltpu.make_async_copy(ob.at[cq], out_part.at[here], s_ob.at[0])
        return pltpu.make_async_copy(ob.at[cq], out_part.at[block(zq, cq)], s_ob.at[cq])

    def output_over(zq):
        here = pl.ds(pl.multiple_of(zq * rows, rows), rows)
        return remote(
            ob.at[other], out_sib.at[here], o_send.at[zq], o_recv.at[zq], {"c": other}
        )

    def partial_over(zq):
        return remote(
            part.at[block(zq, other)], sib.at[zq], p_send.at[zq], p_recv.at[zq], {"c": other}
        )

    def partial_home(zq):
        j = (z - zq + NZ) % NZ - 1
        return remote(
            part.at[block(zq, c)], ring.at[j], r_send.at[zq], r_recv.at[j], {"z": zq}
        )

    piece = rows // 8

    def combine(zq):
        remote(sib.at[zq], sib.at[zq], p_send.at[0], p_recv.at[zq], {"c": other}).wait_recv()

        def step(i, carry):
            here = pl.ds(pl.multiple_of((zq * NC + c) * rows + i * piece, piece), piece)
            there = pl.ds(pl.multiple_of(i * piece, piece), piece)
            total = part[here].astype(F32) + sib[zq, there].astype(F32)
            part[here] = total.astype(BF16)
            return carry

        lax.fori_loop(0, 8, step, 0)

    def place_of(k):
        near = line_order(z, 0)
        mid = line_order(z, 1)
        far = line_order(z, 2)
        return jnp.where(k == 0, z, jnp.where(k == 1, near, jnp.where(k == 2, mid, far)))

    def pair(k, carry):
        zq = place_of(k)

        @pl.when(k == 1)
        def _():
            take(0)
            pl.when(inner)(lambda: take(1))

        @pl.when(k == 2)
        def _():
            pl.when(jnp.logical_not(inner))(lambda: take(1))
            pl.when(inner)(lambda: take(2))

        @pl.when((k == 3) & jnp.logical_not(inner))
        def _():
            take(2)

        def one(j, carry):
            cq = (c + j) % NC
            here = block(zq, cq)

            @pl.when((k == 0) & (j == 0))
            def _():
                for copy in loads:
                    copy.wait()

            @pl.when(j == 1)
            def _():
                arrival(zq, cq).wait_recv()

            load_cot(zq, cq).wait()
            for low, high in TILES:
                high = units if high is None else high
                gate = dot(hv[here], wgv[:, low:high])
                up = dot(hv[here], wuv[:, low:high])
                grad = dot_nt(cv[here], wdv[low:high])
                sig = jax.nn.sigmoid(gate)
                act = gate * sig
                av[here, low:high] = (act * up).astype(BF16)
                duv[here, low:high] = (grad * act).astype(BF16)
                dgv[here, low:high] = (
                    grad * up * (sig * (1.0 + gate * (1.0 - sig)))
                ).astype(BF16)

            if with_down:

                @pl.when((k > 0) & (j == 0))
                def _():
                    output(zq, cq).wait()

                @pl.when((k > 0) & (j == 1))
                def _():
                    output_over(place_of(k - 1)).wait_send()

            else:

                @pl.when(k > 0)
                def _():
                    output(zq, cq).wait()

            ob[cq] = dot(av[here], wdv[...]).astype(BF16)
            if with_down:
                pl.when(j == 0)(output(zq, cq).start)
                pl.when(j == 1)(output_over(zq).start)
            else:
                output(zq, cq).start()
            part[here] = (dot_nt(dgv[here], wgv[...]) + dot_nt(duv[here], wuv[...])).astype(BF16)
            return carry

        lax.fori_loop(0, NC, one, 0)
        partial_over(zq).start()

        @pl.when(k > 1)
        def _():
            before = place_of(k - 1)
            combine(before)
            partial_home(before).start()

        return carry

    lax.fori_loop(0, NZ, pair, 0)
    last = line_order(z, NZ - 2)
    step_d = wide // 6

    def down_grad(t, carry):
        cols = pl.ds(pl.multiple_of(t * step_d, step_d), step_d)
        wdv[:, cols] = dot_tn(av[...], cv[:, cols]).astype(BF16)

        @pl.when(t == 0)
        def _():
            combine(last)
            partial_home(last).start()

        return carry

    lax.fori_loop(0, 6, down_grad, 0)
    outs = [
        pltpu.make_async_copy(wdv, grad_d, s_out.at[0]),
        pltpu.make_async_copy(wgv, grad_g, s_out.at[1]),
        pltpu.make_async_copy(wuv, grad_u, s_out.at[2]),
    ]
    outs[0].start()
    if with_down:
        wires = Wires(scratch[0])
        half, shard = wide // 2, units // (2 * nx)
        left, right = pl.ds(0, half), pl.ds(half, half)

        def term(yq, xq, cols):
            first = (yq * nx + xq) * shard
            return grad_d.at[pl.ds(pl.multiple_of(first, 8), shard), cols]

        along_x, along_y = ("x", nx, x), ("y", 2, y)
        by_x = PlaneScatter(
            wires, lambda xq, yq: term(yq, xq, left), along_x, along_y, scratch[1:7]
        )
        by_y = PlaneScatter(
            wires, lambda yq, xq: term(yq, xq, right), along_y, along_x, scratch[7:13]
        )

    def turned(src, dst, first, last):
        def step(t, carry):
            cols = pl.ds(pl.multiple_of(t * step_d, step_d), step_d)
            dst[cols] = dot_tn(hv[:, cols], src[...]).astype(BF16)
            return carry

        lax.fori_loop(first, last, step, 0)

    turned(dgv, wgv, 0, 1)
    if with_down:
        outs[0].wait()
        by_x.begin()
        by_y.begin()
    turned(dgv, wgv, 1, 6)
    outs[1].start()
    turned(duv, wuv, 0, 6)
    outs[2].start()
    if with_down:
        by_x.relay()
        by_y.relay()
    combine(z)
    for j in range(NZ - 1):
        remote(ring.at[j], ring.at[j], r_send.at[0], r_recv.at[j], {"c": other}).wait_recv()

    def final(i, carry):
        here = pl.ds(pl.multiple_of((z * NC + c) * rows + i * piece, piece), piece)
        there = pl.ds(pl.multiple_of(i * piece, piece), piece)
        total = part[here].astype(F32)
        for j in range(NZ - 1):
            total = total + ring[j, there].astype(F32)
        dh[there] = total
        return carry

    lax.fori_loop(0, 8, final, 0)
    if with_down:
        by_x.finish(down_out.at[:, left])
        by_y.finish(down_out.at[:, right])
        wires.finish()
    pl.when(z < NZ - 1)(send_own(0).wait_send)
    pl.when(z > 0)(send_own(1).wait_send)
    send_own(2).wait_send()
    for k in range(NZ - 1):
        pl.when(inner)(onward(k).wait_send)
        to_sibling(k).wait_send()
        partial_home(line_order(z, k)).wait_send()
    for zq in range(NZ):
        partial_over(zq).wait_send()
    if with_down:
        output(z, c).wait()
        output_over(last).wait_send()
        for zq in range(NZ):
            there = out_sib.at[pl.ds(zq * rows, rows)]
            remote(there, there, o_send.at[0], o_recv.at[zq], {"c": other}).wait_recv()
    else:
        for cq in range(NC):
            output(z, cq).wait()
    for copy in outs[1 if with_down else 0 :]:
        copy.wait()


def mlp(ny, nx, with_down, h, wg, wu, wd, cot, collective_id):
    hbm = pl.BlockSpec(memory_space=pl.ANY)
    vmem = pl.BlockSpec(memory_space=pltpu.VMEM)
    rows, wide = h.shape
    units = wg.shape[1]
    every = NZ * NC * rows
    dma = pltpu.SemaphoreType.DMA
    shard = units // (ny * nx)
    down_scratch = []
    if with_down:
        sends = 2 * ((nx - 1) * 2 + 1 + nx + (nx - 1))
        down_scratch = [dma((NZ,)), dma((NZ,)), dma((sends,))]
        down_scratch += plane_scratch((shard, wide // 2), nx, ny)
        down_scratch += plane_scratch((shard, wide // 2), ny, nx)
    extra_shape, extra_specs, kept = (), (), every
    if with_down:
        kept = NZ * rows
        extra_shape = (
            jax.ShapeDtypeStruct((shard, wide), BF16),
            jax.ShapeDtypeStruct((kept, wide), BF16),
        )
        extra_specs = (vmem, hbm)
    return pl.pallas_call(
        lambda *refs: mlp_kernel(nx, with_down, *refs),
        name="mlp",
        out_shape=(
            jax.ShapeDtypeStruct((rows, wide), F32),
            jax.ShapeDtypeStruct((kept, wide), BF16),
            jax.ShapeDtypeStruct((wide, units), BF16),
            jax.ShapeDtypeStruct((wide, units), BF16),
            jax.ShapeDtypeStruct((units, wide), BF16),
        )
        + extra_shape,
        in_specs=[hbm] * 5,
        out_specs=(vmem, hbm, hbm, hbm, hbm) + extra_specs,
        scratch_shapes=[
            pltpu.VMEM((every, wide), BF16),
            pltpu.VMEM((every, wide), BF16),
            pltpu.VMEM((wide, units), BF16),
            pltpu.VMEM((wide, units), BF16),
            pltpu.VMEM((units, wide), BF16),
            pltpu.VMEM((every, units), BF16),
            pltpu.VMEM((every, units), BF16),
            pltpu.VMEM((every, units), BF16),
            pltpu.VMEM((every, wide), BF16),
            pltpu.VMEM((NZ, rows, wide), BF16),
            pltpu.VMEM((NZ - 1, rows, wide), BF16),
            pltpu.VMEM((NC, rows, wide), BF16),
            dma((4,)),
            dma((NZ, NC)),
            dma((NC,)),
            dma((3,)),
            dma((3,)),
            dma((NZ - 1,)),
            dma((NZ - 1,)),
            dma((NZ, NC)),
            dma((NZ,)),
            dma((NZ,)),
            dma((NZ,)),
            dma((NZ - 1,)),
        ]
        + down_scratch,
        compiler_params=pltpu.CompilerParams(
            collective_id=collective_id, has_side_effects=True, vmem_limit_bytes=63 << 20
        ),
    )(h, wg, wu, wd, cot)


def forward_kernel(nx, b_rows, names, *refs):
    r = types.SimpleNamespace(**dict(zip(names, refs)))
    y, z, x, c = place()
    other = 1 - c
    sib, ypeer = {"c": other}, {"y": 1 - y}
    xpeers = [(x + i + 1) % nx for i in range(nx - 1)]
    planes = [{"x": xp} for xp in xpeers] + [ypeer]
    cross = [{"z": (z + k + 1) % NZ, "c": other} for k in range(NZ - 1)]
    inner = (z > 0) & (z < NZ - 1)
    rows, wide = r.tok.shape
    shard = r.a.shape[0]
    key_width = r.kv_out.shape[1] // 2
    q_width = r.q_out.shape[1]
    qkv_width = q_width + 2 * key_width
    units = r.grad_d.shape[0]
    fs = units // (2 * nx)
    down_rows = r.d.shape[0]
    greet(line_peers(z, c) + cross + planes)
    ao, guo, co = r.ao, r.guo, r.co

    def down_at(yq, xq, cols):
        first = pl.multiple_of((yq * nx + xq) * down_rows, 8)
        return r.do.at[pl.ds(first, down_rows), cols]

    def remote_order(k):
        step = k + 1
        return (z + step // NC) % NZ, (c + step) % NC

    half = wide // 2
    parts = [pl.ds(0, half), pl.ds(half, half)]
    locals_ = [
        pltpu.make_async_copy(r.a, ao.at[y, z, x, c], r.s_local.at[0]),
        pltpu.make_async_copy(r.d, down_at(y, x, pl.ds(0, wide)), r.s_local.at[1]),
        pltpu.make_async_copy(r.tok, co.at[z, c], r.s_local.at[2]),
    ]
    for copy in locals_:
        copy.start()
    wires = Wires(r.send_sems)

    def both_ways(src, dst, sem):
        for peer in planes:
            wires.send(src, dst, sem, peer)

    def relay(ref, sem, peers):
        wires.arrived(ref, sem, sib)
        for peer in peers:
            wires.send(ref, ref, sem, peer)

    own_slot, own_sem = ao.at[y, z, x, c], r.ra.at[y, z, x, c]
    wires.send(r.a, own_slot, own_sem, {"z": jnp.minimum(z + 1, NZ - 1)}, lambda: z < NZ - 1)
    wires.send(r.a, own_slot, own_sem, {"z": jnp.maximum(z - 1, 0)}, lambda: z > 0)
    both_ways(r.a, own_slot, own_sem)
    wires.send(r.a, own_slot, own_sem, sib)
    line = LineGather(wires, r.tok, co, r.rc, z, c)

    def block(zq, cq):
        return pl.ds(pl.multiple_of((zq * NC + cq) * rows, rows), rows)

    hv = r.hv

    def send_own(i):
        here = hv.at[block(z, c)]
        device = (
            {"z": jnp.minimum(z + 1, NZ - 1)},
            {"z": jnp.maximum(z - 1, 0)},
            {"c": other},
        )[i]
        return remote(here, here, r.h_send.at[i], r.h_recv.at[z, c], device)

    def relay_attn(yq, xq, zq, peers):
        slot, sem = ao.at[yq, zq, xq, c], r.ra.at[yq, zq, xq, c]
        wires.arrived(slot, sem, sib)
        for peer in peers:
            wires.send(slot, slot, sem, peer)
        wires.send(slot, slot, sem, sib)

    def attention(gs, us, gu, weights, tail, first_in, qs, os, mid, s_in):
        loads = [
            pltpu.make_async_copy(r.g, gs, s_in.at[0]),
            pltpu.make_async_copy(r.u, us, s_in.at[1]),
        ]
        for copy in loads:
            copy.start()
        for m, (copy, ref) in enumerate(zip(loads, (gs, us))):
            copy.wait()
            for zq, cq, run, first in segments(nx, fs):
                gu[zq, cq, m, :, run : run + fs] = ref[:, first : first + fs]
        keep = pltpu.make_async_copy(gu.at[z, c], guo.at[:, y, z, x, c], r.s_local.at[3])
        keep.start()
        for k in range(NZ - 1):
            zq = line_order(z, k)
            slot, sem = ao.at[y, zq, x, c], r.ra.at[y, zq, x, c]
            wires.arrived(slot, sem, sib)
            onward = jnp.where(zq < z, jnp.minimum(z + 1, NZ - 1), jnp.maximum(z - 1, 0))
            wires.send(slot, slot, sem, {"z": onward}, lambda: inner)
            both_ways(slot, slot, sem)
            wires.send(slot, slot, sem, sib)
        mark = len(wires.started)
        for k in range(NZ * NC - 1):
            zp, cp = remote_order(k)
            wires.send(
                gu.at[zp, cp], guo.at[:, y, z, x, c], r.rt.at[z, c], {"z": zp, "c": cp}
            )
        block_sends = wires.started[mark:]
        del wires.started[mark:]
        line.begin()
        for zq in range(NZ):
            for xp in xpeers:
                relay_attn(y, xp, zq, [ypeer] if zq < NZ // 2 else [])
            relay_attn(1 - y, x, zq, planes[:-1] if zq >= NZ // 2 else [])
        for h in range(2):
            both_ways(r.d.at[:, parts[h]], down_at(y, x, parts[h]), r.rd.at[h, y, x])
        for xp in xpeers:
            for zq in range(NZ):
                relay_attn(1 - y, xp, zq, [])
        locals_[0].wait()
        for yq in range(2):
            for zq in range(NZ):
                for xq in range(nx):
                    wires.arrived(ao.at[yq, zq, xq, other], r.ra.at[yq, zq, xq, other], sib)

        def fetch(first, width):
            return pltpu.make_async_copy(
                ao.at[:, :, :, :, :, pl.ds(first, width)],
                weights.at[:, :, :, :, :, pl.ds(0, width)],
                s_in.at[0],
            )

        tail_copy = pltpu.make_async_copy(
            ao.at[:, :, :, :, :, pl.ds(qkv_width + wide, HD)], tail, s_in.at[1]
        )
        tail_copy.start()
        fetch(0, qkv_width).start()
        x32 = r.x[...].astype(F32)
        tail_copy.wait()
        lane = lax.broadcasted_iota(jnp.int32, (16, HD), 1)
        row = lax.broadcasted_iota(jnp.int32, (16, HD), 0)
        pick = (lane == row).astype(F32).astype(BF16)
        flat_tail = tail[...].reshape(-1, HD)
        gains = dot_nt(pick, flat_tail)
        gain_one, gain_two = gains[0:1], gains[1:2]
        low = lax.broadcasted_iota(jnp.int32, (8, HD), 1) < HD // 2
        pieces = []
        tops = [
            tail[yq, zq, xq, cq, 0:8].astype(F32)
            for yq in range(2)
            for zq in range(NZ)
            for xq in range(nx)
            for cq in range(NC)
        ]
        for i in range(0, len(tops), 2):
            pieces.append(jnp.where(low, pltpu.roll(tops[i], HD // 2, 1), tops[i + 1])[0:1])
        bias = jnp.concatenate(pieces, axis=1)
        rescale = lax.rsqrt(jnp.mean(x32 * x32, axis=-1, keepdims=True) + EPS)
        first_in[...] = (x32 * rescale * gain_one).astype(BF16)
        fetch(0, qkv_width).wait()

        def turn(value):
            return value * r.turn_c[...] - pltpu.roll(value, HD // 2, 1) * r.turn_s[...]

        kv_own = pl.ds(pl.multiple_of(y * rows, rows), rows)
        pre = dot(first_in[...], weights[:, :, :, :, :, q_width:].reshape(wide, 2 * key_width))
        pre = pre + bias[:, q_width:]
        kv_heads = key_width // HD
        for i in range(2 * kv_heads):
            value = pre[:, i * HD : (i + 1) * HD]
            if i < kv_heads:
                value = turn(value)
            r.kvs[kv_own, i * HD : (i + 1) * HD] = value.astype(BF16)
        wires.send(r.kvs.at[kv_own], r.kvs.at[kv_own], r.s_kv, ypeer)
        pre = dot(first_in[...], weights[:, :, :, :, :, :q_width].reshape(wide, q_width))
        pre = pre + bias[:, :q_width]
        heads = q_width // HD
        for i in range(heads):
            cols = slice(i * HD, (i + 1) * HD)
            qs[:, cols] = turn(pre[:, cols]).astype(BF16)
        fetch(qkv_width, wide).start()
        for k in range(NZ * NC - 1):
            zp, cp = remote_order(k)
            wires.arrived(guo.at[:, y, zp, x, cp], r.rt.at[zp, cp], sib)
        keep.wait()
        for m in range(2):
            plane = guo.at[m, y, :, x]
            both_ways(plane, plane, r.rw.at[m, y, x])
        kv_other = r.kvs.at[pl.ds(pl.multiple_of((1 - y) * rows, rows), rows)]
        wires.arrived(kv_other, r.s_kv, ypeer)
        saves = [
            pltpu.make_async_copy(qs, r.q_out, s_in.at[1]),
            pltpu.make_async_copy(r.kvs, r.kv_out, s_in.at[2]),
            pltpu.make_async_copy(os, r.o_out, s_in.at[3]),
            pltpu.make_async_copy(mid, r.mid_out, s_in.at[4]),
        ]
        saves[0].start()
        saves[1].start()
        scale = HD ** (-0.5)
        group = heads // kv_heads
        for kv_head in range(kv_heads):
            k_cols = pl.ds(kv_head * HD, HD)
            v_cols = pl.ds(key_width + kv_head * HD, HD)

            def head(i, carry):
                cols = pl.ds(pl.multiple_of((kv_head * group + i) * HD, HD), HD)
                scores = dot_nt(qs[:, cols], r.kvs[:, k_cols]) * scale
                scores = jnp.where(r.mask[...] > 0, scores, MASKED)
                exponent = jnp.exp(scores - jnp.max(scores, axis=-1, keepdims=True))
                probs = exponent / jnp.sum(exponent, axis=-1, keepdims=True)
                os[:, cols] = dot(probs.astype(BF16), r.kvs[:, v_cols]).astype(BF16)
                return carry

            lax.fori_loop(0, group, head, 0)
            if kv_head == 0:
                line.event(0)
                for xp in xpeers:
                    relay(down_at(y, xp, parts[0]), r.rd.at[0, y, xp], [ypeer])
                    relay(down_at(y, xp, parts[1]), r.rd.at[1, y, xp], [])
                relay(down_at(1 - y, x, parts[1]), r.rd.at[1, 1 - y, x], planes[:-1])
                relay(down_at(1 - y, x, parts[0]), r.rd.at[0, 1 - y, x], [])
        saves[2].start()
        fetch(qkv_width, wide).wait()
        for_out = weights[:, :, :, :, :, :wide].reshape(q_width, wide)
        middle = x32 + dot(os[...], for_out)
        mid[...] = middle
        saves[3].start()
        rescale_two = lax.rsqrt(jnp.mean(middle * middle, axis=-1, keepdims=True) + EPS)
        hv[block(z, c)] = (middle * rescale_two * gain_two).astype(BF16)
        pl.when(z < NZ - 1)(send_own(0).start)
        pl.when(z > 0)(send_own(1).start)
        send_own(2).start()
        wires.finish(block_sends)
        for copy in saves:
            copy.wait()

    block_shape = (shard, units)
    grid = (2, NZ, nx, NC)
    pl.run_scoped(
        attention,
        pltpu.VMEM(r.g.shape, BF16),
        pltpu.VMEM(r.u.shape, BF16),
        pltpu.VMEM((NZ, NC, 2) + block_shape, BF16),
        pltpu.VMEM(grid + (shard, qkv_width), BF16),
        pltpu.VMEM(grid + (shard, HD), BF16),
        pltpu.VMEM((rows, wide), BF16),
        pltpu.VMEM((rows, q_width), BF16),
        pltpu.VMEM((rows, q_width), BF16),
        pltpu.VMEM((rows, wide), F32),
        pltpu.SemaphoreType.DMA((5,)),
    )

    def feed_forward(cv, wgv, wuv, wdv, av, dgv, duv, part, ob, *half_own):
        def arrival(zq, cq):
            here = hv.at[block(zq, cq)]
            return remote(here, here, r.h_send.at[0], r.h_recv.at[zq, cq], sib)

        def onward(k):
            zq = line_order(z, k)
            here = hv.at[block(zq, c)]
            device = {
                "z": jnp.where(zq < z, jnp.minimum(z + 1, NZ - 1), jnp.maximum(z - 1, 0))
            }
            return remote(here, here, r.h_on.at[k], r.h_recv.at[zq, c], device)

        def to_sibling(k):
            zq = line_order(z, k)
            here = hv.at[block(zq, c)]
            return remote(here, here, r.h_sib.at[k], r.h_recv.at[zq, c], sib)

        def take(k):
            arrival(line_order(z, k), c).wait_recv()
            pl.when(inner)(onward(k).start)
            to_sibling(k).start()

        line.event(1)
        for xp in xpeers:
            relay(guo.at[0, y, :, xp], r.rw.at[0, y, xp], [ypeer])
        relay(guo.at[1, 1 - y, :, x], r.rw.at[1, 1 - y, x], planes[:-1])
        for copy in locals_[1:]:
            copy.wait()
        pl.when(inner)(lambda: take(0))
        pl.when(inner)(lambda: take(1))

        def load_cot(zq, cq):
            return pltpu.make_async_copy(co.at[zq, cq], cv.at[block(zq, cq)], r.s_cot.at[zq, cq])

        load_cot(z, c).start()
        line.sibling(z)
        load_cot(z, other).start()
        for xp in xpeers:
            relay(guo.at[1, y, :, xp], r.rw.at[1, y, xp], [])
        relay(guo.at[0, 1 - y, :, x], r.rw.at[0, 1 - y, x], [])
        for xp in xpeers:
            for h in range(2):
                relay(guo.at[h, 1 - y, :, xp], r.rw.at[h, 1 - y, xp], [])
                relay(down_at(1 - y, xp, parts[h]), r.rd.at[h, 1 - y, xp], [])
        loads = [
            pltpu.make_async_copy(guo.at[0], wgv, r.s_load.at[0]),
            pltpu.make_async_copy(guo.at[1], wuv, r.s_load.at[1]),
            pltpu.make_async_copy(r.do, wdv, r.s_load.at[2]),
        ]
        for copy in loads:
            copy.start()
        line.event(2, lambda: inner)

        def output(zq):
            here = pl.ds(pl.multiple_of(zq * rows, rows), rows)
            return pltpu.make_async_copy(ob.at[c], r.out_own.at[here], r.s_ob)

        def output_over(zq):
            here = pl.ds(pl.multiple_of(zq * rows, rows), rows)
            return remote(ob.at[other], r.out_sib.at[here], r.o_send.at[zq], r.o_recv.at[zq], sib)

        def partial_over(zq):
            return remote(
                part.at[block(zq, other)], r.sib.at[zq], r.p_send.at[zq], r.p_recv.at[zq], sib
            )

        def partial_home(zq):
            j = (z - zq + NZ) % NZ - 1
            return remote(
                part.at[block(zq, c)], r.ring.at[j], r.r_send.at[zq], r.r_recv.at[j], {"z": zq}
            )

        piece = rows // 8

        def combine(zq):
            remote(r.sib.at[zq], r.sib.at[zq], r.p_send.at[0], r.p_recv.at[zq], sib).wait_recv()

            def step(i, carry):
                here = pl.ds(pl.multiple_of((zq * NC + c) * rows + i * piece, piece), piece)
                there = pl.ds(pl.multiple_of(i * piece, piece), piece)
                total = part[here].astype(F32) + r.sib[zq, there].astype(F32)
                part[here] = total.astype(BF16)
                return carry

            lax.fori_loop(0, 8, step, 0)

        def place_of(k):
            late = jnp.where(k == 2, line_order(z, 0), line_order(z, 2))
            return jnp.where(k == 0, z, jnp.where(k == 1, line_order(z, 1), late))

        def flat(ref, low, high):
            return ref[:, :, :, :, :, low:high].reshape(wide, high - low)

        def pair(k, carry):
            zq = place_of(k)

            @pl.when(k == 2)
            def _():
                line.event(2, lambda: jnp.logical_not(inner))

            @pl.when(k > 0)
            def _():
                line.sibling(zq)
                load_cot(zq, other).start()
                load_cot(zq, c).start()

            def one(j, carry):
                cq = (other + j) % NC
                here = block(zq, cq)

                @pl.when((k == 0) & (j == 0))
                def _():
                    for copy in loads:
                        copy.wait()

                @pl.when(j == 0)
                def _():
                    arrival(zq, cq).wait_recv()

                @pl.when((k == 0) & (j == 1))
                def _():
                    pl.when(jnp.logical_not(inner))(lambda: take(0))
                    pl.when(jnp.logical_not(inner))(lambda: take(1))
                    pl.when(inner)(lambda: take(2))

                @pl.when((k == 1) & (j == 1) & jnp.logical_not(inner))
                def _():
                    take(2)

                load_cot(zq, cq).wait()
                for low, high in TILES:
                    high = units if high is None else high
                    gate = dot(hv[here], flat(wgv, low, high))
                    up = dot(hv[here], flat(wuv, low, high))
                    grad = dot_nt(cv[here], wdv[low:high])
                    sig = jax.nn.sigmoid(gate)
                    act = gate * sig
                    av[here, low:high] = (act * up).astype(BF16)
                    duv[here, low:high] = (grad * act).astype(BF16)
                    dgv[here, low:high] = (
                        grad * up * (sig * (1.0 + gate * (1.0 - sig)))
                    ).astype(BF16)

                @pl.when((k > 0) & (j == 1))
                def _():
                    output(zq).wait()

                @pl.when((k > 0) & (j == 0))
                def _():
                    output_over(place_of(k - 1)).wait_send()

                ob[cq] = dot(av[here], wdv[...]).astype(BF16)
                pl.when(j == 1)(output(zq).start)
                pl.when(j == 0)(output_over(zq).start)
                part[here] = (
                    dot_nt(dgv[here], flat(wgv, 0, units)) + dot_nt(duv[here], flat(wuv, 0, units))
                ).astype(BF16)
                pl.when(j == 0)(partial_over(zq).start)
                return carry

            lax.fori_loop(0, NC, one, 0)

            @pl.when(k > 0)
            def _():
                combine(zq)
                partial_home(zq).start()

            return carry

        lax.fori_loop(0, NZ, pair, 0)
        last = place_of(NZ - 1)
        step_d = wide // 6

        def down_grad(t, carry):
            cols = pl.ds(pl.multiple_of(t * step_d, step_d), step_d)
            wdv[:, cols] = dot_tn(av[...], cv[:, cols]).astype(BF16)
            return carry

        lax.fori_loop(0, 6, down_grad, 0)
        outs = [
            pltpu.make_async_copy(wdv, r.grad_d, r.s_out.at[0]),
            pltpu.make_async_copy(wgv, r.grad_g, r.s_out.at[1]),
            pltpu.make_async_copy(wuv, r.grad_u, r.s_out.at[2]),
        ]
        outs[0].start()

        def term(yq, xq, cols):
            first = pl.multiple_of((yq * nx + xq) * down_rows, 8)
            return r.grad_d.at[pl.ds(first, down_rows), cols]

        along_x, along_y = ("x", nx, x), ("y", 2, y)
        by_x = PlaneScatter(
            wires,
            lambda xq, yq: term(yq, xq, parts[0]),
            along_x,
            along_y,
            (r.xr1, half_own[0], r.xr2, r.xs1, r.xsl, r.xs2),
        )
        by_y = PlaneScatter(
            wires,
            lambda yq, xq: term(yq, xq, parts[1]),
            along_y,
            along_x,
            (r.yr1, half_own[1], r.yr2, r.ys1, r.ysl, r.ys2),
        )
        step_g = wide // NZ

        def turned(src, dst, first, last):
            def step(t, carry):
                cols = pl.ds(pl.multiple_of(t * step_g, step_g), step_g)
                value = dot_tn(hv[:, cols], src[...]).astype(BF16)
                here = pl.ds((t % 2) * (NZ // 2), NZ // 2)
                dst[t // 2, here] = value.reshape((NZ // 2, nx, NC, shard, units))
                return carry

            lax.fori_loop(first, last, step, 0)

        turned(dgv, wgv, 0, 1)
        outs[0].wait()
        by_x.begin()
        by_y.begin()
        turned(dgv, wgv, 1, NZ)
        outs[1].start()
        turned(duv, wuv, 0, NZ // 2)
        by_x.relay()
        by_y.relay()
        turned(duv, wuv, NZ // 2, NZ)
        outs[2].start()
        combine(z)
        for j in range(NZ - 1):
            here = r.ring.at[j]
            remote(here, here, r.r_send.at[0], r.r_recv.at[j], sib).wait_recv()

        def final(i, carry):
            here = pl.ds(pl.multiple_of((z * NC + c) * rows + i * piece, piece), piece)
            there = pl.ds(pl.multiple_of(i * piece, piece), piece)
            total = part[here].astype(F32)
            for j in range(NZ - 1):
                total = total + r.ring[j, there].astype(F32)
            r.dh[there] = total
            return carry

        lax.fori_loop(0, 8, final, 0)
        by_x.finish(r.down_out.at[:, parts[0]])
        by_y.finish(r.down_out.at[:, parts[1]])
        wires.finish()
        pl.when(z < NZ - 1)(send_own(0).wait_send)
        pl.when(z > 0)(send_own(1).wait_send)
        send_own(2).wait_send()
        for k in range(NZ - 1):
            pl.when(inner)(onward(k).wait_send)
            to_sibling(k).wait_send()
            partial_home(line_order(z, k)).wait_send()
        for zq in range(NZ):
            partial_over(zq).wait_send()
        output(last).wait()
        output_over(last).wait_send()
        for zq in range(NZ):
            there = r.out_sib.at[pl.ds(zq * rows, rows)]
            remote(there, there, r.o_send.at[0], r.o_recv.at[zq], sib).wait_recv()
        for copy in outs[1:]:
            copy.wait()

    every = NZ * NC * rows
    pl.run_scoped(
        feed_forward,
        pltpu.VMEM((every, wide), BF16),
        pltpu.VMEM(grid + block_shape, BF16),
        pltpu.VMEM(grid + block_shape, BF16),
        pltpu.VMEM((units, wide), BF16),
        pltpu.VMEM((every, units), BF16),
        pltpu.VMEM((every, units), BF16),
        pltpu.VMEM((every, units), BF16),
        pltpu.VMEM((every, wide), BF16),
        pltpu.VMEM((NC, rows, wide), BF16),
        pltpu.VMEM((2, down_rows, half), BF16),
        pltpu.VMEM((nx, down_rows, half), BF16),
    )


def forward(ny, nx, b_rows, a, g, u, d, tok, x, mask, turn_c, turn_s, widths, collective_id):
    hbm = pl.BlockSpec(memory_space=pl.ANY)
    vmem = pl.BlockSpec(memory_space=pltpu.VMEM)
    dma = pltpu.SemaphoreType.DMA
    rows, wide = tok.shape
    q_width, key_width = widths
    shard = a.shape[0]
    units = g.shape[1] // (NZ * NC)
    grid = (ny, NZ, nx, NC)
    half_slot = (d.shape[0], wide // 2)
    ins = dict(a=a, g=g, u=u, d=d, tok=tok, x=x, mask=mask, turn_c=turn_c, turn_s=turn_s)
    outs = dict(
        ao=(grid + a.shape, BF16),
        guo=((2,) + grid + (shard, units), BF16),
        do=((units, wide), BF16),
        co=((NZ, NC, rows, wide), BF16),
        q_out=((rows, q_width), BF16),
        kv_out=((2 * rows, 2 * key_width), BF16),
        o_out=((rows, q_width), BF16),
        mid_out=((rows, wide), F32),
        out_own=((NZ * rows, wide), BF16),
        out_sib=((NZ * rows, wide), BF16),
        grad_g=(grid + (shard, units), BF16),
        grad_u=(grid + (shard, units), BF16),
        grad_d=((units, wide), BF16),
        dh=((rows, wide), F32),
        down_out=(d.shape, BF16),
    )
    plane_x = plane_scratch(half_slot, nx, ny)
    plane_y = plane_scratch(half_slot, ny, nx)
    one_plane = (nx - 1) * 2 + 1 + nx + (nx - 1)
    sends = 3 + nx + 3 * (nx + 2) + 7 + 9 + 4 * (2 * nx - 1) + 4 * nx + 6 * nx
    scratch = dict(
        send_sems=dma((sends + 2 * one_plane + 24,)),
        s_local=dma((4,)),
        ra=dma(grid),
        rt=dma((NZ, NC)),
        rw=dma((2, ny, nx)),
        rd=dma((2, ny, nx)),
        rc=dma((NZ, NC)),
        s_kv=dma,
        kvs=pltpu.VMEM((2 * rows, 2 * key_width), BF16),
        hv=pltpu.VMEM((NZ * NC * rows, wide), BF16),
        sib=pltpu.VMEM((NZ, rows, wide), BF16),
        ring=pltpu.VMEM((NZ - 1, rows, wide), BF16),
        s_load=dma((3,)),
        s_cot=dma((NZ, NC)),
        s_ob=dma,
        s_out=dma((3,)),
        h_send=dma((3,)),
        h_on=dma((NZ - 1,)),
        h_sib=dma((NZ - 1,)),
        h_recv=dma((NZ, NC)),
        p_send=dma((NZ,)),
        p_recv=dma((NZ,)),
        r_send=dma((NZ,)),
        r_recv=dma((NZ - 1,)),
        o_send=dma((NZ,)),
        o_recv=dma((NZ,)),
        xr1=plane_x[0],
        xr2=plane_x[2],
        xs1=plane_x[3],
        xsl=plane_x[4],
        xs2=plane_x[5],
        yr1=plane_y[0],
        yr2=plane_y[2],
        ys1=plane_y[3],
        ysl=plane_y[4],
        ys2=plane_y[5],
    )
    names = tuple(ins) + tuple(outs) + tuple(scratch)
    results = pl.pallas_call(
        lambda *refs: forward_kernel(nx, b_rows, names, *refs),
        name="forward",
        out_shape=tuple(jax.ShapeDtypeStruct(*shape) for shape in outs.values()),
        in_specs=[hbm] * 5 + [vmem] * 4,
        out_specs=(hbm,) * 13 + (vmem,) * 2,
        scratch_shapes=list(scratch.values()),
        compiler_params=pltpu.CompilerParams(
            collective_id=collective_id, has_side_effects=True, vmem_limit_bytes=67_043_328
        ),
    )(*ins.values())
    return types.SimpleNamespace(**dict(zip(outs, results)))


def plane_peers(nx, y, x):
    return [{"x": (x + i + 1) % nx} for i in range(nx - 1)] + [{"y": 1 - y}]


def last_scatter_kernel(nx, widths, grads, gate, up, down, result, *rest):
    y, z, x, c = place()
    outs, rest = rest[: len(widths)], rest[len(widths) :]
    gate_out, up_out, down_out, result_out, rest = rest[:4] + (rest[4:],)
    send_sems, blocks, own, sib, line_sum, line_in = rest[:6]
    s_block, s_keep, s_own, s_sib, s_line = rest[6:11]
    half_x, half_y = rest[11:17], rest[17:23]
    gate_bufs, up_bufs, gu = rest[23:29], rest[29:35], rest[35]
    left_bufs, right_bufs, line_bufs = rest[36:42], rest[42:48], rest[48:56]
    cross = [{"z": (z + k + 1) % NZ, "c": 1 - c} for k in range(NZ - 1)]
    greet(line_peers(z, c) + cross + plane_peers(nx, y, x))
    wires = Wires(send_sems)
    along_x, along_y = ("x", nx, x), ("y", 2, y)
    gate_plane = PlaneScatter(
        wires, lambda xq, yq: gate.at[yq, :, xq], along_x, along_y, gate_bufs
    )
    up_plane = PlaneScatter(wires, lambda yq, xq: up.at[yq, :, xq], along_y, along_x, up_bufs)
    cols = down.shape[-1] // 2
    left, right = pl.ds(0, cols), pl.ds(cols, cols)
    left_plane = PlaneScatter(
        wires, lambda xq, yq: down.at[yq, xq, :, left], along_x, along_y, left_bufs
    )
    right_plane = PlaneScatter(
        wires, lambda yq, xq: down.at[yq, xq, :, right], along_y, along_x, right_bufs
    )
    line = LineScatter(wires, result, line_bufs, z, c)
    gate_plane.begin()
    up_plane.begin()
    line.begin()
    n = NZ // 2
    halves = [pl.ds(0, n), pl.ds(n, n)]

    def load(h, yq):
        return pltpu.make_async_copy(
            grads.at[yq, halves[h], :, c], own.at[yq, halves[h]], s_own.at[h, yq]
        )

    for h in range(2):
        for yq in range(2):
            wires.send(
                grads.at[yq, halves[h], :, 1 - c],
                sib.at[yq, halves[h]],
                s_sib.at[h, yq],
                {"c": 1 - c},
            )
            load(h, yq).start()

    def combine(h):
        for yq in range(2):
            load(h, yq).wait()
            wires.arrived(sib.at[yq, halves[h]], s_sib.at[h, yq], {"c": 1 - c})
            for i in range(n):
                zq = h * n + i
                total_into(own.at[yq, zq], [own.at[yq, zq], sib.at[yq, zq]])

    by_x = PlaneScatter(
        wires, lambda xq, yq: own.at[yq, halves[0], xq], along_x, along_y, half_x, True
    )
    by_y = PlaneScatter(
        wires, lambda yq, xq: own.at[yq, halves[1], xq], along_y, along_x, half_y, True
    )
    combine(0)
    by_x.begin()
    combine(1)
    by_y.begin()
    line.hop(3)
    left_plane.begin()
    right_plane.begin()
    line.hop(2)
    gate_plane.relay()
    up_plane.relay()
    line.hop(1)
    by_x.relay()
    by_y.relay()
    left_plane.relay()
    right_plane.relay()
    gate_plane.finish(gu.at[0])
    up_plane.finish(gu.at[1])
    keep = pltpu.make_async_copy(gu.at[:, z, c], blocks.at[z, c], s_keep)
    keep.start()
    for k in range(NZ * NC - 1):
        step = k + 1
        zp, cp = (z + step // NC) % NZ, (c + step) % NC
        wires.send(gu.at[:, zp, cp], blocks.at[z, c], s_block.at[z, c], {"z": zp, "c": cp})
    by_x.finish(line_sum.at[halves[0]])
    by_y.finish(line_sum.at[halves[1]])
    for k in range(NZ - 1):
        zp = (z + k + 1) % NZ
        wires.send(line_sum.at[zp], line_in.at[NZ - 2 - k], s_line.at[NZ - 2 - k], {"z": zp})
    line.finish(result_out)
    left_plane.finish(down_out.at[:, left])
    right_plane.finish(down_out.at[:, right])
    keep.wait()
    for k in range(NZ * NC - 1):
        step = k + 1
        zp, cp = (z + step // NC) % NZ, (c + step) % NC
        wires.arrived(blocks.at[zp, cp], s_block.at[zp, cp], {"c": 1 - c})
    fs = blocks.shape[-1] // (2 * nx)
    for m, out in enumerate((gate_out, up_out)):
        for zq, cq, run, first in segments(nx, fs):
            out[:, first : first + fs] = blocks[zq, cq, m, :, run : run + fs].astype(F32)
    for k in range(NZ - 1):
        wires.arrived(line_in.at[k], s_line.at[k], {"c": 1 - c})
    first = 0
    for out, width in zip(outs, widths):
        columns = slice(first, first + width)
        total = line_sum[z, :, columns].astype(F32)
        for k in range(NZ - 1):
            total = total + line_in[k, :, columns].astype(F32)
        out[...] = total
        first += width
    wires.finish()


def last_scatter(ny, nx, grads, widths, gate, up, down, result, collective_id):
    hbm = pl.BlockSpec(memory_space=pl.ANY)
    vmem = pl.BlockSpec(memory_space=pltpu.VMEM)
    rows, width = grads.shape[4:]
    block = gate.shape[4:]
    slot = (NZ // 2, rows, width)
    gate_slot = (NZ, NC) + block
    down_slot = (down.shape[2], down.shape[3] // 2)
    sends = 4 + 7 + NZ - 1 + 3 * ((nx - 1) * 2 + 1 + nx + (nx - 1)) + NZ + 2 * (NZ - 1)
    spread = block[1] * NZ * NC
    shapes = [(rows, w) for w in widths] + [(rows, spread)] * 2
    shapes += [down.shape[2:], result.shape[2:]]
    return pl.pallas_call(
        lambda *refs: last_scatter_kernel(nx, widths, *refs),
        name="last_scatter",
        out_shape=tuple(jax.ShapeDtypeStruct(shape, F32) for shape in shapes),
        in_specs=[hbm] * 5,
        out_specs=(vmem,) * len(shapes),
        scratch_shapes=[
            pltpu.SemaphoreType.DMA((sends,)),
            pltpu.VMEM((NZ, NC, 2) + block, BF16),
            pltpu.VMEM((ny, NZ, nx, rows, width), BF16),
            pltpu.VMEM((ny, NZ, nx, rows, width), BF16),
            pltpu.VMEM((NZ, rows, width), BF16),
            pltpu.VMEM((NZ - 1, rows, width), BF16),
            pltpu.SemaphoreType.DMA((NZ, NC)),
            pltpu.SemaphoreType.DMA,
            pltpu.SemaphoreType.DMA((2, 2)),
            pltpu.SemaphoreType.DMA((2, 2)),
            pltpu.SemaphoreType.DMA((NZ - 1,)),
        ]
        + plane_scratch(slot, nx, ny, True)
        + plane_scratch(slot, ny, nx, True)
        + plane_scratch(gate_slot, nx, ny)
        + plane_scratch(gate_slot, ny, nx)
        + [pltpu.VMEM((2,) + gate_slot, BF16)]
        + plane_scratch(down_slot, nx, ny)
        + plane_scratch(down_slot, ny, nx)
        + line_scratch(result.shape[2:]),
        compiler_params=pltpu.CompilerParams(
            collective_id=collective_id, has_side_effects=True, vmem_limit_bytes=60 << 20
        ),
    )(grads, gate, up, down, result)


def back_kernel(
    nx,
    key_width,
    b_rows,
    gate,
    up,
    ao,
    kept,
    given,
    mid,
    branch,
    tokens,
    gain,
    attn,
    query,
    kv,
    mask,
    turn_c,
    turn_s,
    gain_term,
    out_q,
    out_k,
    out_v,
    out_o,
    out_tail,
    out_gate,
    out_up,
    out_in,
    out_ring,
    send_sems,
    weights,
    term_o,
    term_q,
    sib_o,
    sib_q,
    line_sum,
    line_in,
    blocks,
    gu,
    d_attn,
    d_qkv,
    d_kv,
    kv_send,
    kv_recv,
    first_in,
    s_weights,
    s_sib,
    s_line,
    s_block,
    s_kv,
    result,
    s_result,
    s_ring,
    s_toward,
    *bufs,
):
    y, z, x, c = place()
    sib = {"c": 1 - c}
    cross = [{"z": (z + k + 1) % NZ, "c": 1 - c} for k in range(NZ - 1)]
    greet(line_peers(z, c) + cross + plane_peers(nx, y, x))
    wires = Wires(send_sems)
    along_x, along_y = ("x", nx, x), ("y", 2, y)
    gate_plane = PlaneScatter(
        wires, lambda xq, yq: gate.at[yq, :, xq], along_x, along_y, bufs[0:6]
    )
    up_plane = PlaneScatter(wires, lambda yq, xq: up.at[yq, :, xq], along_y, along_x, bufs[6:12])
    gate_plane.begin()
    up_plane.begin()
    rows, wide = branch.shape
    q_width = query.shape[1]
    qkv_width = q_width + 2 * key_width
    heads, kv_heads = q_width // HD, key_width // HD
    n = NZ // 2
    halves = [pl.ds(0, n), pl.ds(n, n)]
    tile = n * nx * NC * out_q.shape[0]
    shard = out_q.shape[0]

    def fetch(first, width):
        return pltpu.make_async_copy(
            ao.at[:, :, pl.ds(first, width)], weights.at[:, :, pl.ds(0, width)], s_weights
        )

    fetch(qkv_width, wide).start()

    def fill(term, yq, h, first, value):
        value = value.reshape((n, nx, NC, shard, value.shape[1]))
        term[yq, halves[h], :, :, :, first : first + value.shape[4]] = value.astype(BF16)

    def over(i, term, other, yq, h):
        wires.send(
            term.at[yq, halves[h], :, 1 - c],
            other.at[yq, halves[h]],
            s_sib.at[i, yq, h],
            sib,
        )

    def combine(i, term, other):
        for h in range(2):
            for yq in range(2):
                here = other.at[yq, halves[h]]
                wires.arrived(here, s_sib.at[i, yq, h], sib)
                for zq in range(h * n, h * n + n):
                    for xq in range(nx):
                        mine = term.at[yq, zq, xq, c]
                        total_into(mine, [mine, other.at[yq, zq, xq]], True)

    def planes(term, first):
        return (
            PlaneScatter(
                wires,
                lambda xq, yq: term.at[yq, halves[0], xq, c],
                along_x,
                along_y,
                bufs[first : first + 6],
                True,
            ),
            PlaneScatter(
                wires,
                lambda yq, xq: term.at[yq, halves[1], xq, c],
                along_y,
                along_x,
                bufs[first + 6 : first + 12],
                True,
            ),
        )

    for yq in range(2):
        for h in range(2):
            i = yq * 2 + h
            fill(term_o, yq, h, 0, dot_tn(attn[:, i * tile : (i + 1) * tile], branch[...]))
            over(0, term_o, sib_o, yq, h)

    def landing(sign, k):
        return NZ if k == NZ - 2 else (k if sign > 0 else 2 + k)

    def inside(sign, k):
        return z + k < NZ if sign > 0 else z >= k

    def toward(sign, k):
        at = landing(sign, k - 1)
        return remote(
            result.at[int(sign < 0)],
            out_ring.at[at],
            s_toward.at[2 * (k - 1) + (sign < 0)],
            s_ring.at[at],
            {"z": jnp.clip(z + sign, 0, NZ - 1)},
        )

    def landed(at):
        here = out_ring.at[at]
        remote(here, here, s_toward.at[0], s_ring.at[at], sib).wait_recv()

    def hop(k):
        for sign in (1, -1):
            behind = z > 0 if sign > 0 else z < NZ - 1
            held = result.at[int(sign < 0)]
            if k < NZ - 1:
                pl.when(inside(sign, k + 1))(toward(sign, k + 1).wait_send)

            @pl.when(inside(sign, k))
            def _():
                first = jnp.clip(z + sign * k, 0, NZ - 1) * rows
                here = pl.ds(pl.multiple_of(first, rows), rows)
                loads = [
                    pltpu.make_async_copy(kept.at[here], held, s_result.at[0]),
                    pltpu.make_async_copy(given.at[here], first_in, s_result.at[1]),
                ]
                for copy in loads:
                    copy.start()
                for copy in loads:
                    copy.wait()
                total_into(held, [held, first_in])

            if k < NZ - 1:

                @pl.when(inside(sign, k) & behind)
                def _():
                    at = landing(sign, k)
                    landed(at)
                    copy = pltpu.make_async_copy(out_ring.at[at], result.at[2], s_result.at[0])
                    copy.start()
                    copy.wait()
                    total_into(held, [held, result.at[2]])

            pl.when(inside(sign, k))(toward(sign, k).start)

    hop(3)
    fetch(qkv_width, wide).wait()
    for_out = weights[:, :, :wide].reshape(q_width, wide)
    d_attn[...] = dot_nt(branch[...], for_out).astype(BF16)
    fetch(0, qkv_width).start()
    d_kv[...] = jnp.zeros_like(d_kv)
    scale = HD ** (-0.5)

    def turn_back(value):
        return value * turn_c[...] + pltpu.roll(value, HD // 2, 1) * turn_s[...]

    group = heads // kv_heads
    for kv_head in range(kv_heads):
        k_cols = pl.ds(kv_head * HD, HD)
        v_cols = pl.ds(key_width + kv_head * HD, HD)

        def head(i, carry):
            cols = pl.ds(pl.multiple_of((kv_head * group + i) * HD, HD), HD)
            q_h, do_h = query[:, cols], d_attn[:, cols]
            scores = jnp.where(mask[...] > 0, dot_nt(q_h, kv[:, k_cols]) * scale, MASKED)
            exponent = jnp.exp(scores - jnp.max(scores, axis=-1, keepdims=True))
            probs = exponent / jnp.sum(exponent, axis=-1, keepdims=True)
            d_probs = dot_nt(do_h, kv[:, v_cols])
            inner = jnp.sum(probs * d_probs, axis=-1, keepdims=True)
            d_scores = (probs * (d_probs - inner)).astype(BF16)
            d_qkv[:, cols] = turn_back(dot(d_scores, kv[:, k_cols]) * scale).astype(BF16)
            d_kv[:, k_cols] += dot_tn(d_scores, q_h) * scale
            d_kv[:, v_cols] += dot_tn(probs.astype(BF16), do_h)
            return carry

        lax.fori_loop(0, group, head, 0)
        if kv_head == 0:
            hop(2)

    other_rows = pl.ds(pl.multiple_of((1 - y) * rows, rows), rows)
    own_rows = pl.ds(pl.multiple_of(y * rows, rows), rows)
    kv_send[...] = d_kv[other_rows].astype(BF16)
    hop(1)
    gate_plane.relay()
    wires.send(kv_send, kv_recv, s_kv, {"y": 1 - y})
    up_plane.relay()
    combine(0, term_o, sib_o)
    o_planes = planes(term_o, 12)
    for plane in o_planes:
        plane.begin()
    x32 = tokens[...].astype(F32)
    rescale = lax.rsqrt(jnp.mean(x32 * x32, axis=-1, keepdims=True) + EPS)
    first_in[...] = (x32 * rescale * gain[...]).astype(BF16)
    wires.arrived(kv_recv, s_kv, {"y": 1 - y})
    for kv_head in range(2 * kv_heads):
        cols = pl.ds(kv_head * HD, HD)
        total = d_kv[own_rows, cols] + kv_recv[:, cols].astype(F32)
        if kv_head < kv_heads:
            total = turn_back(total)
        d_qkv[:, pl.ds(q_width + kv_head * HD, HD)] = total.astype(BF16)
    gate_plane.finish(gu.at[0])
    up_plane.finish(gu.at[1])
    keep_block = pltpu.make_async_copy(gu.at[:, z, c], blocks.at[z, c], s_block.at[z, c])
    keep_block.start()
    for k in range(NZ * NC - 1):
        step = k + 1
        zp, cp = (z + step // NC) % NZ, (c + step) % NC
        wires.send(gu.at[:, zp, cp], blocks.at[z, c], s_block.at[z, c], {"z": zp, "c": cp})
    fetch(0, qkv_width).wait()
    for_in = weights[...].reshape(wide, qkv_width)
    d_first = dot_nt(d_qkv[...], for_in)
    normed = x32 * rescale
    scaled = d_first * gain[...]
    d_x = rescale * (scaled - normed * jnp.mean(scaled * normed, axis=-1, keepdims=True))
    out_in[...] = (mid[...] + d_x).astype(BF16)
    first_term = (d_first * normed).astype(BF16)
    lane = lax.broadcasted_iota(jnp.int32, (rows, HD), 1)
    pick_one = (lane == 0).astype(F32).astype(BF16)
    pick_two = (lane == 1).astype(F32).astype(BF16)
    bias_sum = jnp.sum(d_qkv[...].astype(F32), axis=0, keepdims=True)
    top = lax.broadcasted_iota(jnp.int32, (shard, HD), 0) == 0
    wide_bias = jnp.concatenate([bias_sum, bias_sum[:, :HD]], axis=1)
    for yq in range(2):
        for h in range(2):
            i = yq * 2 + h
            cols = slice(i * tile, (i + 1) * tile)
            fill(term_q, yq, h, 0, dot_tn(first_in[:, cols], d_qkv[...]))
            tail = dot_tn(first_term[:, cols], pick_one) + dot_tn(gain_term[:, cols], pick_two)
            for zi in range(n):
                for xq in range(nx):
                    for cq in range(NC):
                        part = ((zi * nx + xq) * NC + cq) * shard
                        place_at = i * (tile // shard) + (zi * nx + xq) * NC + cq
                        first = place_at * b_rows
                        base = (first // HD) * HD
                        bias = wide_bias[:, base : base + HD]
                        bias = pltpu.roll(
                            jnp.broadcast_to(bias, (8, HD)), (HD // 2 - (first - base)) % HD, 1
                        )[:1]
                        keep = lax.broadcasted_iota(jnp.int32, (shard, HD), 1) >= HD // 2
                        mixed = tail[part : part + shard] + jnp.where(top & keep, bias, 0.0)
                        term_q[yq, h * n + zi, xq, cq, :, qkv_width:] = mixed.astype(BF16)
            over(1, term_q, sib_q, yq, h)
    combine(1, term_q, sib_q)
    q_planes = planes(term_q, 24)
    for plane in q_planes:
        plane.begin()
    for plane in o_planes:
        plane.relay()
    for plane in q_planes:
        plane.relay()

    def along_line(i, first, width, pair):
        cols = pl.ds(first, width)
        pair[0].finish(line_sum.at[halves[0], :, cols])
        pair[1].finish(line_sum.at[halves[1], :, cols])
        for k in range(NZ - 1):
            zp, j = (z + k + 1) % NZ, NZ - 2 - k
            wires.send(
                line_sum.at[zp, :, cols], line_in.at[j, :, cols], s_line.at[i, j], {"z": zp}
            )

    q_all = qkv_width + HD
    along_line(0, q_all, wide, o_planes)
    along_line(1, 0, q_all, q_planes)
    keep_block.wait()
    for k in range(NZ * NC - 1):
        step = k + 1
        zp, cp = (z + step // NC) % NZ, (c + step) % NC
        wires.arrived(blocks.at[zp, cp], s_block.at[zp, cp], sib)
    fs = blocks.shape[-1] // (2 * nx)
    for m, out in enumerate((out_gate, out_up)):
        for zq, cq, run, first in segments(nx, fs):
            out[:, first : first + fs] = blocks[zq, cq, m, :, run : run + fs]

    def last(i, out, first, width):
        if i is not None:
            begin, size = (q_all, wide) if i == 0 else (0, q_all)
            for j in range(NZ - 1):
                wires.arrived(line_in.at[j, :, pl.ds(begin, size)], s_line.at[i, j], sib)
        columns = slice(first, first + width)
        total = line_sum[z, :, columns].astype(F32)
        for j in range(NZ - 1):
            total = total + line_in[j, :, columns].astype(F32)
        out[...] = total

    last(0, out_o, q_all, wide)
    last(1, out_q, 0, q_width)
    last(None, out_k, q_width, key_width)
    last(None, out_v, q_width + key_width, key_width)
    last(None, out_tail, qkv_width, HD)
    for sign in (1, -1):
        pl.when(z > 0 if sign > 0 else z < NZ - 1)(lambda: landed(landing(sign, 0)))
        pl.when(inside(sign, 1))(toward(sign, 1).wait_send)
    wires.finish()


def back(ny, nx, b_rows, gate, up, ao, kept, given, args, collective_id):
    hbm = pl.BlockSpec(memory_space=pl.ANY)
    vmem = pl.BlockSpec(memory_space=pltpu.VMEM)
    mid, branch, tokens, gain, attn, query, kv, mask, turn_c, turn_s, gain_term = args
    dma = pltpu.SemaphoreType.DMA
    shard = ao.shape[1]
    block = gate.shape[4:]
    rows, wide = branch.shape
    q_width = query.shape[1]
    key_width = kv.shape[1] // 2
    qkv_width = q_width + 2 * key_width
    q_all = qkv_width + HD
    spread = block[1] * NZ * NC
    one_plane = (nx - 1) * 2 + 1 + nx + (nx - 1)
    sends = 3 * one_plane + 8 + 1 + 7 + 3 * (NZ - 1)
    slot_o, slot_q = (NZ // 2, shard, wide), (NZ // 2, shard, q_all)
    gate_slot = (NZ, NC) + block
    place_all = (ny, NZ, nx, NC, shard)
    shapes = [(shard, q_width), (shard, key_width), (shard, key_width), (shard, wide), (shard, HD)]
    return pl.pallas_call(
        lambda *refs: back_kernel(nx, key_width, b_rows, *refs),
        name="back",
        cost_estimate=pl.CostEstimate(
            flops=100_000_000_000, bytes_accessed=100_000_000, transcendentals=0
        ),
        out_shape=tuple(jax.ShapeDtypeStruct(shape, F32) for shape in shapes)
        + (jax.ShapeDtypeStruct((shard, spread), BF16),) * 2
        + (jax.ShapeDtypeStruct((rows, wide), BF16),)
        + (jax.ShapeDtypeStruct((NZ + 1, rows, wide), BF16),),
        in_specs=[hbm] * 5 + [vmem] * len(args),
        out_specs=(vmem,) * 8 + (hbm,),
        scratch_shapes=[
            dma((sends,)),
            pltpu.VMEM((ny * NZ * nx * NC, shard, qkv_width), BF16),
            pltpu.VMEM(place_all + (wide,), BF16),
            pltpu.VMEM(place_all + (q_all,), BF16),
            pltpu.VMEM((ny, NZ, nx, shard, wide), BF16),
            pltpu.VMEM((ny, NZ, nx, shard, q_all), BF16),
            pltpu.VMEM((NZ, shard, q_all + wide), BF16),
            pltpu.VMEM((NZ - 1, shard, q_all + wide), BF16),
            pltpu.VMEM((NZ, NC, 2) + block, BF16),
            pltpu.VMEM((2,) + gate_slot, BF16),
            pltpu.VMEM((rows, q_width), BF16),
            pltpu.VMEM((rows, qkv_width), BF16),
            pltpu.VMEM((2 * rows, 2 * key_width), F32),
            pltpu.VMEM((rows, 2 * key_width), BF16),
            pltpu.VMEM((rows, 2 * key_width), BF16),
            pltpu.VMEM((rows, wide), BF16),
            dma,
            dma((2, 2, 2)),
            dma((2, NZ - 1)),
            dma((NZ, NC)),
            dma,
            pltpu.VMEM((NZ - 1, rows, wide), BF16),
            dma((2,)),
            dma((NZ + 1,)),
            dma((2 * (NZ - 1),)),
        ]
        + plane_scratch(gate_slot, nx, ny)
        + plane_scratch(gate_slot, ny, nx)
        + plane_scratch(slot_o, nx, ny, True)
        + plane_scratch(slot_o, ny, nx, True)
        + plane_scratch(slot_q, nx, ny, True)
        + plane_scratch(slot_q, ny, nx, True),
        compiler_params=pltpu.CompilerParams(
            collective_id=collective_id, has_side_effects=True, vmem_limit_bytes=67_043_328
        ),
    )(gate, up, ao, kept, given, *args)


def make_body(ny, nx):
    def fused_layer(packed, x, seg_all, gate, up, down, grad_out, widths, b_rows):
        tok_rows = x.shape[0]
        length = seg_all.shape[0]
        seq_place = lax.axis_index("y")
        tok_pos = seq_place * tok_rows + jnp.arange(tok_rows)
        cos_tok, sin_tok = tables(tok_pos)
        all_pos = jnp.arange(length)
        seg_tok = lax.dynamic_slice(seg_all, (seq_place * tok_rows,), (tok_rows,))
        allowed = (tok_pos[:, None] >= all_pos[None, :]) & (seg_tok[:, None] == seg_all[None, :])
        mask = allowed.astype(F32)
        turn_c = jnp.concatenate([cos_tok, cos_tok], axis=1)
        turn_s = jnp.concatenate([sin_tok, -sin_tok], axis=1)
        made = forward(
            ny, nx, b_rows, packed, gate, up, down, grad_out, x, mask, turn_c, turn_s, widths, 0
        )
        lanes = sum(widths) + widths[1] + x.shape[1]
        tail = made.ao[..., lanes : lanes + 2].astype(F32).reshape(-1, 2)
        gain_one, gain_two = tail[:, 0], tail[:, 1]
        middle = made.mid_out
        rescale_two = lax.rsqrt(jnp.mean(middle * middle, axis=-1, keepdims=True) + EPS)
        normed_two = middle * rescale_two
        scaled = made.dh * gain_two
        grad_mid = grad_out.astype(F32) + rescale_two * (
            scaled - normed_two * jnp.mean(scaled * normed_two, axis=-1, keepdims=True)
        )
        args = (
            grad_mid,
            grad_mid.astype(BF16),
            x,
            gain_one[None],
            made.o_out,
            made.q_out,
            made.kv_out,
            mask,
            turn_c,
            turn_s,
            (made.dh * normed_two).astype(BF16),
        )
        outs = back(
            ny,
            nx,
            b_rows,
            made.grad_g,
            made.grad_u,
            made.ao.reshape((-1,) + packed.shape),
            made.out_own,
            made.out_sib,
            args,
            1,
        )
        grad_q, grad_k, grad_v, grad_o, tail_sum, grad_gate_w, grad_up_w, grad_in, ring = outs
        z_place = lax.axis_index("z")
        first_row = z_place * tok_rows
        out_sum = jnp.where(z_place > 0, ring[0].astype(F32), 0.0)
        out_sum += jnp.where(z_place < NZ - 1, ring[2].astype(F32), 0.0)
        for half in (made.out_own, made.out_sib):
            out_sum += lax.dynamic_slice_in_dim(half, first_row, tok_rows).astype(F32)
        return (
            (middle + out_sum).astype(BF16)[None],
            grad_in[None],
            tail_sum[:, 0],
            grad_q,
            grad_k,
            grad_v,
            tail_sum[0, HD // 2 : HD // 2 + b_rows],
            grad_o,
            tail_sum[:, 1],
            grad_gate_w.astype(F32),
            grad_up_w.astype(F32),
            made.down_out.astype(F32),
        )

    def body(
        inputs,
        segment_ids,
        attn_gain,
        q_weight,
        k_weight,
        v_weight,
        qkv_bias,
        o_weight,
        mlp_gain,
        gate_weight,
        up_weight,
        down_weight,
        cotangent,
    ):
        tok_rows = inputs.shape[1]
        hidden_in = inputs[0].astype(F32)
        grad_out = cotangent[0]
        seg_all = segment_ids[0]
        length = seg_all.shape[0]
        seq_place = lax.axis_index("y")
        tok_pos = seq_place * tok_rows + jnp.arange(tok_rows)
        cos_tok, sin_tok = tables(tok_pos)
        query_width = q_weight.shape[1]
        key_width = k_weight.shape[1]
        kv_heads = key_width // HD
        q_heads = query_width // HD
        group = q_heads // kv_heads

        g_rows = attn_gain.shape[0]
        b_rows = qkv_bias.shape[0]
        qkv_width = query_width + 2 * key_width
        extra = jnp.concatenate(
            [
                attn_gain[:, None],
                mlp_gain[:, None],
                jnp.zeros((g_rows, HD // 2 - 2), BF16),
                jnp.broadcast_to(qkv_bias[None], (g_rows, b_rows)),
                jnp.zeros((g_rows, HD // 2 - b_rows), BF16),
            ],
            axis=1,
        )
        packed = jnp.concatenate([q_weight, k_weight, v_weight, o_weight, extra], axis=1)
        fused = g_rows % 16 == 0 and b_rows == HD // 2
        if fused:
            return fused_layer(
                packed,
                inputs[0],
                seg_all,
                gate_weight,
                up_weight,
                down_weight,
                grad_out,
                (query_width, key_width),
                b_rows,
            )
        attn_all, columns_all, down_all, grad_out_all = weight_gather(
            ny,
            nx,
            packed,
            gate_weight,
            up_weight,
            down_weight,
            grad_out,
            0,
        )
        full = attn_all.reshape(-1, packed.shape[1])
        full_qkv = full[:, :qkv_width]
        full_out = full[:, qkv_width : qkv_width + query_width]
        tail = attn_all[..., qkv_width + query_width :].astype(F32)
        gain_one = tail[..., 0].reshape(-1)
        gain_two = tail[..., 1].reshape(-1)
        bias = tail[..., 0, HD // 2 : HD // 2 + b_rows].reshape(-1)
        width = gate_weight.shape[1] // (NZ * NC)
        full_gate = columns_all[0].reshape(-1, width)
        full_up = columns_all[1].reshape(-1, width)
        full_down = down_all.reshape(width, -1)
        grad_out_all = grad_out_all.reshape(-1, grad_out.shape[1])

        rescale_one = lax.rsqrt(jnp.mean(hidden_in * hidden_in, axis=-1, keepdims=True) + EPS)
        normed_one = hidden_in * rescale_one
        input_one = (normed_one * gain_one).astype(BF16)
        qkv_pre = dot(input_one, full_qkv) + bias
        query = rotate(qkv_pre[:, :query_width], cos_tok, sin_tok).astype(BF16)
        key = rotate(qkv_pre[:, query_width : query_width + key_width], cos_tok, sin_tok)
        kv = jnp.concatenate([key, qkv_pre[:, query_width + key_width :]], axis=1).astype(BF16)
        kv_all = lax.all_gather(kv, "y", axis=0, tiled=True)
        key_heads = kv_all[:, :key_width].reshape(length, kv_heads, HD)
        value_heads = kv_all[:, key_width:].reshape(length, kv_heads, HD)
        query_heads = query.reshape(tok_rows, kv_heads, group, HD)
        score_scale = HD ** (-0.5)
        all_pos = jnp.arange(length)
        seg_tok = lax.dynamic_slice(seg_all, (seq_place * tok_rows,), (tok_rows,))
        allowed = (tok_pos[:, None] >= all_pos[None, :]) & (seg_tok[:, None] == seg_all[None, :])
        scores = (
            jnp.einsum("qkgd,pkd->kgqp", query_heads, key_heads, preferred_element_type=F32)
            * score_scale
        )
        masked = jnp.where(allowed[None, None], scores, MASKED)
        row_max = jnp.max(masked, axis=-1, keepdims=True)
        exponent = jnp.exp(masked - row_max)
        row_total = jnp.sum(exponent, axis=-1, keepdims=True)
        probs = exponent / row_total
        probs_low = probs.astype(BF16)
        mixture = jnp.einsum("kgqp,pkd->qkgd", probs_low, value_heads, preferred_element_type=F32)
        attn_tok = mixture.astype(BF16).reshape(tok_rows, query_width)
        middle = hidden_in + dot(attn_tok, full_out)

        rescale_two = lax.rsqrt(jnp.mean(middle * middle, axis=-1, keepdims=True) + EPS)
        normed_two = middle * rescale_two
        input_two = (normed_two * gain_two).astype(BF16)
        by_shard = (ny, NZ, nx, NC, g_rows, width)
        grad_input_two, out_part, part_gate, part_up, *downs = mlp(
            ny, nx, False, input_two, full_gate, full_up, full_down, grad_out_all, 1
        )
        grad_gain_two, grad_mid = norm_back(grad_input_two, normed_two, rescale_two, gain_two)
        grad_mid = grad_mid + grad_out.astype(F32)
        grad_branch = grad_mid.astype(BF16)
        grad_attn = dot_nt(grad_branch, full_out).astype(BF16)
        grad_heads = grad_attn.reshape(tok_rows, kv_heads, group, HD)
        grad_probs = jnp.einsum(
            "qkgd,pkd->kgqp", grad_heads, value_heads, preferred_element_type=F32
        )
        inner_sum = jnp.sum(probs * grad_probs, axis=-1, keepdims=True)
        grad_scores = (probs * (grad_probs - inner_sum)).astype(BF16)
        grad_query = (
            jnp.einsum("kgqp,pkd->qkgd", grad_scores, key_heads, preferred_element_type=F32)
            * score_scale
        ).reshape(tok_rows, query_width)
        grad_key = (
            jnp.einsum("kgqp,qkgd->pkd", grad_scores, query_heads, preferred_element_type=F32)
            * score_scale
        ).reshape(length, key_width)
        grad_value = jnp.einsum(
            "kgqp,qkgd->pkd", probs_low, grad_heads, preferred_element_type=F32
        ).reshape(length, key_width)
        grad_kv = jnp.concatenate([grad_key, grad_value], axis=1).astype(BF16)
        other = lax.dynamic_slice(
            grad_kv, ((1 - seq_place) * tok_rows, 0), (tok_rows, 2 * key_width)
        )
        own = lax.dynamic_slice(grad_kv, (seq_place * tok_rows, 0), (tok_rows, 2 * key_width))
        swapped = lax.ppermute(other, "y", [(0, 1), (1, 0)])
        grad_kv_tok = own.astype(F32) + swapped.astype(F32)
        grad_query_pre = rotate(grad_query, cos_tok, -sin_tok).astype(BF16)
        grad_key_pre = rotate(grad_kv_tok[:, :key_width], cos_tok, -sin_tok).astype(BF16)
        grad_value_pre = grad_kv_tok[:, key_width:].astype(BF16)
        grad_qkv = jnp.concatenate([grad_query_pre, grad_key_pre, grad_value_pre], axis=1)
        grad_qkv_sum = jnp.sum(grad_qkv.astype(F32), axis=0)
        grad_input_one = dot_nt(grad_qkv, full_qkv)
        grad_gain_one, grad_first = norm_back(grad_input_one, normed_one, rescale_one, gain_one)
        grad_total = grad_mid + grad_first
        shards = ny * NZ * nx * NC
        tail_grads = jnp.concatenate(
            [
                grad_gain_one[:, None],
                grad_gain_two[:, None],
                jnp.broadcast_to(
                    grad_qkv_sum.reshape(shards, 1, b_rows), (shards, g_rows, b_rows)
                ).reshape(-1, b_rows),
                jnp.zeros((shards * g_rows, HD - 2 - b_rows), F32),
            ],
            axis=1,
        )
        grad_attn_w = jnp.concatenate(
            [
                dot_tn(input_one, grad_qkv).astype(BF16),
                dot_tn(attn_tok, grad_branch).astype(BF16),
                tail_grads.astype(BF16),
            ],
            axis=1,
        )
        widths = (query_width, key_width, key_width, query_width, HD)
        pieces = (NZ, NC, tok_rows // 32, 32, hidden_in.shape[1])
        outs = last_scatter(
            ny,
            nx,
            grad_attn_w.reshape((ny, NZ, nx, NC, g_rows, -1)),
            widths,
            part_gate.reshape(by_shard),
            part_up.reshape(by_shard),
            downs[0].reshape((ny, nx) + down_weight.shape),
            out_part.reshape(pieces),
            3,
        )
        grad_q, grad_k, grad_v, grad_o, tail_sum = outs[:5]
        grad_gate_w, grad_up_w, grad_down_w, out_sum = outs[5:]
        output = (middle + out_sum.reshape(middle.shape)).astype(BF16)[None]
        return (
            output,
            grad_total.astype(BF16)[None],
            tail_sum[:, 0],
            grad_q,
            grad_k,
            grad_v,
            tail_sum[0, 2 : 2 + b_rows],
            grad_o,
            tail_sum[:, 1],
            grad_gate_w,
            grad_up_w,
            grad_down_w,
        )

    return body


def solution(mesh):
    ny = mesh.shape["seq"]
    nx = mesh.shape["fsdp"] // (NZ * NC)
    grid = Mesh(mesh.devices.reshape(ny, NZ, nx, NC), ALL)
    tokens = P(("z", "x", "c"), "y", None)
    rows = P(ALL, None)
    vec = P(ALL)
    return jax.shard_map(
        make_body(ny, nx),
        mesh=grid,
        in_specs=(
            tokens,
            P(("z", "x", "c"), None),
            vec,
            rows,
            rows,
            rows,
            vec,
            rows,
            vec,
            rows,
            rows,
            rows,
            tokens,
        ),
        out_specs=(tokens, tokens, vec, rows, rows, rows, vec, rows, vec, rows, rows, rows),
        check_vma=False,
    )
```

```python
import types

import jax
import jax.numpy as jnp
from jax import lax
from jax.experimental import pallas as pl
from jax.experimental.pallas import tpu as pltpu
from jax.sharding import Mesh, PartitionSpec as P

HD = 128
EPS = 1e-06
ROPE_BASE = 1000000.0
MASKED = -1e30
NZ = 4
NC = 2
ALL = ("y", "z", "x", "c")
TP = ("z", "c")
DP = ("y", "x")
F32 = jnp.float32
BF16 = jnp.bfloat16


def tables(positions):
    freq = ROPE_BASE ** (-jnp.arange(0, HD, 2).astype(F32) / HD)
    angle = positions.astype(F32)[:, None] * freq[None, :]
    return (jnp.cos(angle), jnp.sin(angle))


def rotate(values, cosine, sine):
    count = values.shape[0]
    split = values.reshape(count, -1, HD)
    half = HD // 2
    first = split[..., :half]
    second = split[..., half:]
    cos_b = cosine[:, None, :]
    sin_b = sine[:, None, :]
    turned = jnp.concatenate(
        [first * cos_b - second * sin_b, second * cos_b + first * sin_b], axis=-1
    )
    return turned.reshape(count, -1)


def dot(a, b):
    return jnp.dot(a, b, preferred_element_type=F32)


def dot_nt(a, b):
    return lax.dot_general(a, b, (((1,), (1,)), ((), ())), preferred_element_type=F32)


def dot_tn(a, b):
    return lax.dot_general(a, b, (((0,), (0,)), ((), ())), preferred_element_type=F32)


def norm_back(grad_normed, normed, rescale, gain_vec):
    grad_gain = jnp.sum(grad_normed * normed, axis=0)
    scaled = grad_normed * gain_vec
    grad_x = rescale * (scaled - normed * jnp.mean(scaled * normed, axis=-1, keepdims=True))
    return (grad_gain, grad_x)


class Wires:
    def __init__(self, sems):
        self.sems = sems
        self.used = 0
        self.started = []

    def send(self, src, dst, recv_sem, device, cond=None):
        copy = pltpu.make_async_remote_copy(
            src_ref=src,
            dst_ref=dst,
            send_sem=self.sems.at[self.used],
            recv_sem=recv_sem,
            device_id=device,
            device_id_type=pl.DeviceIdType.MESH,
        )
        if cond is None:
            copy.start()
        else:
            pl.when(cond())(copy.start)
        self.started.append((still(src), self.used, cond))
        self.used += 1

    def arrived(self, dst, recv_sem, device):
        pltpu.make_async_remote_copy(
            src_ref=dst,
            dst_ref=dst,
            send_sem=self.sems.at[0],
            recv_sem=recv_sem,
            device_id=device,
            device_id_type=pl.DeviceIdType.MESH,
        ).wait_recv()

    def finish(self, sent=None):
        for src, used, cond in self.started if sent is None else sent:
            sem = self.sems.at[used]
            src = taken(*src)
            copy = pltpu.make_async_remote_copy(
                src_ref=src,
                dst_ref=src,
                send_sem=sem,
                recv_sem=sem,
                device_id={"c": 1 - lax.axis_index("c")},
                device_id_type=pl.DeviceIdType.MESH,
            )
            if cond is None:
                copy.wait_send()
            else:
                pl.when(cond())(copy.wait_send)


def still(ref):
    steps = []
    for step in getattr(ref, "transforms", ()):
        steps.append([i.size if isinstance(i, pl.Slice) else None for i in step.indices])
    return getattr(ref, "ref", ref), steps


def taken(view, steps):
    for step in steps:
        view = view.at[tuple(0 if size is None else pl.ds(0, size) for size in step)]
    return view


def line_order(z, k):
    if k == 0:
        return z + 1 - 2 * (z % 2)
    if k == 1:
        return 2 - z // 2
    return 3 - 3 * (z // 2)


def greet(peers):
    barrier = pltpu.get_barrier_semaphore()
    for peer in peers:
        pl.semaphore_signal(
            barrier, inc=1, device_id=peer, device_id_type=pl.DeviceIdType.MESH
        )
    pl.semaphore_wait(barrier, len(peers))


def place():
    return tuple(lax.axis_index(name) for name in ALL)


def line_peers(z, c):
    peers = [{"c": 1 - c}]
    for k in range(NZ - 1):
        peers.append({"z": (z + k + 1) % NZ})
    return peers


class LineGather:
    def __init__(self, wires, own, out, recv, z, c):
        self.wires, self.own, self.out, self.recv, self.z, self.c = wires, own, out, recv, z, c

    def begin(self):
        w, z, c = self.wires, self.z, self.c
        dst, sem = self.out.at[z, c], self.recv.at[z, c]
        w.send(self.own, dst, sem, {"z": jnp.minimum(z + 1, NZ - 1)}, lambda: z < NZ - 1)
        w.send(self.own, dst, sem, {"z": jnp.maximum(z - 1, 0)}, lambda: z > 0)
        w.send(self.own, dst, sem, {"c": 1 - c})

    def event(self, k, cond=None):
        w, z, c = self.wires, self.z, self.c
        zq = line_order(z, k)
        slot, sem = self.out.at[zq, c], self.recv.at[zq, c]
        if cond is None:
            w.arrived(slot, sem, {"c": 1 - c})
        else:
            pl.when(cond())(lambda: w.arrived(slot, sem, {"c": 1 - c}))
        onward = jnp.where(zq < z, jnp.minimum(z + 1, NZ - 1), jnp.maximum(z - 1, 0))
        inner = lambda: (z > 0) & (z < NZ - 1)
        both = inner if cond is None else lambda: inner() & cond()
        w.send(slot, slot, sem, {"z": onward}, both)
        w.send(slot, slot, sem, {"c": 1 - c}, cond)

    def sibling(self, zq):
        w, c = self.wires, self.c
        w.arrived(self.out.at[zq, 1 - c], self.recv.at[zq, 1 - c], {"c": 1 - c})


def segments(nx, fs):
    for yq in range(2):
        for zq in range(NZ):
            for xq in range(nx):
                for cq in range(NC):
                    first = (((yq * NZ + zq) * nx + xq) * NC + cq) * fs
                    yield zq, cq, (yq * nx + xq) * fs, first


def weight_gather_kernel(
    nx, a, g, u, d, tok, ao, guo, do, co, gu, send_sems, local_sems, ra, rt, rw, rd, rc
):
    y, z, x, c = place()
    sib = {"c": 1 - c}
    ypeer = {"y": 1 - y}
    xpeers = [(x + i + 1) % nx for i in range(nx - 1)]
    planes = [{"x": xp} for xp in xpeers] + [ypeer]
    cross = [{"z": (z + k + 1) % NZ, "c": 1 - c} for k in range(NZ - 1)]
    greet(line_peers(z, c) + cross + planes)
    locals_ = [
        pltpu.make_async_copy(a, ao.at[y, z, x, c], local_sems.at[0]),
        pltpu.make_async_copy(d, do.at[y, x], local_sems.at[1]),
        pltpu.make_async_copy(tok, co.at[z, c], local_sems.at[2]),
    ]
    keep = pltpu.make_async_copy(gu.at[z, c], guo.at[:, y, z, x, c], local_sems.at[3])
    for copy in locals_:
        copy.start()
    wires = Wires(send_sems)

    def both_ways(src, dst, sem):
        for peer in planes:
            wires.send(src, dst, sem, peer)

    own_slot, own_sem = ao.at[y, z, x, c], ra.at[y, z, x, c]
    wires.send(a, own_slot, own_sem, {"z": jnp.minimum(z + 1, NZ - 1)}, lambda: z < NZ - 1)
    wires.send(a, own_slot, own_sem, {"z": jnp.maximum(z - 1, 0)}, lambda: z > 0)
    both_ways(a, own_slot, own_sem)
    wires.send(a, own_slot, own_sem, sib)
    fs = gu.shape[-1] // (2 * nx)
    for m, shard in enumerate((g, u)):
        for zq, cq, run, first in segments(nx, fs):
            gu[zq, cq, m, :, run : run + fs] = shard[:, first : first + fs]
    keep.start()
    for k in range(NZ - 1):
        zq = line_order(z, k)
        slot, sem = ao.at[y, zq, x, c], ra.at[y, zq, x, c]
        wires.arrived(slot, sem, sib)
        onward = jnp.where(zq < z, jnp.minimum(z + 1, NZ - 1), jnp.maximum(z - 1, 0))
        wires.send(slot, slot, sem, {"z": onward}, lambda: (z > 0) & (z < NZ - 1))
        both_ways(slot, slot, sem)
        wires.send(slot, slot, sem, sib)

    for k in range(NZ * NC - 1):
        step = k + 1
        zp, cp = (z + step // NC) % NZ, (c + step) % NC
        wires.send(
            gu.at[zp, cp], guo.at[:, y, z, x, c], rt.at[z, c], {"z": zp, "c": cp}
        )
    line = LineGather(wires, tok, co, rc, z, c)
    line.begin()
    half = d.shape[1] // 2
    parts = [pl.ds(0, half), pl.ds(half, half)]
    for h in range(2):
        both_ways(d.at[:, parts[h]], do.at[y, x, :, parts[h]], rd.at[h, y, x])

    def relay_attn(yq, xq, zq, peers):
        slot, sem = ao.at[yq, zq, xq, c], ra.at[yq, zq, xq, c]
        wires.arrived(slot, sem, sib)
        for peer in peers:
            wires.send(slot, slot, sem, peer)
        wires.send(slot, slot, sem, sib)

    for zq in range(NZ):
        for xp in xpeers:
            relay_attn(y, xp, zq, [ypeer] if zq < NZ // 2 else [])
        relay_attn(1 - y, x, zq, planes[:-1] if zq >= NZ // 2 else [])

    for k in range(NZ * NC - 1):
        step = k + 1
        zp, cp = (z + step // NC) % NZ, (c + step) % NC
        wires.arrived(guo.at[:, y, zp, x, cp], rt.at[zp, cp], sib)
    keep.wait()
    for m in range(2):
        plane = guo.at[m, y, :, x]
        both_ways(plane, plane, rw.at[m, y, x])
    line.event(0)

    def relay(ref, sem, peers):
        wires.arrived(ref, sem, sib)
        for peer in peers:
            wires.send(ref, ref, sem, peer)

    for xp in xpeers:
        relay(do.at[y, xp, :, parts[0]], rd.at[0, y, xp], [ypeer])
        relay(do.at[y, xp, :, parts[1]], rd.at[1, y, xp], [])
    relay(do.at[1 - y, x, :, parts[1]], rd.at[1, 1 - y, x], planes[:-1])
    relay(do.at[1 - y, x, :, parts[0]], rd.at[0, 1 - y, x], [])
    for xp in xpeers:
        for zq in range(NZ):
            relay_attn(1 - y, xp, zq, [])
    line.event(1)
    for xp in xpeers:
        relay(guo.at[0, y, :, xp], rw.at[0, y, xp], [ypeer])
    relay(guo.at[1, 1 - y, :, x], rw.at[1, 1 - y, x], planes[:-1])
    line.event(2)
    for xp in xpeers:
        relay(guo.at[1, y, :, xp], rw.at[1, y, xp], [])
    relay(guo.at[0, 1 - y, :, x], rw.at[0, 1 - y, x], [])
    for xp in xpeers:
        for h in range(2):
            relay(do.at[1 - y, xp, :, parts[h]], rd.at[h, 1 - y, xp], [])
            relay(guo.at[h, 1 - y, :, xp], rw.at[h, 1 - y, xp], [])
    for zq in range(NZ):
        line.sibling(zq)
    for yq in range(2):
        for zq in range(NZ):
            for xq in range(nx):
                wires.arrived(ao.at[yq, zq, xq, 1 - c], ra.at[yq, zq, xq, 1 - c], sib)
    wires.finish()
    for copy in locals_:
        copy.wait()


def weight_gather(ny, nx, a, g, u, d, tok, collective_id):
    sends = 3 + (nx + 1) + 3 * (nx + 2)
    sends += 7 + 9 + 2 * nx
    sends += 4 * nx + 2 * (nx - 1) + 2 * (nx - 1)
    sends += 2 * nx + 2 * (nx - 1) + 4 * (nx - 1) + 2 * (nx - 1)
    hbm = pl.BlockSpec(memory_space=pl.ANY)
    vmem = pl.BlockSpec(memory_space=pltpu.VMEM)
    grid = (ny, NZ, nx, NC)
    block = g.shape[:1] + (g.shape[1] // (NZ * NC),)
    return pl.pallas_call(
        lambda *refs: weight_gather_kernel(nx, *refs),
        name="weight_gather",
        out_shape=(
            jax.ShapeDtypeStruct(grid + a.shape, BF16),
            jax.ShapeDtypeStruct((2,) + grid + block, BF16),
            jax.ShapeDtypeStruct((ny, nx) + d.shape, BF16),
            jax.ShapeDtypeStruct((NZ, NC) + tok.shape, BF16),
        ),
        in_specs=[hbm, vmem, vmem, hbm, hbm],
        out_specs=(hbm,) * 4,
        scratch_shapes=[
            pltpu.VMEM((NZ, NC, 2) + block, BF16),
            pltpu.SemaphoreType.DMA((sends + 16,)),
            pltpu.SemaphoreType.DMA((4,)),
            pltpu.SemaphoreType.DMA(grid),
            pltpu.SemaphoreType.DMA((NZ, NC)),
            pltpu.SemaphoreType.DMA((2, ny, nx)),
            pltpu.SemaphoreType.DMA((2, ny, nx)),
            pltpu.SemaphoreType.DMA((NZ, NC)),
        ],
        compiler_params=pltpu.CompilerParams(
            collective_id=collective_id, has_side_effects=True
        ),
    )(a, g, u, d, tok)


def total_into(dst, refs, flat=None):
    flat = len(dst.shape) == 2

    def entry(i, carry):
        here = (slice(None), pl.ds(pl.multiple_of(i * 128, 128), 128)) if flat else i
        total = refs[0][here].astype(F32)
        for ref in refs[1:]:
            total = total + ref[here].astype(F32)
        dst[here] = total.astype(dst.dtype)
        return carry

    lax.fori_loop(0, dst.shape[1] // 128 if flat else dst.shape[0], entry, 0)


class PlaneScatter:
    def __init__(self, wires, src, first, second, bufs, loaded=False):
        self.wires, self.src = wires, src
        self.name_a, self.size_a, self.a = first
        self.name_b, self.size_b, self.b = second
        self.r1, self.own, self.r2, self.s1, self.sl, self.s2 = bufs
        self.loaded = loaded

    def mine(self, b):
        return self.src(self.a, b) if self.loaded else self.own.at[b]

    def order(self):
        return [(self.b + i + 1) % self.size_b for i in range(self.size_b)]

    def begin(self):
        for b in self.order():
            for i in range(self.size_a - 1):
                peer, j = (self.a + i + 1) % self.size_a, self.size_a - 2 - i
                self.wires.send(
                    self.src(peer, b), self.r1.at[j, b], self.s1.at[j, b], {self.name_a: peer}
                )
            if not self.loaded:
                self.load(b).start()

    def load(self, b):
        return pltpu.make_async_copy(self.src(self.a, b), self.own.at[b], self.sl.at[b])

    def gathered(self, b):
        if not self.loaded:
            self.load(b).wait()
        for j in range(self.size_a - 1):
            self.wires.arrived(self.r1.at[j, b], self.s1.at[j, b], {self.name_a: self.a})
        return [self.mine(b)] + [self.r1.at[j, b] for j in range(self.size_a - 1)]

    def relay(self):
        for i, b in enumerate(self.order()[:-1]):
            j = self.size_b - 2 - i
            total_into(self.mine(b), self.gathered(b))
            self.wires.send(self.mine(b), self.r2.at[j], self.s2.at[j], {self.name_b: b})

    def finish(self, dst):
        refs = self.gathered(self.b)
        for j in range(self.size_b - 1):
            self.wires.arrived(self.r2.at[j], self.s2.at[j], {self.name_b: self.b})
            refs.append(self.r2.at[j])
        total_into(dst, refs)


def plane_scratch(slot, size_a, size_b, loaded=False):
    own = (1,) * (1 + len(slot)) if loaded else (size_b,) + slot
    return [
        pltpu.VMEM((size_a - 1, size_b) + slot, BF16),
        pltpu.VMEM(own, BF16),
        pltpu.VMEM((size_b - 1,) + slot, BF16),
        pltpu.SemaphoreType.DMA((size_a - 1, size_b)),
        pltpu.SemaphoreType.DMA((size_b,)),
        pltpu.SemaphoreType.DMA((size_b - 1,)),
    ]


class LineScatter:
    def __init__(self, wires, part, bufs, z, c):
        self.wires, self.part, self.z, self.c = wires, part, z, c
        self.own, self.sib, self.left, self.right = bufs[:4]
        self.s_own, self.s_sib, self.s_left, self.s_right = bufs[4:]

    def order(self):
        return [line_order(self.z, k) for k in (2, 1, 0)] + [self.z]

    def load(self, zq):
        return pltpu.make_async_copy(
            self.part.at[zq, self.c], self.own.at[zq], self.s_own.at[zq]
        )

    def begin(self):
        for zq in self.order():
            self.wires.send(
                self.part.at[zq, 1 - self.c],
                self.sib.at[zq],
                self.s_sib.at[zq],
                {"c": 1 - self.c},
            )
            self.load(zq).start()

    def ready(self, zq):
        self.load(zq).wait()
        self.wires.arrived(self.sib.at[zq], self.s_sib.at[zq], {"c": 1 - self.c})

    def hop(self, k):
        z = self.z
        for sign, buf, sems in ((1, self.left, self.s_left), (-1, self.right, self.s_right)):
            target = z + sign * k
            inside = (target < NZ) if sign > 0 else (target >= 0)
            behind = (z > 0) if sign > 0 else (z < NZ - 1)
            target = jnp.clip(target, 0, NZ - 1)
            own, sib = self.own.at[target], self.sib.at[target]

            @pl.when(inside)
            def _():
                self.ready(target)

            if k < NZ - 1:

                @pl.when(inside & behind)
                def _():
                    self.wires.arrived(buf.at[k], sems.at[k], {"z": z})
                    total_into(own, [own, sib, buf.at[k]])

                @pl.when(inside & jnp.logical_not(behind))
                def _():
                    total_into(own, [own, sib])

            else:

                @pl.when(inside)
                def _():
                    total_into(own, [own, sib])

            onward = jnp.clip(z + sign, 0, NZ - 1)
            self.wires.send(own, buf.at[k - 1], sems.at[k - 1], {"z": onward}, lambda: inside)

    def finish(self, dst):
        z = self.z
        self.ready(z)
        own, sib = self.own.at[z], self.sib.at[z]

        @pl.when(z > 0)
        def _():
            self.wires.arrived(self.left.at[0], self.s_left.at[0], {"z": z})

        @pl.when(z < NZ - 1)
        def _():
            self.wires.arrived(self.right.at[0], self.s_right.at[0], {"z": z})

        @pl.when(z == 0)
        def _():
            total_into(dst, [own, sib, self.right.at[0]])

        @pl.when(z == NZ - 1)
        def _():
            total_into(dst, [own, sib, self.left.at[0]])

        @pl.when((z > 0) & (z < NZ - 1))
        def _():
            total_into(dst, [own, sib, self.left.at[0], self.right.at[0]])


def line_scratch(slot):
    return [
        pltpu.VMEM((NZ,) + slot, BF16),
        pltpu.VMEM((NZ,) + slot, BF16),
        pltpu.VMEM((NZ - 1,) + slot, BF16),
        pltpu.VMEM((NZ - 1,) + slot, BF16),
        pltpu.SemaphoreType.DMA((NZ,)),
        pltpu.SemaphoreType.DMA((NZ,)),
        pltpu.SemaphoreType.DMA((NZ - 1,)),
        pltpu.SemaphoreType.DMA((NZ - 1,)),
    ]


TILES = ((0, 640), (640, None))


def remote(src, dst, send_sem, recv_sem, device):
    return pltpu.make_async_remote_copy(
        src_ref=src,
        dst_ref=dst,
        send_sem=send_sem,
        recv_sem=recv_sem,
        device_id=device,
        device_id_type=pl.DeviceIdType.MESH,
    )


def mlp_kernel(
    nx,
    with_down,
    h,
    wg,
    wu,
    wd,
    cot,
    dh,
    out_part,
    grad_g,
    grad_u,
    grad_d,
    *scratch,
):
    if with_down:
        down_out, out_sib, scratch = scratch[0], scratch[1], scratch[2:]
    (
        hv,
        cv,
        wgv,
        wuv,
        wdv,
        av,
        dgv,
        duv,
        part,
        sib,
        ring,
        ob,
        s_load,
        s_cot,
        s_ob,
        s_out,
        h_send,
        h_on,
        h_sib,
        h_recv,
        p_send,
        p_recv,
        r_send,
        r_recv,
    ) = scratch[: 24]
    scratch = scratch[24:]
    if with_down:
        o_send, o_recv, scratch = scratch[0], scratch[1], scratch[2:]
    y, z, x, c = place()
    rows, wide = h.shape
    units = wg.shape[1]
    other = 1 - c
    inner = (z > 0) & (z < NZ - 1)
    greet(line_peers(z, c) + (plane_peers(nx, y, x) if with_down else []))

    def block(zq, cq):
        return pl.ds(pl.multiple_of((zq * NC + cq) * rows, rows), rows)

    loads = [
        pltpu.make_async_copy(h, hv.at[block(z, c)], s_load.at[0]),
        pltpu.make_async_copy(wg, wgv, s_load.at[1]),
        pltpu.make_async_copy(wu, wuv, s_load.at[2]),
        pltpu.make_async_copy(wd, wdv, s_load.at[3]),
    ]

    def load_cot(zq, cq):
        return pltpu.make_async_copy(
            cot.at[block(zq, cq)], cv.at[block(zq, cq)], s_cot.at[zq, cq]
        )

    def send_own(i):
        there = hv.at[block(z, c)]
        device = (
            {"z": jnp.minimum(z + 1, NZ - 1)},
            {"z": jnp.maximum(z - 1, 0)},
            {"c": other},
        )[i]
        return remote(h, there, h_send.at[i], h_recv.at[z, c], device)

    pl.when(z < NZ - 1)(send_own(0).start)
    pl.when(z > 0)(send_own(1).start)
    send_own(2).start()
    for copy in loads[:3]:
        copy.start()
    load_cot(z, c).start()
    loads[3].start()
    load_cot(z, other).start()
    for k in range(NZ - 1):
        for i in range(NC):
            load_cot(line_order(z, k), (c + i) % NC).start()

    def arrival(zq, cq):
        here = hv.at[block(zq, cq)]
        return remote(here, here, h_send.at[0], h_recv.at[zq, cq], {"c": other})

    def onward(k):
        zq = line_order(z, k)
        here = hv.at[block(zq, c)]
        device = {"z": jnp.where(zq < z, jnp.minimum(z + 1, NZ - 1), jnp.maximum(z - 1, 0))}
        return remote(here, here, h_on.at[k], h_recv.at[zq, c], device)

    def to_sibling(k):
        zq = line_order(z, k)
        here = hv.at[block(zq, c)]
        return remote(here, here, h_sib.at[k], h_recv.at[zq, c], {"c": other})

    def take(k):
        arrival(line_order(z, k), c).wait_recv()
        pl.when(inner)(onward(k).start)
        to_sibling(k).start()

    def output(zq, cq):
        if with_down:
            here = pl.ds(pl.multiple_of(zq * rows, rows), rows)
            return pltpu.make_async_copy(ob.at[cq], out_part.at[here], s_ob.at[0])
        return pltpu.make_async_copy(ob.at[cq], out_part.at[block(zq, cq)], s_ob.at[cq])

    def output_over(zq):
        here = pl.ds(pl.multiple_of(zq * rows, rows), rows)
        return remote(
            ob.at[other], out_sib.at[here], o_send.at[zq], o_recv.at[zq], {"c": other}
        )

    def partial_over(zq):
        return remote(
            part.at[block(zq, other)], sib.at[zq], p_send.at[zq], p_recv.at[zq], {"c": other}
        )

    def partial_home(zq):
        j = (z - zq + NZ) % NZ - 1
        return remote(
            part.at[block(zq, c)], ring.at[j], r_send.at[zq], r_recv.at[j], {"z": zq}
        )

    piece = rows // 8

    def combine(zq):
        remote(sib.at[zq], sib.at[zq], p_send.at[0], p_recv.at[zq], {"c": other}).wait_recv()

        def step(i, carry):
            here = pl.ds(pl.multiple_of((zq * NC + c) * rows + i * piece, piece), piece)
            there = pl.ds(pl.multiple_of(i * piece, piece), piece)
            total = part[here].astype(F32) + sib[zq, there].astype(F32)
            part[here] = total.astype(BF16)
            return carry

        lax.fori_loop(0, 8, step, 0)

    def place_of(k):
        near = line_order(z, 0)
        mid = line_order(z, 1)
        far = line_order(z, 2)
        return jnp.where(k == 0, z, jnp.where(k == 1, near, jnp.where(k == 2, mid, far)))

    def pair(k, carry):
        zq = place_of(k)

        @pl.when(k == 1)
        def _():
            take(0)
            pl.when(inner)(lambda: take(1))

        @pl.when(k == 2)
        def _():
            pl.when(jnp.logical_not(inner))(lambda: take(1))
            pl.when(inner)(lambda: take(2))

        @pl.when((k == 3) & jnp.logical_not(inner))
        def _():
            take(2)

        def one(j, carry):
            cq = (c + j) % NC
            here = block(zq, cq)

            @pl.when((k == 0) & (j == 0))
            def _():
                for copy in loads:
                    copy.wait()

            @pl.when(j == 1)
            def _():
                arrival(zq, cq).wait_recv()

            load_cot(zq, cq).wait()
            for low, high in TILES:
                high = units if high is None else high
                gate = dot(hv[here], wgv[:, low:high])
                up = dot(hv[here], wuv[:, low:high])
                grad = dot_nt(cv[here], wdv[low:high])
                sig = jax.nn.sigmoid(gate)
                act = gate * sig
                av[here, low:high] = (act * up).astype(BF16)
                duv[here, low:high] = (grad * act).astype(BF16)
                dgv[here, low:high] = (
                    grad * up * (sig * (1.0 + gate * (1.0 - sig)))
                ).astype(BF16)

            if with_down:

                @pl.when((k > 0) & (j == 0))
                def _():
                    output(zq, cq).wait()

                @pl.when((k > 0) & (j == 1))
                def _():
                    output_over(place_of(k - 1)).wait_send()

            else:

                @pl.when(k > 0)
                def _():
                    output(zq, cq).wait()

            ob[cq] = dot(av[here], wdv[...]).astype(BF16)
            if with_down:
                pl.when(j == 0)(output(zq, cq).start)
                pl.when(j == 1)(output_over(zq).start)
            else:
                output(zq, cq).start()
            part[here] = (dot_nt(dgv[here], wgv[...]) + dot_nt(duv[here], wuv[...])).astype(BF16)
            return carry

        lax.fori_loop(0, NC, one, 0)
        partial_over(zq).start()

        @pl.when(k > 1)
        def _():
            before = place_of(k - 1)
            combine(before)
            partial_home(before).start()

        return carry

    lax.fori_loop(0, NZ, pair, 0)
    last = line_order(z, NZ - 2)
    step_d = wide // 6

    def down_grad(t, carry):
        cols = pl.ds(pl.multiple_of(t * step_d, step_d), step_d)
        wdv[:, cols] = dot_tn(av[...], cv[:, cols]).astype(BF16)

        @pl.when(t == 0)
        def _():
            combine(last)
            partial_home(last).start()

        return carry

    lax.fori_loop(0, 6, down_grad, 0)
    outs = [
        pltpu.make_async_copy(wdv, grad_d, s_out.at[0]),
        pltpu.make_async_copy(wgv, grad_g, s_out.at[1]),
        pltpu.make_async_copy(wuv, grad_u, s_out.at[2]),
    ]
    outs[0].start()
    if with_down:
        wires = Wires(scratch[0])
        half, shard = wide // 2, units // (2 * nx)
        left, right = pl.ds(0, half), pl.ds(half, half)

        def term(yq, xq, cols):
            first = (yq * nx + xq) * shard
            return grad_d.at[pl.ds(pl.multiple_of(first, 8), shard), cols]

        along_x, along_y = ("x", nx, x), ("y", 2, y)
        by_x = PlaneScatter(
            wires, lambda xq, yq: term(yq, xq, left), along_x, along_y, scratch[1:7]
        )
        by_y = PlaneScatter(
            wires, lambda yq, xq: term(yq, xq, right), along_y, along_x, scratch[7:13]
        )

    def turned(src, dst, first, last):
        def step(t, carry):
            cols = pl.ds(pl.multiple_of(t * step_d, step_d), step_d)
            dst[cols] = dot_tn(hv[:, cols], src[...]).astype(BF16)
            return carry

        lax.fori_loop(first, last, step, 0)

    turned(dgv, wgv, 0, 1)
    if with_down:
        outs[0].wait()
        by_x.begin()
        by_y.begin()
    turned(dgv, wgv, 1, 6)
    outs[1].start()
    turned(duv, wuv, 0, 6)
    outs[2].start()
    if with_down:
        by_x.relay()
        by_y.relay()
    combine(z)
    for j in range(NZ - 1):
        remote(ring.at[j], ring.at[j], r_send.at[0], r_recv.at[j], {"c": other}).wait_recv()

    def final(i, carry):
        here = pl.ds(pl.multiple_of((z * NC + c) * rows + i * piece, piece), piece)
        there = pl.ds(pl.multiple_of(i * piece, piece), piece)
        total = part[here].astype(F32)
        for j in range(NZ - 1):
            total = total + ring[j, there].astype(F32)
        dh[there] = total
        return carry

    lax.fori_loop(0, 8, final, 0)
    if with_down:
        by_x.finish(down_out.at[:, left])
        by_y.finish(down_out.at[:, right])
        wires.finish()
    pl.when(z < NZ - 1)(send_own(0).wait_send)
    pl.when(z > 0)(send_own(1).wait_send)
    send_own(2).wait_send()
    for k in range(NZ - 1):
        pl.when(inner)(onward(k).wait_send)
        to_sibling(k).wait_send()
        partial_home(line_order(z, k)).wait_send()
    for zq in range(NZ):
        partial_over(zq).wait_send()
    if with_down:
        output(z, c).wait()
        output_over(last).wait_send()
        for zq in range(NZ):
            there = out_sib.at[pl.ds(zq * rows, rows)]
            remote(there, there, o_send.at[0], o_recv.at[zq], {"c": other}).wait_recv()
    else:
        for cq in range(NC):
            output(z, cq).wait()
    for copy in outs[1 if with_down else 0 :]:
        copy.wait()


def mlp(ny, nx, with_down, h, wg, wu, wd, cot, collective_id):
    hbm = pl.BlockSpec(memory_space=pl.ANY)
    vmem = pl.BlockSpec(memory_space=pltpu.VMEM)
    rows, wide = h.shape
    units = wg.shape[1]
    every = NZ * NC * rows
    dma = pltpu.SemaphoreType.DMA
    shard = units // (ny * nx)
    down_scratch = []
    if with_down:
        sends = 2 * ((nx - 1) * 2 + 1 + nx + (nx - 1))
        down_scratch = [dma((NZ,)), dma((NZ,)), dma((sends,))]
        down_scratch += plane_scratch((shard, wide // 2), nx, ny)
        down_scratch += plane_scratch((shard, wide // 2), ny, nx)
    extra_shape, extra_specs, kept = (), (), every
    if with_down:
        kept = NZ * rows
        extra_shape = (
            jax.ShapeDtypeStruct((shard, wide), BF16),
            jax.ShapeDtypeStruct((kept, wide), BF16),
        )
        extra_specs = (vmem, hbm)
    return pl.pallas_call(
        lambda *refs: mlp_kernel(nx, with_down, *refs),
        name="mlp",
        out_shape=(
            jax.ShapeDtypeStruct((rows, wide), F32),
            jax.ShapeDtypeStruct((kept, wide), BF16),
            jax.ShapeDtypeStruct((wide, units), BF16),
            jax.ShapeDtypeStruct((wide, units), BF16),
            jax.ShapeDtypeStruct((units, wide), BF16),
        )
        + extra_shape,
        in_specs=[hbm] * 5,
        out_specs=(vmem, hbm, hbm, hbm, hbm) + extra_specs,
        scratch_shapes=[
            pltpu.VMEM((every, wide), BF16),
            pltpu.VMEM((every, wide), BF16),
            pltpu.VMEM((wide, units), BF16),
            pltpu.VMEM((wide, units), BF16),
            pltpu.VMEM((units, wide), BF16),
            pltpu.VMEM((every, units), BF16),
            pltpu.VMEM((every, units), BF16),
            pltpu.VMEM((every, units), BF16),
            pltpu.VMEM((every, wide), BF16),
            pltpu.VMEM((NZ, rows, wide), BF16),
            pltpu.VMEM((NZ - 1, rows, wide), BF16),
            pltpu.VMEM((NC, rows, wide), BF16),
            dma((4,)),
            dma((NZ, NC)),
            dma((NC,)),
            dma((3,)),
            dma((3,)),
            dma((NZ - 1,)),
            dma((NZ - 1,)),
            dma((NZ, NC)),
            dma((NZ,)),
            dma((NZ,)),
            dma((NZ,)),
            dma((NZ - 1,)),
        ]
        + down_scratch,
        compiler_params=pltpu.CompilerParams(
            collective_id=collective_id, has_side_effects=True, vmem_limit_bytes=63 << 20
        ),
    )(h, wg, wu, wd, cot)


def forward_kernel(nx, b_rows, names, *refs):
    r = types.SimpleNamespace(**dict(zip(names, refs)))
    y, z, x, c = place()
    other = 1 - c
    sib, ypeer = {"c": other}, {"y": 1 - y}
    xpeers = [(x + i + 1) % nx for i in range(nx - 1)]
    planes = [{"x": xp} for xp in xpeers] + [ypeer]
    cross = [{"z": (z + k + 1) % NZ, "c": other} for k in range(NZ - 1)]
    inner = (z > 0) & (z < NZ - 1)
    rows, wide = r.tok.shape
    shard = r.a.shape[0]
    key_width = r.kv_out.shape[1] // 2
    q_width = r.q_out.shape[1]
    qkv_width = q_width + 2 * key_width
    units = r.grad_d.shape[0]
    fs = units // (2 * nx)
    down_rows = r.d.shape[0]
    greet(line_peers(z, c) + cross + planes)
    ao, guo, co = r.ao, r.guo, r.co

    def down_at(yq, xq, cols):
        first = pl.multiple_of((yq * nx + xq) * down_rows, 8)
        return r.do.at[pl.ds(first, down_rows), cols]

    def remote_order(k):
        step = k + 1
        return (z + step // NC) % NZ, (c + step) % NC

    half = wide // 2
    parts = [pl.ds(0, half), pl.ds(half, half)]
    locals_ = [
        pltpu.make_async_copy(r.a, ao.at[y, z, x, c], r.s_local.at[0]),
        pltpu.make_async_copy(r.d, down_at(y, x, pl.ds(0, wide)), r.s_local.at[1]),
        pltpu.make_async_copy(r.tok, co.at[z, c], r.s_local.at[2]),
    ]
    for copy in locals_:
        copy.start()
    wires = Wires(r.send_sems)

    def both_ways(src, dst, sem):
        for peer in planes:
            wires.send(src, dst, sem, peer)

    def relay(ref, sem, peers):
        wires.arrived(ref, sem, sib)
        for peer in peers:
            wires.send(ref, ref, sem, peer)

    own_slot, own_sem = ao.at[y, z, x, c], r.ra.at[y, z, x, c]
    wires.send(r.a, own_slot, own_sem, {"z": jnp.minimum(z + 1, NZ - 1)}, lambda: z < NZ - 1)
    wires.send(r.a, own_slot, own_sem, {"z": jnp.maximum(z - 1, 0)}, lambda: z > 0)
    both_ways(r.a, own_slot, own_sem)
    wires.send(r.a, own_slot, own_sem, sib)
    line = LineGather(wires, r.tok, co, r.rc, z, c)

    def block(zq, cq):
        return pl.ds(pl.multiple_of((zq * NC + cq) * rows, rows), rows)

    hv = r.hv

    def send_own(i):
        here = hv.at[block(z, c)]
        device = (
            {"z": jnp.minimum(z + 1, NZ - 1)},
            {"z": jnp.maximum(z - 1, 0)},
            {"c": other},
        )[i]
        return remote(here, here, r.h_send.at[i], r.h_recv.at[z, c], device)

    def relay_attn(yq, xq, zq, peers):
        slot, sem = ao.at[yq, zq, xq, c], r.ra.at[yq, zq, xq, c]
        wires.arrived(slot, sem, sib)
        for peer in peers:
            wires.send(slot, slot, sem, peer)
        wires.send(slot, slot, sem, sib)

    def attention(gs, us, gu, weights, tail, first_in, qs, os, mid, s_in):
        loads = [
            pltpu.make_async_copy(r.g, gs, s_in.at[0]),
            pltpu.make_async_copy(r.u, us, s_in.at[1]),
        ]
        for copy in loads:
            copy.start()
        for m, (copy, ref) in enumerate(zip(loads, (gs, us))):
            copy.wait()
            for zq, cq, run, first in segments(nx, fs):
                gu[zq, cq, m, :, run : run + fs] = ref[:, first : first + fs]
        keep = pltpu.make_async_copy(gu.at[z, c], guo.at[:, y, z, x, c], r.s_local.at[3])
        keep.start()
        for k in range(NZ - 1):
            zq = line_order(z, k)
            slot, sem = ao.at[y, zq, x, c], r.ra.at[y, zq, x, c]
            wires.arrived(slot, sem, sib)
            onward = jnp.where(zq < z, jnp.minimum(z + 1, NZ - 1), jnp.maximum(z - 1, 0))
            wires.send(slot, slot, sem, {"z": onward}, lambda: inner)
            both_ways(slot, slot, sem)
            wires.send(slot, slot, sem, sib)
        mark = len(wires.started)
        for k in range(NZ * NC - 1):
            zp, cp = remote_order(k)
            wires.send(
                gu.at[zp, cp], guo.at[:, y, z, x, c], r.rt.at[z, c], {"z": zp, "c": cp}
            )
        block_sends = wires.started[mark:]
        del wires.started[mark:]
        line.begin()
        for zq in range(NZ):
            for xp in xpeers:
                relay_attn(y, xp, zq, [ypeer] if zq < NZ // 2 else [])
            relay_attn(1 - y, x, zq, planes[:-1] if zq >= NZ // 2 else [])
        for h in range(2):
            both_ways(r.d.at[:, parts[h]], down_at(y, x, parts[h]), r.rd.at[h, y, x])
        for xp in xpeers:
            for zq in range(NZ):
                relay_attn(1 - y, xp, zq, [])
        locals_[0].wait()
        for yq in range(2):
            for zq in range(NZ):
                for xq in range(nx):
                    wires.arrived(ao.at[yq, zq, xq, other], r.ra.at[yq, zq, xq, other], sib)

        def fetch(first, width):
            return pltpu.make_async_copy(
                ao.at[:, :, :, :, :, pl.ds(first, width)],
                weights.at[:, :, :, :, :, pl.ds(0, width)],
                s_in.at[0],
            )

        tail_copy = pltpu.make_async_copy(
            ao.at[:, :, :, :, :, pl.ds(qkv_width + wide, HD)], tail, s_in.at[1]
        )
        tail_copy.start()
        fetch(0, qkv_width).start()
        x32 = r.x[...].astype(F32)
        tail_copy.wait()
        lane = lax.broadcasted_iota(jnp.int32, (16, HD), 1)
        row = lax.broadcasted_iota(jnp.int32, (16, HD), 0)
        pick = (lane == row).astype(F32).astype(BF16)
        flat_tail = tail[...].reshape(-1, HD)
        gains = dot_nt(pick, flat_tail)
        gain_one, gain_two = gains[0:1], gains[1:2]
        r.gains_out[...] = gains[0:8]
        low = lax.broadcasted_iota(jnp.int32, (8, HD), 1) < HD // 2
        pieces = []
        tops = [
            tail[yq, zq, xq, cq, 0:8].astype(F32)
            for yq in range(2)
            for zq in range(NZ)
            for xq in range(nx)
            for cq in range(NC)
        ]
        for i in range(0, len(tops), 2):
            pieces.append(jnp.where(low, pltpu.roll(tops[i], HD // 2, 1), tops[i + 1])[0:1])
        bias = jnp.concatenate(pieces, axis=1)
        rescale = lax.rsqrt(jnp.mean(x32 * x32, axis=-1, keepdims=True) + EPS)
        first_in[...] = (x32 * rescale * gain_one).astype(BF16)
        fetch(0, qkv_width).wait()

        def turn(value):
            return value * r.turn_c[...] - pltpu.roll(value, HD // 2, 1) * r.turn_s[...]

        kv_own = pl.ds(pl.multiple_of(y * rows, rows), rows)
        pre = dot(first_in[...], weights[:, :, :, :, :, q_width:].reshape(wide, 2 * key_width))
        pre = pre + bias[:, q_width:]
        kv_heads = key_width // HD
        for i in range(2 * kv_heads):
            value = pre[:, i * HD : (i + 1) * HD]
            if i < kv_heads:
                value = turn(value)
            r.kvs[kv_own, i * HD : (i + 1) * HD] = value.astype(BF16)
        wires.send(r.kvs.at[kv_own], r.kvs.at[kv_own], r.s_kv, ypeer)
        for k in range(NZ * NC - 1):
            zp, cp = remote_order(k)
            wires.arrived(guo.at[:, y, zp, x, cp], r.rt.at[zp, cp], sib)
        keep.wait()
        for m in range(2):
            plane = guo.at[m, y, :, x]
            both_ways(plane, plane, r.rw.at[m, y, x])
        pre = dot(first_in[...], weights[:, :, :, :, :, :q_width].reshape(wide, q_width))
        pre = pre + bias[:, :q_width]
        heads = q_width // HD
        for i in range(heads):
            cols = slice(i * HD, (i + 1) * HD)
            qs[:, cols] = turn(pre[:, cols]).astype(BF16)
        fetch(qkv_width, wide).start()
        kv_other = r.kvs.at[pl.ds(pl.multiple_of((1 - y) * rows, rows), rows)]
        wires.arrived(kv_other, r.s_kv, ypeer)
        saves = [
            pltpu.make_async_copy(qs, r.q_out, s_in.at[1]),
            pltpu.make_async_copy(r.kvs, r.kv_out, s_in.at[2]),
            pltpu.make_async_copy(os, r.o_out, s_in.at[3]),
            pltpu.make_async_copy(mid, r.mid_out, s_in.at[4]),
        ]
        saves[0].start()
        saves[1].start()
        scale = HD ** (-0.5)
        group = heads // kv_heads
        for kv_head in range(kv_heads):
            k_cols = pl.ds(kv_head * HD, HD)
            v_cols = pl.ds(key_width + kv_head * HD, HD)

            def head(i, carry):
                cols = pl.ds(pl.multiple_of((kv_head * group + i) * HD, HD), HD)
                scores = dot_nt(qs[:, cols], r.kvs[:, k_cols]) * scale
                scores = jnp.where(r.mask[...] > 0, scores, MASKED)
                exponent = jnp.exp(scores - jnp.max(scores, axis=-1, keepdims=True))
                probs = exponent / jnp.sum(exponent, axis=-1, keepdims=True)
                os[:, cols] = dot(probs.astype(BF16), r.kvs[:, v_cols]).astype(BF16)
                return carry

            lax.fori_loop(0, group, head, 0)
            if kv_head == 0:
                line.event(0)
                for xp in xpeers:
                    relay(down_at(y, xp, parts[0]), r.rd.at[0, y, xp], [ypeer])
                    relay(down_at(y, xp, parts[1]), r.rd.at[1, y, xp], [])
                relay(down_at(1 - y, x, parts[1]), r.rd.at[1, 1 - y, x], planes[:-1])
                relay(down_at(1 - y, x, parts[0]), r.rd.at[0, 1 - y, x], [])
        saves[2].start()
        fetch(qkv_width, wide).wait()
        for_out = weights[:, :, :, :, :, :wide].reshape(q_width, wide)
        middle = x32 + dot(os[...], for_out)
        mid[...] = middle
        saves[3].start()
        rescale_two = lax.rsqrt(jnp.mean(middle * middle, axis=-1, keepdims=True) + EPS)
        hv[block(z, c)] = (middle * rescale_two * gain_two).astype(BF16)
        pl.when(z < NZ - 1)(send_own(0).start)
        pl.when(z > 0)(send_own(1).start)
        send_own(2).start()
        wires.finish(block_sends)
        for copy in saves:
            copy.wait()

    block_shape = (shard, units)
    grid = (2, NZ, nx, NC)
    pl.run_scoped(
        attention,
        pltpu.VMEM(r.g.shape, BF16),
        pltpu.VMEM(r.u.shape, BF16),
        pltpu.VMEM((NZ, NC, 2) + block_shape, BF16),
        pltpu.VMEM(grid + (shard, qkv_width), BF16),
        pltpu.VMEM(grid + (shard, HD), BF16),
        pltpu.VMEM((rows, wide), BF16),
        pltpu.VMEM((rows, q_width), BF16),
        pltpu.VMEM((rows, q_width), BF16),
        pltpu.VMEM((rows, wide), F32),
        pltpu.SemaphoreType.DMA((5,)),
    )

    def feed_forward(cv, wgv, wuv, wdv, av, dgv, duv, part, ob, *half_own):
        def arrival(zq, cq):
            here = hv.at[block(zq, cq)]
            return remote(here, here, r.h_send.at[0], r.h_recv.at[zq, cq], sib)

        def onward(k):
            zq = line_order(z, k)
            here = hv.at[block(zq, c)]
            device = {
                "z": jnp.where(zq < z, jnp.minimum(z + 1, NZ - 1), jnp.maximum(z - 1, 0))
            }
            return remote(here, here, r.h_on.at[k], r.h_recv.at[zq, c], device)

        def to_sibling(k):
            zq = line_order(z, k)
            here = hv.at[block(zq, c)]
            return remote(here, here, r.h_sib.at[k], r.h_recv.at[zq, c], sib)

        def take(k):
            arrival(line_order(z, k), c).wait_recv()
            pl.when(inner)(onward(k).start)
            to_sibling(k).start()

        line.event(1)
        for xp in xpeers:
            relay(guo.at[0, y, :, xp], r.rw.at[0, y, xp], [ypeer])
        relay(guo.at[1, 1 - y, :, x], r.rw.at[1, 1 - y, x], planes[:-1])
        for copy in locals_[1:]:
            copy.wait()
        pl.when(inner)(lambda: take(0))
        pl.when(inner)(lambda: take(1))

        def load_cot(zq, cq):
            return pltpu.make_async_copy(co.at[zq, cq], cv.at[block(zq, cq)], r.s_cot.at[zq, cq])

        load_cot(z, c).start()
        line.sibling(z)
        load_cot(z, other).start()
        for xp in xpeers:
            relay(guo.at[1, y, :, xp], r.rw.at[1, y, xp], [])
        relay(guo.at[0, 1 - y, :, x], r.rw.at[0, 1 - y, x], [])
        for xp in xpeers:
            for h in range(2):
                relay(guo.at[h, 1 - y, :, xp], r.rw.at[h, 1 - y, xp], [])
                relay(down_at(1 - y, xp, parts[h]), r.rd.at[h, 1 - y, xp], [])
        loads = [
            pltpu.make_async_copy(guo.at[0], wgv, r.s_load.at[0]),
            pltpu.make_async_copy(guo.at[1], wuv, r.s_load.at[1]),
            pltpu.make_async_copy(r.do, wdv, r.s_load.at[2]),
        ]
        for copy in loads:
            copy.start()
        line.event(2, lambda: inner)

        def output(zq):
            here = pl.ds(pl.multiple_of(zq * rows, rows), rows)
            return pltpu.make_async_copy(ob.at[c], r.out_own.at[here], r.s_ob)

        def output_over(zq):
            here = pl.ds(pl.multiple_of(zq * rows, rows), rows)
            return remote(ob.at[other], r.out_sib.at[here], r.o_send.at[zq], r.o_recv.at[zq], sib)

        def partial_over(zq):
            return remote(
                part.at[block(zq, other)], r.sib.at[zq], r.p_send.at[zq], r.p_recv.at[zq], sib
            )

        def partial_home(zq):
            j = (z - zq + NZ) % NZ - 1
            return remote(
                part.at[block(zq, c)], r.ring.at[j], r.r_send.at[zq], r.r_recv.at[j], {"z": zq}
            )

        piece = rows // 8

        def combine(zq):
            remote(r.sib.at[zq], r.sib.at[zq], r.p_send.at[0], r.p_recv.at[zq], sib).wait_recv()

            def step(i, carry):
                here = pl.ds(pl.multiple_of((zq * NC + c) * rows + i * piece, piece), piece)
                there = pl.ds(pl.multiple_of(i * piece, piece), piece)
                total = part[here].astype(F32) + r.sib[zq, there].astype(F32)
                part[here] = total.astype(BF16)
                return carry

            lax.fori_loop(0, 8, step, 0)

        def place_of(k):
            late = jnp.where(k == 2, line_order(z, 0), line_order(z, 2))
            return jnp.where(k == 0, z, jnp.where(k == 1, line_order(z, 1), late))

        def flat(ref, low, high):
            return ref[:, :, :, :, :, low:high].reshape(wide, high - low)

        def pair(k, carry):
            zq = place_of(k)

            @pl.when(k == 2)
            def _():
                line.event(2, lambda: jnp.logical_not(inner))

            @pl.when(k > 0)
            def _():
                line.sibling(zq)
                load_cot(zq, other).start()
                load_cot(zq, c).start()

            def one(j, carry):
                cq = (other + j) % NC
                here = block(zq, cq)

                @pl.when((k == 0) & (j == 0))
                def _():
                    for copy in loads:
                        copy.wait()

                @pl.when(j == 0)
                def _():
                    arrival(zq, cq).wait_recv()

                @pl.when((k == 0) & (j == 1))
                def _():
                    pl.when(jnp.logical_not(inner))(lambda: take(0))
                    pl.when(jnp.logical_not(inner))(lambda: take(1))
                    pl.when(inner)(lambda: take(2))

                @pl.when((k == 1) & (j == 1) & jnp.logical_not(inner))
                def _():
                    take(2)

                load_cot(zq, cq).wait()
                for low, high in TILES:
                    high = units if high is None else high
                    gate = dot(hv[here], flat(wgv, low, high))
                    up = dot(hv[here], flat(wuv, low, high))
                    grad = dot_nt(cv[here], wdv[low:high])
                    sig = jax.nn.sigmoid(gate)
                    act = gate * sig
                    av[here, low:high] = (act * up).astype(BF16)
                    duv[here, low:high] = (grad * act).astype(BF16)
                    dgv[here, low:high] = (
                        grad * up * (sig * (1.0 + gate * (1.0 - sig)))
                    ).astype(BF16)

                @pl.when((k > 0) & (j == 1))
                def _():
                    output(zq).wait()

                @pl.when((k > 0) & (j == 0))
                def _():
                    output_over(place_of(k - 1)).wait_send()

                ob[cq] = dot(av[here], wdv[...]).astype(BF16)
                pl.when(j == 1)(output(zq).start)
                pl.when(j == 0)(output_over(zq).start)
                part[here] = (
                    dot_nt(dgv[here], flat(wgv, 0, units)) + dot_nt(duv[here], flat(wuv, 0, units))
                ).astype(BF16)
                pl.when(j == 0)(partial_over(zq).start)
                return carry

            lax.fori_loop(0, NC, one, 0)

            @pl.when(k > 0)
            def _():
                combine(zq)
                partial_home(zq).start()

            return carry

        lax.fori_loop(0, NZ, pair, 0)
        last = place_of(NZ - 1)
        step_d = wide // 6

        def down_grad(t, carry):
            cols = pl.ds(pl.multiple_of(t * step_d, step_d), step_d)
            wdv[:, cols] = dot_tn(av[...], cv[:, cols]).astype(BF16)
            return carry

        lax.fori_loop(0, 6, down_grad, 0)
        outs = [
            pltpu.make_async_copy(wdv, r.grad_d, r.s_out.at[0]),
            pltpu.make_async_copy(wgv, r.grad_g, r.s_out.at[1]),
            pltpu.make_async_copy(wuv, r.grad_u, r.s_out.at[2]),
        ]
        outs[0].start()

        def term(yq, xq, cols):
            first = pl.multiple_of((yq * nx + xq) * down_rows, 8)
            return r.grad_d.at[pl.ds(first, down_rows), cols]

        along_x, along_y = ("x", nx, x), ("y", 2, y)
        by_x = PlaneScatter(
            wires,
            lambda xq, yq: term(yq, xq, parts[0]),
            along_x,
            along_y,
            (r.xr1, half_own[0], r.xr2, r.xs1, r.xsl, r.xs2),
        )
        by_y = PlaneScatter(
            wires,
            lambda yq, xq: term(yq, xq, parts[1]),
            along_y,
            along_x,
            (r.yr1, half_own[1], r.yr2, r.ys1, r.ysl, r.ys2),
        )
        step_g = wide // NZ

        def turned(src, dst, first, last):
            def step(t, carry):
                cols = pl.ds(pl.multiple_of(t * step_g, step_g), step_g)
                value = dot_tn(hv[:, cols], src[...]).astype(BF16)
                here = pl.ds((t % 2) * (NZ // 2), NZ // 2)
                dst[t // 2, here] = value.reshape((NZ // 2, nx, NC, shard, units))
                return carry

            lax.fori_loop(first, last, step, 0)

        turned(dgv, wgv, 0, 1)
        outs[0].wait()
        by_x.begin()
        by_y.begin()
        turned(dgv, wgv, 1, NZ)
        outs[1].start()
        turned(duv, wuv, 0, NZ // 2)
        by_x.relay()
        by_y.relay()
        turned(duv, wuv, NZ // 2, NZ)
        outs[2].start()
        combine(z)
        for j in range(NZ - 1):
            here = r.ring.at[j]
            remote(here, here, r.r_send.at[0], r.r_recv.at[j], sib).wait_recv()

        def final(i, carry):
            here = pl.ds(pl.multiple_of((z * NC + c) * rows + i * piece, piece), piece)
            there = pl.ds(pl.multiple_of(i * piece, piece), piece)
            total = part[here].astype(F32)
            for j in range(NZ - 1):
                total = total + r.ring[j, there].astype(F32)
            r.dh[there] = total
            return carry

        lax.fori_loop(0, 8, final, 0)
        by_x.finish(r.down_out.at[:, parts[0]])
        by_y.finish(r.down_out.at[:, parts[1]])
        wires.finish()
        pl.when(z < NZ - 1)(send_own(0).wait_send)
        pl.when(z > 0)(send_own(1).wait_send)
        send_own(2).wait_send()
        for k in range(NZ - 1):
            pl.when(inner)(onward(k).wait_send)
            to_sibling(k).wait_send()
            partial_home(line_order(z, k)).wait_send()
        for zq in range(NZ):
            partial_over(zq).wait_send()
        output(last).wait()
        output_over(last).wait_send()
        for zq in range(NZ):
            there = r.out_sib.at[pl.ds(zq * rows, rows)]
            remote(there, there, r.o_send.at[0], r.o_recv.at[zq], sib).wait_recv()
        for copy in outs[1:]:
            copy.wait()

    every = NZ * NC * rows
    pl.run_scoped(
        feed_forward,
        pltpu.VMEM((every, wide), BF16),
        pltpu.VMEM(grid + block_shape, BF16),
        pltpu.VMEM(grid + block_shape, BF16),
        pltpu.VMEM((units, wide), BF16),
        pltpu.VMEM((every, units), BF16),
        pltpu.VMEM((every, units), BF16),
        pltpu.VMEM((every, units), BF16),
        pltpu.VMEM((every, wide), BF16),
        pltpu.VMEM((NC, rows, wide), BF16),
        pltpu.VMEM((2, down_rows, half), BF16),
        pltpu.VMEM((nx, down_rows, half), BF16),
    )


def forward(ny, nx, b_rows, a, g, u, d, tok, x, mask, turn_c, turn_s, widths, collective_id):
    hbm = pl.BlockSpec(memory_space=pl.ANY)
    vmem = pl.BlockSpec(memory_space=pltpu.VMEM)
    dma = pltpu.SemaphoreType.DMA
    rows, wide = tok.shape
    q_width, key_width = widths
    shard = a.shape[0]
    units = g.shape[1] // (NZ * NC)
    grid = (ny, NZ, nx, NC)
    half_slot = (d.shape[0], wide // 2)
    ins = dict(a=a, g=g, u=u, d=d, tok=tok, x=x, mask=mask, turn_c=turn_c, turn_s=turn_s)
    outs = dict(
        ao=(grid + a.shape, BF16),
        guo=((2,) + grid + (shard, units), BF16),
        do=((units, wide), BF16),
        co=((NZ, NC, rows, wide), BF16),
        q_out=((rows, q_width), BF16),
        kv_out=((2 * rows, 2 * key_width), BF16),
        o_out=((rows, q_width), BF16),
        mid_out=((rows, wide), F32),
        out_own=((NZ * rows, wide), BF16),
        out_sib=((NZ * rows, wide), BF16),
        grad_g=(grid + (shard, units), BF16),
        grad_u=(grid + (shard, units), BF16),
        grad_d=((units, wide), BF16),
        dh=((rows, wide), F32),
        down_out=(d.shape, BF16),
        gains_out=((8, wide), F32),
    )
    plane_x = plane_scratch(half_slot, nx, ny)
    plane_y = plane_scratch(half_slot, ny, nx)
    one_plane = (nx - 1) * 2 + 1 + nx + (nx - 1)
    sends = 3 + nx + 3 * (nx + 2) + 7 + 9 + 4 * (2 * nx - 1) + 4 * nx + 6 * nx
    scratch = dict(
        send_sems=dma((sends + 2 * one_plane + 24,)),
        s_local=dma((4,)),
        ra=dma(grid),
        rt=dma((NZ, NC)),
        rw=dma((2, ny, nx)),
        rd=dma((2, ny, nx)),
        rc=dma((NZ, NC)),
        s_kv=dma,
        kvs=pltpu.VMEM((2 * rows, 2 * key_width), BF16),
        hv=pltpu.VMEM((NZ * NC * rows, wide), BF16),
        sib=pltpu.VMEM((NZ, rows, wide), BF16),
        ring=pltpu.VMEM((NZ - 1, rows, wide), BF16),
        s_load=dma((3,)),
        s_cot=dma((NZ, NC)),
        s_ob=dma,
        s_out=dma((3,)),
        h_send=dma((3,)),
        h_on=dma((NZ - 1,)),
        h_sib=dma((NZ - 1,)),
        h_recv=dma((NZ, NC)),
        p_send=dma((NZ,)),
        p_recv=dma((NZ,)),
        r_send=dma((NZ,)),
        r_recv=dma((NZ - 1,)),
        o_send=dma((NZ,)),
        o_recv=dma((NZ,)),
        xr1=plane_x[0],
        xr2=plane_x[2],
        xs1=plane_x[3],
        xsl=plane_x[4],
        xs2=plane_x[5],
        yr1=plane_y[0],
        yr2=plane_y[2],
        ys1=plane_y[3],
        ysl=plane_y[4],
        ys2=plane_y[5],
    )
    names = tuple(ins) + tuple(outs) + tuple(scratch)
    results = pl.pallas_call(
        lambda *refs: forward_kernel(nx, b_rows, names, *refs),
        name="forward",
        out_shape=tuple(jax.ShapeDtypeStruct(*shape) for shape in outs.values()),
        in_specs=[hbm] * 5 + [vmem] * 4,
        out_specs=(hbm,) * 13 + (vmem,) * 3,
        scratch_shapes=list(scratch.values()),
        compiler_params=pltpu.CompilerParams(
            collective_id=collective_id, has_side_effects=True, vmem_limit_bytes=67_043_328
        ),
    )(*ins.values())
    return types.SimpleNamespace(**dict(zip(outs, results)))


def plane_peers(nx, y, x):
    return [{"x": (x + i + 1) % nx} for i in range(nx - 1)] + [{"y": 1 - y}]


def last_scatter_kernel(nx, widths, grads, gate, up, down, result, *rest):
    y, z, x, c = place()
    outs, rest = rest[: len(widths)], rest[len(widths) :]
    gate_out, up_out, down_out, result_out, rest = rest[:4] + (rest[4:],)
    send_sems, blocks, own, sib, line_sum, line_in = rest[:6]
    s_block, s_keep, s_own, s_sib, s_line = rest[6:11]
    half_x, half_y = rest[11:17], rest[17:23]
    gate_bufs, up_bufs, gu = rest[23:29], rest[29:35], rest[35]
    left_bufs, right_bufs, line_bufs = rest[36:42], rest[42:48], rest[48:56]
    cross = [{"z": (z + k + 1) % NZ, "c": 1 - c} for k in range(NZ - 1)]
    greet(line_peers(z, c) + cross + plane_peers(nx, y, x))
    wires = Wires(send_sems)
    along_x, along_y = ("x", nx, x), ("y", 2, y)
    gate_plane = PlaneScatter(
        wires, lambda xq, yq: gate.at[yq, :, xq], along_x, along_y, gate_bufs
    )
    up_plane = PlaneScatter(wires, lambda yq, xq: up.at[yq, :, xq], along_y, along_x, up_bufs)
    cols = down.shape[-1] // 2
    left, right = pl.ds(0, cols), pl.ds(cols, cols)
    left_plane = PlaneScatter(
        wires, lambda xq, yq: down.at[yq, xq, :, left], along_x, along_y, left_bufs
    )
    right_plane = PlaneScatter(
        wires, lambda yq, xq: down.at[yq, xq, :, right], along_y, along_x, right_bufs
    )
    line = LineScatter(wires, result, line_bufs, z, c)
    gate_plane.begin()
    up_plane.begin()
    line.begin()
    n = NZ // 2
    halves = [pl.ds(0, n), pl.ds(n, n)]

    def load(h, yq):
        return pltpu.make_async_copy(
            grads.at[yq, halves[h], :, c], own.at[yq, halves[h]], s_own.at[h, yq]
        )

    for h in range(2):
        for yq in range(2):
            wires.send(
                grads.at[yq, halves[h], :, 1 - c],
                sib.at[yq, halves[h]],
                s_sib.at[h, yq],
                {"c": 1 - c},
            )
            load(h, yq).start()

    def combine(h):
        for yq in range(2):
            load(h, yq).wait()
            wires.arrived(sib.at[yq, halves[h]], s_sib.at[h, yq], {"c": 1 - c})
            for i in range(n):
                zq = h * n + i
                total_into(own.at[yq, zq], [own.at[yq, zq], sib.at[yq, zq]])

    by_x = PlaneScatter(
        wires, lambda xq, yq: own.at[yq, halves[0], xq], along_x, along_y, half_x, True
    )
    by_y = PlaneScatter(
        wires, lambda yq, xq: own.at[yq, halves[1], xq], along_y, along_x, half_y, True
    )
    combine(0)
    by_x.begin()
    combine(1)
    by_y.begin()
    line.hop(3)
    left_plane.begin()
    right_plane.begin()
    line.hop(2)
    gate_plane.relay()
    up_plane.relay()
    line.hop(1)
    by_x.relay()
    by_y.relay()
    left_plane.relay()
    right_plane.relay()
    gate_plane.finish(gu.at[0])
    up_plane.finish(gu.at[1])
    keep = pltpu.make_async_copy(gu.at[:, z, c], blocks.at[z, c], s_keep)
    keep.start()
    for k in range(NZ * NC - 1):
        step = k + 1
        zp, cp = (z + step // NC) % NZ, (c + step) % NC
        wires.send(gu.at[:, zp, cp], blocks.at[z, c], s_block.at[z, c], {"z": zp, "c": cp})
    by_x.finish(line_sum.at[halves[0]])
    by_y.finish(line_sum.at[halves[1]])
    for k in range(NZ - 1):
        zp = (z + k + 1) % NZ
        wires.send(line_sum.at[zp], line_in.at[NZ - 2 - k], s_line.at[NZ - 2 - k], {"z": zp})
    line.finish(result_out)
    left_plane.finish(down_out.at[:, left])
    right_plane.finish(down_out.at[:, right])
    keep.wait()
    for k in range(NZ * NC - 1):
        step = k + 1
        zp, cp = (z + step // NC) % NZ, (c + step) % NC
        wires.arrived(blocks.at[zp, cp], s_block.at[zp, cp], {"c": 1 - c})
    fs = blocks.shape[-1] // (2 * nx)
    for m, out in enumerate((gate_out, up_out)):
        for zq, cq, run, first in segments(nx, fs):
            out[:, first : first + fs] = blocks[zq, cq, m, :, run : run + fs].astype(F32)
    for k in range(NZ - 1):
        wires.arrived(line_in.at[k], s_line.at[k], {"c": 1 - c})
    first = 0
    for out, width in zip(outs, widths):
        columns = slice(first, first + width)
        total = line_sum[z, :, columns].astype(F32)
        for k in range(NZ - 1):
            total = total + line_in[k, :, columns].astype(F32)
        out[...] = total
        first += width
    wires.finish()


def last_scatter(ny, nx, grads, widths, gate, up, down, result, collective_id):
    hbm = pl.BlockSpec(memory_space=pl.ANY)
    vmem = pl.BlockSpec(memory_space=pltpu.VMEM)
    rows, width = grads.shape[4:]
    block = gate.shape[4:]
    slot = (NZ // 2, rows, width)
    gate_slot = (NZ, NC) + block
    down_slot = (down.shape[2], down.shape[3] // 2)
    sends = 4 + 7 + NZ - 1 + 3 * ((nx - 1) * 2 + 1 + nx + (nx - 1)) + NZ + 2 * (NZ - 1)
    spread = block[1] * NZ * NC
    shapes = [(rows, w) for w in widths] + [(rows, spread)] * 2
    shapes += [down.shape[2:], result.shape[2:]]
    return pl.pallas_call(
        lambda *refs: last_scatter_kernel(nx, widths, *refs),
        name="last_scatter",
        out_shape=tuple(jax.ShapeDtypeStruct(shape, F32) for shape in shapes),
        in_specs=[hbm] * 5,
        out_specs=(vmem,) * len(shapes),
        scratch_shapes=[
            pltpu.SemaphoreType.DMA((sends,)),
            pltpu.VMEM((NZ, NC, 2) + block, BF16),
            pltpu.VMEM((ny, NZ, nx, rows, width), BF16),
            pltpu.VMEM((ny, NZ, nx, rows, width), BF16),
            pltpu.VMEM((NZ, rows, width), BF16),
            pltpu.VMEM((NZ - 1, rows, width), BF16),
            pltpu.SemaphoreType.DMA((NZ, NC)),
            pltpu.SemaphoreType.DMA,
            pltpu.SemaphoreType.DMA((2, 2)),
            pltpu.SemaphoreType.DMA((2, 2)),
            pltpu.SemaphoreType.DMA((NZ - 1,)),
        ]
        + plane_scratch(slot, nx, ny, True)
        + plane_scratch(slot, ny, nx, True)
        + plane_scratch(gate_slot, nx, ny)
        + plane_scratch(gate_slot, ny, nx)
        + [pltpu.VMEM((2,) + gate_slot, BF16)]
        + plane_scratch(down_slot, nx, ny)
        + plane_scratch(down_slot, ny, nx)
        + line_scratch(result.shape[2:]),
        compiler_params=pltpu.CompilerParams(
            collective_id=collective_id, has_side_effects=True, vmem_limit_bytes=60 << 20
        ),
    )(grads, gate, up, down, result)


def back_kernel(
    nx,
    key_width,
    b_rows,
    gate,
    up,
    ao,
    kept,
    given,
    mid,
    branch,
    tokens,
    gain,
    attn,
    query,
    kv,
    mask,
    turn_c,
    turn_s,
    gain_term,
    out_q,
    out_k,
    out_v,
    out_o,
    out_tail,
    out_gate,
    out_up,
    out_in,
    out_ring,
    send_sems,
    weights,
    term_o,
    term_q,
    sib_o,
    sib_q,
    line_sum,
    line_in,
    blocks,
    gu,
    d_attn,
    d_qkv,
    d_kv,
    kv_send,
    kv_recv,
    first_in,
    s_weights,
    s_sib,
    s_line,
    s_block,
    s_kv,
    result,
    s_result,
    s_ring,
    s_toward,
    *bufs,
):
    y, z, x, c = place()
    sib = {"c": 1 - c}
    cross = [{"z": (z + k + 1) % NZ, "c": 1 - c} for k in range(NZ - 1)]
    greet(line_peers(z, c) + cross + plane_peers(nx, y, x))
    wires = Wires(send_sems)
    along_x, along_y = ("x", nx, x), ("y", 2, y)
    gate_plane = PlaneScatter(
        wires, lambda xq, yq: gate.at[yq, :, xq], along_x, along_y, bufs[0:6]
    )
    up_plane = PlaneScatter(wires, lambda yq, xq: up.at[yq, :, xq], along_y, along_x, bufs[6:12])
    gate_plane.begin()
    up_plane.begin()
    rows, wide = branch.shape
    q_width = query.shape[1]
    qkv_width = q_width + 2 * key_width
    heads, kv_heads = q_width // HD, key_width // HD
    n = NZ // 2
    halves = [pl.ds(0, n), pl.ds(n, n)]
    tile = n * nx * NC * out_q.shape[0]
    shard = out_q.shape[0]

    def fetch(first, width):
        return pltpu.make_async_copy(
            ao.at[:, :, pl.ds(first, width)], weights.at[:, :, pl.ds(0, width)], s_weights
        )

    fetch(qkv_width, wide).start()

    def fill(term, yq, h, first, value):
        value = value.reshape((n, nx, NC, shard, value.shape[1]))
        term[yq, halves[h], :, :, :, first : first + value.shape[4]] = value.astype(BF16)

    def over(i, term, other, yq, h):
        wires.send(
            term.at[yq, halves[h], :, 1 - c],
            other.at[yq, halves[h]],
            s_sib.at[i, yq, h],
            sib,
        )

    def combine(i, term, other):
        for h in range(2):
            for yq in range(2):
                here = other.at[yq, halves[h]]
                wires.arrived(here, s_sib.at[i, yq, h], sib)
                for zq in range(h * n, h * n + n):
                    for xq in range(nx):
                        mine = term.at[yq, zq, xq, c]
                        total_into(mine, [mine, other.at[yq, zq, xq]], True)

    def planes(term, first):
        return (
            PlaneScatter(
                wires,
                lambda xq, yq: term.at[yq, halves[0], xq, c],
                along_x,
                along_y,
                bufs[first : first + 6],
                True,
            ),
            PlaneScatter(
                wires,
                lambda yq, xq: term.at[yq, halves[1], xq, c],
                along_y,
                along_x,
                bufs[first + 6 : first + 12],
                True,
            ),
        )

    for yq in range(2):
        for h in range(2):
            i = yq * 2 + h
            fill(term_o, yq, h, 0, dot_tn(attn[:, i * tile : (i + 1) * tile], branch[...]))
            over(0, term_o, sib_o, yq, h)

    def landing(sign, k):
        return NZ if k == NZ - 2 else (k if sign > 0 else 2 + k)

    def inside(sign, k):
        return z + k < NZ if sign > 0 else z >= k

    def toward(sign, k):
        at = landing(sign, k - 1)
        return remote(
            result.at[int(sign < 0)],
            out_ring.at[at],
            s_toward.at[2 * (k - 1) + (sign < 0)],
            s_ring.at[at],
            {"z": jnp.clip(z + sign, 0, NZ - 1)},
        )

    def landed(at):
        here = out_ring.at[at]
        remote(here, here, s_toward.at[0], s_ring.at[at], sib).wait_recv()

    def hop(k):
        for sign in (1, -1):
            behind = z > 0 if sign > 0 else z < NZ - 1
            held = result.at[int(sign < 0)]
            if k < NZ - 1:
                pl.when(inside(sign, k + 1))(toward(sign, k + 1).wait_send)

            @pl.when(inside(sign, k))
            def _():
                first = jnp.clip(z + sign * k, 0, NZ - 1) * rows
                here = pl.ds(pl.multiple_of(first, rows), rows)
                loads = [
                    pltpu.make_async_copy(kept.at[here], held, s_result.at[0]),
                    pltpu.make_async_copy(given.at[here], first_in, s_result.at[1]),
                ]
                for copy in loads:
                    copy.start()
                for copy in loads:
                    copy.wait()
                total_into(held, [held, first_in])

            if k < NZ - 1:

                @pl.when(inside(sign, k) & behind)
                def _():
                    at = landing(sign, k)
                    landed(at)
                    copy = pltpu.make_async_copy(out_ring.at[at], result.at[2], s_result.at[0])
                    copy.start()
                    copy.wait()
                    total_into(held, [held, result.at[2]])

            pl.when(inside(sign, k))(toward(sign, k).start)

    hop(3)
    fetch(qkv_width, wide).wait()
    for_out = weights[:, :, :wide].reshape(q_width, wide)
    d_attn[...] = dot_nt(branch[...], for_out).astype(BF16)
    fetch(0, qkv_width).start()
    d_kv[...] = jnp.zeros_like(d_kv)
    scale = HD ** (-0.5)

    def turn_back(value):
        return value * turn_c[...] + pltpu.roll(value, HD // 2, 1) * turn_s[...]

    group = heads // kv_heads
    for kv_head in range(kv_heads):
        k_cols = pl.ds(kv_head * HD, HD)
        v_cols = pl.ds(key_width + kv_head * HD, HD)

        def head(i, carry):
            cols = pl.ds(pl.multiple_of((kv_head * group + i) * HD, HD), HD)
            q_h, do_h = query[:, cols], d_attn[:, cols]
            scores = jnp.where(mask[...] > 0, dot_nt(q_h, kv[:, k_cols]) * scale, MASKED)
            exponent = jnp.exp(scores - jnp.max(scores, axis=-1, keepdims=True))
            probs = exponent / jnp.sum(exponent, axis=-1, keepdims=True)
            d_probs = dot_nt(do_h, kv[:, v_cols])
            inner = jnp.sum(probs * d_probs, axis=-1, keepdims=True)
            d_scores = (probs * (d_probs - inner)).astype(BF16)
            d_qkv[:, cols] = turn_back(dot(d_scores, kv[:, k_cols]) * scale).astype(BF16)
            d_kv[:, k_cols] += dot_tn(d_scores, q_h) * scale
            d_kv[:, v_cols] += dot_tn(probs.astype(BF16), do_h)
            return carry

        lax.fori_loop(0, group, head, 0)
        if kv_head == 0:
            hop(2)

    other_rows = pl.ds(pl.multiple_of((1 - y) * rows, rows), rows)
    own_rows = pl.ds(pl.multiple_of(y * rows, rows), rows)
    kv_send[...] = d_kv[other_rows].astype(BF16)
    hop(1)
    gate_plane.relay()
    wires.send(kv_send, kv_recv, s_kv, {"y": 1 - y})
    up_plane.relay()
    combine(0, term_o, sib_o)
    o_planes = planes(term_o, 12)
    for plane in o_planes:
        plane.begin()
    x32 = tokens[...].astype(F32)
    rescale = lax.rsqrt(jnp.mean(x32 * x32, axis=-1, keepdims=True) + EPS)
    first_in[...] = (x32 * rescale * gain[...]).astype(BF16)
    wires.arrived(kv_recv, s_kv, {"y": 1 - y})
    for kv_head in range(2 * kv_heads):
        cols = pl.ds(kv_head * HD, HD)
        total = d_kv[own_rows, cols] + kv_recv[:, cols].astype(F32)
        if kv_head < kv_heads:
            total = turn_back(total)
        d_qkv[:, pl.ds(q_width + kv_head * HD, HD)] = total.astype(BF16)
    gate_plane.finish(gu.at[0])
    up_plane.finish(gu.at[1])
    keep_block = pltpu.make_async_copy(gu.at[:, z, c], blocks.at[z, c], s_block.at[z, c])
    keep_block.start()
    for k in range(NZ * NC - 1):
        step = k + 1
        zp, cp = (z + step // NC) % NZ, (c + step) % NC
        wires.send(gu.at[:, zp, cp], blocks.at[z, c], s_block.at[z, c], {"z": zp, "c": cp})
    fetch(0, qkv_width).wait()
    for_in = weights[...].reshape(wide, qkv_width)
    d_first = dot_nt(d_qkv[...], for_in)
    normed = x32 * rescale
    scaled = d_first * gain[...]
    d_x = rescale * (scaled - normed * jnp.mean(scaled * normed, axis=-1, keepdims=True))
    out_in[...] = (mid[...] + d_x).astype(BF16)
    first_term = (d_first * normed).astype(BF16)
    lane = lax.broadcasted_iota(jnp.int32, (rows, HD), 1)
    pick_one = (lane == 0).astype(F32).astype(BF16)
    pick_two = (lane == 1).astype(F32).astype(BF16)
    bias_sum = jnp.sum(d_qkv[...].astype(F32), axis=0, keepdims=True)
    top = lax.broadcasted_iota(jnp.int32, (shard, HD), 0) == 0
    wide_bias = jnp.concatenate([bias_sum, bias_sum[:, :HD]], axis=1)
    for yq in range(2):
        for h in range(2):
            i = yq * 2 + h
            cols = slice(i * tile, (i + 1) * tile)
            fill(term_q, yq, h, 0, dot_tn(first_in[:, cols], d_qkv[...]))
            tail = dot_tn(first_term[:, cols], pick_one) + dot_tn(gain_term[:, cols], pick_two)
            for zi in range(n):
                for xq in range(nx):
                    for cq in range(NC):
                        part = ((zi * nx + xq) * NC + cq) * shard
                        place_at = i * (tile // shard) + (zi * nx + xq) * NC + cq
                        first = place_at * b_rows
                        base = (first // HD) * HD
                        bias = wide_bias[:, base : base + HD]
                        bias = pltpu.roll(
                            jnp.broadcast_to(bias, (8, HD)), (HD // 2 - (first - base)) % HD, 1
                        )[:1]
                        keep = lax.broadcasted_iota(jnp.int32, (shard, HD), 1) >= HD // 2
                        mixed = tail[part : part + shard] + jnp.where(top & keep, bias, 0.0)
                        term_q[yq, h * n + zi, xq, cq, :, qkv_width:] = mixed.astype(BF16)
            over(1, term_q, sib_q, yq, h)
    combine(1, term_q, sib_q)
    q_planes = planes(term_q, 24)
    for plane in q_planes:
        plane.begin()
    for plane in o_planes:
        plane.relay()
    for plane in q_planes:
        plane.relay()

    def along_line(i, first, width, pair):
        cols = pl.ds(first, width)
        pair[0].finish(line_sum.at[halves[0], :, cols])
        pair[1].finish(line_sum.at[halves[1], :, cols])
        for k in range(NZ - 1):
            zp, j = (z + k + 1) % NZ, NZ - 2 - k
            wires.send(
                line_sum.at[zp, :, cols], line_in.at[j, :, cols], s_line.at[i, j], {"z": zp}
            )

    q_all = qkv_width + HD
    along_line(0, q_all, wide, o_planes)
    along_line(1, 0, q_all, q_planes)
    keep_block.wait()
    for k in range(NZ * NC - 1):
        step = k + 1
        zp, cp = (z + step // NC) % NZ, (c + step) % NC
        wires.arrived(blocks.at[zp, cp], s_block.at[zp, cp], sib)
    fs = blocks.shape[-1] // (2 * nx)
    for m, out in enumerate((out_gate, out_up)):
        for zq, cq, run, first in segments(nx, fs):
            out[:, first : first + fs] = blocks[zq, cq, m, :, run : run + fs]

    def last(i, out, first, width):
        if i is not None:
            begin, size = (q_all, wide) if i == 0 else (0, q_all)
            for j in range(NZ - 1):
                wires.arrived(line_in.at[j, :, pl.ds(begin, size)], s_line.at[i, j], sib)
        columns = slice(first, first + width)
        total = line_sum[z, :, columns].astype(F32)
        for j in range(NZ - 1):
            total = total + line_in[j, :, columns].astype(F32)
        out[...] = total

    last(0, out_o, q_all, wide)
    last(1, out_q, 0, q_width)
    last(None, out_k, q_width, key_width)
    last(None, out_v, q_width + key_width, key_width)
    last(None, out_tail, qkv_width, HD)
    for sign in (1, -1):
        pl.when(z > 0 if sign > 0 else z < NZ - 1)(lambda: landed(landing(sign, 0)))
        pl.when(inside(sign, 1))(toward(sign, 1).wait_send)
    wires.finish()


def back(ny, nx, b_rows, gate, up, ao, kept, given, args, collective_id):
    hbm = pl.BlockSpec(memory_space=pl.ANY)
    vmem = pl.BlockSpec(memory_space=pltpu.VMEM)
    mid, branch, tokens, gain, attn, query, kv, mask, turn_c, turn_s, gain_term = args
    dma = pltpu.SemaphoreType.DMA
    shard = ao.shape[1]
    block = gate.shape[4:]
    rows, wide = branch.shape
    q_width = query.shape[1]
    key_width = kv.shape[1] // 2
    qkv_width = q_width + 2 * key_width
    q_all = qkv_width + HD
    spread = block[1] * NZ * NC
    one_plane = (nx - 1) * 2 + 1 + nx + (nx - 1)
    sends = 3 * one_plane + 8 + 1 + 7 + 3 * (NZ - 1)
    slot_o, slot_q = (NZ // 2, shard, wide), (NZ // 2, shard, q_all)
    gate_slot = (NZ, NC) + block
    place_all = (ny, NZ, nx, NC, shard)
    shapes = [(shard, q_width), (shard, key_width), (shard, key_width), (shard, wide), (shard, HD)]
    return pl.pallas_call(
        lambda *refs: back_kernel(nx, key_width, b_rows, *refs),
        name="back",
        cost_estimate=pl.CostEstimate(
            flops=100_000_000_000, bytes_accessed=100_000_000, transcendentals=0
        ),
        out_shape=tuple(jax.ShapeDtypeStruct(shape, F32) for shape in shapes)
        + (jax.ShapeDtypeStruct((shard, spread), BF16),) * 2
        + (jax.ShapeDtypeStruct((rows, wide), BF16),)
        + (jax.ShapeDtypeStruct((NZ + 1, rows, wide), BF16),),
        in_specs=[hbm] * 5 + [vmem] * len(args),
        out_specs=(vmem,) * 8 + (hbm,),
        scratch_shapes=[
            dma((sends,)),
            pltpu.VMEM((ny * NZ * nx * NC, shard, qkv_width), BF16),
            pltpu.VMEM(place_all + (wide,), BF16),
            pltpu.VMEM(place_all + (q_all,), BF16),
            pltpu.VMEM((ny, NZ, nx, shard, wide), BF16),
            pltpu.VMEM((ny, NZ, nx, shard, q_all), BF16),
            pltpu.VMEM((NZ, shard, q_all + wide), BF16),
            pltpu.VMEM((NZ - 1, shard, q_all + wide), BF16),
            pltpu.VMEM((NZ, NC, 2) + block, BF16),
            pltpu.VMEM((2,) + gate_slot, BF16),
            pltpu.VMEM((rows, q_width), BF16),
            pltpu.VMEM((rows, qkv_width), BF16),
            pltpu.VMEM((2 * rows, 2 * key_width), F32),
            pltpu.VMEM((rows, 2 * key_width), BF16),
            pltpu.VMEM((rows, 2 * key_width), BF16),
            pltpu.VMEM((rows, wide), BF16),
            dma,
            dma((2, 2, 2)),
            dma((2, NZ - 1)),
            dma((NZ, NC)),
            dma,
            pltpu.VMEM((NZ - 1, rows, wide), BF16),
            dma((2,)),
            dma((NZ + 1,)),
            dma((2 * (NZ - 1),)),
        ]
        + plane_scratch(gate_slot, nx, ny)
        + plane_scratch(gate_slot, ny, nx)
        + plane_scratch(slot_o, nx, ny, True)
        + plane_scratch(slot_o, ny, nx, True)
        + plane_scratch(slot_q, nx, ny, True)
        + plane_scratch(slot_q, ny, nx, True),
        compiler_params=pltpu.CompilerParams(
            collective_id=collective_id, has_side_effects=True, vmem_limit_bytes=67_043_328
        ),
    )(gate, up, ao, kept, given, *args)


def make_body(ny, nx):
    def fused_layer(packed, x, seg_all, gate, up, down, grad_out, widths, b_rows):
        tok_rows = x.shape[0]
        length = seg_all.shape[0]
        seq_place = lax.axis_index("y")
        tok_pos = seq_place * tok_rows + jnp.arange(tok_rows)
        cos_tok, sin_tok = tables(tok_pos)
        all_pos = jnp.arange(length)
        seg_tok = lax.dynamic_slice(seg_all, (seq_place * tok_rows,), (tok_rows,))
        allowed = (tok_pos[:, None] >= all_pos[None, :]) & (seg_tok[:, None] == seg_all[None, :])
        mask = allowed.astype(F32)
        turn_c = jnp.concatenate([cos_tok, cos_tok], axis=1)
        turn_s = jnp.concatenate([sin_tok, -sin_tok], axis=1)
        made = forward(
            ny, nx, b_rows, packed, gate, up, down, grad_out, x, mask, turn_c, turn_s, widths, 0
        )
        gain_one, gain_two = made.gains_out[0:1], made.gains_out[1:2]
        middle = made.mid_out
        rescale_two = lax.rsqrt(jnp.mean(middle * middle, axis=-1, keepdims=True) + EPS)
        normed_two = middle * rescale_two
        scaled = made.dh * gain_two
        grad_mid = grad_out.astype(F32) + rescale_two * (
            scaled - normed_two * jnp.mean(scaled * normed_two, axis=-1, keepdims=True)
        )
        args = (
            grad_mid,
            grad_mid.astype(BF16),
            x,
            gain_one,
            made.o_out,
            made.q_out,
            made.kv_out,
            mask,
            turn_c,
            turn_s,
            (made.dh * normed_two).astype(BF16),
        )
        outs = back(
            ny,
            nx,
            b_rows,
            made.grad_g,
            made.grad_u,
            made.ao.reshape((-1,) + packed.shape),
            made.out_own,
            made.out_sib,
            args,
            1,
        )
        grad_q, grad_k, grad_v, grad_o, tail_sum, grad_gate_w, grad_up_w, grad_in, ring = outs
        z_place = lax.axis_index("z")
        first_row = z_place * tok_rows
        out_sum = jnp.where(z_place > 0, ring[0].astype(F32), 0.0)
        out_sum += jnp.where(z_place < NZ - 1, ring[2].astype(F32), 0.0)
        for half in (made.out_own, made.out_sib):
            out_sum += lax.dynamic_slice_in_dim(half, first_row, tok_rows).astype(F32)
        return (
            (middle + out_sum).astype(BF16)[None],
            grad_in[None],
            tail_sum[:, 0],
            grad_q,
            grad_k,
            grad_v,
            tail_sum[0, HD // 2 : HD // 2 + b_rows],
            grad_o,
            tail_sum[:, 1],
            grad_gate_w.astype(F32),
            grad_up_w.astype(F32),
            made.down_out.astype(F32),
        )

    def body(
        inputs,
        segment_ids,
        attn_gain,
        q_weight,
        k_weight,
        v_weight,
        qkv_bias,
        o_weight,
        mlp_gain,
        gate_weight,
        up_weight,
        down_weight,
        cotangent,
    ):
        tok_rows = inputs.shape[1]
        hidden_in = inputs[0].astype(F32)
        grad_out = cotangent[0]
        seg_all = segment_ids[0]
        length = seg_all.shape[0]
        seq_place = lax.axis_index("y")
        tok_pos = seq_place * tok_rows + jnp.arange(tok_rows)
        cos_tok, sin_tok = tables(tok_pos)
        query_width = q_weight.shape[1]
        key_width = k_weight.shape[1]
        kv_heads = key_width // HD
        q_heads = query_width // HD
        group = q_heads // kv_heads

        g_rows = attn_gain.shape[0]
        b_rows = qkv_bias.shape[0]
        qkv_width = query_width + 2 * key_width
        extra = jnp.concatenate(
            [
                attn_gain[:, None],
                mlp_gain[:, None],
                jnp.zeros((g_rows, HD // 2 - 2), BF16),
                jnp.broadcast_to(qkv_bias[None], (g_rows, b_rows)),
                jnp.zeros((g_rows, HD // 2 - b_rows), BF16),
            ],
            axis=1,
        )
        packed = jnp.concatenate([q_weight, k_weight, v_weight, o_weight, extra], axis=1)
        fused = g_rows % 16 == 0 and b_rows == HD // 2
        if fused:
            return fused_layer(
                packed,
                inputs[0],
                seg_all,
                gate_weight,
                up_weight,
                down_weight,
                grad_out,
                (query_width, key_width),
                b_rows,
            )
        attn_all, columns_all, down_all, grad_out_all = weight_gather(
            ny,
            nx,
            packed,
            gate_weight,
            up_weight,
            down_weight,
            grad_out,
            0,
        )
        full = attn_all.reshape(-1, packed.shape[1])
        full_qkv = full[:, :qkv_width]
        full_out = full[:, qkv_width : qkv_width + query_width]
        tail = attn_all[..., qkv_width + query_width :].astype(F32)
        gain_one = tail[..., 0].reshape(-1)
        gain_two = tail[..., 1].reshape(-1)
        bias = tail[..., 0, HD // 2 : HD // 2 + b_rows].reshape(-1)
        width = gate_weight.shape[1] // (NZ * NC)
        full_gate = columns_all[0].reshape(-1, width)
        full_up = columns_all[1].reshape(-1, width)
        full_down = down_all.reshape(width, -1)
        grad_out_all = grad_out_all.reshape(-1, grad_out.shape[1])

        rescale_one = lax.rsqrt(jnp.mean(hidden_in * hidden_in, axis=-1, keepdims=True) + EPS)
        normed_one = hidden_in * rescale_one
        input_one = (normed_one * gain_one).astype(BF16)
        qkv_pre = dot(input_one, full_qkv) + bias
        query = rotate(qkv_pre[:, :query_width], cos_tok, sin_tok).astype(BF16)
        key = rotate(qkv_pre[:, query_width : query_width + key_width], cos_tok, sin_tok)
        kv = jnp.concatenate([key, qkv_pre[:, query_width + key_width :]], axis=1).astype(BF16)
        kv_all = lax.all_gather(kv, "y", axis=0, tiled=True)
        key_heads = kv_all[:, :key_width].reshape(length, kv_heads, HD)
        value_heads = kv_all[:, key_width:].reshape(length, kv_heads, HD)
        query_heads = query.reshape(tok_rows, kv_heads, group, HD)
        score_scale = HD ** (-0.5)
        all_pos = jnp.arange(length)
        seg_tok = lax.dynamic_slice(seg_all, (seq_place * tok_rows,), (tok_rows,))
        allowed = (tok_pos[:, None] >= all_pos[None, :]) & (seg_tok[:, None] == seg_all[None, :])
        scores = (
            jnp.einsum("qkgd,pkd->kgqp", query_heads, key_heads, preferred_element_type=F32)
            * score_scale
        )
        masked = jnp.where(allowed[None, None], scores, MASKED)
        row_max = jnp.max(masked, axis=-1, keepdims=True)
        exponent = jnp.exp(masked - row_max)
        row_total = jnp.sum(exponent, axis=-1, keepdims=True)
        probs = exponent / row_total
        probs_low = probs.astype(BF16)
        mixture = jnp.einsum("kgqp,pkd->qkgd", probs_low, value_heads, preferred_element_type=F32)
        attn_tok = mixture.astype(BF16).reshape(tok_rows, query_width)
        middle = hidden_in + dot(attn_tok, full_out)

        rescale_two = lax.rsqrt(jnp.mean(middle * middle, axis=-1, keepdims=True) + EPS)
        normed_two = middle * rescale_two
        input_two = (normed_two * gain_two).astype(BF16)
        by_shard = (ny, NZ, nx, NC, g_rows, width)
        grad_input_two, out_part, part_gate, part_up, *downs = mlp(
            ny, nx, False, input_two, full_gate, full_up, full_down, grad_out_all, 1
        )
        grad_gain_two, grad_mid = norm_back(grad_input_two, normed_two, rescale_two, gain_two)
        grad_mid = grad_mid + grad_out.astype(F32)
        grad_branch = grad_mid.astype(BF16)
        grad_attn = dot_nt(grad_branch, full_out).astype(BF16)
        grad_heads = grad_attn.reshape(tok_rows, kv_heads, group, HD)
        grad_probs = jnp.einsum(
            "qkgd,pkd->kgqp", grad_heads, value_heads, preferred_element_type=F32
        )
        inner_sum = jnp.sum(probs * grad_probs, axis=-1, keepdims=True)
        grad_scores = (probs * (grad_probs - inner_sum)).astype(BF16)
        grad_query = (
            jnp.einsum("kgqp,pkd->qkgd", grad_scores, key_heads, preferred_element_type=F32)
            * score_scale
        ).reshape(tok_rows, query_width)
        grad_key = (
            jnp.einsum("kgqp,qkgd->pkd", grad_scores, query_heads, preferred_element_type=F32)
            * score_scale
        ).reshape(length, key_width)
        grad_value = jnp.einsum(
            "kgqp,qkgd->pkd", probs_low, grad_heads, preferred_element_type=F32
        ).reshape(length, key_width)
        grad_kv = jnp.concatenate([grad_key, grad_value], axis=1).astype(BF16)
        other = lax.dynamic_slice(
            grad_kv, ((1 - seq_place) * tok_rows, 0), (tok_rows, 2 * key_width)
        )
        own = lax.dynamic_slice(grad_kv, (seq_place * tok_rows, 0), (tok_rows, 2 * key_width))
        swapped = lax.ppermute(other, "y", [(0, 1), (1, 0)])
        grad_kv_tok = own.astype(F32) + swapped.astype(F32)
        grad_query_pre = rotate(grad_query, cos_tok, -sin_tok).astype(BF16)
        grad_key_pre = rotate(grad_kv_tok[:, :key_width], cos_tok, -sin_tok).astype(BF16)
        grad_value_pre = grad_kv_tok[:, key_width:].astype(BF16)
        grad_qkv = jnp.concatenate([grad_query_pre, grad_key_pre, grad_value_pre], axis=1)
        grad_qkv_sum = jnp.sum(grad_qkv.astype(F32), axis=0)
        grad_input_one = dot_nt(grad_qkv, full_qkv)
        grad_gain_one, grad_first = norm_back(grad_input_one, normed_one, rescale_one, gain_one)
        grad_total = grad_mid + grad_first
        shards = ny * NZ * nx * NC
        tail_grads = jnp.concatenate(
            [
                grad_gain_one[:, None],
                grad_gain_two[:, None],
                jnp.broadcast_to(
                    grad_qkv_sum.reshape(shards, 1, b_rows), (shards, g_rows, b_rows)
                ).reshape(-1, b_rows),
                jnp.zeros((shards * g_rows, HD - 2 - b_rows), F32),
            ],
            axis=1,
        )
        grad_attn_w = jnp.concatenate(
            [
                dot_tn(input_one, grad_qkv).astype(BF16),
                dot_tn(attn_tok, grad_branch).astype(BF16),
                tail_grads.astype(BF16),
            ],
            axis=1,
        )
        widths = (query_width, key_width, key_width, query_width, HD)
        pieces = (NZ, NC, tok_rows // 32, 32, hidden_in.shape[1])
        outs = last_scatter(
            ny,
            nx,
            grad_attn_w.reshape((ny, NZ, nx, NC, g_rows, -1)),
            widths,
            part_gate.reshape(by_shard),
            part_up.reshape(by_shard),
            downs[0].reshape((ny, nx) + down_weight.shape),
            out_part.reshape(pieces),
            3,
        )
        grad_q, grad_k, grad_v, grad_o, tail_sum = outs[:5]
        grad_gate_w, grad_up_w, grad_down_w, out_sum = outs[5:]
        output = (middle + out_sum.reshape(middle.shape)).astype(BF16)[None]
        return (
            output,
            grad_total.astype(BF16)[None],
            tail_sum[:, 0],
            grad_q,
            grad_k,
            grad_v,
            tail_sum[0, 2 : 2 + b_rows],
            grad_o,
            tail_sum[:, 1],
            grad_gate_w,
            grad_up_w,
            grad_down_w,
        )

    return body


def solution(mesh):
    ny = mesh.shape["seq"]
    nx = mesh.shape["fsdp"] // (NZ * NC)
    grid = Mesh(mesh.devices.reshape(ny, NZ, nx, NC), ALL)
    tokens = P(("z", "x", "c"), "y", None)
    rows = P(ALL, None)
    vec = P(ALL)
    return jax.shard_map(
        make_body(ny, nx),
        mesh=grid,
        in_specs=(
            tokens,
            P(("z", "x", "c"), None),
            vec,
            rows,
            rows,
            rows,
            vec,
            rows,
            vec,
            rows,
            rows,
            rows,
            tokens,
        ),
        out_specs=(tokens, tokens, vec, rows, rows, rows, vec, rows, vec, rows, rows, rows),
        check_vma=False,
    )
```
